32 devices in a mesh: rep: 2 (over y), fsdp: 4 (over z), seq: 4 (over x, core).
Axes of the slice: x: 2, y: 2, z: 4, core: 2. Of those that a mesh axis runs over, the one named last changes fastest.
Arguments:
- latents: bfloat16 [8, 1024, 1152], P(('rep', 'fsdp'), 'seq'), may hold values from -6 to 6
- cond: bfloat16 [8, 1152], P(('rep', 'fsdp')), may hold values from -6 to 6
- w_ada: bfloat16 [1152, 6912], P(('fsdp', 'seq')), may hold values from -0.25 to 0.25
- b_ada: bfloat16 [6912], P(('fsdp', 'seq')), may hold values from -3 to 3
- w_qkv: bfloat16 [1152, 3456], P(('fsdp', 'seq')), may hold values from -0.1875 to 0.1875
- b_qv: bfloat16 [2304], P(('fsdp', 'seq')), may hold values from -3 to 3
- w_out: bfloat16 [1152, 1152], P(('fsdp', 'seq')), may hold values from -1.5 to 1.5
- b_out: bfloat16 [1152], P(('fsdp', 'seq')), may hold values from -3 to 3
- w_one: bfloat16 [1152, 4608], P(('fsdp', 'seq')), may hold values from -0.1875 to 0.1875
- b_one: bfloat16 [4608], P(('fsdp', 'seq')), may hold values from -3 to 3
- w_two: bfloat16 [4608, 1152], P(('fsdp', 'seq')), may hold values from -0.09375 to 0.09375
- b_two: bfloat16 [1152], P(('fsdp', 'seq')), may hold values from -3 to 3
- cotangent: bfloat16 [8, 1024, 1152], P(('rep', 'fsdp'), 'seq'), may hold values from -6 to 6
Outputs:
- block_out: bfloat16 [8, 1024, 1152], P(('rep', 'fsdp'), 'seq')
- grad_latents: float32 [8, 1024, 1152], P(('rep', 'fsdp'), 'seq')
- grad_cond: float32 [8, 1152], P(('rep', 'fsdp'))
- grad_w_ada: float32 [1152, 6912], P(('fsdp', 'seq'))
- grad_b_ada: float32 [6912], P(('fsdp', 'seq'))
- grad_w_qkv: float32 [1152, 3456], P(('fsdp', 'seq'))
- grad_b_qv: float32 [2304], P(('fsdp', 'seq'))
- grad_w_out: float32 [1152, 1152], P(('fsdp', 'seq'))
- grad_b_out: float32 [1152], P(('fsdp', 'seq'))
- grad_w_one: float32 [1152, 4608], P(('fsdp', 'seq'))
- grad_b_one: float32 [4608], P(('fsdp', 'seq'))
- grad_w_two: float32 [4608, 1152], P(('fsdp', 'seq'))
- grad_b_two: float32 [1152], P(('fsdp', 'seq'))
The draws below stay inside these ranges and needn't reach their ends.
All inputs are finite; a program needn't handle non-finite values.
Results may differ from the reference program's by a relative error of at most 0.014.
The reference program's roundings to bfloat16 on the way count: a program that leaves them out, or rounds other values in their place, can miss the bound.
Values may be sent and summed in bfloat16 or wider, within the bound.
A program may use at most 448 MiB of HBM per device.

```python
import math
import jax
import jax.numpy as jnp
from jax import lax

D = 1152
H = 16
FF = 4608
SEQ_LEN = 1024
BATCH = 8


def spiked(values, rng, source, target, parts, factor):
    owner, partner = [(jnp.arange(values.shape[axis_at]) // (values.shape[axis_at] // parts)).reshape([-1 if axis == axis_at else 1 for axis in range(values.ndim)]) for axis_at in (source, target)]
    chosen = jax.random.permutation(rng, parts)[partner]
    strong = (owner == chosen) | (owner == (partner + parts // 2) % parts)
    return jnp.where(strong, factor * values, values)


def block_levels(own_key, shape, cuts, smallest, largest):
    factor_of, own = 1.0, jax.random.fold_in(own_key, 6)
    for axis_at, shards_of in cuts:
        heights = jnp.exp(jax.random.uniform(jax.random.fold_in(own, axis_at), (shards_of,), jnp.float32, smallest / len(cuts), largest / len(cuts)))
        factor_of = factor_of * jnp.repeat(heights, shape[axis_at] // shards_of).reshape([-1 if axis == axis_at else 1 for axis in range(len(shape))])
    return factor_of


def scatter_about(key, dims, spread, bound, cuts=(), dtype=jnp.bfloat16):
    loudness = block_levels(key, dims, cuts, -0.22, 0.18) if cuts else 1.0
    entries = jax.random.normal(key, dims, jnp.float32) * spread * loudness
    return jnp.minimum(jnp.maximum(entries, -bound), bound).astype(dtype)


def noise_with(rng, shape, deviation, bound, shards, heavy, held_as=jnp.bfloat16):
    array = deviation * jax.random.normal(rng, shape, jnp.float32)
    if shards:
        array = array * block_levels(rng, shape, shards, -0.22, 0.18)
    return jnp.clip(spiked(array, jax.random.fold_in(rng, 3), *heavy), -bound, bound).astype(held_as)


def setup_inputs(seed: int = 0) -> dict:
    key_list = jax.random.split(jax.random.key(seed), 14)
    return {
        "latents": scatter_about(key_list[0], (BATCH, SEQ_LEN, D), 1.0, 6.0, ((0, 8), (1, 4))),
        "cond": scatter_about(key_list[1], (BATCH, D), 1.0, 6.0, ((0, 8),)),
        "w_ada": noise_with(key_list[2], (D, 6 * D), D ** -0.5, 0.25, ((0, 16),), (0, 1, 16, 2.0)),
        "b_ada": scatter_about(key_list[3], (6 * D,), 0.5, 3.0, ((0, 16),)),
        "w_qkv": scatter_about(key_list[4], (D, 3 * D), D ** -0.5, 0.1875, ((0, 16),)),
        "b_qv": scatter_about(key_list[5], (2 * D,), 0.5, 3.0, ((0, 16),)),
        "w_out": scatter_about(key_list[6], (D, D), (D // 64) ** -0.5, 1.5, ((0, 16),)),
        "b_out": scatter_about(key_list[7], (D,), 0.5, 3.0, ((0, 16),)),
        "w_one": scatter_about(key_list[8], (D, FF), D ** -0.5, 0.1875, ((0, 16),)),
        "b_one": scatter_about(key_list[9], (FF,), 0.5, 3.0, ((0, 16),)),
        "w_two": scatter_about(key_list[10], (FF, D), FF ** -0.5, 0.09375, ((0, 16),)),
        "b_two": scatter_about(key_list[11], (D,), 0.5, 3.0, ((0, 16),)),
        "cotangent": scatter_about(key_list[12], (BATCH, SEQ_LEN, D), 1.0, 6.0, ((0, 8), (1, 4))),
    }


@jax.custom_vjp
def low(v):
    return lax.optimization_barrier(v.astype(jnp.bfloat16)).astype(jnp.float32)

@jax.custom_vjp
def low_back(v):
    return v

def low_keep(v):
    return (low(v), None)

def low_pass(kept, grad):
    return (grad,)

def back_keep(v):
    return (v, None)

def back_low(kept, grad):
    return (low(grad),)
low.defvjp(low_keep, low_pass)
low_back.defvjp(back_keep, back_low)
epsilon = 1e-06
gelu_coef = math.sqrt(2.0 / math.pi)

def matmul(left, right):
    return jnp.dot(left, right, precision=lax.Precision.HIGHEST)

def norm_rows(values):
    center = values - lax.optimization_barrier(jnp.mean(values, axis=-1, keepdims=True))
    return center * lax.rsqrt(lax.optimization_barrier(jnp.mean(center * center, axis=-1, keepdims=True)) + epsilon)

def gelu_tanh(values):
    inner = gelu_coef * (values + 0.044715 * values * values * values)
    return 0.5 * values * (1.0 + jnp.tanh(inner))

def attend(triple):
    queries, key_rows, val_rows = triple
    scores = low_back(matmul(queries, key_rows.T) * queries.shape[-1] ** (-0.5))
    highest = lax.optimization_barrier(jnp.max(scores, axis=-1, keepdims=True))
    raised = jnp.exp(scores - highest)
    attn_probs = low(raised / lax.optimization_barrier(jnp.sum(raised, axis=-1, keepdims=True)))
    return matmul(attn_probs, val_rows)

def forward(latent, cond_vec, w_ada, b_ada, w_qkv, b_qv, w_out, b_out, w_one, b_one, w_two, b_two):
    length, width = latent.shape
    head_count = H
    head_size = width // head_count
    silu_cond = low(cond_vec * jax.nn.sigmoid(cond_vec))
    modulation = low_back(matmul(silu_cond[None, :], w_ada)[0] + b_ada)
    shift_one, scale_one, gate_one, shift_two, scale_two, gate_two = jnp.split(modulation, 6)
    mixed_one = low(norm_rows(latent) * (1.0 + scale_one) + shift_one)
    bias_full = jnp.concatenate([b_qv[:width], jnp.zeros((width,), jnp.float32), b_qv[width:]])
    projected = low(low_back(matmul(mixed_one, w_qkv) + bias_full))
    split_heads = projected.reshape(length, 3, head_count, head_size).transpose(1, 2, 0, 3)
    attended = lax.map(jax.checkpoint(attend), (split_heads[0], split_heads[1], split_heads[2]))
    merged = low(low_back(attended.transpose(1, 0, 2).reshape(length, width)))
    branch_one = low_back(matmul(merged, w_out) + b_out)
    residual = latent + gate_one * branch_one
    mixed_two = low(norm_rows(residual) * (1.0 + scale_two) + shift_two)
    hidden_pre = low_back(matmul(mixed_two, w_one) + b_one)
    hidden_act = low(gelu_tanh(hidden_pre))
    branch_two = low_back(matmul(hidden_act, w_two) + b_two)
    return residual + gate_two * branch_two

def reference(latents, cond, w_ada, b_ada, w_qkv, b_qv, w_out, b_out, w_one, b_one, w_two, b_two, cotangent):
    weights = tuple((weight.astype(jnp.float32) for weight in (w_ada, b_ada, w_qkv, b_qv, w_out, b_out, w_one, b_one, w_two, b_two)))
    start_grads = tuple((jnp.zeros(weight.shape, jnp.float32) for weight in weights))

    def one_latent(totals, item):
        latent, cond_vec, grad_out = item
        result, pullback = jax.vjp(forward, latent.astype(jnp.float32), cond_vec.astype(jnp.float32), *weights)
        grads = pullback(grad_out.astype(jnp.float32))
        summed = tuple((total + grad for total, grad in zip(totals, grads[2:])))
        return (summed, (result.astype(jnp.bfloat16), grads[0], grads[1]))
    totals, outputs = lax.scan(one_latent, start_grads, (latents, cond, cotangent))
    return (outputs[0], outputs[1], outputs[2], totals[0], totals[1], totals[2], totals[3], totals[4], totals[5], totals[6], totals[7], totals[8], totals[9])
```

```python
import math

import jax
import jax.numpy as jnp
from jax import lax
from jax.experimental import pallas as pl
from jax.experimental.pallas import tpu as pltpu
from jax.sharding import PartitionSpec as P

H = 16
epsilon = 1e-06
gelu_coef = math.sqrt(2.0 / math.pi)
log2e = math.log2(math.e)
BF = jnp.bfloat16
F32 = jnp.float32
LANES = 128
VM = pl.BlockSpec(memory_space=pltpu.VMEM)
HB = pl.BlockSpec(memory_space=pl.ANY)
DMA = pltpu.SemaphoreType.DMA


def params(ident, mib):
    return pltpu.CompilerParams(
        collective_id=ident, has_side_effects=True, vmem_limit_bytes=mib * 1024 * 1024
    )


def remote(src, dst, send, recv, device):
    return pltpu.make_async_remote_copy(
        src_ref=src,
        dst_ref=dst,
        send_sem=send,
        recv_sem=recv,
        device_id=device,
        device_id_type=pl.DeviceIdType.MESH,
    )


def local(src, dst, sem):
    return pltpu.make_async_copy(src, dst, sem)


def await_bytes(like, sem):
    pltpu.make_async_copy(like, like, sem).wait()


def each(start, stop, body):
    def step(index, carry):
        body(index)
        return carry

    lax.fori_loop(start, stop, step, 0)


def greet(count, device_of):
    gate = pltpu.get_barrier_semaphore()
    each(
        1,
        count,
        lambda i: pl.semaphore_signal(
            gate, 1, device_id=device_of(i), device_id_type=pl.DeviceIdType.MESH
        ),
    )
    return count - 1


def greet_wait(count):
    pl.semaphore_wait(pltpu.get_barrier_semaphore(), count)


def norm_stats(values):
    center = values - jnp.mean(values, axis=-1, keepdims=True)
    inv_std = lax.rsqrt(jnp.mean(center * center, axis=-1, keepdims=True) + epsilon)
    return (center * inv_std, inv_std)


def norm_back(grad, normed, inv_std):
    return inv_std * (
        grad
        - jnp.mean(grad, axis=-1, keepdims=True)
        - normed * jnp.mean(grad * normed, axis=-1, keepdims=True)
    )


def mm(left, right):
    return jnp.dot(left, right, preferred_element_type=F32)


def mm_nt(left, right):
    return lax.dot_general(left, right, (((1,), (1,)), ((), ())), preferred_element_type=F32)


def mm_tn(left, right):
    return lax.dot_general(left, right, (((0,), (0,)), ((), ())), preferred_element_type=F32)


class Place:
    def __init__(self, sizes):
        self.R, self.F, self.S = sizes
        self.G = self.F * self.S
        self.y = lax.axis_index("rep")
        self.z = lax.axis_index("fsdp")
        self.s = lax.axis_index("seq")
        self.me = self.z * self.S + self.s
        self.mine = lax.rem(self.s, 2) == self.y

    def zs(self, i):
        return lax.rem(self.z + i, self.F)

    def zs_back(self, i):
        return lax.rem(self.z - i + self.F, self.F)

    def ss(self, i):
        return lax.rem(self.s + i, self.S)

    def ss_back(self, i):
        return lax.rem(self.s - i + self.S, self.S)

    def flip(self):
        return {"rep": 1 - self.y}


class ColumnGather:
    sems = (6,)

    def __init__(self, at, src, dst, sem):
        self.at, self.src, self.dst, self.sem = at, src, dst, sem

    @staticmethod
    def scratch(F):
        return DMA((7, F))

    def start(self):
        at, src, dst, sem = self.at, self.src, self.dst, self.sem
        local(src.at[at.s], dst.at[at.me], sem.at[0, 0]).start()

        def near(j):
            t = at.ss(j)
            remote(src.at[t], dst.at[at.me], sem.at[1, 0], sem.at[2, 0], {"seq": t}).start()

        each(1, at.S, near)

        @pl.when(at.mine)
        def _():
            def far(i):
                def one(j):
                    t = at.ss(j)
                    remote(
                        src.at[t],
                        dst.at[at.me],
                        sem.at[3, i],
                        sem.at[4, i],
                        {"fsdp": at.zs(i), "seq": t},
                    ).start()

                each(0, at.S, one)

            each(1, at.F, far)

    def half(self):
        return self.dst.at[pl.ds(0, self.at.S // 2)]

    def forward(self):
        at, dst, sem = self.at, self.dst, self.sem

        def far(i):
            await_bytes(self.half(), sem.at[4, i])

            def one(k):
                slot = at.zs_back(i) * at.S + 2 * k + at.y
                remote(
                    dst.at[slot], dst.at[slot], sem.at[5, i], sem.at[6, i], at.flip()
                ).start()

            each(0, at.S // 2, one)

        each(1, at.F, far)

    def finish(self):
        at, src, dst, sem = self.at, self.src, self.dst, self.sem
        local(src.at[at.s], dst.at[at.me], sem.at[0, 0]).wait()
        near = dst.at[pl.ds(0, at.S - 1)]
        await_bytes(near, sem.at[1, 0])
        await_bytes(near, sem.at[2, 0])

        @pl.when(at.mine)
        def _():
            each(1, at.F, lambda i: await_bytes(src, sem.at[3, i]))

        def far(i):
            await_bytes(self.half(), sem.at[5, i])
            await_bytes(self.half(), sem.at[6, i])

        each(1, at.F, far)


class RowGather:
    def __init__(self, at, src, dst, sem):
        self.at, self.src, self.dst, self.sem = at, src, dst, sem

    @staticmethod
    def scratch(F):
        return DMA((5, F))

    def start(self):
        at, src, dst, sem = self.at, self.src, self.dst, self.sem
        local(src, dst.at[at.z], sem.at[0, 0]).start()

        def far(i):
            remote(
                src.at[at.y], dst.at[at.z, at.y], sem.at[1, i], sem.at[2, i], {"fsdp": at.zs(i)}
            ).start()

        each(1, at.F, far)

    def forward(self):
        at, dst, sem = self.at, self.dst, self.sem

        def far(i):
            block = dst.at[at.zs_back(i), at.y]
            await_bytes(block, sem.at[2, i])
            remote(block, block, sem.at[3, i], sem.at[4, i], at.flip()).start()

        each(1, at.F, far)

    def finish(self):
        at, src, dst, sem = self.at, self.src, self.dst, self.sem
        local(src, dst.at[at.z], sem.at[0, 0]).wait()

        def far(i):
            block = dst.at[0, 0]
            await_bytes(block, sem.at[1, i])
            await_bytes(block, sem.at[3, i])
            await_bytes(block, sem.at[4, i])

        each(1, at.F, far)


class FullGather:
    def __init__(self, at, src, dst, sem):
        self.at, self.src, self.dst, self.sem = at, src, dst, sem

    @staticmethod
    def scratch(F):
        return DMA((5, F))

    def spread(self, i, block):
        at, sem = self.at, self.sem

        def one(j):
            remote(block, block, sem.at[3, i], sem.at[4, i], {"seq": at.ss(j)}).start()

        each(1, at.S, one)

    def start(self):
        at, src, dst, sem = self.at, self.src, self.dst, self.sem
        mine = dst.at[at.z, at.s]
        local(src, mine, sem.at[0, 0]).start()

        def far(i):
            remote(src, mine, sem.at[1, i], sem.at[2, i], {"fsdp": at.zs(i)}).start()

        each(1, at.F, far)

    def forward(self):
        at, src, dst, sem = self.at, self.src, self.dst, self.sem
        local(src, dst.at[at.z, at.s], sem.at[0, 0]).wait()
        self.spread(0, dst.at[at.z, at.s])

        def far(i):
            block = dst.at[at.zs_back(i), at.s]
            await_bytes(block, sem.at[2, i])
            self.spread(i, block)

        each(1, at.F, far)

    def finish(self):
        at, src, dst, sem = self.at, self.src, self.dst, self.sem
        others = dst.at[0, pl.ds(0, at.S - 1)]

        def far(i):
            await_bytes(others, sem.at[3, i])
            await_bytes(others, sem.at[4, i])

        each(0, at.F, far)
        each(1, at.F, lambda i: await_bytes(src, sem.at[1, i]))


def front_kernel(
    sizes,
    cond,
    w_ada,
    bias_slot,
    latents,
    w_qkv,
    w_one,
    w_two,
    w_out,
    bias_pack,
    mixed,
    mod,
    silu_all,
    pack_all,
    g_qkv,
    g_one,
    g_two,
    g_out,
    silu_src,
    part,
    parts_in,
    mod_src,
    mod_in,
    qkv_src,
    one_src,
    silu_sem,
    part_sem,
    mod_sem,
    pack_sem,
    qkv_sem,
    one_sem,
    two_sem,
    out_sem,
):
    at = Place(sizes)
    R, F, S, G = at.R, at.F, at.S, at.G
    D = latents.shape[1]
    C = D // S
    rows = silu_all.shape[2]
    block = one_src.shape[2] // F
    greet(G, lambda i: {"fsdp": lax.rem(at.me + i, G) // S, "seq": lax.rem(at.me + i, S)})
    greet(2 * F, lambda i: {"rep": lax.rem(at.y + i // F, 2), "fsdp": at.zs(i)})
    gate = pltpu.get_barrier_semaphore()
    pl.semaphore_wait(gate, G - 1 + 2 * F - 1)

    value = cond[...].astype(F32)
    silu = (value * jax.nn.sigmoid(value)).astype(BF).astype(F32)
    for g in range(G):
        silu_src[g] = silu[:, g * rows : (g + 1) * rows]
    slot = at.y * F + at.z

    def cond_copy(i):
        z_to = at.zs(i)
        return remote(
            silu_src.at[z_to * S + at.s],
            silu_all.at[slot],
            silu_sem.at[0, i],
            silu_sem.at[1, i],
            {"rep": lax.rem(at.y + i // F, 2), "fsdp": z_to},
        )

    each(1, 2 * F, lambda i: cond_copy(i).start())
    local(silu_src.at[at.me], silu_all.at[slot], silu_sem.at[0, 0]).start()

    def pack_copy(i):
        to = lax.rem(at.me + i, G)
        return remote(
            bias_pack,
            pack_all.at[at.me],
            pack_sem.at[0, 0],
            pack_sem.at[1, 0],
            {"fsdp": to // S, "seq": lax.rem(to, S)},
        )

    local(bias_pack, pack_all.at[at.me], pack_sem.at[2, 0]).start()
    each(1, G, lambda i: pack_copy(i).start())

    for t in range(S):
        for j in range(3):
            qkv_src[t, :, j * C : (j + 1) * C] = w_qkv[:, j * D + t * C : j * D + (t + 1) * C]
    qkv = ColumnGather(at, qkv_src, g_qkv, qkv_sem)
    one = ColumnGather(at, one_src, g_one, one_sem)
    two = RowGather(at, w_two, g_two, two_sem)
    out = FullGather(at, w_out, g_out, out_sem)
    qkv.start()
    out.start()
    for t in range(S):
        for f in range(F):
            col = (f * S + t) * block
            one_src[t, :, f * block : (f + 1) * block] = w_one[:, col : col + block]
    one.start()
    two.start()

    local(silu_src.at[at.me], silu_all.at[slot], silu_sem.at[0, 0]).wait()
    each(1, 2 * F, lambda i: cond_copy(i).wait())
    left = jnp.concatenate([silu_all[at.y * F + f] for f in range(F)], axis=0).astype(BF)
    sums = mm(left, w_ada[...]) + bias_slot[...]
    for f in range(F):
        for v in range(6):
            for t in range(S):
                col = v * D + t * C
                part[f * S + t, v : v + 1, :] = sums[f : f + 1, col : col + C]

    def part_copy(i):
        to = lax.rem(at.me + i, G)
        return remote(
            part.at[to],
            parts_in.at[at.me],
            part_sem.at[0, i],
            part_sem.at[1, i],
            {"fsdp": to // S, "seq": lax.rem(to, S)},
        )

    each(1, G, lambda i: part_copy(i).start())
    local(part.at[at.me], parts_in.at[at.me], part_sem.at[0, 0]).start()
    local(part.at[at.me], parts_in.at[at.me], part_sem.at[0, 0]).wait()
    each(1, G, lambda i: part_copy(i).wait())
    total = parts_in[0]
    for g in range(1, G):
        total = total + parts_in[g]
    mod_src[...] = total

    def mod_copy(i):
        return remote(
            mod_src, mod_in.at[at.s], mod_sem.at[0, i], mod_sem.at[1, i], {"seq": at.ss(i)}
        )

    each(1, S, lambda i: mod_copy(i).start())
    mod_in[at.s] = total
    each(1, S, lambda i: mod_copy(i).wait())
    for t in range(S):
        mod[:, t * C : (t + 1) * C] = mod_in[t]

    shift = mod[0:1, :]
    scale = mod[1:2, :]
    step = min(64, latents.shape[0])

    def norm(i):
        at_rows = pl.ds(i * step, step)
        normed, _ = norm_stats(latents[at_rows, :].astype(F32))
        mixed[at_rows, :] = (normed * (1.0 + scale) + shift).astype(BF)

    each(0, latents.shape[0] // step, norm)

    local(bias_pack, pack_all.at[at.me], pack_sem.at[2, 0]).wait()
    others = pack_all.at[pl.ds(0, G - 1)]
    await_bytes(others, pack_sem.at[0, 0])
    await_bytes(others, pack_sem.at[1, 0])
    qkv.forward()
    out.forward()
    one.forward()
    two.forward()
    qkv.finish()
    out.finish()
    one.finish()
    two.finish()


def front(sizes, cond, w_ada, bias_slot, latents, w_qkv, w_one, w_two, w_out, bias_pack):
    R, F, S = sizes
    G = F * S
    rows, width = w_out.shape
    C = width // S
    hidden = w_one.shape[1] // S
    length = latents.shape[0]
    shape = jax.ShapeDtypeStruct
    return pl.pallas_call(
        lambda *refs: front_kernel(sizes, *refs),
        name="front",
        out_shape=(
            shape((length, width), BF),
            shape((6, width), F32),
            shape((R * F, 1, rows), F32),
            shape((G,) + bias_pack.shape, F32),
            shape((G, rows, 3 * C), BF),
            shape((G, rows, hidden), BF),
            shape((F,) + w_two.shape, BF),
            shape((F, S) + w_out.shape, BF),
        ),
        in_specs=[VM, VM, VM, VM, VM, VM, HB, HB, VM],
        out_specs=(VM, VM, VM, VM, HB, HB, HB, HB),
        scratch_shapes=[
            pltpu.VMEM((G, 1, rows), F32),
            pltpu.VMEM((G, 6, C), F32),
            pltpu.VMEM((G, 6, C), F32),
            pltpu.VMEM((6, C), F32),
            pltpu.VMEM((S, 6, C), F32),
            pltpu.VMEM((S, rows, 3 * C), BF),
            pltpu.VMEM((S, rows, hidden), BF),
            DMA((2, 2 * F)),
            DMA((2, G)),
            DMA((2, S)),
            DMA((3, 1)),
            ColumnGather.scratch(F),
            ColumnGather.scratch(F),
            RowGather.scratch(F),
            FullGather.scratch(F),
        ],
        compiler_params=params(1, 40),
    )(cond, w_ada, bias_slot, latents, w_qkv, w_one, w_two, w_out, bias_pack)
def attend_kernel(
    sizes,
    mixed,
    w_qkv,
    bias,
    mod,
    latents,
    w_out,
    bias_out,
    mixed_all,
    heads,
    log_sums,
    merged,
    branch_one,
    mixed_two,
    val_flip,
    att,
    merged_in,
    mix_sem,
    att_sem,
):
    at = Place(sizes)
    S = at.S
    L, D = mixed.shape
    C = D // S
    T = S * L
    local_heads = H // S
    size = D // H
    greet_wait(greet(S, lambda i: {"seq": at.ss(i)}))

    def mix_copy(j):
        return remote(
            mixed,
            mixed_all.at[at.s],
            mix_sem.at[0, j],
            mix_sem.at[1, j],
            {"seq": lax.bitwise_xor(at.s, j)},
        )

    each(1, S, lambda j: mix_copy(j).start())
    mixed_all[at.s] = mixed[...]

    pad = jnp.zeros((L, LANES - size), BF)

    def project(j):
        t = lax.bitwise_xor(at.s, j)

        @pl.when(j > 0)
        def _():
            mix_copy(j).wait()

        rows = pl.ds(pl.multiple_of(t * L, L), L)
        done = (mm(mixed_all[t], w_qkv[...]) + bias[...]).astype(BF)
        for c in range(3 * local_heads):
            heads[c, rows, :] = jnp.concatenate([done[:, c * size : (c + 1) * size], pad], axis=1)

    each(0, S, project)

    for h in range(local_heads):
        val_flip[h] = heads[2 * local_heads + h].T

    def att_copy(j):
        t = lax.bitwise_xor(at.s, j)
        return remote(
            att.at[t], merged_in.at[at.s], att_sem.at[0, j], att_sem.at[1, j], {"seq": t}
        )

    factor = size ** (-0.5) * log2e

    def attention(index):
        j = S - 1 - index
        t = lax.bitwise_xor(at.s, j)
        rows = pl.ds(pl.multiple_of(t * L, L), L)
        for h in range(local_heads):
            scores = mm_nt(heads[local_heads + h], heads[h, rows, :]) * factor
            highest = jnp.max(scores, axis=0, keepdims=True)
            raised = jnp.exp2(scores - highest)
            summed = jnp.sum(raised, axis=0, keepdims=True)
            result = mm(val_flip[h], raised.astype(BF)) / summed
            log_sums[h, t] = highest + jnp.log2(summed)
            att[t, :, h * size : (h + 1) * size] = result.T[:, :size].astype(BF)

        @pl.when(j > 0)
        def _():
            att_copy(j).start()

    each(0, S, attention)
    merged_in[at.s] = att[at.s]
    each(1, S, lambda j: att_copy(j).wait())
    for t in range(S):
        merged[:, t * C : (t + 1) * C] = merged_in[t]

    gate_one = mod[2:3, :]
    shift = mod[3:4, :]
    scale = mod[4:5, :]
    step = min(64, L)

    def project_out(i):
        rows = pl.ds(pl.multiple_of(i * step, step), step)
        branch = mm(merged[rows, :], w_out[...]) + bias_out[...]
        branch_one[rows, :] = branch
        residual = latents[rows, :].astype(F32) + gate_one * branch
        normed, _ = norm_stats(residual)
        mixed_two[rows, :] = (normed * (1.0 + scale) + shift).astype(BF)

    each(0, L // step, project_out)


def attend(sizes, mixed, w_qkv, bias, mod, latents, w_out, bias_out):
    S = sizes[2]
    L, D = mixed.shape
    C = D // S
    T = S * L
    local_heads = H // S
    shape = jax.ShapeDtypeStruct
    return pl.pallas_call(
        lambda *refs: attend_kernel(sizes, *refs),
        name="attend",
        out_shape=(
            shape((S, L, D), BF),
            shape((3 * local_heads, T, LANES), BF),
            shape((local_heads, S, 1, L), F32),
            shape((L, D), BF),
            shape((L, D), F32),
            shape((L, D), BF),
        ),
        in_specs=[VM] * 7,
        out_specs=(VM,) * 6,
        scratch_shapes=[
            pltpu.VMEM((local_heads, LANES, T), BF),
            pltpu.VMEM((S, L, C), BF),
            pltpu.VMEM((S, L, C), BF),
            DMA((2, S)),
            DMA((2, S)),
        ],
        compiler_params=params(2, 60),
    )(mixed, w_qkv, bias, mod, latents, w_out, bias_out)


def mlp_kernel(
    sizes,
    mixed_two,
    cotangent,
    mod,
    w_one,
    bias_one,
    w_two,
    bias_two,
    branch_one,
    latents,
    w_out,
    merged,
    block_out,
    grad_resid,
    grad_heads,
    grad_w_one,
    grad_w_two,
    grad_w_out,
    grad_b_one,
    grad_b_two,
    grad_b_out,
    mod_sums,
    mix_all,
    grad_all,
    act_all,
    pre_all,
    branch_src,
    mix_src,
    branch_in,
    mix_in,
    grad_branch,
    in_sem,
    branch_sem,
    mix_sem,
):
    at = Place(sizes)
    S = at.S
    L, D = mixed_two.shape
    C = D // S
    hidden = w_one.shape[1]
    greet_wait(greet(S, lambda i: {"seq": at.ss(i)}))
    gate_one = mod[2:3, :]
    scale = mod[4:5, :]
    gate_two = mod[5:6, :]

    def peer(j):
        return lax.bitwise_xor(at.s, j)

    def mixed_copy(j):
        return remote(
            mixed_two, mix_all.at[at.s], in_sem.at[0, j], in_sem.at[1, j], {"seq": peer(j)}
        )

    def grad_copy(j):
        return remote(
            grad_all.at[at.s],
            grad_all.at[at.s],
            in_sem.at[2, j],
            in_sem.at[3, j],
            {"seq": peer(j)},
        )

    each(1, S, lambda j: mixed_copy(j).start())
    grad_all[at.s] = (gate_two * cotangent[...].astype(F32)).astype(BF)
    each(1, S, lambda j: grad_copy(j).start())
    mix_all[at.s] = mixed_two[...]

    def branch_copy(j):
        return remote(
            branch_src.at[peer(j)],
            branch_in.at[j],
            branch_sem.at[0, j],
            branch_sem.at[1, j],
            {"seq": peer(j)},
        )

    def mix_copy(j):
        return remote(
            mix_src.at[peer(j)],
            mix_in.at[j],
            mix_sem.at[0, j],
            mix_sem.at[1, j],
            {"seq": peer(j)},
        )

    def block(j):
        t = peer(j)

        @pl.when(j > 0)
        def _():
            mixed_copy(j).wait()
            grad_copy(j).wait()

        step = min(128, L)

        def part(i):
            rows = pl.ds(pl.multiple_of(i * step, step), step)
            pre = mm(mix_all[t, rows, :], w_one[...]) + bias_one[...]
            square = pre * pre
            inner = gelu_coef * (pre + 0.044715 * square * pre)
            tanh_val = jnp.tanh(inner)
            half = 0.5 * (1.0 + tanh_val)
            act = (pre * half).astype(BF)
            act_all[t, rows, :] = act
            slope = half + 0.5 * pre * (1.0 - tanh_val * tanh_val) * gelu_coef * (
                1.0 + 3.0 * 0.044715 * square
            )
            grad_pre = (mm_nt(grad_all[t, rows, :], w_two[...]) * slope).astype(BF)
            pre_all[t, rows, :] = grad_pre
            mix_src[t, rows, :] = mm_nt(grad_pre, w_one[...]).astype(BF)
            branch_src[t, rows, :] = mm(act, w_two[...]).astype(BF)

        each(0, L // step, part)

        @pl.when(j > 0)
        def _():
            mix_copy(j).start()
            branch_copy(j).start()

    each(0, S, block)

    def flat(ref, cols):
        return ref[:, :, cols].reshape(S * L, -1)

    step = 128 if hidden % 128 == 0 else hidden
    for i in range(hidden // step):
        cols = slice(i * step, (i + 1) * step)
        grads = pre_all[:, :, cols].reshape(S * L, step)
        grad_b_one[:, cols] = jnp.sum(grads.astype(F32), axis=0, keepdims=True)
    wide = 384 if hidden % 384 == 0 else hidden
    for i in range(hidden // wide):
        cols = slice(i * wide, (i + 1) * wide)
        grad_w_one[:, cols] = mm_tn(
            mix_all[...].reshape(S * L, D), pre_all[:, :, cols].reshape(S * L, wide)
        ).astype(BF)
        grad_w_two[cols, :] = mm_tn(
            act_all[:, :, cols].reshape(S * L, wide), grad_all[...].reshape(S * L, D)
        ).astype(BF)
    grad_b_two[...] = jnp.sum(grad_all[at.s].astype(F32), axis=0, keepdims=True)

    each(1, S, lambda j: mix_copy(j).wait())
    step = min(32, L)
    mod_sums[...] = jnp.zeros_like(mod_sums)
    grad_b_out[...] = jnp.zeros_like(grad_b_out)

    def gather(src, incoming, rows):
        total = src[at.s, rows, :].astype(F32)
        for j in range(1, S):
            total = total + incoming[j, rows, :].astype(F32)
        return total

    def back(i):
        rows = pl.ds(pl.multiple_of(i * step, step), step)
        grad_mixed = gather(mix_src, mix_in, rows)
        branch = branch_one[rows, :]
        residual = latents[rows, :].astype(F32) + gate_one * branch
        normed, inv_std = norm_stats(residual)
        grad_out = cotangent[rows, :].astype(F32)
        grad = grad_out + norm_back(grad_mixed * (1.0 + scale), normed, inv_std)
        grad_resid[rows, :] = grad
        low = (gate_one * grad).astype(BF)
        grad_branch[rows, :] = low
        mod_sums[2:3, :] += jnp.sum(grad * branch, axis=0, keepdims=True)
        mod_sums[3:4, :] += jnp.sum(grad_mixed, axis=0, keepdims=True)
        mod_sums[4:5, :] += jnp.sum(grad_mixed * normed, axis=0, keepdims=True)
        grad_b_out[...] += jnp.sum(low.astype(F32), axis=0, keepdims=True)

    each(0, L // step, back)
    grad_merged = mm_nt(grad_branch[...], w_out[...]).astype(BF)
    for t in range(S):
        grad_heads[t] = grad_merged[:, t * C : (t + 1) * C]
    wide = 384
    for i in range(D // wide):
        cols = slice(i * wide, (i + 1) * wide)
        grad_w_out[:, cols] = mm_tn(merged[...], grad_branch[:, cols]).astype(BF)

    each(1, S, lambda j: branch_copy(j).wait())

    def finish(i):
        rows = pl.ds(pl.multiple_of(i * step, step), step)
        branch_two = gather(branch_src, branch_in, rows) + bias_two[...]
        residual = latents[rows, :].astype(F32) + gate_one * branch_one[rows, :]
        block_out[rows, :] = (residual + gate_two * branch_two).astype(BF)
        grad_out = cotangent[rows, :].astype(F32)
        mod_sums[5:6, :] += jnp.sum(grad_out * branch_two, axis=0, keepdims=True)

    each(0, L // step, finish)


def mlp(sizes, mixed_two, cotangent, mod, w_one, b_one, w_two, b_two, branch, latents, w_out, merged):
    S = sizes[2]
    L, D = mixed_two.shape
    C = D // S
    hidden = w_one.shape[1]
    shape = jax.ShapeDtypeStruct
    tokens = (S, L, D)
    return pl.pallas_call(
        lambda *refs: mlp_kernel(sizes, *refs),
        name="mlp",
        out_shape=(
            shape((L, D), BF),
            shape((L, D), F32),
            shape((S, L, C), BF),
            shape((D, hidden), BF),
            shape((hidden, D), BF),
            shape((D, D), BF),
            shape((1, hidden), F32),
            shape((1, D), F32),
            shape((1, D), F32),
            shape((6, D), F32),
        ),
        in_specs=[VM] * 11,
        out_specs=(VM,) * 10,
        scratch_shapes=[
            pltpu.VMEM(tokens, BF),
            pltpu.VMEM(tokens, BF),
            pltpu.VMEM((S, L, hidden), BF),
            pltpu.VMEM((S, L, hidden), BF),
            pltpu.VMEM(tokens, BF),
            pltpu.VMEM(tokens, BF),
            pltpu.VMEM(tokens, BF),
            pltpu.VMEM(tokens, BF),
            pltpu.VMEM((L, D), BF),
            DMA((4, S)),
            DMA((2, S)),
            DMA((2, S)),
        ],
        compiler_params=params(3, 60),
    )(mixed_two, cotangent, mod, w_one, b_one, w_two, b_two, branch, latents, w_out, merged)


def attend_back_kernel(
    sizes,
    grad_heads,
    heads,
    log_sums,
    mixed_all,
    w_qkv,
    latents,
    mod,
    grad_resid,
    sums_in,
    grad_latents,
    grad_w_qkv,
    grad_b_qkv,
    mod_sums,
    grad_in,
    key_flip,
    key_grad,
    val_grad,
    grad_proj,
    mix_src,
    mix_in,
    in_sem,
    mix_sem,
):
    at = Place(sizes)
    S = at.S
    _, L, C = grad_heads.shape
    D = latents.shape[1]
    local_heads = H // S
    size = D // H
    greet_wait(greet(S, lambda i: {"seq": at.ss(i)}))

    def peer(j):
        return lax.bitwise_xor(at.s, j)

    def in_copy(j):
        return remote(
            grad_heads.at[peer(j)],
            grad_in.at[at.s],
            in_sem.at[0, j],
            in_sem.at[1, j],
            {"seq": peer(j)},
        )

    each(1, S, lambda j: in_copy(j).start())
    grad_in[at.s] = grad_heads[at.s]
    for h in range(local_heads):
        key_flip[h] = heads[local_heads + h].T
    key_grad[...] = jnp.zeros_like(key_grad)
    val_grad[...] = jnp.zeros_like(val_grad)
    factor = size ** (-0.5) * log2e
    score_scale = size ** (-0.5)
    pad = jnp.zeros((L, LANES - size), BF)

    def block(j):
        t = peer(j)

        @pl.when(j > 0)
        def _():
            in_copy(j).wait()

        rows = pl.ds(pl.multiple_of(t * L, L), L)
        for h in range(local_heads):
            query = heads[h, rows, :]
            grad = jnp.concatenate([grad_in[t, :, h * size : (h + 1) * size], pad], axis=1)
            scores = mm_nt(heads[local_heads + h], query) * factor
            probs = jnp.exp2(scores - log_sums[h, t])
            grad_probs = mm_nt(heads[2 * local_heads + h], grad)
            inner = jnp.sum(probs * grad_probs, axis=0, keepdims=True)
            grad_scores = (probs * (grad_probs - inner)).astype(BF)
            query_grad = mm(key_flip[h], grad_scores) * score_scale
            grad_proj[t, :, h * size : (h + 1) * size] = query_grad.T[:, :size].astype(BF)
            key_grad[h] += mm(grad_scores, query)
            val_grad[h] += mm(probs.astype(BF), grad)

    each(0, S, block)
    for h in range(local_heads):
        low = (key_grad[h] * score_scale)[:, :size].astype(BF)
        grad_proj[:, :, C + h * size : C + (h + 1) * size] = low.reshape(S, L, size)
        low = val_grad[h][:, :size].astype(BF)
        grad_proj[:, :, 2 * C + h * size : 2 * C + (h + 1) * size] = low.reshape(S, L, size)

    def mix_copy(j):
        return remote(
            mix_src.at[peer(j)],
            mix_in.at[j],
            mix_sem.at[0, j],
            mix_sem.at[1, j],
            {"seq": peer(j)},
        )

    def spread(index):
        j = S - 1 - index
        t = peer(j)
        mix_src[t] = mm_nt(grad_proj[t], w_qkv[...]).astype(BF)

        @pl.when(j > 0)
        def _():
            mix_copy(j).start()

    each(0, S, spread)
    wide = 288 if C % 288 == 0 else C
    tokens = mixed_all[...].reshape(S * L, D)
    grads = grad_proj[...].reshape(S * L, 3 * C)
    grad_w_qkv[...] = mm_tn(tokens, grads).astype(BF)
    grad_b_qkv[...] = jnp.sum(grads.astype(F32), axis=0, keepdims=True)

    each(1, S, lambda j: mix_copy(j).wait())
    step = min(32, L)
    mod_sums[...] = sums_in[...]
    scale = mod[1:2, :]

    def back(i):
        rows = pl.ds(pl.multiple_of(i * step, step), step)
        grad_mixed = mix_src[at.s, rows, :].astype(F32)
        for j in range(1, S):
            grad_mixed = grad_mixed + mix_in[j, rows, :].astype(F32)
        normed, inv_std = norm_stats(latents[rows, :].astype(F32))
        grad_latents[rows, :] = grad_resid[rows, :] + norm_back(
            grad_mixed * (1.0 + scale), normed, inv_std
        )
        mod_sums[0:1, :] += jnp.sum(grad_mixed, axis=0, keepdims=True)
        mod_sums[1:2, :] += jnp.sum(grad_mixed * normed, axis=0, keepdims=True)

    each(0, L // step, back)


def attend_back(sizes, grad_heads, heads, log_sums, mixed_all, w_qkv, latents, mod, grad_resid, sums):
    S, L, C = grad_heads.shape
    D = latents.shape[1]
    T = S * L
    local_heads = H // S
    shape = jax.ShapeDtypeStruct
    return pl.pallas_call(
        lambda *refs: attend_back_kernel(sizes, *refs),
        name="attend_back",
        out_shape=(
            shape((L, D), F32),
            shape((D, 3 * C), BF),
            shape((1, 3 * C), F32),
            shape((6, D), F32),
        ),
        in_specs=[VM] * 9,
        out_specs=(VM,) * 4,
        scratch_shapes=[
            pltpu.VMEM((S, L, C), BF),
            pltpu.VMEM((local_heads, LANES, T), BF),
            pltpu.VMEM((local_heads, T, LANES), F32),
            pltpu.VMEM((local_heads, T, LANES), F32),
            pltpu.VMEM((S, L, 3 * C), BF),
            pltpu.VMEM((S, L, D), BF),
            pltpu.VMEM((S, L, D), BF),
            DMA((2, S)),
            DMA((2, S)),
        ],
        compiler_params=params(4, 60),
    )(grad_heads, heads, log_sums, mixed_all, w_qkv, latents, mod, grad_resid, sums)
class ColumnScatter:
    def __init__(self, at, src, got, stage, inn, done, sem):
        self.at, self.src, self.got, self.stage = at, src, got, stage
        self.inn, self.done, self.sem = inn, done, sem

    @staticmethod
    def scratch(sizes, rows, cols):
        R, F, S = sizes
        return [
            pltpu.VMEM((F, S // 2, rows, cols), BF),
            pltpu.VMEM((F, S // 2, rows, cols), BF),
            pltpu.VMEM((F * S, rows, cols), BF),
            pltpu.VMEM((S, rows, cols), BF),
            DMA((6, F)),
        ]

    def start(self):
        at = self.at

        def far(i):
            z_to = at.zs(i)

            def one(k):
                remote(
                    self.src.at[z_to * at.S + 2 * k + 1 - at.y],
                    self.got.at[z_to, k],
                    self.sem.at[0, i],
                    self.sem.at[1, i],
                    at.flip(),
                ).start()

            each(0, at.S // 2, one)

        each(0, at.F, far)

    def scatter(self):
        at = self.at

        def far(index):
            i = lax.rem(index + 1, at.F)
            z_to = at.zs(i)
            await_bytes(self.got.at[0], self.sem.at[1, i])

            def one(k):
                s_to = 2 * k + at.y
                total = self.src[z_to * at.S + s_to].astype(F32) + self.got[z_to, k].astype(F32)
                low = total.astype(BF)
                home = (i == 0) & (s_to == at.s)
                self.stage[z_to, k] = low

                @pl.when(home)
                def _():
                    self.inn[at.me] = low

                @pl.when(jnp.logical_not(home))
                def _():
                    remote(
                        self.stage.at[z_to, k],
                        self.inn.at[at.me],
                        self.sem.at[2, i],
                        self.sem.at[3, 0],
                        {"fsdp": z_to, "seq": s_to},
                    ).start()

            each(0, at.S // 2, one)

        each(0, at.F, far)

    def total(self):
        at = self.at

        @pl.when(at.mine)
        def _():
            await_bytes(self.inn.at[pl.ds(0, at.G - 1)], self.sem.at[3, 0])

            def one(t):
                total = self.inn[t].astype(F32)
                for f in range(1, at.F):
                    total = total + self.inn[f * at.S + t].astype(F32)
                self.done[t] = total.astype(BF)

            each(0, at.S, one)
            remote(
                self.done, self.done, self.sem.at[4, 0], self.sem.at[5, 0], at.flip()
            ).start()

    def finish(self):
        at = self.at
        half = self.got.at[0]
        each(0, at.F, lambda i: await_bytes(half, self.sem.at[0, i]))
        each(1, at.F, lambda i: await_bytes(half, self.sem.at[2, i]))

        @pl.when(at.mine)
        def _():
            if at.S > 2:
                await_bytes(self.got.at[0, pl.ds(0, at.S // 2 - 1)], self.sem.at[2, 0])
            await_bytes(self.done, self.sem.at[4, 0])

        @pl.when(jnp.logical_not(at.mine))
        def _():
            await_bytes(half, self.sem.at[2, 0])
            await_bytes(self.done, self.sem.at[5, 0])


class RowScatter:
    def __init__(self, at, src, got, stage, inn, done, sem):
        self.at, self.src, self.got, self.stage = at, src, got, stage
        self.inn, self.done, self.sem = inn, done, sem

    @staticmethod
    def scratch(sizes, rows, cols):
        R, F, S = sizes
        return [
            pltpu.VMEM((F, rows, cols), BF),
            pltpu.VMEM((F, rows, cols), BF),
            pltpu.VMEM((F, rows, cols), BF),
            pltpu.VMEM((2, rows, cols), BF),
            DMA((6, F)),
        ]

    def start(self):
        at = self.at

        def far(i):
            z_to = at.zs(i)
            remote(
                self.src.at[z_to, 1 - at.y],
                self.got.at[z_to],
                self.sem.at[0, i],
                self.sem.at[1, i],
                at.flip(),
            ).start()

        each(0, at.F, far)

    def out_copy(self, i):
        at = self.at
        return remote(
            self.stage.at[at.zs(i)],
            self.inn.at[at.z],
            self.sem.at[2, i],
            self.sem.at[3, i],
            {"fsdp": at.zs(i)},
        )

    def scatter(self):
        at = self.at

        def far(index):
            i = lax.rem(index + 1, at.F)
            z_to = at.zs(i)
            await_bytes(self.got.at[0], self.sem.at[1, i])
            total = self.src[z_to, at.y].astype(F32) + self.got[z_to].astype(F32)
            self.stage[z_to] = total.astype(BF)

            @pl.when(i > 0)
            def _():
                self.out_copy(i).start()

        each(0, at.F, far)

    def total(self):
        at = self.at
        self.inn[at.z] = self.stage[at.z]
        each(1, at.F, lambda i: self.out_copy(i).wait())
        total = self.inn[0].astype(F32)
        for f in range(1, at.F):
            total = total + self.inn[f].astype(F32)
        self.done[at.y] = total.astype(BF)
        half = self.done.at[at.y]
        remote(half, half, self.sem.at[4, 0], self.sem.at[5, 0], at.flip()).start()

    def finish(self):
        at = self.at
        each(0, at.F, lambda i: await_bytes(self.got.at[0], self.sem.at[0, i]))
        await_bytes(self.done.at[0], self.sem.at[4, 0])
        await_bytes(self.done.at[0], self.sem.at[5, 0])


class FullScatter:
    def __init__(self, at, src, got, stage, inn, swap, sem):
        self.at, self.src, self.got, self.stage = at, src, got, stage
        self.inn, self.swap, self.sem = inn, swap, sem

    @staticmethod
    def scratch(sizes, rows, cols):
        R, F, S = sizes
        return [
            pltpu.VMEM((S, F, rows, cols), BF),
            pltpu.VMEM((F, rows, cols), BF),
            pltpu.VMEM((F, rows, cols), BF),
            pltpu.VMEM((2, rows, cols), BF),
            DMA((6, max(F, S))),
        ]

    def start(self):
        at = self.at

        def near(j):
            def one(f):
                remote(
                    self.src.at[f, at.ss(j)],
                    self.got.at[j, f],
                    self.sem.at[0, j],
                    self.sem.at[1, j],
                    {"seq": at.ss(j)},
                ).start()

            each(0, at.F, one)

        each(1, at.S, near)

    def out_copy(self, i):
        at = self.at
        return remote(
            self.stage.at[at.zs(i)],
            self.inn.at[at.z],
            self.sem.at[2, i],
            self.sem.at[3, i],
            {"fsdp": at.zs(i)},
        )

    def scatter(self):
        at = self.at

        def arrived(j):
            await_bytes(self.got.at[0], self.sem.at[0, j])
            await_bytes(self.got.at[0], self.sem.at[1, j])

        each(1, at.S, arrived)

        def far(i):
            z_to = at.zs(i)
            total = self.src[z_to, at.s].astype(F32)
            for j in range(1, at.S):
                total = total + self.got[j, z_to].astype(F32)
            self.stage[z_to] = total.astype(BF)

            @pl.when(i > 0)
            def _():
                self.out_copy(i).start()

        each(0, at.F, far)

    def total(self):
        at = self.at
        self.inn[at.z] = self.stage[at.z]
        each(1, at.F, lambda i: self.out_copy(i).wait())
        total = self.inn[0].astype(F32)
        for f in range(1, at.F):
            total = total + self.inn[f].astype(F32)
        self.swap[at.y] = total.astype(BF)
        mine = self.swap.at[at.y]
        remote(mine, mine, self.sem.at[4, 0], self.sem.at[5, 0], at.flip()).start()

    def finish(self):
        await_bytes(self.swap.at[0], self.sem.at[4, 0])
        await_bytes(self.swap.at[0], self.sem.at[5, 0])


class Tail:
    def __init__(self, at, sums, first_in, mod_src, mod_all, small_src, small_in, cond_src, cond_in, pieces, sem):
        self.at, self.sums, self.first_in = at, sums, first_in
        self.mod_src, self.mod_all = mod_src, mod_all
        self.small_src, self.small_in = small_src, small_in
        self.cond_src, self.cond_in, self.pieces, self.sem = cond_src, cond_in, pieces, sem

    @staticmethod
    def scratch(sizes, D, hidden, rows):
        R, F, S = sizes
        G = F * S
        C = D // S
        pack = 2 * D // G + 2 * rows + hidden // F
        wide = max(D, hidden, 3 * C)
        return [
            pltpu.VMEM((10, wide), F32),
            pltpu.VMEM((S, 10, wide), F32),
            pltpu.VMEM((6, D), BF),
            pltpu.VMEM((R * F, 6, D), BF),
            pltpu.VMEM((F, 1, pack), F32),
            pltpu.VMEM((R * F, 1, pack), F32),
            pltpu.VMEM((R * F, 1, rows), F32),
            pltpu.VMEM((G, 1, rows), F32),
            pltpu.VMEM((G, 1, pack), F32),
            DMA((8, max(S, 2 * F, G))),
        ]

    def first_copy(self, j):
        at = self.at
        return remote(
            self.sums, self.first_in.at[at.s], self.sem.at[0, j], self.sem.at[1, j], {"seq": at.ss(j)}
        )

    def start(self, mod_sums, b_one, b_two, b_out, b_qkv):
        sums = self.sums
        D = mod_sums.shape[1]
        hidden = b_one.shape[1]
        sums[...] = jnp.zeros_like(sums)
        sums[0:6, 0:D] = mod_sums[...]
        sums[6:7, 0:hidden] = b_one[...]
        sums[7:8, 0:D] = b_two[...]
        sums[8:9, 0:D] = b_out[...]
        sums[9:10, 0 : b_qkv.shape[1]] = b_qkv[...]
        each(1, self.at.S, lambda j: self.first_copy(j).start())
        self.first_in[self.at.s] = sums[...]

    def wide_copies(self, i):
        at = self.at
        slot = at.y * at.F + at.z
        device = {"rep": lax.rem(at.y + i // at.F, 2), "fsdp": at.zs(i)}
        return (
            remote(self.mod_src, self.mod_all.at[slot], self.sem.at[2, i], self.sem.at[3, i], device),
            remote(
                self.small_src.at[at.zs(i)],
                self.small_in.at[slot],
                self.sem.at[4, i],
                self.sem.at[5, i],
                device,
            ),
        )

    def middle(self, D, hidden, rows):
        at = self.at
        F, S, G = at.F, at.S, at.G
        C = D // S
        qv = 2 * D // G
        each(1, S, lambda j: self.first_copy(j).wait())
        total = self.first_in[0]
        for t in range(1, S):
            total = total + self.first_in[t]
        self.mod_src[...] = total[0:6, 0:D].astype(BF)
        for g in range(G):
            g_half = g % (G // 2)
            t = g_half // (F // 2)
            col = (g_half % (F // 2)) * qv + (2 * C if g >= G // 2 else 0)
            self.pieces[g, :, 0:qv] = self.first_in[t, 9:10, col : col + qv]
            self.pieces[g, :, qv : qv + rows] = total[8:9, g * rows : (g + 1) * rows]
            self.pieces[g, :, qv + rows : qv + 2 * rows] = total[7:8, g * rows : (g + 1) * rows]
        block = hidden // F
        for f in range(F):
            self.small_src[f, :, 0 : qv + 2 * rows] = self.pieces[f * S + at.s][:, 0 : qv + 2 * rows]
            self.small_src[f, :, qv + 2 * rows :] = self.sums[6:7, f * block : (f + 1) * block]

        def send(i):
            first, second = self.wide_copies(i)
            first.start()
            second.start()

        each(1, 2 * F, send)
        slot = at.y * F + at.z
        self.mod_all[slot] = self.mod_src[...]
        self.small_in[slot] = self.small_src[at.z]

    def cond_copy(self, i):
        at = self.at
        to = lax.rem(at.me + i, at.G)
        return remote(
            self.cond_src.at[at.y * at.F + to // at.S],
            self.cond_in.at[at.me],
            self.sem.at[6, i],
            self.sem.at[7, i],
            {"fsdp": to // at.S, "seq": lax.rem(to, at.S)},
        )

    def owners(self, silu_all, w_ada, grad_w_ada, grad_b_ada, flat_sum, b_pieces, small_out):
        at = self.at
        F, G = at.F, at.G
        D = self.mod_src.shape[1]
        width = grad_b_ada.shape[1]

        def arrive(i):
            first, second = self.wide_copies(i)
            first.wait()
            second.wait()

        each(1, 2 * F, arrive)
        cond = None
        for v in range(6):
            rows = self.mod_all[:, v, :]
            part = mm_nt(rows, w_ada[:, v * D : (v + 1) * D])
            cond = part if cond is None else cond + part
        for i in range(2 * F):
            self.cond_src[i] = cond[i : i + 1, :]
        each(1, G, lambda i: self.cond_copy(i).start())
        self.cond_in[at.me] = self.cond_src[at.y * F + at.z]
        silu = silu_all[:, 0, :].astype(BF)
        for v in range(6):
            rows = self.mod_all[:, v, :]
            grad_w_ada[:, v * D : (v + 1) * D] = mm_tn(silu, rows)
            flat_sum[:, v * D : (v + 1) * D] = jnp.sum(rows.astype(F32), axis=0, keepdims=True)
        for g in range(G):
            b_pieces[g] = flat_sum[:, g * width : (g + 1) * width]
        grad_b_ada[...] = b_pieces[at.me]
        total = self.small_in[0]
        for i in range(1, 2 * F):
            total = total + self.small_in[i]
        small_out[...] = total

    def finish(self, cond, grad_cond):
        at = self.at
        rows = self.cond_in.shape[2]
        each(1, at.G, lambda i: self.cond_copy(i).wait())
        for g in range(at.G):
            cols = slice(g * rows, (g + 1) * rows)
            value = cond[:, cols].astype(F32)
            gate = jax.nn.sigmoid(value)
            grad_cond[:, cols] = self.cond_in[g] * gate * (1.0 + value * (1.0 - gate))


def sums_kernel(sizes, *refs):
    at = Place(sizes)
    R, F, S, G = at.R, at.F, at.S, at.G
    qkv_g, one_g, two_g, out_g, mod_sums, b_one, b_two, b_out, b_qkv, silu_all, w_ada, cond = refs[:12]
    o_qkv, o_one, o_two, o_out, o_ada, o_b_ada, o_small, o_cond = refs[12:20]
    rest = list(refs[20:])
    qkv = ColumnScatter(at, qkv_g, *rest[0:5])
    one = ColumnScatter(at, one_g, *rest[5:10])
    two = RowScatter(at, two_g, *rest[10:15])
    out = FullScatter(at, out_g, *rest[15:20])
    tail = Tail(at, *rest[20:30])
    flat_sum, b_pieces = rest[30:32]
    rows, D = o_out.shape
    C = D // S
    hidden = one_g.shape[2]
    greet(G, lambda i: {"fsdp": lax.rem(at.me + i, G) // S, "seq": lax.rem(at.me + i, S)})
    greet(2 * F, lambda i: {"rep": lax.rem(at.y + i // F, 2), "fsdp": at.zs(i)})
    greet_wait(G - 1 + 2 * F - 1)
    tail.start(mod_sums, b_one, b_two, b_out, b_qkv)
    out.start()
    two.start()
    one.start()
    qkv.start()
    tail.middle(D, hidden, rows)
    out.scatter()
    tail.owners(silu_all, w_ada, o_ada, o_b_ada, flat_sum, b_pieces, o_small)
    two.scatter()
    one.scatter()
    qkv.scatter()
    tail.finish(cond, o_cond)
    out.total()
    two.total()
    one.total()
    qkv.total()
    out.finish()
    o_out[...] = out.swap[0].astype(F32) + out.swap[1].astype(F32)
    two.finish()
    for p in range(2):
        o_two[p] = two.done[p].astype(F32)
    one.finish()
    block = hidden // F
    for t in range(S):
        for f in range(F):
            col = (f * S + t) * block
            o_one[:, col : col + block] = one.done[t, :, f * block : (f + 1) * block].astype(F32)
    qkv.finish()
    for t in range(S):
        for j in range(3):
            o_qkv[:, j * D + t * C : j * D + (t + 1) * C] = qkv.done[
                t, :, j * C : (j + 1) * C
            ].astype(F32)


def sums(sizes, qkv_g, one_g, two_g, out_g, mod_sums, b_one, b_two, b_out, b_qkv, silu_all, w_ada, cond):
    R, F, S = sizes
    G = F * S
    D = cond.shape[1]
    rows = w_ada.shape[0]
    hidden = one_g.shape[2]
    width = w_ada.shape[1] // G
    shape = jax.ShapeDtypeStruct
    pack = 2 * D // G + 2 * rows + hidden // F
    return pl.pallas_call(
        lambda *refs: sums_kernel(sizes, *refs),
        name="sums",
        out_shape=(
            shape((rows, 3 * D), F32),
            shape((rows, hidden * S), F32),
            shape(two_g.shape[1:], F32),
            shape((rows, D), F32),
            shape(w_ada.shape, F32),
            shape((1, width), F32),
            shape((1, pack), F32),
            shape((1, D), F32),
        ),
        in_specs=[VM] * 12,
        out_specs=(VM,) * 8,
        scratch_shapes=ColumnScatter.scratch(sizes, rows, qkv_g.shape[2])
        + ColumnScatter.scratch(sizes, rows, hidden)
        + RowScatter.scratch(sizes, two_g.shape[2], D)
        + FullScatter.scratch(sizes, rows, D)
        + Tail.scratch(sizes, D, hidden, rows)
        + [pltpu.VMEM((1, w_ada.shape[1]), F32), pltpu.VMEM((G, 1, width), F32)],
        compiler_params=params(5, 62),
    )(qkv_g, one_g, two_g, out_g, mod_sums, b_one, b_two, b_out, b_qkv, silu_all, w_ada, cond)


def on_device(
    latents, cond, w_ada, b_ada, w_qkv, b_qv, w_out, b_out, w_one, b_one, w_two, b_two, cotangent
):
    sizes = R, F, S = tuple(lax.axis_size(name) for name in ("rep", "fsdp", "seq"))
    G = F * S
    _, L, D = latents.shape
    C = D // S
    hidden = w_one.shape[1] // S
    rows = w_ada.shape[0]
    qv = b_qv.shape[0]
    owner = lax.axis_index(("fsdp", "seq"))
    s = lax.axis_index("seq")
    width = b_ada.shape[0]
    bias_slot = lax.dynamic_update_slice(
        jnp.zeros((w_ada.shape[1],), F32), b_ada.astype(F32), (owner * width,)
    )[None]
    bias_pack = jnp.concatenate([b_qv, b_out, b_two, b_one]).astype(F32)[None]
    tokens = latents[0]
    two_rows = w_two.shape[0]
    mixed, mod, silu_all, packs, g_qkv, g_one, g_two, g_out = front(
        sizes,
        cond,
        w_ada,
        bias_slot,
        tokens,
        w_qkv,
        w_one,
        w_two.reshape(2, two_rows // 2, D),
        w_out,
        bias_pack,
    )
    packs = packs[:, 0]
    half = G // 2
    own = F // 2
    q_bias = lax.dynamic_slice_in_dim(packs[:half, :qv], s * own, own, 0).reshape(1, C)
    v_bias = lax.dynamic_slice_in_dim(packs[half:, :qv], s * own, own, 0).reshape(1, C)
    qkv_bias = jnp.concatenate([q_bias, jnp.zeros((1, C), F32), v_bias], axis=1)
    bias_out = packs[:, qv : qv + rows].reshape(1, D)
    bias_two = packs[:, qv + rows : qv + 2 * rows].reshape(1, D)
    bias_one = lax.dynamic_index_in_dim(
        packs[:, qv + 2 * rows :].reshape(F, S, -1), s, 1, False
    ).reshape(1, hidden)
    full_qkv = g_qkv.reshape(D, 3 * C)
    full_one = g_one.reshape(D, hidden)
    full_two = g_two.reshape(hidden, D)
    full_out = g_out.reshape(D, D)
    mixed_all, heads, log_sums, merged, branch_one, mixed_two = attend(
        sizes, mixed, full_qkv, qkv_bias, mod, tokens, full_out, bias_out
    )
    (
        block_out,
        grad_resid,
        grad_heads,
        one_g,
        two_g,
        out_g,
        grad_b_one,
        grad_b_two,
        grad_b_out,
        mod_sums,
    ) = mlp(
        sizes,
        mixed_two,
        cotangent[0],
        mod,
        full_one,
        bias_one,
        full_two,
        bias_two,
        branch_one,
        tokens,
        full_out,
        merged,
    )
    grad_latents, qkv_g, grad_b_qkv, mod_sums = attend_back(
        sizes, grad_heads, heads, log_sums, mixed_all, full_qkv, tokens, mod, grad_resid, mod_sums
    )
    o_qkv, o_one, o_two, o_out, o_ada, o_b_ada, o_small, o_cond = sums(
        sizes,
        qkv_g.reshape(G, rows, 3 * C),
        one_g.reshape(G, rows, hidden),
        two_g.reshape(F, 2, two_rows // 2, D),
        out_g.reshape(F, S, rows, D),
        mod_sums,
        grad_b_one,
        grad_b_two,
        grad_b_out,
        grad_b_qkv,
        silu_all,
        w_ada,
        cond,
    )
    small = o_small[0]
    return (
        block_out[None],
        grad_latents[None],
        o_cond,
        o_ada,
        o_b_ada[0],
        o_qkv,
        small[:qv],
        o_out,
        small[qv : qv + rows],
        o_one,
        small[qv + 2 * rows :],
        o_two.reshape(two_rows, D),
        small[qv + rows : qv + 2 * rows],
    )


def solution(mesh):
    owned = P(("fsdp", "seq"), None)
    owned_bias = P(("fsdp", "seq"))
    token_spec = P(("rep", "fsdp"), "seq", None)
    cond_spec = P(("rep", "fsdp"), None)
    weights = (owned, owned_bias) * 5
    in_specs = (token_spec, cond_spec) + weights + (token_spec,)
    out_specs = (token_spec, token_spec, cond_spec) + weights
    return jax.shard_map(
        on_device, mesh=mesh, in_specs=in_specs, out_specs=out_specs, check_vma=False
    )
```

```python
import math

import jax
import jax.numpy as jnp
from jax import lax
from jax.experimental import pallas as pl
from jax.experimental.pallas import tpu as pltpu
from jax.sharding import PartitionSpec as P

H = 16
epsilon = 1e-06
gelu_coef = math.sqrt(2.0 / math.pi)
log2e = math.log2(math.e)
BF = jnp.bfloat16
F32 = jnp.float32
LANES = 128
VM = pl.BlockSpec(memory_space=pltpu.VMEM)
HB = pl.BlockSpec(memory_space=pl.ANY)
DMA = pltpu.SemaphoreType.DMA


def params(ident, mib):
    return pltpu.CompilerParams(
        collective_id=ident, has_side_effects=True, vmem_limit_bytes=mib * 1024 * 1024
    )


def remote(src, dst, send, recv, device):
    return pltpu.make_async_remote_copy(
        src_ref=src,
        dst_ref=dst,
        send_sem=send,
        recv_sem=recv,
        device_id=device,
        device_id_type=pl.DeviceIdType.MESH,
    )


def local(src, dst, sem):
    return pltpu.make_async_copy(src, dst, sem)


def await_bytes(like, sem):
    pltpu.make_async_copy(like, like, sem).wait()


def each(start, stop, body):
    def step(index, carry):
        body(index)
        return carry

    lax.fori_loop(start, stop, step, 0)


def greet(count, device_of):
    gate = pltpu.get_barrier_semaphore()
    each(
        1,
        count,
        lambda i: pl.semaphore_signal(
            gate, 1, device_id=device_of(i), device_id_type=pl.DeviceIdType.MESH
        ),
    )
    return count - 1


def greet_wait(count):
    pl.semaphore_wait(pltpu.get_barrier_semaphore(), count)


def norm_stats(values):
    center = values - jnp.mean(values, axis=-1, keepdims=True)
    inv_std = lax.rsqrt(jnp.mean(center * center, axis=-1, keepdims=True) + epsilon)
    return (center * inv_std, inv_std)


def norm_back(grad, normed, inv_std):
    return inv_std * (
        grad
        - jnp.mean(grad, axis=-1, keepdims=True)
        - normed * jnp.mean(grad * normed, axis=-1, keepdims=True)
    )


def mm(left, right):
    return jnp.dot(left, right, preferred_element_type=F32)


def mm_nt(left, right):
    return lax.dot_general(left, right, (((1,), (1,)), ((), ())), preferred_element_type=F32)


def mm_tn(left, right):
    return lax.dot_general(left, right, (((0,), (0,)), ((), ())), preferred_element_type=F32)


class Place:
    def __init__(self, sizes):
        self.R, self.F, self.S = sizes
        self.G = self.F * self.S
        self.y = lax.axis_index("rep")
        self.z = lax.axis_index("fsdp")
        self.s = lax.axis_index("seq")
        self.me = self.z * self.S + self.s
        self.mine = lax.rem(self.s, 2) == self.y

    def zs(self, i):
        return lax.rem(self.z + i, self.F)

    def zs_back(self, i):
        return lax.rem(self.z - i + self.F, self.F)

    def ss(self, i):
        return lax.rem(self.s + i, self.S)

    def ss_back(self, i):
        return lax.rem(self.s - i + self.S, self.S)

    def flip(self):
        return {"rep": 1 - self.y}

    def peer(self, j):
        return lax.bitwise_xor(self.s, j)


class SeqGather:
    def __init__(self, at, dst, sem):
        self.at, self.dst, self.sem = at, dst, sem

    @staticmethod
    def scratch(S):
        return DMA((4, S))

    def direct(self, j):
        at, block = self.at, self.dst.at[self.at.s]
        return remote(block, block, self.sem.at[0, j], self.sem.at[1, j], {"seq": at.peer(j)})

    def handed(self, j):
        at = self.at
        block = self.dst.at[at.peer(j)]
        return remote(block, block, self.sem.at[2, j], self.sem.at[3, j], {"seq": at.peer(1)})

    def start(self):
        for j in range(3, self.at.S, 2):
            self.direct(j).start()
        self.direct(1).start()

    def arrive(self, index):
        @pl.when(index == 1)
        def _():
            self.direct(1).wait()

        if self.at.S > 2:

            @pl.when((index >= 2) & (lax.rem(index, 2) == 0))
            def _():
                self.direct(index + 1).wait()
                self.handed(index + 1).start()

            @pl.when((index >= 2) & (lax.rem(index, 2) == 1))
            def _():
                self.handed(index).wait()


def arrival(index):
    return jnp.where(index < 2, index, lax.bitwise_xor(index, 1))


class SeqSum:
    def __init__(self, at, src, near, inn, sem):
        self.at, self.src, self.near, self.inn, self.sem = at, src, near, inn, sem

    @staticmethod
    def scratch(S, rows, cols):
        return [
            pltpu.VMEM((S, rows, cols), BF),
            pltpu.VMEM((S // 2, rows, cols), BF),
            pltpu.VMEM((S // 2, rows, cols), BF),
            DMA((4, S)),
        ]

    def sibling(self, j):
        at = self.at
        return remote(
            self.src.at[at.peer(j)],
            self.near.at[j // 2],
            self.sem.at[0, j],
            self.sem.at[1, j],
            {"seq": at.peer(1)},
        )

    def direct(self, j):
        at = self.at
        return remote(
            self.src.at[at.peer(j)],
            self.inn.at[j // 2],
            self.sem.at[2, j],
            self.sem.at[3, j],
            {"seq": at.peer(j)},
        )

    def send(self, index):
        @pl.when((index == 1) | ((index >= 2) & (lax.rem(index, 2) == 0)))
        def _():
            self.sibling(lax.bitwise_or(index, 1)).start()

        if self.at.S > 2:

            @pl.when((index >= 2) & (lax.rem(index, 2) == 1))
            def _():
                j = index - 1
                self.sibling(index).wait()
                t = self.at.peer(j)
                step = min(64, self.src.shape[1])

                def add(i):
                    rows = pl.ds(pl.multiple_of(i * step, step), step)
                    both = self.src[t, rows, :].astype(F32) + self.near[j // 2, rows, :].astype(F32)
                    self.src[t, rows, :] = both.astype(BF)

                each(0, self.src.shape[1] // step, add)
                self.direct(j).start()

    def wait(self):
        self.sibling(1).wait()
        for j in range(2, self.at.S, 2):
            self.direct(j).wait()

    def total(self, rows):
        value = self.src[self.at.s, rows, :].astype(F32) + self.near[0, rows, :].astype(F32)
        for k in range(1, self.at.S // 2):
            value = value + self.inn[k, rows, :].astype(F32)
        return value


class ColumnGather:
    sems = (6,)

    def __init__(self, at, src, dst, sem):
        self.at, self.src, self.dst, self.sem = at, src, dst, sem

    @staticmethod
    def scratch(F):
        return DMA((7, F))

    def start(self):
        at, src, dst, sem = self.at, self.src, self.dst, self.sem
        local(src.at[at.s], dst.at[at.me], sem.at[0, 0]).start()

        def near(j):
            t = at.ss(j)
            remote(src.at[t], dst.at[at.me], sem.at[1, 0], sem.at[2, 0], {"seq": t}).start()

        each(1, at.S, near)

        @pl.when(at.mine)
        def _():
            def far(i):
                def one(j):
                    t = at.ss(j)
                    remote(
                        src.at[t],
                        dst.at[at.me],
                        sem.at[3, i],
                        sem.at[4, i],
                        {"fsdp": at.zs(i), "seq": t},
                    ).start()

                each(0, at.S, one)

            each(1, at.F, far)

    def half(self):
        return self.dst.at[pl.ds(0, self.at.S // 2)]

    def forward(self):
        at, dst, sem = self.at, self.dst, self.sem

        def far(i):
            await_bytes(self.half(), sem.at[4, i])

            def one(k):
                slot = at.zs_back(i) * at.S + 2 * k + at.y
                remote(
                    dst.at[slot], dst.at[slot], sem.at[5, i], sem.at[6, i], at.flip()
                ).start()

            each(0, at.S // 2, one)

        each(1, at.F, far)

    def finish(self):
        at, src, dst, sem = self.at, self.src, self.dst, self.sem
        local(src.at[at.s], dst.at[at.me], sem.at[0, 0]).wait()
        near = dst.at[pl.ds(0, at.S - 1)]
        await_bytes(near, sem.at[1, 0])
        await_bytes(near, sem.at[2, 0])

        @pl.when(at.mine)
        def _():
            each(1, at.F, lambda i: await_bytes(src, sem.at[3, i]))

        def far(i):
            await_bytes(self.half(), sem.at[5, i])
            await_bytes(self.half(), sem.at[6, i])

        each(1, at.F, far)


class RowGather:
    def __init__(self, at, src, dst, sem):
        self.at, self.src, self.dst, self.sem = at, src, dst, sem

    @staticmethod
    def scratch(F):
        return DMA((5, F))

    def start(self):
        at, src, dst, sem = self.at, self.src, self.dst, self.sem
        local(src, dst.at[at.z], sem.at[0, 0]).start()

        def far(i):
            remote(
                src.at[at.y], dst.at[at.z, at.y], sem.at[1, i], sem.at[2, i], {"fsdp": at.zs(i)}
            ).start()

        each(1, at.F, far)

    def forward(self):
        at, dst, sem = self.at, self.dst, self.sem

        def far(i):
            block = dst.at[at.zs_back(i), at.y]
            await_bytes(block, sem.at[2, i])
            remote(block, block, sem.at[3, i], sem.at[4, i], at.flip()).start()

        each(1, at.F, far)

    def finish(self):
        at, src, dst, sem = self.at, self.src, self.dst, self.sem
        local(src, dst.at[at.z], sem.at[0, 0]).wait()

        def far(i):
            block = dst.at[0, 0]
            await_bytes(block, sem.at[1, i])
            await_bytes(block, sem.at[3, i])
            await_bytes(block, sem.at[4, i])

        each(1, at.F, far)


class FullGather:
    def __init__(self, at, src, dst, sem):
        self.at, self.src, self.dst, self.sem = at, src, dst, sem

    @staticmethod
    def scratch(F):
        return DMA((5, F))

    def spread(self, i, block):
        at, sem = self.at, self.sem

        def one(j):
            remote(block, block, sem.at[3, i], sem.at[4, i], {"seq": at.ss(j)}).start()

        each(1, at.S, one)

    def start(self):
        at, src, dst, sem = self.at, self.src, self.dst, self.sem
        mine = dst.at[at.z, at.s]
        local(src, mine, sem.at[0, 0]).start()

        def far(i):
            remote(src, mine, sem.at[1, i], sem.at[2, i], {"fsdp": at.zs(i)}).start()

        each(1, at.F, far)

    def forward(self):
        at, src, dst, sem = self.at, self.src, self.dst, self.sem
        local(src, dst.at[at.z, at.s], sem.at[0, 0]).wait()
        self.spread(0, dst.at[at.z, at.s])

        def far(i):
            block = dst.at[at.zs_back(i), at.s]
            await_bytes(block, sem.at[2, i])
            self.spread(i, block)

        each(1, at.F, far)

    def finish(self):
        at, src, dst, sem = self.at, self.src, self.dst, self.sem
        others = dst.at[0, pl.ds(0, at.S - 1)]

        def far(i):
            await_bytes(others, sem.at[3, i])
            await_bytes(others, sem.at[4, i])

        each(0, at.F, far)
        each(1, at.F, lambda i: await_bytes(src, sem.at[1, i]))


def forward_kernel(sizes, *refs):
    at = Place(sizes)
    R, F, S, G = at.R, at.F, at.S, at.G
    cond, w_ada, bias_slot, latents, cotangent, w_qkv, w_one, bias_pack, w_two, w_out = refs[:10]
    mixed_all, heads, log_sums, merged, branch_one, mixed_two = refs[10:16]
    mod, silu_all, grad_all, full_qkv, full_out, bias_one, bias_two, g_one, g_two = refs[16:25]
    silu_src, part, parts_in, mod_src, mod_in, qkv_src, one_src, pack_all = refs[25:33]
    g_qkv, g_out, wide, bias_qkv, bias_out, val_flip, att, merged_in = refs[33:41]
    silu_sem, part_sem, mod_sem, pack_sem, qkv_sem, one_sem, two_sem, out_sem = refs[41:49]
    mixed_sem, grad_sem, att_sem = refs[49:52]
    L, D = latents.shape
    C = D // S
    T = S * L
    local_heads = H // S
    size = D // H
    rows_own = silu_all.shape[2]
    hidden = one_src.shape[2]
    block = hidden // F
    greet(G, lambda i: {"fsdp": lax.rem(at.me + i, G) // S, "seq": lax.rem(at.me + i, S)})
    greet(2 * F, lambda i: {"rep": lax.rem(at.y + i // F, 2), "fsdp": at.zs(i)})
    greet_wait(G - 1 + 2 * F - 1)

    value = cond[...].astype(F32)
    silu = (value * jax.nn.sigmoid(value)).astype(BF).astype(F32)
    for g in range(G):
        silu_src[g] = silu[:, g * rows_own : (g + 1) * rows_own]
    slot = at.y * F + at.z

    def cond_copy(i):
        z_to = at.zs(i)
        return remote(
            silu_src.at[z_to * S + at.s],
            silu_all.at[slot],
            silu_sem.at[0, i],
            silu_sem.at[1, i],
            {"rep": lax.rem(at.y + i // F, 2), "fsdp": z_to},
        )

    each(1, 2 * F, lambda i: cond_copy(i).start())
    silu_all[slot] = silu_src[at.me]

    def pack_copy(i):
        to = lax.rem(at.me + i, G)
        return remote(
            bias_pack,
            pack_all.at[at.me],
            pack_sem.at[0, 0],
            pack_sem.at[1, 0],
            {"fsdp": to // S, "seq": lax.rem(to, S)},
        )

    each(1, G, lambda i: pack_copy(i).start())
    pack_all[at.me] = bias_pack[...]

    qkv = ColumnGather(at, qkv_src, g_qkv, qkv_sem)
    one = ColumnGather(at, one_src, g_one, one_sem)
    two = RowGather(at, w_two, g_two, two_sem)
    out = FullGather(at, w_out, g_out, out_sem)
    for t in range(S):
        for j in range(3):
            qkv_src[t, :, j * C : (j + 1) * C] = w_qkv[:, j * D + t * C : j * D + (t + 1) * C]
    qkv.start()
    for t in range(S):
        for f in range(F):
            col = (f * S + t) * block
            one_src[t, :, f * block : (f + 1) * block] = w_one[:, col : col + block]

    each(1, 2 * F, lambda i: cond_copy(i).wait())
    left = jnp.concatenate([silu_all[at.y * F + f] for f in range(F)], axis=0).astype(BF)
    sums = mm(left, w_ada[...]) + bias_slot[...]
    for f in range(F):
        for v in range(6):
            for t in range(S):
                col = v * D + t * C
                part[f * S + t, v : v + 1, :] = sums[f : f + 1, col : col + C]

    def part_copy(i):
        to = lax.rem(at.me + i, G)
        return remote(
            part.at[to],
            parts_in.at[at.me],
            part_sem.at[0, i],
            part_sem.at[1, i],
            {"fsdp": to // S, "seq": lax.rem(to, S)},
        )

    each(1, G, lambda i: part_copy(i).start())
    parts_in[at.me] = part[at.me]
    each(1, G, lambda i: part_copy(i).wait())
    total = parts_in[0]
    for g in range(1, G):
        total = total + parts_in[g]
    mod_src[...] = total

    def mod_copy(i):
        return remote(
            mod_src, mod_in.at[at.s], mod_sem.at[0, i], mod_sem.at[1, i], {"seq": at.ss(i)}
        )

    each(1, S, lambda i: mod_copy(i).start())
    mod_in[at.s] = total
    each(1, S, lambda i: mod_copy(i).wait())
    for t in range(S):
        mod[:, t * C : (t + 1) * C] = mod_in[t]

    step = min(64, L)

    def norm(i):
        at_rows = pl.ds(pl.multiple_of(i * step, step), step)
        normed, _ = norm_stats(latents[at_rows, :].astype(F32))
        mixed_all[at.s, at_rows, :] = (normed * (1.0 + mod[1:2, :]) + mod[0:1, :]).astype(BF)

    each(0, L // step, norm)
    gather = SeqGather(at, mixed_all, mixed_sem)
    gather.start()
    out.start()

    others = pack_all.at[pl.ds(0, G - 1)]
    await_bytes(others, pack_sem.at[0, 0])
    await_bytes(others, pack_sem.at[1, 0])
    qv = 2 * D // G
    own = F // 2
    bias_qkv[...] = jnp.zeros_like(bias_qkv)
    for i in range(own):
        bias_qkv[:, i * qv : (i + 1) * qv] = pack_all[at.s * own + i][:, 0:qv]
        bias_qkv[:, 2 * C + i * qv : 2 * C + (i + 1) * qv] = pack_all[G // 2 + at.s * own + i][
            :, 0:qv
        ]
    for g in range(G):
        cols = slice(g * rows_own, (g + 1) * rows_own)
        bias_out[:, cols] = pack_all[g][:, qv : qv + rows_own]
        bias_two[:, cols] = pack_all[g][:, qv + rows_own : qv + 2 * rows_own]
    for f in range(F):
        bias_one[:, f * block : (f + 1) * block] = pack_all[f * S + at.s][:, qv + 2 * rows_own :]

    qkv.forward()
    one.start()
    two.start()
    grad_all[at.s] = (mod[5:6, :] * cotangent[...].astype(F32)).astype(BF)
    grad_gather = SeqGather(at, grad_all, grad_sem)
    grad_gather.start()
    qkv.finish()

    def join(slabs, whole):
        cols = whole.shape[1]
        for g in range(G):
            wide[g * rows_own : (g + 1) * rows_own, 0:cols] = slabs(g).astype(F32)
        tall = 128 if D % 128 == 0 else D

        def cast(i):
            at_rows = pl.ds(pl.multiple_of(i * tall, tall), tall)
            whole[at_rows, :] = wide[at_rows, 0:cols].astype(BF)

        each(0, D // tall, cast)

    join(lambda g: g_qkv[g], full_qkv)

    pad = jnp.zeros((L, LANES - size), BF)

    def project(index):
        gather.arrive(index)
        t = at.peer(arrival(index))
        at_rows = pl.ds(pl.multiple_of(t * L, L), L)
        done = (mm(mixed_all[t], full_qkv[...]) + bias_qkv[...]).astype(BF)
        for c in range(3 * local_heads):
            heads[c, at_rows, :] = jnp.concatenate(
                [done[:, c * size : (c + 1) * size], pad], axis=1
            )

    each(0, S, project)
    out.forward()
    for h in range(local_heads):
        val_flip[h] = heads[2 * local_heads + h].T

    def att_copy(j):
        t = at.peer(j)
        return remote(
            att.at[t], merged_in.at[at.s], att_sem.at[0, j], att_sem.at[1, j], {"seq": t}
        )

    factor = size ** (-0.5) * log2e

    def attention(index):
        j = S - 1 - index
        t = at.peer(j)
        at_rows = pl.ds(pl.multiple_of(t * L, L), L)
        for h in range(local_heads):
            scores = mm_nt(heads[local_heads + h], heads[h, at_rows, :]) * factor
            highest = jnp.max(scores, axis=0, keepdims=True)
            raised = jnp.exp2(scores - highest)
            summed = jnp.sum(raised, axis=0, keepdims=True)
            result = mm(val_flip[h], raised.astype(BF)) / summed
            log_sums[h, t] = highest + jnp.log2(summed)
            att[t, :, h * size : (h + 1) * size] = result.T[:, :size].astype(BF)

        @pl.when(j > 0)
        def _():
            att_copy(j).start()

    each(0, S, attention)
    merged_in[at.s] = att[at.s]
    out.finish()
    join(lambda g: g_out[g // S, g % S], full_out)
    one.forward()
    each(1, S, lambda j: att_copy(j).wait())
    for t in range(S):
        merged[:, t * C : (t + 1) * C] = merged_in[t]

    def project_out(i):
        at_rows = pl.ds(pl.multiple_of(i * step, step), step)
        branch = mm(merged[at_rows, :], full_out[...]) + bias_out[...]
        branch_one[at_rows, :] = branch
        residual = latents[at_rows, :].astype(F32) + mod[2:3, :] * branch
        normed, _ = norm_stats(residual)
        mixed_two[at_rows, :] = (normed * (1.0 + mod[4:5, :]) + mod[3:4, :]).astype(BF)

    each(0, L // step, project_out)
    each(1, S, grad_gather.arrive)
    two.forward()
    one.finish()
    two.finish()


def forward(sizes, cond, w_ada, bias_slot, latents, cotangent, w_qkv, w_one, bias_pack, w_two, w_out):
    R, F, S = sizes
    G = F * S
    rows, D = w_out.shape
    L = latents.shape[0]
    T = S * L
    C = D // S
    local_heads = H // S
    hidden = w_one.shape[1] // S
    shape = jax.ShapeDtypeStruct
    return pl.pallas_call(
        lambda *refs: forward_kernel(sizes, *refs),
        name="forward",
        out_shape=(
            shape((S, L, D), BF),
            shape((3 * local_heads, T, LANES), BF),
            shape((local_heads, S, 1, L), F32),
            shape((L, D), BF),
            shape((L, D), F32),
            shape((L, D), BF),
            shape((6, D), F32),
            shape((R * F, 1, rows), F32),
            shape((S, L, D), BF),
            shape((D, 3 * C), BF),
            shape((D, D), BF),
            shape((1, hidden), F32),
            shape((1, D), F32),
            shape((G, rows, hidden), BF),
            shape((F,) + w_two.shape, BF),
        ),
        in_specs=[VM] * 8 + [HB] * 2,
        out_specs=(VM,) * 13 + (HB,) * 2,
        scratch_shapes=[
            pltpu.VMEM((G, 1, rows), F32),
            pltpu.VMEM((G, 6, C), F32),
            pltpu.VMEM((G, 6, C), F32),
            pltpu.VMEM((6, C), F32),
            pltpu.VMEM((S, 6, C), F32),
            pltpu.VMEM((S, rows, 3 * C), BF),
            pltpu.VMEM((S, rows, hidden), BF),
            pltpu.VMEM((G,) + bias_pack.shape, F32),
            pltpu.VMEM((G, rows, 3 * C), BF),
            pltpu.VMEM((F, S, rows, D), BF),
            pltpu.VMEM((D, max(D, 3 * C)), F32),
            pltpu.VMEM((1, 3 * C), F32),
            pltpu.VMEM((1, D), F32),
            pltpu.VMEM((local_heads, LANES, T), BF),
            pltpu.VMEM((S, L, C), BF),
            pltpu.VMEM((S, L, C), BF),
            DMA((2, 2 * F)),
            DMA((2, G)),
            DMA((2, S)),
            DMA((2, 1)),
            ColumnGather.scratch(F),
            ColumnGather.scratch(F),
            RowGather.scratch(F),
            FullGather.scratch(F),
            SeqGather.scratch(S),
            SeqGather.scratch(S),
            DMA((2, S)),
        ],
        compiler_params=params(1, 60),
    )(cond, w_ada, bias_slot, latents, cotangent, w_qkv, w_one, bias_pack, w_two, w_out)


def mlp_kernel(
    sizes,
    mixed_two,
    grad_all,
    cotangent,
    mod,
    w_one,
    bias_one,
    w_two,
    bias_two,
    branch_one,
    latents,
    w_out,
    merged,
    block_out,
    grad_resid,
    grad_heads,
    grad_w_one,
    grad_w_two,
    grad_w_out,
    grad_b_one,
    grad_b_two,
    grad_b_out,
    mod_sums,
    mix_all,
    act_all,
    pre_all,
    grad_branch,
    mixed_sem,
    *rest,
):
    branch_refs, mix_refs = rest[:4], rest[4:]
    at = Place(sizes)
    S = at.S
    L, D = mixed_two.shape
    C = D // S
    hidden = w_one.shape[1]
    greet_wait(greet(S, lambda i: {"seq": at.ss(i)}))
    gate_one = mod[2:3, :]
    scale = mod[4:5, :]
    gate_two = mod[5:6, :]

    mixed_gather = SeqGather(at, mix_all, mixed_sem)
    branch_sum = SeqSum(at, *branch_refs)
    mix_sum = SeqSum(at, *mix_refs)
    branch_src = branch_refs[0]
    mix_src = mix_refs[0]
    mix_all[at.s] = mixed_two[...]
    mixed_gather.start()

    def block(index):
        mixed_gather.arrive(index)
        t = at.peer(arrival(index))
        step = min(128, L)

        def part(i):
            rows = pl.ds(pl.multiple_of(i * step, step), step)
            pre = mm(mix_all[t, rows, :], w_one[...]) + bias_one[...]
            square = pre * pre
            inner = gelu_coef * (pre + 0.044715 * square * pre)
            tanh_val = jnp.tanh(inner)
            half = 0.5 * (1.0 + tanh_val)
            act = (pre * half).astype(BF)
            act_all[t, rows, :] = act
            slope = half + 0.5 * pre * (1.0 - tanh_val * tanh_val) * gelu_coef * (
                1.0 + 3.0 * 0.044715 * square
            )
            grad_pre = (mm_nt(grad_all[t, rows, :], w_two[...]) * slope).astype(BF)
            pre_all[t, rows, :] = grad_pre
            mix_src[t, rows, :] = mm_nt(grad_pre, w_one[...]).astype(BF)
            branch_src[t, rows, :] = mm(act, w_two[...]).astype(BF)

        each(0, L // step, part)

        mix_sum.send(index)
        branch_sum.send(index)

    each(0, S, block)

    step = 128 if hidden % 128 == 0 else hidden
    for i in range(hidden // step):
        cols = slice(i * step, (i + 1) * step)
        grads = pre_all[:, :, cols].reshape(S * L, step)
        grad_b_one[:, cols] = jnp.sum(grads.astype(F32), axis=0, keepdims=True)
    wide = 384 if hidden % 384 == 0 else hidden
    for i in range(hidden // wide):
        cols = slice(i * wide, (i + 1) * wide)
        grad_w_one[:, cols] = mm_tn(
            mix_all[...].reshape(S * L, D), pre_all[:, :, cols].reshape(S * L, wide)
        ).astype(BF)
        grad_w_two[cols, :] = mm_tn(
            act_all[:, :, cols].reshape(S * L, wide), grad_all[...].reshape(S * L, D)
        ).astype(BF)
    grad_b_two[...] = jnp.sum(grad_all[at.s].astype(F32), axis=0, keepdims=True)

    mix_sum.wait()
    step = min(32, L)
    mod_sums[...] = jnp.zeros_like(mod_sums)
    grad_b_out[...] = jnp.zeros_like(grad_b_out)

    def back(i):
        rows = pl.ds(pl.multiple_of(i * step, step), step)
        grad_mixed = mix_sum.total(rows)
        branch = branch_one[rows, :]
        residual = latents[rows, :].astype(F32) + gate_one * branch
        normed, inv_std = norm_stats(residual)
        grad_out = cotangent[rows, :].astype(F32)
        grad = grad_out + norm_back(grad_mixed * (1.0 + scale), normed, inv_std)
        grad_resid[rows, :] = grad
        low = (gate_one * grad).astype(BF)
        grad_branch[rows, :] = low
        mod_sums[2:3, :] += jnp.sum(grad * branch, axis=0, keepdims=True)
        mod_sums[3:4, :] += jnp.sum(grad_mixed, axis=0, keepdims=True)
        mod_sums[4:5, :] += jnp.sum(grad_mixed * normed, axis=0, keepdims=True)
        grad_b_out[...] += jnp.sum(low.astype(F32), axis=0, keepdims=True)

    each(0, L // step, back)
    grad_merged = mm_nt(grad_branch[...], w_out[...]).astype(BF)
    for t in range(S):
        grad_heads[t] = grad_merged[:, t * C : (t + 1) * C]
    wide = 384
    for i in range(D // wide):
        cols = slice(i * wide, (i + 1) * wide)
        grad_w_out[:, cols] = mm_tn(merged[...], grad_branch[:, cols]).astype(BF)

    branch_sum.wait()

    def finish(i):
        rows = pl.ds(pl.multiple_of(i * step, step), step)
        branch_two = branch_sum.total(rows) + bias_two[...]
        residual = latents[rows, :].astype(F32) + gate_one * branch_one[rows, :]
        block_out[rows, :] = (residual + gate_two * branch_two).astype(BF)
        grad_out = cotangent[rows, :].astype(F32)
        mod_sums[5:6, :] += jnp.sum(grad_out * branch_two, axis=0, keepdims=True)

    each(0, L // step, finish)


def mlp(sizes, mixed_two, *args):
    S = sizes[2]
    L, D = mixed_two.shape
    C = D // S
    hidden = args[3].shape[1]
    shape = jax.ShapeDtypeStruct
    tokens = (S, L, D)
    return pl.pallas_call(
        lambda *refs: mlp_kernel(sizes, *refs),
        name="mlp",
        out_shape=(
            shape((L, D), BF),
            shape((L, D), F32),
            shape((S, L, C), BF),
            shape((D, hidden), BF),
            shape((hidden, D), BF),
            shape((D, D), BF),
            shape((1, hidden), F32),
            shape((1, D), F32),
            shape((1, D), F32),
            shape((6, D), F32),
        ),
        in_specs=[VM] * 12,
        out_specs=(VM,) * 10,
        scratch_shapes=[
            pltpu.VMEM(tokens, BF),
            pltpu.VMEM((S, L, hidden), BF),
            pltpu.VMEM((S, L, hidden), BF),
            pltpu.VMEM((L, D), BF),
            SeqGather.scratch(S),
        ]
        + SeqSum.scratch(S, L, D)
        + SeqSum.scratch(S, L, D),
        compiler_params=params(3, 60),
    )(mixed_two, *args)


class ColumnScatter:
    def __init__(self, at, src, got, stage, inn, done, sem):
        self.at, self.src, self.got, self.stage = at, src, got, stage
        self.inn, self.done, self.sem = inn, done, sem

    @staticmethod
    def scratch(sizes, rows, cols):
        R, F, S = sizes
        return [
            pltpu.VMEM((F, S // 2, rows, cols), BF),
            pltpu.VMEM((F, S // 2, rows, cols), BF),
            pltpu.VMEM((F * S, rows, cols), BF),
            DMA((7, F)),
        ]

    def start(self):
        at = self.at

        def far(i):
            z_to = at.zs(i)

            def one(k):
                slot = z_to * at.S + 2 * k + at.y
                local(self.src.at[slot], self.stage.at[z_to, k], self.sem.at[6, i]).start()
                remote(
                    self.src.at[z_to * at.S + 2 * k + 1 - at.y],
                    self.got.at[z_to, k],
                    self.sem.at[0, i],
                    self.sem.at[1, i],
                    at.flip(),
                ).start()

            each(0, at.S // 2, one)

        each(0, at.F, far)

    def scatter(self):
        at = self.at

        def far(index):
            i = lax.rem(index + 1, at.F)
            z_to = at.zs(i)
            await_bytes(self.got.at[0], self.sem.at[1, i])
            await_bytes(self.got.at[0], self.sem.at[6, i])

            def one(k):
                s_to = 2 * k + at.y
                total = self.stage[z_to, k].astype(F32) + self.got[z_to, k].astype(F32)
                low = total.astype(BF)
                home = (i == 0) & (s_to == at.s)
                self.stage[z_to, k] = low

                @pl.when(home)
                def _():
                    self.inn[at.me] = low

                @pl.when(jnp.logical_not(home))
                def _():
                    remote(
                        self.stage.at[z_to, k],
                        self.inn.at[at.me],
                        self.sem.at[2, i],
                        self.sem.at[3, 0],
                        {"fsdp": z_to, "seq": s_to},
                    ).start()

            each(0, at.S // 2, one)

        each(0, at.F, far)

    def total(self):
        at = self.at

        @pl.when(at.mine)
        def _():
            await_bytes(self.inn.at[pl.ds(0, at.G - 1)], self.sem.at[3, 0])

            def one(t):
                total = self.inn[t].astype(F32)
                for f in range(1, at.F):
                    total = total + self.inn[f * at.S + t].astype(F32)
                self.done[t] = total.astype(BF)

            each(0, at.S, one)
            remote(
                self.done, self.done, self.sem.at[4, 0], self.sem.at[5, 0], at.flip()
            ).start()

    def finish(self):
        at = self.at
        half = self.got.at[0]
        each(0, at.F, lambda i: await_bytes(half, self.sem.at[0, i]))
        each(1, at.F, lambda i: await_bytes(half, self.sem.at[2, i]))

        @pl.when(at.mine)
        def _():
            if at.S > 2:
                await_bytes(self.got.at[0, pl.ds(0, at.S // 2 - 1)], self.sem.at[2, 0])
            await_bytes(self.done, self.sem.at[4, 0])

        @pl.when(jnp.logical_not(at.mine))
        def _():
            await_bytes(half, self.sem.at[2, 0])
            await_bytes(self.done, self.sem.at[5, 0])


class RowScatter:
    def __init__(self, at, src, got, stage, inn, done, sem):
        self.at, self.src, self.got, self.stage = at, src, got, stage
        self.inn, self.done, self.sem = inn, done, sem

    @staticmethod
    def scratch(sizes, rows, cols):
        R, F, S = sizes
        return [
            pltpu.VMEM((F, rows, cols), BF),
            pltpu.VMEM((F, rows, cols), BF),
            pltpu.VMEM((F, rows, cols), BF),
            DMA((7, F)),
        ]

    def start(self):
        at = self.at

        def far(i):
            z_to = at.zs(i)
            local(self.src.at[z_to, at.y], self.stage.at[z_to], self.sem.at[6, i]).start()
            remote(
                self.src.at[z_to, 1 - at.y],
                self.got.at[z_to],
                self.sem.at[0, i],
                self.sem.at[1, i],
                at.flip(),
            ).start()

        each(0, at.F, far)

    def out_copy(self, i):
        at = self.at
        return remote(
            self.stage.at[at.zs(i)],
            self.inn.at[at.z],
            self.sem.at[2, i],
            self.sem.at[3, i],
            {"fsdp": at.zs(i)},
        )

    def scatter(self):
        at = self.at

        def far(index):
            i = lax.rem(index + 1, at.F)
            z_to = at.zs(i)
            await_bytes(self.got.at[0], self.sem.at[1, i])
            await_bytes(self.got.at[0], self.sem.at[6, i])
            total = self.stage[z_to].astype(F32) + self.got[z_to].astype(F32)
            self.stage[z_to] = total.astype(BF)

            @pl.when(i > 0)
            def _():
                self.out_copy(i).start()

        each(0, at.F, far)

    def total(self):
        at = self.at
        self.inn[at.z] = self.stage[at.z]
        each(1, at.F, lambda i: self.out_copy(i).wait())
        total = self.inn[0].astype(F32)
        for f in range(1, at.F):
            total = total + self.inn[f].astype(F32)
        self.done[at.y] = total.astype(BF)
        half = self.done.at[at.y]
        remote(half, half, self.sem.at[4, 0], self.sem.at[5, 0], at.flip()).start()

    def finish(self):
        at = self.at
        each(0, at.F, lambda i: await_bytes(self.got.at[0], self.sem.at[0, i]))
        await_bytes(self.done.at[0], self.sem.at[4, 0])
        await_bytes(self.done.at[0], self.sem.at[5, 0])


class FullScatter:
    def __init__(self, at, src, got, stage, inn, swap, sem):
        self.at, self.src, self.got, self.stage = at, src, got, stage
        self.inn, self.swap, self.sem = inn, swap, sem

    @staticmethod
    def scratch(sizes, rows, cols):
        R, F, S = sizes
        return [
            pltpu.VMEM((S, F, rows, cols), BF),
            pltpu.VMEM((F, rows, cols), BF),
            pltpu.VMEM((F, rows, cols), BF),
            DMA((6, max(F, S))),
        ]

    def start(self):
        at = self.at

        def near(j):
            def one(f):
                remote(
                    self.src.at[f, at.ss(j)],
                    self.got.at[j, f],
                    self.sem.at[0, j],
                    self.sem.at[1, j],
                    {"seq": at.ss(j)},
                ).start()

            each(0, at.F, one)

        each(1, at.S, near)
        local(self.src.at[:, at.s], self.stage, self.sem.at[0, 0]).start()

    def out_copy(self, i):
        at = self.at
        return remote(
            self.stage.at[at.zs(i)],
            self.inn.at[at.z],
            self.sem.at[2, i],
            self.sem.at[3, i],
            {"fsdp": at.zs(i)},
        )

    def scatter(self):
        at = self.at

        def arrived(j):
            await_bytes(self.got.at[0], self.sem.at[0, j])
            await_bytes(self.got.at[0], self.sem.at[1, j])

        each(1, at.S, arrived)
        local(self.src.at[:, at.s], self.stage, self.sem.at[0, 0]).wait()

        def far(i):
            z_to = at.zs(i)
            total = self.stage[z_to].astype(F32)
            for j in range(1, at.S):
                total = total + self.got[j, z_to].astype(F32)
            self.stage[z_to] = total.astype(BF)

            @pl.when(i > 0)
            def _():
                self.out_copy(i).start()

        each(0, at.F, far)

    def total(self):
        at = self.at
        self.inn[at.z] = self.stage[at.z]
        each(1, at.F, lambda i: self.out_copy(i).wait())
        total = self.inn[0].astype(F32)
        for f in range(1, at.F):
            total = total + self.inn[f].astype(F32)
        self.swap[at.y] = total.astype(BF)
        mine = self.swap.at[at.y]
        remote(mine, mine, self.sem.at[4, 0], self.sem.at[5, 0], at.flip()).start()

    def finish(self):
        await_bytes(self.swap.at[0], self.sem.at[4, 0])
        await_bytes(self.swap.at[0], self.sem.at[5, 0])


class Tail:
    def __init__(self, at, mod_all, sums, first_in, mod_src, small_src, small_in, cond_src, cond_in, pieces, sem):
        self.at, self.sums, self.first_in = at, sums, first_in
        self.mod_src, self.mod_all = mod_src, mod_all
        self.small_src, self.small_in = small_src, small_in
        self.cond_src, self.cond_in, self.pieces, self.sem = cond_src, cond_in, pieces, sem

    @staticmethod
    def scratch(sizes, D, hidden, rows):
        R, F, S = sizes
        G = F * S
        C = D // S
        pack = 2 * D // G + 2 * rows + hidden // F
        wide = max(D, hidden, 3 * C)
        return [
            pltpu.VMEM((10, wide), F32),
            pltpu.VMEM((S, 10, wide), F32),
            pltpu.VMEM((6, D), BF),
            pltpu.VMEM((F, 1, pack), F32),
            pltpu.VMEM((R * F, 1, pack), F32),
            pltpu.VMEM((R * F, 1, rows), F32),
            pltpu.VMEM((G, 1, rows), F32),
            pltpu.VMEM((G, 1, pack), F32),
            DMA((8, max(S, 2 * F, G))),
        ]

    def first_copy(self, j):
        at = self.at
        return remote(
            self.sums, self.first_in.at[at.s], self.sem.at[0, j], self.sem.at[1, j], {"seq": at.ss(j)}
        )

    def start(self, mod_sums, b_one, b_two, b_out, b_qkv):
        sums = self.sums
        D = mod_sums.shape[1]
        hidden = b_one.shape[1]
        sums[...] = jnp.zeros_like(sums)
        sums[0:6, 0:D] = mod_sums[...]
        sums[6:7, 0:hidden] = b_one[...]
        sums[7:8, 0:D] = b_two[...]
        sums[8:9, 0:D] = b_out[...]
        sums[9:10, 0 : b_qkv.shape[1]] = b_qkv[...]
        each(1, self.at.S, lambda j: self.first_copy(j).start())
        self.first_in[self.at.s] = sums[...]

    def wide_copies(self, i):
        at = self.at
        slot = at.y * at.F + at.z
        device = {"rep": lax.rem(at.y + i // at.F, 2), "fsdp": at.zs(i)}
        return (
            remote(self.mod_src, self.mod_all.at[slot], self.sem.at[2, i], self.sem.at[3, i], device),
            remote(
                self.small_src.at[at.zs(i)],
                self.small_in.at[slot],
                self.sem.at[4, i],
                self.sem.at[5, i],
                device,
            ),
        )

    def middle(self, D, hidden, rows):
        at = self.at
        F, S, G = at.F, at.S, at.G
        C = D // S
        qv = 2 * D // G
        each(1, S, lambda j: self.first_copy(j).wait())
        total = self.first_in[0]
        for t in range(1, S):
            total = total + self.first_in[t]
        self.mod_src[...] = total[0:6, 0:D].astype(BF)
        for g in range(G):
            g_half = g % (G // 2)
            t = g_half // (F // 2)
            col = (g_half % (F // 2)) * qv + (2 * C if g >= G // 2 else 0)
            self.pieces[g, :, 0:qv] = self.first_in[t, 9:10, col : col + qv]
            self.pieces[g, :, qv : qv + rows] = total[8:9, g * rows : (g + 1) * rows]
            self.pieces[g, :, qv + rows : qv + 2 * rows] = total[7:8, g * rows : (g + 1) * rows]
        block = hidden // F
        for f in range(F):
            self.small_src[f, :, 0 : qv + 2 * rows] = self.pieces[f * S + at.s][:, 0 : qv + 2 * rows]
            self.small_src[f, :, qv + 2 * rows :] = self.sums[6:7, f * block : (f + 1) * block]

        def send(i):
            first, second = self.wide_copies(i)
            first.start()
            second.start()

        each(1, 2 * F, send)
        slot = at.y * F + at.z
        self.mod_all[slot] = self.mod_src[...]
        self.small_in[slot] = self.small_src[at.z]

    def cond_copy(self, i):
        at = self.at
        to = lax.rem(at.me + i, at.G)
        return remote(
            self.cond_src.at[at.y * at.F + to // at.S],
            self.cond_in.at[at.me],
            self.sem.at[6, i],
            self.sem.at[7, i],
            {"fsdp": to // at.S, "seq": lax.rem(to, at.S)},
        )

    def owners(self, w_ada, small_out):
        at = self.at
        F, G = at.F, at.G
        D = self.mod_src.shape[1]

        def arrive(i):
            first, second = self.wide_copies(i)
            first.wait()
            second.wait()

        each(1, 2 * F, arrive)
        cond = None
        for v in range(6):
            rows = self.mod_all[:, v, :]
            part = mm_nt(rows, w_ada[:, v * D : (v + 1) * D])
            cond = part if cond is None else cond + part
        for i in range(2 * F):
            self.cond_src[i] = cond[i : i + 1, :]
        each(1, G, lambda i: self.cond_copy(i).start())
        self.cond_in[at.me] = self.cond_src[at.y * F + at.z]
        total = self.small_in[0]
        for i in range(1, 2 * F):
            total = total + self.small_in[i]
        small_out[...] = total

    def finish(self, cond, grad_cond):
        at = self.at
        rows = self.cond_in.shape[2]
        each(1, at.G, lambda i: self.cond_copy(i).wait())
        for g in range(at.G):
            cols = slice(g * rows, (g + 1) * rows)
            value = cond[:, cols].astype(F32)
            gate = jax.nn.sigmoid(value)
            grad_cond[:, cols] = self.cond_in[g] * gate * (1.0 + value * (1.0 - gate))


def backward_kernel(sizes, *refs):
    at = Place(sizes)
    R, F, S, G = at.R, at.F, at.S, at.G
    grad_heads, heads, log_sums, mixed_all, w_qkv, latents, mod, grad_resid, sums_in = refs[:9]
    one_g, two_g, out_g, b_one, b_two, b_out, w_ada, cond = refs[9:17]
    grad_latents, o_qkv, o_one, o_two, o_out, o_mod, o_small, o_cond = refs[17:25]
    grad_in, key_flip, key_grad, val_grad, grad_proj, qkv_wide, qkv_g, mod_sums, b_qkv, in_sem = refs[25:35]
    rest = list(refs[35:])
    mix_sum = SeqSum(at, *rest[0:4])
    mix_src = rest[0]
    qkv = ColumnScatter(at, qkv_g, *rest[4:7], o_qkv, rest[7])
    one = ColumnScatter(at, one_g, *rest[8:11], o_one, rest[11])
    two = RowScatter(at, two_g, *rest[12:15], o_two, rest[15])
    out = FullScatter(at, out_g, *rest[16:19], o_out, rest[19])
    tail = Tail(at, o_mod, *rest[20:29])
    _, L, C = grad_heads.shape
    rows_own, D = o_out.shape[1:]
    hidden = one_g.shape[2]
    local_heads = H // S
    size = D // H
    greet(G, lambda i: {"fsdp": lax.rem(at.me + i, G) // S, "seq": lax.rem(at.me + i, S)})
    greet(2 * F, lambda i: {"rep": lax.rem(at.y + i // F, 2), "fsdp": at.zs(i)})
    greet_wait(G - 1 + 2 * F - 1)

    def in_copy(j):
        return remote(
            grad_heads.at[at.peer(j)],
            grad_in.at[at.s],
            in_sem.at[0, j],
            in_sem.at[1, j],
            {"seq": at.peer(j)},
        )

    each(1, S, lambda j: in_copy(j).start())
    two.start()
    out.start()
    one.start()
    grad_in[at.s] = grad_heads[at.s]
    for h in range(local_heads):
        key_flip[h] = heads[local_heads + h].T
    key_grad[...] = jnp.zeros_like(key_grad)
    val_grad[...] = jnp.zeros_like(val_grad)
    factor = size ** (-0.5) * log2e
    score_scale = size ** (-0.5)
    pad = jnp.zeros((L, LANES - size), BF)

    def block(j):
        t = at.peer(j)

        @pl.when(j > 0)
        def _():
            in_copy(j).wait()

        rows = pl.ds(pl.multiple_of(t * L, L), L)
        for h in range(local_heads):
            query = heads[h, rows, :]
            grad = jnp.concatenate([grad_in[t, :, h * size : (h + 1) * size], pad], axis=1)
            scores = mm_nt(heads[local_heads + h], query) * factor
            probs = jnp.exp2(scores - log_sums[h, t])
            grad_probs = mm_nt(heads[2 * local_heads + h], grad)
            inner = jnp.sum(probs * grad_probs, axis=0, keepdims=True)
            grad_scores = (probs * (grad_probs - inner)).astype(BF)
            query_grad = mm(key_flip[h], grad_scores) * score_scale
            grad_proj[t, :, h * size : (h + 1) * size] = query_grad.T[:, :size].astype(BF)
            key_grad[h] += mm(grad_scores, query)
            val_grad[h] += mm(probs.astype(BF), grad)

    each(0, S, block)
    for h in range(local_heads):
        low = (key_grad[h] * score_scale)[:, :size].astype(BF)
        grad_proj[:, :, C + h * size : C + (h + 1) * size] = low.reshape(S, L, size)
        low = val_grad[h][:, :size].astype(BF)
        grad_proj[:, :, 2 * C + h * size : 2 * C + (h + 1) * size] = low.reshape(S, L, size)

    def spread(index):
        t = at.peer(arrival(index))
        mix_src[t] = mm_nt(grad_proj[t], w_qkv[...]).astype(BF)
        mix_sum.send(index)

    each(0, S, lambda index: spread(lax.rem(index + 2, S)))
    grads = grad_proj[...].reshape(S * L, 3 * C)
    qkv_wide[...] = mm_tn(mixed_all[...].reshape(S * L, D), grads)
    for g in range(G):
        qkv_g[g] = qkv_wide[g * rows_own : (g + 1) * rows_own, :].astype(BF)
    qkv.start()
    b_qkv[...] = jnp.sum(grads.astype(F32), axis=0, keepdims=True)

    two.scatter()
    out.scatter()
    mix_sum.wait()
    step = min(32, L)
    mod_sums[...] = sums_in[...]
    scale = mod[1:2, :]

    def back(i):
        rows = pl.ds(pl.multiple_of(i * step, step), step)
        grad_mixed = mix_sum.total(rows)
        normed, inv_std = norm_stats(latents[rows, :].astype(F32))
        grad_latents[rows, :] = grad_resid[rows, :] + norm_back(
            grad_mixed * (1.0 + scale), normed, inv_std
        )
        mod_sums[0:1, :] += jnp.sum(grad_mixed, axis=0, keepdims=True)
        mod_sums[1:2, :] += jnp.sum(grad_mixed * normed, axis=0, keepdims=True)

    each(0, L // step, back)
    tail.start(mod_sums, b_one, b_two, b_out, b_qkv)
    one.scatter()
    tail.middle(D, hidden, rows_own)
    out.total()
    two.total()
    tail.owners(w_ada, o_small)
    qkv.scatter()
    one.total()
    tail.finish(cond, o_cond)
    qkv.total()
    out.finish()
    two.finish()
    one.finish()
    qkv.finish()


def backward(sizes, *args):
    R, F, S = sizes
    G = F * S
    grad_heads, latents = args[0], args[5]
    one_g, two_g, w_ada = args[9], args[10], args[15]
    _, L, C = grad_heads.shape
    D = latents.shape[1]
    T = S * L
    local_heads = H // S
    rows = w_ada.shape[0]
    hidden = one_g.shape[2]
    pack = 2 * D // G + 2 * rows + hidden // F
    shape = jax.ShapeDtypeStruct
    return pl.pallas_call(
        lambda *refs: backward_kernel(sizes, *refs),
        name="backward",
        out_shape=(
            shape((L, D), F32),
            shape((S, rows, 3 * C), BF),
            shape((S, rows, hidden), BF),
            shape(two_g.shape[1:], BF),
            shape((2, rows, D), BF),
            shape((R * F, 6, D), BF),
            shape((1, pack), F32),
            shape((1, D), F32),
        ),
        in_specs=[VM] * 9 + [HB] * 3 + [VM] * 5,
        out_specs=(VM,) * 8,
        scratch_shapes=[
            pltpu.VMEM((S, L, C), BF),
            pltpu.VMEM((local_heads, LANES, T), BF),
            pltpu.VMEM((local_heads, T, LANES), F32),
            pltpu.VMEM((local_heads, T, LANES), F32),
            pltpu.VMEM((S, L, 3 * C), BF),
            pltpu.VMEM((D, 3 * C), F32),
            pltpu.VMEM((G, rows, 3 * C), BF),
            pltpu.VMEM((6, D), F32),
            pltpu.VMEM((1, 3 * C), F32),
            DMA((2, S)),
        ]
        + SeqSum.scratch(S, L, D)
        + ColumnScatter.scratch(sizes, rows, 3 * C)
        + ColumnScatter.scratch(sizes, rows, hidden)
        + RowScatter.scratch(sizes, two_g.shape[2], D)
        + FullScatter.scratch(sizes, rows, D)
        + Tail.scratch(sizes, D, hidden, rows),
        compiler_params=params(4, 60),
    )(*args)


def assemble_kernel(sizes, qkv, one, two, out, mod_all, silu_all, o_qkv, o_one, o_two, o_out, o_ada, o_b_ada, flat, pieces):
    R, F, S = sizes
    G = F * S
    D = o_out.shape[1]
    C = D // S
    hidden = one.shape[2]
    o_out[...] = out[0].astype(F32) + out[1].astype(F32)
    for p in range(2):
        o_two[p] = two[p].astype(F32)
    block = hidden // F
    for t in range(S):
        for f in range(F):
            col = (f * S + t) * block
            o_one[:, col : col + block] = one[t, :, f * block : (f + 1) * block].astype(F32)
        for j in range(3):
            o_qkv[:, j * D + t * C : j * D + (t + 1) * C] = qkv[t, :, j * C : (j + 1) * C].astype(F32)
    silu = silu_all[:, 0, :].astype(BF)
    width = o_b_ada.shape[1]
    for v in range(6):
        rows = mod_all[:, v, :]
        o_ada[:, v * D : (v + 1) * D] = mm_tn(silu, rows)
        flat[:, v * D : (v + 1) * D] = jnp.sum(rows.astype(F32), axis=0, keepdims=True)
    for g in range(G):
        pieces[g] = flat[:, g * width : (g + 1) * width]
    o_b_ada[...] = pieces[lax.axis_index("fsdp") * S + lax.axis_index("seq")]


def assemble(sizes, qkv, one, two, out, mod_all, silu_all):
    R, F, S = sizes
    G = F * S
    rows, D = out.shape[1:]
    shape = jax.ShapeDtypeStruct
    return pl.pallas_call(
        lambda *refs: assemble_kernel(sizes, *refs),
        name="assemble",
        out_shape=(
            shape((rows, 3 * D), F32),
            shape((rows, one.shape[2] * S), F32),
            shape(two.shape, F32),
            shape((rows, D), F32),
            shape((rows, 6 * D), F32),
            shape((1, 6 * D // G), F32),
        ),
        in_specs=[VM] * 6,
        out_specs=(VM,) * 6,
        scratch_shapes=[pltpu.VMEM((1, 6 * D), F32), pltpu.VMEM((G, 1, 6 * D // G), F32)],
        compiler_params=pltpu.CompilerParams(vmem_limit_bytes=40 * 1024 * 1024),
    )(qkv, one, two, out, mod_all, silu_all)


def on_device(
    latents, cond, w_ada, b_ada, w_qkv, b_qv, w_out, b_out, w_one, b_one, w_two, b_two, cotangent
):
    sizes = R, F, S = tuple(lax.axis_size(name) for name in ("rep", "fsdp", "seq"))
    G = F * S
    _, L, D = latents.shape
    hidden = w_one.shape[1] // S
    rows = w_ada.shape[0]
    qv = b_qv.shape[0]
    owner = lax.axis_index(("fsdp", "seq"))
    width = b_ada.shape[0]
    bias_slot = lax.dynamic_update_slice(
        jnp.zeros((w_ada.shape[1],), F32), b_ada.astype(F32), (owner * width,)
    )[None]
    bias_pack = jnp.concatenate([b_qv, b_out, b_two, b_one]).astype(F32)[None]
    tokens = latents[0]
    two_rows = w_two.shape[0]
    (
        mixed_all,
        heads,
        log_sums,
        merged,
        branch_one,
        mixed_two,
        mod,
        silu_all,
        grad_all,
        full_qkv,
        full_out,
        bias_one,
        bias_two,
        g_one,
        g_two,
    ) = forward(
        sizes,
        cond,
        w_ada,
        bias_slot,
        tokens,
        cotangent[0],
        w_qkv,
        w_one,
        bias_pack,
        w_two.reshape(2, two_rows // 2, D),
        w_out,
    )
    full_one = g_one.reshape(D, hidden)
    full_two = g_two.reshape(hidden, D)
    (
        block_out,
        grad_resid,
        grad_heads,
        one_g,
        two_g,
        out_g,
        grad_b_one,
        grad_b_two,
        grad_b_out,
        mod_sums,
    ) = mlp(
        sizes,
        mixed_two,
        grad_all,
        cotangent[0],
        mod,
        full_one,
        bias_one,
        full_two,
        bias_two,
        branch_one,
        tokens,
        full_out,
        merged,
    )
    grad_latents, qkv_sum, one_sum, two_sum, out_sum, mod_all, o_small, o_cond = backward(
        sizes,
        grad_heads,
        heads,
        log_sums,
        mixed_all,
        full_qkv,
        tokens,
        mod,
        grad_resid,
        mod_sums,
        one_g.reshape(G, rows, hidden),
        two_g.reshape(F, 2, two_rows // 2, D),
        out_g.reshape(F, S, rows, D),
        grad_b_one,
        grad_b_two,
        grad_b_out,
        w_ada,
        cond,
    )
    o_qkv, o_one, o_two, o_out, o_ada, o_b_ada = assemble(
        sizes, qkv_sum, one_sum, two_sum, out_sum, mod_all, silu_all
    )
    small = o_small[0]
    return (
        block_out[None],
        grad_latents[None],
        o_cond,
        o_ada,
        o_b_ada[0],
        o_qkv,
        small[:qv],
        o_out,
        small[qv : qv + rows],
        o_one,
        small[qv + 2 * rows :],
        o_two.reshape(two_rows, D),
        small[qv + rows : qv + 2 * rows],
    )


def solution(mesh):
    owned = P(("fsdp", "seq"), None)
    owned_bias = P(("fsdp", "seq"))
    token_spec = P(("rep", "fsdp"), "seq", None)
    cond_spec = P(("rep", "fsdp"), None)
    weights = (owned, owned_bias) * 5
    in_specs = (token_spec, cond_spec) + weights + (token_spec,)
    out_specs = (token_spec, token_spec, cond_spec) + weights
    return jax.shard_map(
        on_device, mesh=mesh, in_specs=in_specs, out_specs=out_specs, check_vma=False
    )
```

```python
import math

import jax
import jax.numpy as jnp
from jax import lax
from jax.experimental import pallas as pl
from jax.experimental.pallas import tpu as pltpu
from jax.sharding import PartitionSpec as P

H = 16
epsilon = 1e-06
gelu_coef = math.sqrt(2.0 / math.pi)
log2e = math.log2(math.e)
BF = jnp.bfloat16
F32 = jnp.float32
LANES = 128
VM = pl.BlockSpec(memory_space=pltpu.VMEM)
HB = pl.BlockSpec(memory_space=pl.ANY)
DMA = pltpu.SemaphoreType.DMA


def params(ident, mib):
    return pltpu.CompilerParams(
        collective_id=ident, has_side_effects=True, vmem_limit_bytes=mib * 1024 * 1024
    )


def remote(src, dst, send, recv, device):
    return pltpu.make_async_remote_copy(
        src_ref=src,
        dst_ref=dst,
        send_sem=send,
        recv_sem=recv,
        device_id=device,
        device_id_type=pl.DeviceIdType.MESH,
    )


def local(src, dst, sem):
    return pltpu.make_async_copy(src, dst, sem)


def await_bytes(like, sem):
    pltpu.make_async_copy(like, like, sem).wait()


class Moves:
    def __init__(self, sem, *pairs):
        self.copies = [local(pair[0], pair[1], sem.at[i]) for i, pair in enumerate(pairs)]

    def start(self, *which):
        for i in which or range(len(self.copies)):
            self.copies[i].start()

    def wait(self, *which):
        for i in which or range(len(self.copies)):
            self.copies[i].wait()


def each(start, stop, body):
    def step(index, carry):
        body(index)
        return carry

    lax.fori_loop(start, stop, step, 0)


def greet(count, device_of):
    gate = pltpu.get_barrier_semaphore()
    each(
        1,
        count,
        lambda i: pl.semaphore_signal(
            gate, 1, device_id=device_of(i), device_id_type=pl.DeviceIdType.MESH
        ),
    )
    return count - 1


def greet_wait(count):
    pl.semaphore_wait(pltpu.get_barrier_semaphore(), count)


def norm_stats(values):
    center = values - jnp.mean(values, axis=-1, keepdims=True)
    inv_std = lax.rsqrt(jnp.mean(center * center, axis=-1, keepdims=True) + epsilon)
    return (center * inv_std, inv_std)


def norm_back(grad, normed, inv_std):
    return inv_std * (
        grad
        - jnp.mean(grad, axis=-1, keepdims=True)
        - normed * jnp.mean(grad * normed, axis=-1, keepdims=True)
    )


def mm(left, right):
    return jnp.dot(left, right, preferred_element_type=F32)


def mm_nt(left, right):
    return lax.dot_general(left, right, (((1,), (1,)), ((), ())), preferred_element_type=F32)


def mm_tn(left, right):
    return lax.dot_general(left, right, (((0,), (0,)), ((), ())), preferred_element_type=F32)


class Place:
    def __init__(self, sizes):
        self.R, self.F, self.S = sizes
        self.G = self.F * self.S
        self.y = lax.axis_index("rep")
        self.z = lax.axis_index("fsdp")
        self.s = lax.axis_index("seq")
        self.me = self.z * self.S + self.s
        self.mine = lax.rem(self.s, 2) == self.y
        self.steps = (2, 1, 3) if self.F == 4 else tuple(range(1, self.F))

    def zs(self, i):
        return lax.rem(self.z + i, self.F)

    def zs_back(self, i):
        return lax.rem(self.z - i + self.F, self.F)

    def ss(self, i):
        return lax.rem(self.s + i, self.S)

    def ss_back(self, i):
        return lax.rem(self.s - i + self.S, self.S)

    def flip(self):
        return {"rep": 1 - self.y}

    def peer(self, j):
        return lax.bitwise_xor(self.s, j)


class SeqGather:
    def __init__(self, at, dst, sem):
        self.at, self.dst, self.sem = at, dst, sem

    @staticmethod
    def scratch(S):
        return DMA((4, S))

    def direct(self, j):
        at, block = self.at, self.dst.at[self.at.s]
        return remote(block, block, self.sem.at[0, j], self.sem.at[1, j], {"seq": at.peer(j)})

    def handed(self, j):
        at = self.at
        block = self.dst.at[at.peer(j)]
        return remote(block, block, self.sem.at[2, j], self.sem.at[3, j], {"seq": at.peer(1)})

    def start(self):
        for j in range(3, self.at.S, 2):
            self.direct(j).start()
        self.direct(1).start()

    def arrive(self, index):
        @pl.when(index == 1)
        def _():
            self.direct(1).wait()

        if self.at.S > 2:

            @pl.when((index >= 2) & (lax.rem(index, 2) == 0))
            def _():
                self.direct(index + 1).wait()
                self.handed(index + 1).start()

            @pl.when((index >= 2) & (lax.rem(index, 2) == 1))
            def _():
                self.handed(index).wait()


def arrival(index):
    return jnp.where(index < 2, index, lax.bitwise_xor(index, 1))


class SeqSum:
    def __init__(self, at, src, near, inn, sem):
        self.at, self.src, self.near, self.inn, self.sem = at, src, near, inn, sem

    @staticmethod
    def scratch(S, rows, cols):
        return [
            pltpu.VMEM((S, rows, cols), BF),
            pltpu.VMEM((S // 2, rows, cols), BF),
            pltpu.VMEM((S // 2, rows, cols), BF),
            DMA((4, S)),
        ]

    def sibling(self, j):
        at = self.at
        return remote(
            self.src.at[at.peer(j)],
            self.near.at[j // 2],
            self.sem.at[0, j],
            self.sem.at[1, j],
            {"seq": at.peer(1)},
        )

    def direct(self, j):
        at = self.at
        return remote(
            self.src.at[at.peer(j)],
            self.inn.at[j // 2],
            self.sem.at[2, j],
            self.sem.at[3, j],
            {"seq": at.peer(j)},
        )

    def send(self, index):
        @pl.when((index == 1) | ((index >= 2) & (lax.rem(index, 2) == 0)))
        def _():
            self.sibling(lax.bitwise_or(index, 1)).start()

        if self.at.S > 2:

            @pl.when((index >= 2) & (lax.rem(index, 2) == 1))
            def _():
                j = index - 1
                self.sibling(index).wait()
                t = self.at.peer(j)
                step = min(64, self.src.shape[1])

                def add(i):
                    rows = pl.ds(pl.multiple_of(i * step, step), step)
                    both = self.src[t, rows, :].astype(F32) + self.near[j // 2, rows, :].astype(F32)
                    self.src[t, rows, :] = both.astype(BF)

                each(0, self.src.shape[1] // step, add)
                self.direct(j).start()

    def wait(self):
        self.sibling(1).wait()
        for j in range(2, self.at.S, 2):
            self.direct(j).wait()

    def total(self, rows):
        value = self.src[self.at.s, rows, :].astype(F32) + self.near[0, rows, :].astype(F32)
        for k in range(1, self.at.S // 2):
            value = value + self.inn[k, rows, :].astype(F32)
        return value


class FarGather:
    relayed = True

    def __init__(self, at, dst, sem):
        self.at, self.dst, self.sem = at, dst, sem
        self.line = self.relayed and at.F == 4

    @staticmethod
    def scratch(F):
        return DMA((7, F))

    def send(self, z_from, z_to, kind):
        pieces = self.half(z_from)
        held = self.origin() if kind == 0 else pieces
        for source, piece in zip(held, pieces):
            remote(
                source, piece, self.sem.at[kind, z_to], self.sem.at[2, z_from], {"fsdp": z_to}
            ).start()

    def origin(self):
        return self.half(self.at.z)

    def await_half(self, row, z):
        await_bytes(self.like(), self.sem.at[row, z])

    def around(self, step, body):
        at = self.at

        @pl.when(at.z >= step)
        def _():
            body(at.z - step)

        @pl.when(at.z + step < at.F)
        def _():
            body(at.z + step)

    def direct(self, step, body):
        if self.line and step == 3:
            return
        self.around(step, body)

    def start_far(self):
        for step in self.at.steps:
            self.direct(step, lambda z_to: self.send(self.at.z, z_to, 0))

    def service(self, step):
        at = self.at

        def take(z_from):
            self.await_half(2, z_from)
            for piece in self.half(z_from):
                remote(
                    piece, piece, self.sem.at[3, z_from], self.sem.at[4, z_from], at.flip()
                ).start()

        self.around(step, take)
        if self.line and step == 2:

            @pl.when((at.z == 1) | (at.z == 2))
            def _():
                far = jnp.where(at.z == 1, 3, 0)
                end = 3 - far
                self.send(far, end, 1)

    def finish_far(self):
        at = self.at

        def swapped(z_from):
            self.await_half(3, z_from)
            self.await_half(4, z_from)

        for step in range(1, at.F):
            self.around(step, swapped)
            self.direct(step, lambda z_to: self.await_half(0, z_to))
        if self.line:

            @pl.when((at.z == 1) | (at.z == 2))
            def _():
                self.await_half(1, jnp.where(at.z == 1, 0, 3))


class ColumnGather(FarGather):
    def __init__(self, at, src, dst, sem):
        super().__init__(at, dst, sem)
        self.src = src

    def half(self, z):
        at = self.at
        return [self.dst.at[z * at.S + 2 * k + at.y] for k in range(at.S // 2)]

    def like(self):
        return self.dst.at[pl.ds(0, self.at.S // 2)]

    def start(self):
        at, src, dst, sem = self.at, self.src, self.dst, self.sem

        def near(j):
            t = at.ss(j)
            remote(src.at[t], dst.at[at.me], sem.at[5, 0], sem.at[6, 0], {"seq": t}).start()

        each(1, at.S, near)
        local(src.at[at.s], dst.at[at.me], sem.at[5, 1]).start()

    def near_done(self):
        at, dst, sem = self.at, self.dst, self.sem
        local(self.src.at[at.s], dst.at[at.me], sem.at[5, 1]).wait()
        near = dst.at[pl.ds(0, at.S - 1)]
        await_bytes(near, sem.at[5, 0])
        await_bytes(near, sem.at[6, 0])


class RowGather(FarGather):
    def __init__(self, at, src, dst, sem):
        super().__init__(at, dst, sem)
        self.src = src

    def half(self, z):
        return [self.dst.at[z, self.at.y]]

    def origin(self):
        return [self.src.at[self.at.y]]

    def like(self):
        return self.dst.at[0, 0]

    def start(self):
        at = self.at
        local(self.src, self.dst.at[at.z], self.sem.at[5, 0]).start()

    def near_done(self):
        at = self.at
        local(self.src, self.dst.at[at.z], self.sem.at[5, 0]).wait()


class OwnGather(FarGather):
    relayed = False

    def __init__(self, at, src, dst, sem):
        super().__init__(at, dst, sem)
        self.src = src

    def half(self, z):
        return [self.dst.at[self.at.s, z]]

    def origin(self):
        return [self.src]

    def like(self):
        return self.src

    def start(self):
        at = self.at
        local(self.src, self.dst.at[at.s, at.z], self.sem.at[5, 0]).start()

    def near_done(self):
        at = self.at
        local(self.src, self.dst.at[at.s, at.z], self.sem.at[5, 0]).wait()

    def start_far(self):
        pl.when(self.at.mine)(super().start_far)

    def service(self, step):
        take = super().service
        pl.when(self.at.mine)(lambda: take(step))

    def finish_far(self):
        at = self.at

        def sent(z_from):
            self.await_half(3, z_from)

        def swapped(z_from):
            self.await_half(4, z_from)

        @pl.when(at.mine)
        def _():
            for step in range(1, at.F):
                self.around(step, sent)
                self.direct(step, lambda z_to: self.await_half(0, z_to))
            if self.line:

                @pl.when((at.z == 1) | (at.z == 2))
                def _():
                    self.await_half(1, jnp.where(at.z == 1, 0, 3))

        @pl.when(jnp.logical_not(at.mine))
        def _():
            for step in range(1, at.F):
                self.around(step, swapped)


def forward_kernel(sizes, *refs):
    at = Place(sizes)
    R, F, S, G = at.R, at.F, at.S, at.G
    cond, bias_slot, bias_pack, i_latents, i_cotangent, i_ada, i_qkv, i_one, w_two, w_out = refs[:10]
    o_mixed, o_heads, o_merged, o_branch, o_mix, o_grad, o_full_qkv, o_full_out = refs[10:18]
    log_sums, mod, silu_all, bias_one, bias_two, g_one, g_two = refs[18:25]
    silu_src, part, parts_in, mod_src, mod_in, qkv_src, one_src, pack_all = refs[25:33]
    g_qkv, g_out, wide, bias_qkv, bias_out, val_flip, att, merged_in = refs[33:41]
    silu_sem, part_sem, mod_sem, pack_sem, qkv_sem, one_sem, two_sem, out_sem = refs[41:49]
    mixed_sem, grad_sem, att_sem, mix_sem, spread_sem, load_sem, save_sem = refs[49:56]
    latents, cotangent, w_ada, w_qkv, w_one = refs[56:61]
    mixed_all, heads, merged, branch_one, mix_all, grad_all, full_qkv, full_out = refs[61:69]
    loads = Moves(
        load_sem,
        (i_qkv, w_qkv),
        (i_ada, w_ada),
        (i_one, w_one),
        (i_latents, latents),
        (i_cotangent, cotangent),
    )
    loads.start()
    saves = Moves(
        save_sem,
        (mixed_all, o_mixed),
        (heads, o_heads),
        (merged, o_merged),
        (branch_one, o_branch),
        (mix_all, o_mix),
        (grad_all, o_grad),
        (full_qkv, o_full_qkv),
        (full_out, o_full_out),
    )
    L, D = latents.shape
    C = D // S
    T = S * L
    local_heads = H // S
    size = D // H
    rows_own = silu_all.shape[2]
    hidden = one_src.shape[2]
    block = hidden // F
    greet(G, lambda i: {"fsdp": lax.rem(at.me + i, G) // S, "seq": lax.rem(at.me + i, S)})
    greet(2 * F, lambda i: {"rep": lax.rem(at.y + i // F, 2), "fsdp": at.zs(i)})
    greet_wait(G - 1 + 2 * F - 1)

    value = cond[...].astype(F32)
    silu = (value * jax.nn.sigmoid(value)).astype(BF).astype(F32)
    for g in range(G):
        silu_src[g] = silu[:, g * rows_own : (g + 1) * rows_own]
    slot = at.y * F + at.z

    def cond_copy(i):
        z_to = at.zs(i)
        return remote(
            silu_src.at[z_to * S + at.s],
            silu_all.at[slot],
            silu_sem.at[0, i],
            silu_sem.at[1, i],
            {"rep": lax.rem(at.y + i // F, 2), "fsdp": z_to},
        )

    each(1, 2 * F, lambda i: cond_copy(i).start())
    silu_all[slot] = silu_src[at.me]

    def pack_copy(i):
        to = lax.rem(at.me + i, G)
        return remote(
            bias_pack,
            pack_all.at[at.me],
            pack_sem.at[0, 0],
            pack_sem.at[1, 0],
            {"fsdp": to // S, "seq": lax.rem(to, S)},
        )

    each(1, G, lambda i: pack_copy(i).start())
    pack_all[at.me] = bias_pack[...]

    qkv = ColumnGather(at, qkv_src, g_qkv, qkv_sem)
    one = ColumnGather(at, one_src, g_one, one_sem)
    two = RowGather(at, w_two, g_two, two_sem)
    out = OwnGather(at, w_out, g_out, out_sem)
    loads.wait(0)
    for t in range(S):
        for j in range(3):
            qkv_src[t, :, j * C : (j + 1) * C] = w_qkv[:, j * D + t * C : j * D + (t + 1) * C]

    qkv.start()
    two.start()
    out.start()

    each(1, 2 * F, lambda i: cond_copy(i).wait())
    left = jnp.concatenate([silu_all[at.y * F + f] for f in range(F)], axis=0).astype(BF)
    loads.wait(1)
    sums = mm(left, w_ada[...]) + bias_slot[...]
    for f in range(F):
        for v in range(6):
            for t in range(S):
                col = v * D + t * C
                part[f * S + t, v : v + 1, :] = sums[f : f + 1, col : col + C]

    def part_copy(i):
        to = lax.rem(at.me + i, G)
        return remote(
            part.at[to],
            parts_in.at[at.me],
            part_sem.at[0, i],
            part_sem.at[1, i],
            {"fsdp": to // S, "seq": lax.rem(to, S)},
        )

    each(1, G, lambda i: part_copy(i).start())
    parts_in[at.me] = part[at.me]
    loads.wait(2)
    for t in range(S):
        for f in range(F):
            col = (f * S + t) * block
            one_src[t, :, f * block : (f + 1) * block] = w_one[:, col : col + block]
    qkv.near_done()
    qkv.start_far()
    each(1, G, lambda i: part_copy(i).wait())
    total = parts_in[0]
    for g in range(1, G):
        total = total + parts_in[g]
    mod_src[...] = total

    def mod_copy(i):
        return remote(
            mod_src, mod_in.at[at.s], mod_sem.at[0, i], mod_sem.at[1, i], {"seq": at.ss(i)}
        )

    each(1, S, lambda i: mod_copy(i).start())
    one.start()
    mod_in[at.s] = total
    out.start_far()
    each(1, S, lambda i: mod_copy(i).wait())
    for t in range(S):
        mod[:, t * C : (t + 1) * C] = mod_in[t]

    loads.wait(3)
    step = min(64, L)

    def norm(i):
        at_rows = pl.ds(pl.multiple_of(i * step, step), step)
        normed, _ = norm_stats(latents[at_rows, :].astype(F32))
        mixed_all[at.s, at_rows, :] = (normed * (1.0 + mod[1:2, :]) + mod[0:1, :]).astype(BF)

    each(0, L // step, norm)
    gather = SeqGather(at, mixed_all, mixed_sem)
    gather.start()
    loads.wait(4)
    grad_all[at.s] = (mod[5:6, :] * cotangent[...].astype(F32)).astype(BF)
    grad_gather = SeqGather(at, grad_all, grad_sem)
    grad_gather.start()
    one.near_done()
    qkv.service(at.steps[0])
    one.start_far()
    out.near_done()
    two.near_done()

    others = pack_all.at[pl.ds(0, G - 1)]
    await_bytes(others, pack_sem.at[0, 0])
    await_bytes(others, pack_sem.at[1, 0])
    qv = 2 * D // G
    own = F // 2
    bias_qkv[...] = jnp.zeros_like(bias_qkv)
    for i in range(own):
        bias_qkv[:, i * qv : (i + 1) * qv] = pack_all[at.s * own + i][:, 0:qv]
        bias_qkv[:, 2 * C + i * qv : 2 * C + (i + 1) * qv] = pack_all[G // 2 + at.s * own + i][
            :, 0:qv
        ]
    for g in range(G):
        cols = slice(g * rows_own, (g + 1) * rows_own)
        bias_out[:, cols] = pack_all[g][:, qv : qv + rows_own]
        bias_two[:, cols] = pack_all[g][:, qv + rows_own : qv + 2 * rows_own]
    for f in range(F):
        bias_one[:, f * block : (f + 1) * block] = pack_all[f * S + at.s][:, qv + 2 * rows_own :]

    for i in at.steps[1:]:
        qkv.service(i)
    for i in at.steps:
        out.service(i)
    qkv.finish_far()

    def join(slabs, whole):
        cols = whole.shape[1]
        for g in range(G):
            wide[g * rows_own : (g + 1) * rows_own, 0:cols] = slabs(g).astype(F32)
        tall = 128 if D % 128 == 0 else D

        def cast(i):
            at_rows = pl.ds(pl.multiple_of(i * tall, tall), tall)
            whole[at_rows, :] = wide[at_rows, 0:cols].astype(BF)

        each(0, D // tall, cast)

    join(lambda g: g_qkv[g], full_qkv)
    saves.start(6)

    pad = jnp.zeros((L, LANES - size), BF)

    def project(index):
        gather.arrive(index)
        t = at.peer(arrival(index))
        at_rows = pl.ds(pl.multiple_of(t * L, L), L)
        done = (mm(mixed_all[t], full_qkv[...]) + bias_qkv[...]).astype(BF)
        for c in range(3 * local_heads):
            heads[c, at_rows, :] = jnp.concatenate(
                [done[:, c * size : (c + 1) * size], pad], axis=1
            )

    each(0, S, project)
    saves.start(0, 1)
    out.finish_far()
    spread = SeqGather(at, g_out, spread_sem)
    spread.start()
    each(1, S, grad_gather.arrive)
    saves.start(5)
    for h in range(local_heads):
        val_flip[h] = heads[2 * local_heads + h].T

    def att_copy(j):
        t = at.peer(j)
        return remote(
            att.at[t], merged_in.at[at.s], att_sem.at[0, j], att_sem.at[1, j], {"seq": t}
        )

    factor = size ** (-0.5) * log2e

    def attention(index):
        j = S - 1 - index
        t = at.peer(j)
        at_rows = pl.ds(pl.multiple_of(t * L, L), L)
        for h in range(local_heads):
            scores = mm_nt(heads[local_heads + h], heads[h, at_rows, :]) * factor
            highest = jnp.max(scores, axis=0, keepdims=True)
            raised = jnp.exp2(scores - highest)
            summed = jnp.sum(raised, axis=0, keepdims=True)
            result = mm(val_flip[h], raised.astype(BF)) / summed
            log_sums[h, t] = highest + jnp.log2(summed)
            att[t, :, h * size : (h + 1) * size] = result.T[:, :size].astype(BF)

        @pl.when(j > 0)
        def _():
            att_copy(j).start()

        @pl.when(index == S // 2)
        def _():
            one.service(at.steps[0])
            one.service(at.steps[1])
            two.start_far()

    each(0, S, attention)
    merged_in[at.s] = att[at.s]
    each(1, S, spread.arrive)
    join(lambda g: g_out[g % S, g // S], full_out)
    saves.start(7)
    each(1, S, lambda j: att_copy(j).wait())
    for t in range(S):
        merged[:, t * C : (t + 1) * C] = merged_in[t]
    saves.start(2)

    def project_out(i):
        at_rows = pl.ds(pl.multiple_of(i * step, step), step)
        branch = mm(merged[at_rows, :], full_out[...]) + bias_out[...]
        branch_one[at_rows, :] = branch
        residual = latents[at_rows, :].astype(F32) + mod[2:3, :] * branch
        normed, _ = norm_stats(residual)
        mix_all[at.s, at_rows, :] = (normed * (1.0 + mod[4:5, :]) + mod[3:4, :]).astype(BF)

    each(0, L // step, project_out)
    saves.start(3)
    mix_gather = SeqGather(at, mix_all, mix_sem)
    mix_gather.start()
    for i in at.steps[2:]:
        one.service(i)
    for i in at.steps:
        two.service(i)
    one.finish_far()
    each(1, S, mix_gather.arrive)
    saves.start(4)
    two.finish_far()
    saves.wait()


def forward(sizes, cond, bias_slot, bias_pack, latents, cotangent, w_ada, w_qkv, w_one, w_two, w_out):
    R, F, S = sizes
    G = F * S
    rows, D = w_out.shape
    L = latents.shape[0]
    T = S * L
    C = D // S
    local_heads = H // S
    hidden = w_one.shape[1] // S
    shape = jax.ShapeDtypeStruct
    kept = (
        ((S, L, D), BF),
        ((3 * local_heads, T, LANES), BF),
        ((L, D), BF),
        ((L, D), F32),
        ((S, L, D), BF),
        ((S, L, D), BF),
        ((D, 3 * C), BF),
        ((D, D), BF),
    )
    return pl.pallas_call(
        lambda *refs: forward_kernel(sizes, *refs),
        name="forward",
        out_shape=tuple(shape(*item) for item in kept)
        + (
            shape((local_heads, S, 1, L), F32),
            shape((6, D), F32),
            shape((R * F, 1, rows), F32),
            shape((1, hidden), F32),
            shape((1, D), F32),
            shape((G, rows, hidden), BF),
            shape((F,) + w_two.shape, BF),
        ),
        in_specs=[VM] * 3 + [HB] * 7,
        out_specs=(HB,) * 8 + (VM,) * 5 + (HB,) * 2,
        scratch_shapes=[
            pltpu.VMEM((G, 1, rows), F32),
            pltpu.VMEM((G, 6, C), F32),
            pltpu.VMEM((G, 6, C), F32),
            pltpu.VMEM((6, C), F32),
            pltpu.VMEM((S, 6, C), F32),
            pltpu.VMEM((S, rows, 3 * C), BF),
            pltpu.VMEM((S, rows, hidden), BF),
            pltpu.VMEM((G,) + bias_pack.shape, F32),
            pltpu.VMEM((G, rows, 3 * C), BF),
            pltpu.VMEM((S, F, rows, D), BF),
            pltpu.VMEM((D, max(D, 3 * C)), F32),
            pltpu.VMEM((1, 3 * C), F32),
            pltpu.VMEM((1, D), F32),
            pltpu.VMEM((local_heads, LANES, T), BF),
            pltpu.VMEM((S, L, C), BF),
            pltpu.VMEM((S, L, C), BF),
            DMA((2, 2 * F)),
            DMA((2, G)),
            DMA((2, S)),
            DMA((2, 1)),
            ColumnGather.scratch(F),
            ColumnGather.scratch(F),
            RowGather.scratch(F),
            OwnGather.scratch(F),
            SeqGather.scratch(S),
            SeqGather.scratch(S),
            DMA((2, S)),
            SeqGather.scratch(S),
            SeqGather.scratch(S),
            DMA((5,)),
            DMA((8,)),
        ]
        + [pltpu.VMEM(x.shape, x.dtype) for x in (latents, cotangent, w_ada, w_qkv, w_one)]
        + [pltpu.VMEM(*item) for item in kept],
        compiler_params=params(1, 60),
    )(cond, bias_slot, bias_pack, latents, cotangent, w_ada, w_qkv, w_one, w_two, w_out)


class RowScatter:
    def __init__(self, at, src, got, stage, sem):
        self.at, self.src, self.got, self.stage, self.sem = at, src, got, stage, sem

    def start(self):
        at = self.at

        def far(i):
            z_to = at.zs(i)
            remote(
                self.src.at[z_to, 1 - at.y],
                self.got.at[z_to],
                self.sem.at[0, i],
                self.sem.at[1, i],
                at.flip(),
            ).start()

        each(0, at.F, far)

    def reduce(self):
        at = self.at

        def far(i):
            z_to = at.zs(i)
            await_bytes(self.got.at[0], self.sem.at[0, i])
            await_bytes(self.got.at[0], self.sem.at[1, i])
            total = self.src[z_to, at.y].astype(F32) + self.got[z_to].astype(F32)
            self.stage[z_to] = total.astype(BF)

        each(0, at.F, far)


class Line:
    def line_up(self):
        at = self.at
        self.line = at.F == 4
        self.inner = self.line & ((at.z == 1) | (at.z == 2))
        self.end = self.line & ((at.z == 0) | (at.z == 3))
        self.opposite = jnp.where(at.z < 2, 3, 0)
        self.beside = jnp.where(at.z == 0, 1, 2)


class RowOwner(Line):
    def __init__(self, at, stage, inn, done, far, sem):
        self.at, self.stage, self.inn, self.done, self.far, self.sem = at, stage, inn, done, far, sem
        self.line_up()

    @staticmethod
    def scratch(F, shape):
        return [pltpu.VMEM(shape, BF), pltpu.VMEM(shape[1:], BF), DMA((5, F))]

    def out_copy(self, z_to):
        at = self.at
        return remote(
            self.stage.at[z_to],
            self.inn.at[at.z],
            self.sem.at[0, z_to],
            self.sem.at[1, at.z],
            {"fsdp": z_to},
        )

    def far_copy(self):
        return remote(
            self.stage.at[self.opposite],
            self.far,
            self.sem.at[0, self.opposite],
            self.sem.at[4, 0],
            {"fsdp": self.beside},
        )

    def start(self):
        at = self.at

        @pl.when(self.end)
        def _():
            self.far_copy().start()
            self.inn[self.opposite] = jnp.zeros_like(self.far)

        def one(i):
            z_to = at.zs(i)

            @pl.when(jnp.logical_not(self.line & (z_to == self.opposite)))
            def _():
                self.out_copy(z_to).start()

        each(1, at.F, one)
        self.inn[at.z] = self.stage[at.z]

    def relay(self):
        @pl.when(self.inner)
        def _():
            await_bytes(self.far, self.sem.at[4, 0])
            z_to = self.opposite
            both = self.stage[z_to].astype(F32) + self.far[...].astype(F32)
            self.stage[z_to] = both.astype(BF)
            self.out_copy(z_to).start()

    def total(self):
        at = self.at

        def arrived(i):
            z = at.zs(i)
            await_bytes(self.far, self.sem.at[0, z])

            @pl.when(jnp.logical_not(self.end & (z == self.opposite)))
            def _():
                await_bytes(self.far, self.sem.at[1, z])

        each(1, at.F, arrived)
        total = self.inn[0].astype(F32)
        for f in range(1, at.F):
            total = total + self.inn[f].astype(F32)
        self.done[at.y] = total.astype(BF)
        half = self.done.at[at.y]
        remote(half, half, self.sem.at[2, 0], self.sem.at[3, 0], at.flip()).start()

    def finish(self):
        await_bytes(self.done.at[0], self.sem.at[2, 0])
        await_bytes(self.done.at[0], self.sem.at[3, 0])


class FullScatter:
    def __init__(self, at, src, near, got, stage, inn, other, done, sem):
        self.at, self.src, self.near, self.got, self.stage = at, src, near, got, stage
        self.inn, self.other, self.done, self.sem = inn, other, done, sem

    @staticmethod
    def scratch(sizes, rows, cols):
        R, F, S = sizes
        return [
            pltpu.VMEM((S // 2, F, rows, cols), BF),
            pltpu.VMEM((S // 2, F, rows, cols), BF),
            pltpu.VMEM((F, rows, cols), BF),
            pltpu.VMEM((F, rows, cols), BF),
            pltpu.VMEM((F, rows, cols), BF),
            DMA((10, max(F, S))),
        ]

    def sibling(self, j):
        at = self.at
        return remote(
            self.src.at[at.peer(j)],
            self.near.at[j // 2],
            self.sem.at[0, j],
            self.sem.at[1, j],
            {"seq": at.peer(1)},
        )

    def direct(self, j):
        at = self.at
        return remote(
            self.near.at[j // 2],
            self.got.at[j // 2],
            self.sem.at[2, j],
            self.sem.at[3, j],
            {"seq": at.peer(j)},
        )

    def start(self):
        for j in range(3, self.at.S, 2):
            self.sibling(j).start()
        self.sibling(1).start()

    def cross(self):
        at = self.at
        for j in range(2, at.S, 2):
            self.sibling(j + 1).wait()
            k = j // 2

            def add(f):
                both = self.near[k, f].astype(F32) + self.src[at.peer(j), f].astype(F32)
                self.near[k, f] = both.astype(BF)

            each(0, at.F, add)
            self.direct(j).start()
        self.sibling(1).wait()

    def out_copy(self, i):
        at = self.at
        return remote(
            self.stage.at[at.zs(i)],
            self.inn.at[at.z],
            self.sem.at[4, i],
            self.sem.at[5, i],
            {"fsdp": at.zs(i)},
        )

    def scatter(self):
        at = self.at
        for j in range(2, at.S, 2):
            self.direct(j).wait()

        def far(i):
            z_to = at.zs(i)
            total = self.src[at.s, z_to].astype(F32) + self.near[0, z_to].astype(F32)
            for k in range(1, at.S // 2):
                total = total + self.got[k, z_to].astype(F32)
            self.stage[z_to] = total.astype(BF)

        each(0, at.F, far)

        @pl.when(jnp.logical_not(at.mine))
        def _():
            self.swap_copy().start()

    def swap_copy(self):
        return remote(self.stage, self.other, self.sem.at[6, 0], self.sem.at[7, 0], self.at.flip())

    def along(self):
        at = self.at

        @pl.when(at.mine)
        def _():
            await_bytes(self.other, self.sem.at[7, 0])

            def one(i):
                z_to = at.zs(i)
                both = self.stage[z_to].astype(F32) + self.other[z_to].astype(F32)
                self.stage[z_to] = both.astype(BF)

                @pl.when(i > 0)
                def _():
                    self.out_copy(i).start()

            each(0, at.F, one)
            self.inn[at.z] = self.stage[at.z]

        @pl.when(jnp.logical_not(at.mine))
        def _():
            await_bytes(self.other, self.sem.at[6, 0])

    def total(self):
        at = self.at

        @pl.when(at.mine)
        def _():
            each(1, at.F, lambda i: self.out_copy(i).wait())
            total = self.inn[0].astype(F32)
            for f in range(1, at.F):
                total = total + self.inn[f].astype(F32)
            self.done[...] = total.astype(BF)
            remote(
                self.done, self.done, self.sem.at[8, 0], self.sem.at[9, 0], at.flip()
            ).start()

    def finish(self):
        at = self.at

        @pl.when(at.mine)
        def _():
            await_bytes(self.done, self.sem.at[8, 0])

        @pl.when(jnp.logical_not(at.mine))
        def _():
            await_bytes(self.done, self.sem.at[9, 0])


def mlp_kernel(sizes, *refs):
    at = Place(sizes)
    R, F, S, G = at.R, at.F, at.S, at.G
    mod, bias_one, bias_two = refs[:3]
    given = refs[3:12]
    block_out, o_resid, o_heads, o_w_one, o_two_sum, o_out_g = refs[12:18]
    grad_b_one, grad_b_two, grad_b_out, mod_sums = refs[18:22]
    act_all, pre_wide, pre_all, grad_branch, wide, two_g, two_got, two_sem = refs[22:30]
    branch_refs, mix_refs = refs[30:34], refs[34:38]
    load_sem, save_sem = refs[38:40]
    held = refs[40:49]
    w_one, mix_all, w_two, grad_all, latents, branch_one, cotangent, w_out, merged = held
    grad_resid, grad_heads, grad_w_one, two_sum, out_g = refs[49:54]
    loads = Moves(load_sem, *zip(given, held))
    loads.start()
    saves = Moves(
        save_sem,
        (grad_w_one, o_w_one),
        (grad_resid, o_resid),
        (grad_heads, o_heads),
        (out_g, o_out_g),
        (two_sum, o_two_sum),
    )
    _, L, D = mix_all.shape
    C = D // S
    hidden = w_one.shape[1]
    tokens = S * L
    greet(S, lambda i: {"seq": at.ss(i)})
    greet(2, lambda i: at.flip())
    greet_wait(S)
    gate_one = mod[2:3, :]
    scale = mod[4:5, :]
    gate_two = mod[5:6, :]
    branch_sum = SeqSum(at, *branch_refs)
    mix_sum = SeqSum(at, *mix_refs)
    branch_src = branch_refs[0]
    mix_src = mix_refs[0]
    two = RowScatter(at, two_g, two_got, two_sum, two_sem)
    step = min(128, L)

    def ahead(order):
        index = lax.rem(order + 2, S)
        t = at.peer(arrival(index))

        def part(i):
            rows = pl.ds(pl.multiple_of(i * step, step), step)
            pre = mm(mix_all[t, rows, :], w_one[...]) + bias_one[...]
            pre_wide[t, rows, :] = pre
            inner = gelu_coef * (pre + 0.044715 * pre * pre * pre)
            act = (0.5 * pre * (1.0 + jnp.tanh(inner))).astype(BF)
            act_all[t, rows, :] = act
            branch_src[t, rows, :] = mm(act, w_two[...]).astype(BF)

        each(0, L // step, part)
        branch_sum.send(index)

    loads.wait(0, 1, 2)
    each(0, S, ahead)
    loads.wait(3)
    column = 384 if hidden % 384 == 0 else hidden
    for i in range(hidden // column):
        cols = slice(i * column, (i + 1) * column)
        wide[cols, :] = mm_tn(
            act_all[:, :, cols].reshape(tokens, column), grad_all[...].reshape(tokens, D)
        )
    part_rows = two_g.shape[2]
    for f in range(F):
        for half in range(2):
            first = (2 * f + half) * part_rows
            two_g[f, half] = wide[first : first + part_rows, :].astype(BF)
    two.start()

    def behind(order):
        index = lax.rem(order + 2, S)
        t = at.peer(arrival(index))

        def part(i):
            rows = pl.ds(pl.multiple_of(i * step, step), step)
            pre = pre_wide[t, rows, :]
            square = pre * pre
            tanh_val = jnp.tanh(gelu_coef * (pre + 0.044715 * square * pre))
            slope = 0.5 * (1.0 + tanh_val) + 0.5 * pre * (
                1.0 - tanh_val * tanh_val
            ) * gelu_coef * (1.0 + 3.0 * 0.044715 * square)
            grad_pre = (mm_nt(grad_all[t, rows, :], w_two[...]) * slope).astype(BF)
            pre_all[t, rows, :] = grad_pre
            mix_src[t, rows, :] = mm_nt(grad_pre, w_one[...]).astype(BF)

        each(0, L // step, part)
        mix_sum.send(index)

    each(0, S, behind)
    for i in range(hidden // column):
        cols = slice(i * column, (i + 1) * column)
        grads = pre_all[:, :, cols].reshape(tokens, column)
        grad_w_one[:, cols] = mm_tn(mix_all[...].reshape(tokens, D), grads).astype(BF)
        grad_b_one[:, cols] = jnp.sum(grads.astype(F32), axis=0, keepdims=True)
    grad_b_two[...] = jnp.sum(grad_all[at.s].astype(F32), axis=0, keepdims=True)
    saves.start(0)
    loads.wait(4, 5, 6, 7, 8)

    mix_sum.wait()
    step_back = min(32, L)
    mod_sums[...] = jnp.zeros_like(mod_sums)
    grad_b_out[...] = jnp.zeros_like(grad_b_out)

    def back(i):
        rows = pl.ds(pl.multiple_of(i * step_back, step_back), step_back)
        grad_mixed = mix_sum.total(rows)
        branch = branch_one[rows, :]
        residual = latents[rows, :].astype(F32) + gate_one * branch
        normed, inv_std = norm_stats(residual)
        grad_out = cotangent[rows, :].astype(F32)
        grad = grad_out + norm_back(grad_mixed * (1.0 + scale), normed, inv_std)
        grad_resid[rows, :] = grad
        low = (gate_one * grad).astype(BF)
        grad_branch[rows, :] = low
        mod_sums[2:3, :] += jnp.sum(grad * branch, axis=0, keepdims=True)
        mod_sums[3:4, :] += jnp.sum(grad_mixed, axis=0, keepdims=True)
        mod_sums[4:5, :] += jnp.sum(grad_mixed * normed, axis=0, keepdims=True)
        grad_b_out[...] += jnp.sum(low.astype(F32), axis=0, keepdims=True)

    each(0, L // step_back, back)
    grad_merged = mm_nt(grad_branch[...], w_out[...]).astype(BF)
    for t in range(S):
        grad_heads[t] = grad_merged[:, t * C : (t + 1) * C]
    saves.start(1, 2)
    for i in range(D // 384):
        cols = slice(i * 384, (i + 1) * 384)
        wide[:D, cols] = mm_tn(merged[...], grad_branch[:, cols])
    rows_own = out_g.shape[2]
    for f in range(F):
        for t in range(S):
            first = (f * S + t) * rows_own
            out_g[t, f] = wide[first : first + rows_own, :].astype(BF)
    saves.start(3)

    branch_sum.wait()

    def finish(i):
        rows = pl.ds(pl.multiple_of(i * step_back, step_back), step_back)
        branch_two = branch_sum.total(rows) + bias_two[...]
        residual = latents[rows, :].astype(F32) + gate_one * branch_one[rows, :]
        block_out[rows, :] = (residual + gate_two * branch_two).astype(BF)
        grad_out = cotangent[rows, :].astype(F32)
        mod_sums[5:6, :] += jnp.sum(grad_out * branch_two, axis=0, keepdims=True)

    each(0, L // step_back, finish)
    two.reduce()
    saves.start(4)
    saves.wait()


def mlp(sizes, *args):
    R, F, S = sizes
    G = F * S
    D, hidden = args[3].shape
    L = args[7].shape[0]
    C = D // S
    half = hidden // F // 2
    shape = jax.ShapeDtypeStruct
    kept = (
        ((L, D), F32),
        ((S, L, C), BF),
        ((D, hidden), BF),
        ((F, half, D), BF),
        ((S, F, D // G, D), BF),
    )
    return pl.pallas_call(
        lambda *refs: mlp_kernel(sizes, *refs),
        name="mlp",
        out_shape=(shape((L, D), BF),)
        + tuple(shape(*item) for item in kept)
        + (
            shape((1, hidden), F32),
            shape((1, D), F32),
            shape((1, D), F32),
            shape((6, D), F32),
        ),
        in_specs=[VM] * 3 + [HB] * 9,
        out_specs=(VM,) + (HB,) * 5 + (VM,) * 4,
        scratch_shapes=[
            pltpu.VMEM((S, L, hidden), BF),
            pltpu.VMEM((S, L, hidden), F32),
            pltpu.VMEM((S, L, hidden), BF),
            pltpu.VMEM((L, D), BF),
            pltpu.VMEM((max(hidden, D), D), F32),
            pltpu.VMEM((F, 2, half, D), BF),
            pltpu.VMEM((F, half, D), BF),
            DMA((2, F)),
        ]
        + SeqSum.scratch(S, L, D)
        + SeqSum.scratch(S, L, D)
        + [DMA((9,)), DMA((5,))]
        + [pltpu.VMEM(x.shape, x.dtype) for x in args[3:]]
        + [pltpu.VMEM(*item) for item in kept],
        compiler_params=params(3, 60),
    )(*args)


class ColumnScatter(Line):
    def __init__(self, at, src, got, stage, inn, far, done, sem):
        self.at, self.src, self.got, self.stage = at, src, got, stage
        self.inn, self.far, self.done, self.sem = inn, far, done, sem
        self.line_up()

    @staticmethod
    def scratch(sizes, rows, cols):
        R, F, S = sizes
        return [
            pltpu.VMEM((F, S // 2, rows, cols), BF),
            pltpu.VMEM((F, S // 2, rows, cols), BF),
            pltpu.VMEM((F * S, rows, cols), BF),
            pltpu.VMEM((S // 2, rows, cols), BF),
            DMA((8, F)),
        ]

    def start(self):
        at = self.at

        def far(i):
            z_to = at.zs(i)

            def one(k):
                slot = z_to * at.S + 2 * k + at.y
                local(self.src.at[slot], self.stage.at[z_to, k], self.sem.at[6, i]).start()
                remote(
                    self.src.at[z_to * at.S + 2 * k + 1 - at.y],
                    self.got.at[z_to, k],
                    self.sem.at[0, z_to],
                    self.sem.at[1, z_to],
                    at.flip(),
                ).start()

            each(0, at.S // 2, one)

        each(0, at.F, far)

    def send(self, z_to, k):
        at = self.at
        s_to = 2 * k + at.y
        home = (z_to == at.z) & (s_to == at.s)

        @pl.when(home)
        def _():
            self.inn[at.me] = self.stage[z_to, k]

        @pl.when(jnp.logical_not(home))
        def _():
            remote(
                self.stage.at[z_to, k],
                self.inn.at[at.me],
                self.sem.at[2, z_to],
                self.sem.at[3, 0],
                {"fsdp": z_to, "seq": s_to},
            ).start()

    def scatter(self):
        at = self.at

        def step(index):
            i = lax.rem(index + 2, at.F)
            z_to = at.zs(i)
            await_bytes(self.got.at[0], self.sem.at[1, z_to])
            await_bytes(self.got.at[0], self.sem.at[6, i])

            def one(k):
                total = self.stage[z_to, k].astype(F32) + self.got[z_to, k].astype(F32)
                self.stage[z_to, k] = total.astype(BF)

                @pl.when(jnp.logical_not(self.line & (z_to == self.opposite)))
                def _():
                    self.send(z_to, k)

            each(0, at.S // 2, one)

            @pl.when(self.end & (z_to == self.opposite))
            def _():
                remote(
                    self.stage.at[z_to],
                    self.far,
                    self.sem.at[2, z_to],
                    self.sem.at[7, 0],
                    {"fsdp": self.beside},
                ).start()

        each(0, at.F, step)

    def relay(self):
        at = self.at

        @pl.when(self.inner)
        def _():
            await_bytes(self.far, self.sem.at[7, 0])
            z_to = self.opposite

            def one(k):
                total = self.stage[z_to, k].astype(F32) + self.far[k].astype(F32)
                self.stage[z_to, k] = total.astype(BF)
                self.send(z_to, k)

            each(0, at.S // 2, one)

    def total(self):
        at = self.at

        @pl.when(at.mine & self.end)
        def _():
            await_bytes(self.inn.at[pl.ds(0, max(1, at.G - 1 - at.S))], self.sem.at[3, 0])

            def clear(t):
                slot = self.opposite * at.S + t
                self.inn[slot] = jnp.zeros_like(self.done[0])

            each(0, at.S, clear)

        @pl.when(at.mine & jnp.logical_not(self.end))
        def _():
            await_bytes(self.inn.at[pl.ds(0, at.G - 1)], self.sem.at[3, 0])

        @pl.when(at.mine)
        def _():
            def one(t):
                total = self.inn[t].astype(F32)
                for f in range(1, at.F):
                    total = total + self.inn[f * at.S + t].astype(F32)
                self.done[t] = total.astype(BF)

            each(0, at.S, one)
            remote(
                self.done, self.done, self.sem.at[4, 0], self.sem.at[5, 0], at.flip()
            ).start()

    def finish(self):
        at = self.at
        half = self.got.at[0]
        each(0, at.F, lambda z: await_bytes(half, self.sem.at[0, z]))
        each(1, at.F, lambda i: await_bytes(half, self.sem.at[2, at.zs(i)]))

        @pl.when(at.mine)
        def _():
            if at.S > 2:
                await_bytes(self.got.at[0, pl.ds(0, at.S // 2 - 1)], self.sem.at[2, at.z])
            await_bytes(self.done, self.sem.at[4, 0])

        @pl.when(jnp.logical_not(at.mine))
        def _():
            await_bytes(half, self.sem.at[2, at.z])
            await_bytes(self.done, self.sem.at[5, 0])


class Tail:
    def __init__(self, at, mod_all, sums, first_in, mod_src, small_src, small_in, cond_src, cond_in, pieces, sem):
        self.at, self.sums, self.first_in = at, sums, first_in
        self.mod_src, self.mod_all = mod_src, mod_all
        self.small_src, self.small_in = small_src, small_in
        self.cond_src, self.cond_in, self.pieces, self.sem = cond_src, cond_in, pieces, sem

    @staticmethod
    def scratch(sizes, D, hidden, rows):
        R, F, S = sizes
        G = F * S
        C = D // S
        pack = 2 * D // G + 2 * rows + hidden // F
        wide = max(D, hidden, 3 * C)
        return [
            pltpu.VMEM((10, wide), F32),
            pltpu.VMEM((S, 10, wide), F32),
            pltpu.VMEM((6, D), BF),
            pltpu.VMEM((F, 1, pack), F32),
            pltpu.VMEM((R * F, 1, pack), F32),
            pltpu.VMEM((R * F, 1, rows), F32),
            pltpu.VMEM((G, 1, rows), F32),
            pltpu.VMEM((G, 1, pack), F32),
            DMA((8, max(S, 2 * F, G))),
        ]

    def first_copy(self, j):
        at = self.at
        return remote(
            self.sums, self.first_in.at[at.s], self.sem.at[0, j], self.sem.at[1, j], {"seq": at.ss(j)}
        )

    def start(self, mod_sums, b_one, b_two, b_out, b_qkv):
        sums = self.sums
        D = mod_sums.shape[1]
        hidden = b_one.shape[1]
        sums[...] = jnp.zeros_like(sums)
        sums[0:6, 0:D] = mod_sums[...]
        sums[6:7, 0:hidden] = b_one[...]
        sums[7:8, 0:D] = b_two[...]
        sums[8:9, 0:D] = b_out[...]
        sums[9:10, 0 : b_qkv.shape[1]] = b_qkv[...]
        each(1, self.at.S, lambda j: self.first_copy(j).start())
        self.first_in[self.at.s] = sums[...]

    def wide_copies(self, i):
        at = self.at
        slot = at.y * at.F + at.z
        device = {"rep": lax.rem(at.y + i // at.F, 2), "fsdp": at.zs(i)}
        return (
            remote(self.mod_src, self.mod_all.at[slot], self.sem.at[2, i], self.sem.at[3, i], device),
            remote(
                self.small_src.at[at.zs(i)],
                self.small_in.at[slot],
                self.sem.at[4, i],
                self.sem.at[5, i],
                device,
            ),
        )

    def middle(self, D, hidden, rows):
        at = self.at
        F, S, G = at.F, at.S, at.G
        C = D // S
        qv = 2 * D // G
        each(1, S, lambda j: self.first_copy(j).wait())
        total = self.first_in[0]
        for t in range(1, S):
            total = total + self.first_in[t]
        self.mod_src[...] = total[0:6, 0:D].astype(BF)
        for g in range(G):
            g_half = g % (G // 2)
            t = g_half // (F // 2)
            col = (g_half % (F // 2)) * qv + (2 * C if g >= G // 2 else 0)
            self.pieces[g, :, 0:qv] = self.first_in[t, 9:10, col : col + qv]
            self.pieces[g, :, qv : qv + rows] = total[8:9, g * rows : (g + 1) * rows]
            self.pieces[g, :, qv + rows : qv + 2 * rows] = total[7:8, g * rows : (g + 1) * rows]
        block = hidden // F
        for f in range(F):
            self.small_src[f, :, 0 : qv + 2 * rows] = self.pieces[f * S + at.s][:, 0 : qv + 2 * rows]
            self.small_src[f, :, qv + 2 * rows :] = self.sums[6:7, f * block : (f + 1) * block]

        def send(i):
            first, second = self.wide_copies(i)
            first.start()
            second.start()

        each(1, 2 * F, send)
        slot = at.y * F + at.z
        self.mod_all[slot] = self.mod_src[...]
        self.small_in[slot] = self.small_src[at.z]

    def cond_copy(self, i):
        at = self.at
        to = lax.rem(at.me + i, at.G)
        return remote(
            self.cond_src.at[at.y * at.F + to // at.S],
            self.cond_in.at[at.me],
            self.sem.at[6, i],
            self.sem.at[7, i],
            {"fsdp": to // at.S, "seq": lax.rem(to, at.S)},
        )

    def owners(self, w_ada, small_out):
        at = self.at
        F, G = at.F, at.G
        D = self.mod_src.shape[1]

        def arrive(i):
            first, second = self.wide_copies(i)
            first.wait()
            second.wait()

        each(1, 2 * F, arrive)
        cond = None
        for v in range(6):
            rows = self.mod_all[:, v, :]
            part = mm_nt(rows, w_ada[:, v * D : (v + 1) * D])
            cond = part if cond is None else cond + part
        for i in range(2 * F):
            self.cond_src[i] = cond[i : i + 1, :]
        each(1, G, lambda i: self.cond_copy(i).start())
        self.cond_in[at.me] = self.cond_src[at.y * F + at.z]
        total = self.small_in[0]
        for i in range(1, 2 * F):
            total = total + self.small_in[i]
        small_out[...] = total

    def finish(self, cond, grad_cond):
        at = self.at
        rows = self.cond_in.shape[2]
        each(1, at.G, lambda i: self.cond_copy(i).wait())
        for g in range(at.G):
            cols = slice(g * rows, (g + 1) * rows)
            value = cond[:, cols].astype(F32)
            gate = jax.nn.sigmoid(value)
            grad_cond[:, cols] = self.cond_in[g] * gate * (1.0 + value * (1.0 - gate))


def backward_kernel(sizes, *refs):
    at = Place(sizes)
    R, F, S, G = at.R, at.F, at.S, at.G
    grad_heads, heads, two_g, out_g, w_qkv, mixed_all, latents, grad_resid, w_ada = refs[-9:]
    log_sums, mod, sums_in, b_one, b_two, b_out, cond, one_g = refs[:8]
    given = refs[8:17]
    grad_latents, o_qkv, o_one, o_two, o_out, o_mod, o_small, o_cond = refs[17:25]
    grad_in, key_flip, key_grad, val_grad, grad_proj, qkv_wide, qkv_g, mod_sums, b_qkv, in_sem = refs[25:35]
    rest = list(refs[35:])
    mix_sum = SeqSum(at, *rest[0:4])
    mix_src = rest[0]
    qkv = ColumnScatter(at, qkv_g, *rest[4:8], o_qkv, rest[8])
    one = ColumnScatter(at, one_g, *rest[9:13], o_one, rest[13])
    two = RowOwner(at, two_g, rest[14], o_two, rest[15], rest[16])
    out = FullScatter(at, out_g, *rest[17:22], o_out, rest[22])
    tail = Tail(at, o_mod, *rest[23:32])
    load_sem = rest[32]
    held = rest[33:42]
    loads = Moves(load_sem, *zip(given, held))
    loads.start()
    _, L, C = grad_heads.shape
    rows_own, D = o_out.shape
    hidden = one_g.shape[2]
    local_heads = H // S
    size = D // H
    greet(G, lambda i: {"fsdp": lax.rem(at.me + i, G) // S, "seq": lax.rem(at.me + i, S)})
    greet(2 * F, lambda i: {"rep": lax.rem(at.y + i // F, 2), "fsdp": at.zs(i)})
    greet_wait(G - 1 + 2 * F - 1)

    def in_copy(j):
        return remote(
            grad_heads.at[at.peer(j)],
            grad_in.at[at.s],
            in_sem.at[0, j],
            in_sem.at[1, j],
            {"seq": at.peer(j)},
        )

    loads.wait(0)
    each(1, S, lambda j: in_copy(j).start())
    one.start()
    loads.wait(1, 2, 3)
    two.start()
    out.start()
    grad_in[at.s] = grad_heads[at.s]
    for h in range(local_heads):
        key_flip[h] = heads[local_heads + h].T
    key_grad[...] = jnp.zeros_like(key_grad)
    val_grad[...] = jnp.zeros_like(val_grad)
    factor = size ** (-0.5) * log2e
    score_scale = size ** (-0.5)
    pad = jnp.zeros((L, LANES - size), BF)

    def block(j):
        t = at.peer(j)

        @pl.when(j > 0)
        def _():
            in_copy(j).wait()

        rows = pl.ds(pl.multiple_of(t * L, L), L)
        for h in range(local_heads):
            query = heads[h, rows, :]
            grad = jnp.concatenate([grad_in[t, :, h * size : (h + 1) * size], pad], axis=1)
            scores = mm_nt(heads[local_heads + h], query) * factor
            probs = jnp.exp2(scores - log_sums[h, t])
            grad_probs = mm_nt(heads[2 * local_heads + h], grad)
            inner = jnp.sum(probs * grad_probs, axis=0, keepdims=True)
            grad_scores = (probs * (grad_probs - inner)).astype(BF)
            query_grad = mm(key_flip[h], grad_scores) * score_scale
            grad_proj[t, :, h * size : (h + 1) * size] = query_grad.T[:, :size].astype(BF)
            key_grad[h] += mm(grad_scores, query)
            val_grad[h] += mm(probs.astype(BF), grad)

    block(0)
    out.cross()
    each(1, S, block)
    two.relay()
    for h in range(local_heads):
        low = (key_grad[h] * score_scale)[:, :size].astype(BF)
        grad_proj[:, :, C + h * size : C + (h + 1) * size] = low.reshape(S, L, size)
        low = val_grad[h][:, :size].astype(BF)
        grad_proj[:, :, 2 * C + h * size : 2 * C + (h + 1) * size] = low.reshape(S, L, size)

    loads.wait(4, 5)

    def spread(index):
        t = at.peer(arrival(index))
        mix_src[t] = mm_nt(grad_proj[t], w_qkv[...]).astype(BF)
        mix_sum.send(index)

    each(0, S, lambda index: spread(lax.rem(index + 2, S)))
    one.scatter()
    out.scatter()
    grads = grad_proj[...].reshape(S * L, 3 * C)
    qkv_wide[...] = mm_tn(mixed_all[...].reshape(S * L, D), grads)
    for g in range(G):
        qkv_g[g] = qkv_wide[g * rows_own : (g + 1) * rows_own, :].astype(BF)
    qkv.start()
    b_qkv[...] = jnp.sum(grads.astype(F32), axis=0, keepdims=True)
    mix_sum.wait()
    loads.wait(6, 7, 8)
    step = min(32, L)
    mod_sums[...] = sums_in[...]
    scale = mod[1:2, :]

    def back(i):
        rows = pl.ds(pl.multiple_of(i * step, step), step)
        grad_mixed = mix_sum.total(rows)
        normed, inv_std = norm_stats(latents[rows, :].astype(F32))
        grad_latents[rows, :] = grad_resid[rows, :] + norm_back(
            grad_mixed * (1.0 + scale), normed, inv_std
        )
        mod_sums[0:1, :] += jnp.sum(grad_mixed, axis=0, keepdims=True)
        mod_sums[1:2, :] += jnp.sum(grad_mixed * normed, axis=0, keepdims=True)

    each(0, L // step, back)
    tail.start(mod_sums, b_one, b_two, b_out, b_qkv)
    out.along()
    one.relay()
    two.total()
    tail.middle(D, hidden, rows_own)
    qkv.scatter()
    out.total()
    one.total()
    qkv.relay()
    tail.owners(w_ada, o_small)
    tail.finish(cond, o_cond)
    qkv.total()
    out.finish()
    two.finish()
    one.finish()
    qkv.finish()


def backward(sizes, *args):
    R, F, S = sizes
    G = F * S
    one_g, grad_heads, two_g = args[7], args[8], args[10]
    latents, w_ada = args[14], args[16]
    _, L, C = grad_heads.shape
    D = latents.shape[1]
    T = S * L
    local_heads = H // S
    rows = w_ada.shape[0]
    hidden = one_g.shape[2]
    pack = 2 * D // G + 2 * rows + hidden // F
    shape = jax.ShapeDtypeStruct
    return pl.pallas_call(
        lambda *refs: backward_kernel(sizes, *refs),
        name="backward",
        out_shape=(
            shape((L, D), F32),
            shape((S, rows, 3 * C), BF),
            shape((S, rows, hidden), BF),
            shape((2,) + two_g.shape[1:], BF),
            shape((rows, D), BF),
            shape((R * F, 6, D), BF),
            shape((1, pack), F32),
            shape((1, D), F32),
        ),
        in_specs=[VM] * 7 + [HB] * 10,
        out_specs=(VM,) * 8,
        scratch_shapes=[
            pltpu.VMEM((S, L, C), BF),
            pltpu.VMEM((local_heads, LANES, T), BF),
            pltpu.VMEM((local_heads, T, LANES), F32),
            pltpu.VMEM((local_heads, T, LANES), F32),
            pltpu.VMEM((S, L, 3 * C), BF),
            pltpu.VMEM((D, 3 * C), F32),
            pltpu.VMEM((G, rows, 3 * C), BF),
            pltpu.VMEM((6, D), F32),
            pltpu.VMEM((1, 3 * C), F32),
            DMA((2, S)),
        ]
        + SeqSum.scratch(S, L, D)
        + ColumnScatter.scratch(sizes, rows, 3 * C)
        + ColumnScatter.scratch(sizes, rows, hidden)
        + RowOwner.scratch(F, two_g.shape)
        + FullScatter.scratch(sizes, rows, D)
        + Tail.scratch(sizes, D, hidden, rows)
        + [DMA((9,))]
        + [pltpu.VMEM(x.shape, x.dtype) for x in args[8:]],
        compiler_params=params(4, 60),
    )(*args)


def assemble_kernel(sizes, qkv, one, two, out, mod_all, silu_all, o_qkv, o_one, o_two, o_out, o_ada, o_b_ada, flat, pieces):
    R, F, S = sizes
    G = F * S
    D = o_out.shape[1]
    C = D // S
    hidden = one.shape[2]
    o_out[...] = out[...].astype(F32)
    for p in range(2):
        o_two[p] = two[p].astype(F32)
    block = hidden // F
    for t in range(S):
        for f in range(F):
            col = (f * S + t) * block
            o_one[:, col : col + block] = one[t, :, f * block : (f + 1) * block].astype(F32)
        for j in range(3):
            o_qkv[:, j * D + t * C : j * D + (t + 1) * C] = qkv[t, :, j * C : (j + 1) * C].astype(F32)
    silu = silu_all[:, 0, :].astype(BF)
    width = o_b_ada.shape[1]
    for v in range(6):
        rows = mod_all[:, v, :]
        o_ada[:, v * D : (v + 1) * D] = mm_tn(silu, rows)
        flat[:, v * D : (v + 1) * D] = jnp.sum(rows.astype(F32), axis=0, keepdims=True)
    for g in range(G):
        pieces[g] = flat[:, g * width : (g + 1) * width]
    o_b_ada[...] = pieces[lax.axis_index("fsdp") * S + lax.axis_index("seq")]


def assemble(sizes, qkv, one, two, out, mod_all, silu_all):
    R, F, S = sizes
    G = F * S
    rows, D = out.shape
    shape = jax.ShapeDtypeStruct
    return pl.pallas_call(
        lambda *refs: assemble_kernel(sizes, *refs),
        name="assemble",
        out_shape=(
            shape((rows, 3 * D), F32),
            shape((rows, one.shape[2] * S), F32),
            shape(two.shape, F32),
            shape((rows, D), F32),
            shape((rows, 6 * D), F32),
            shape((1, 6 * D // G), F32),
        ),
        in_specs=[VM] * 6,
        out_specs=(VM,) * 6,
        scratch_shapes=[pltpu.VMEM((1, 6 * D), F32), pltpu.VMEM((G, 1, 6 * D // G), F32)],
        compiler_params=pltpu.CompilerParams(vmem_limit_bytes=40 * 1024 * 1024),
    )(qkv, one, two, out, mod_all, silu_all)


def on_device(
    latents, cond, w_ada, b_ada, w_qkv, b_qv, w_out, b_out, w_one, b_one, w_two, b_two, cotangent
):
    sizes = R, F, S = tuple(lax.axis_size(name) for name in ("rep", "fsdp", "seq"))
    G = F * S
    _, L, D = latents.shape
    hidden = w_one.shape[1] // S
    rows = w_ada.shape[0]
    qv = b_qv.shape[0]
    owner = lax.axis_index(("fsdp", "seq"))
    width = b_ada.shape[0]
    bias_slot = lax.dynamic_update_slice(
        jnp.zeros((w_ada.shape[1],), F32), b_ada.astype(F32), (owner * width,)
    )[None]
    bias_pack = jnp.concatenate([b_qv, b_out, b_two, b_one]).astype(F32)[None]
    tokens = latents[0]
    two_rows = w_two.shape[0]
    (
        mixed_all,
        heads,
        merged,
        branch_one,
        mix_all,
        grad_all,
        full_qkv,
        full_out,
        log_sums,
        mod,
        silu_all,
        bias_one,
        bias_two,
        g_one,
        g_two,
    ) = forward(
        sizes,
        cond,
        bias_slot,
        bias_pack,
        tokens,
        cotangent[0],
        w_ada,
        w_qkv,
        w_one,
        w_two.reshape(2, two_rows // 2, D),
        w_out,
    )
    full_one = g_one.reshape(D, hidden)
    full_two = g_two.reshape(hidden, D)
    (
        block_out,
        grad_resid,
        grad_heads,
        one_g,
        two_g,
        out_g,
        grad_b_one,
        grad_b_two,
        grad_b_out,
        mod_sums,
    ) = mlp(
        sizes,
        mod,
        bias_one,
        bias_two,
        full_one,
        mix_all,
        full_two,
        grad_all,
        tokens,
        branch_one,
        cotangent[0],
        full_out,
        merged,
    )
    grad_latents, qkv_sum, one_sum, two_sum, out_sum, mod_all, o_small, o_cond = backward(
        sizes,
        log_sums,
        mod,
        mod_sums,
        grad_b_one,
        grad_b_two,
        grad_b_out,
        cond,
        one_g.reshape(G, rows, hidden),
        grad_heads,
        heads,
        two_g,
        out_g,
        full_qkv,
        mixed_all,
        tokens,
        grad_resid,
        w_ada,
    )
    o_qkv, o_one, o_two, o_out, o_ada, o_b_ada = assemble(
        sizes, qkv_sum, one_sum, two_sum, out_sum, mod_all, silu_all
    )
    small = o_small[0]
    return (
        block_out[None],
        grad_latents[None],
        o_cond,
        o_ada,
        o_b_ada[0],
        o_qkv,
        small[:qv],
        o_out,
        small[qv : qv + rows],
        o_one,
        small[qv + 2 * rows :],
        o_two.reshape(two_rows, D),
        small[qv + rows : qv + 2 * rows],
    )


def solution(mesh):
    owned = P(("fsdp", "seq"), None)
    owned_bias = P(("fsdp", "seq"))
    token_spec = P(("rep", "fsdp"), "seq", None)
    cond_spec = P(("rep", "fsdp"), None)
    weights = (owned, owned_bias) * 5
    in_specs = (token_spec, cond_spec) + weights + (token_spec,)
    out_specs = (token_spec, token_spec, cond_spec) + weights
    return jax.shard_map(
        on_device, mesh=mesh, in_specs=in_specs, out_specs=out_specs, check_vma=False
    )
```

```python
import math

import jax
import jax.numpy as jnp
from jax import lax
from jax.experimental import pallas as pl
from jax.experimental.pallas import tpu as pltpu
from jax.sharding import PartitionSpec as P

H = 16
epsilon = 1e-06
gelu_coef = math.sqrt(2.0 / math.pi)
log2e = math.log2(math.e)
BF = jnp.bfloat16
F32 = jnp.float32
LANES = 128
VM = pl.BlockSpec(memory_space=pltpu.VMEM)
HB = pl.BlockSpec(memory_space=pl.ANY)
DMA = pltpu.SemaphoreType.DMA


def params(ident, mib):
    return pltpu.CompilerParams(
        collective_id=ident, has_side_effects=True, vmem_limit_bytes=mib * 1024 * 1024
    )


def remote(src, dst, send, recv, device):
    return pltpu.make_async_remote_copy(
        src_ref=src,
        dst_ref=dst,
        send_sem=send,
        recv_sem=recv,
        device_id=device,
        device_id_type=pl.DeviceIdType.MESH,
    )


def local(src, dst, sem):
    return pltpu.make_async_copy(src, dst, sem)


def await_bytes(like, sem):
    pltpu.make_async_copy(like, like, sem).wait()


class Moves:
    def __init__(self, sem, *pairs):
        self.copies = [local(pair[0], pair[1], sem.at[i]) for i, pair in enumerate(pairs)]

    def start(self, *which):
        for i in which or range(len(self.copies)):
            self.copies[i].start()

    def wait(self, *which):
        for i in which or range(len(self.copies)):
            self.copies[i].wait()


def each(start, stop, body):
    def step(index, carry):
        body(index)
        return carry

    lax.fori_loop(start, stop, step, 0)


def greet(count, device_of):
    gate = pltpu.get_barrier_semaphore()
    each(
        1,
        count,
        lambda i: pl.semaphore_signal(
            gate, 1, device_id=device_of(i), device_id_type=pl.DeviceIdType.MESH
        ),
    )
    return count - 1


def greet_wait(count):
    pl.semaphore_wait(pltpu.get_barrier_semaphore(), count)


def norm_stats(values):
    center = values - jnp.mean(values, axis=-1, keepdims=True)
    inv_std = lax.rsqrt(jnp.mean(center * center, axis=-1, keepdims=True) + epsilon)
    return (center * inv_std, inv_std)


def norm_back(grad, normed, inv_std):
    return inv_std * (
        grad
        - jnp.mean(grad, axis=-1, keepdims=True)
        - normed * jnp.mean(grad * normed, axis=-1, keepdims=True)
    )


def mm(left, right):
    return jnp.dot(left, right, preferred_element_type=F32)


def mm_nt(left, right):
    return lax.dot_general(left, right, (((1,), (1,)), ((), ())), preferred_element_type=F32)


def mm_tn(left, right):
    return lax.dot_general(left, right, (((0,), (0,)), ((), ())), preferred_element_type=F32)


class Place:
    def __init__(self, sizes):
        self.R, self.F, self.S = sizes
        self.G = self.F * self.S
        self.y = lax.axis_index("rep")
        self.z = lax.axis_index("fsdp")
        self.s = lax.axis_index("seq")
        self.me = self.z * self.S + self.s
        self.mine = lax.rem(self.s, 2) == self.y
        self.steps = (2, 1, 3) if self.F == 4 else tuple(range(1, self.F))

    def zs(self, i):
        return lax.rem(self.z + i, self.F)

    def zs_back(self, i):
        return lax.rem(self.z - i + self.F, self.F)

    def ss(self, i):
        return lax.rem(self.s + i, self.S)

    def ss_back(self, i):
        return lax.rem(self.s - i + self.S, self.S)

    def flip(self):
        return {"rep": 1 - self.y}

    def peer(self, j):
        return lax.bitwise_xor(self.s, j)


class SeqGather:
    def __init__(self, at, dst, sem):
        self.at, self.dst, self.sem = at, dst, sem

    @staticmethod
    def scratch(S):
        return DMA((4, S))

    def direct(self, j):
        at, block = self.at, self.dst.at[self.at.s]
        return remote(block, block, self.sem.at[0, j], self.sem.at[1, j], {"seq": at.peer(j)})

    def handed(self, j):
        at = self.at
        block = self.dst.at[at.peer(j)]
        return remote(block, block, self.sem.at[2, j], self.sem.at[3, j], {"seq": at.peer(1)})

    def start(self):
        for j in range(3, self.at.S, 2):
            self.direct(j).start()
        self.direct(1).start()

    def arrive(self, index):
        @pl.when(index == 1)
        def _():
            self.direct(1).wait()

        if self.at.S > 2:

            @pl.when((index >= 2) & (lax.rem(index, 2) == 0))
            def _():
                self.direct(index + 1).wait()
                self.handed(index + 1).start()

            @pl.when((index >= 2) & (lax.rem(index, 2) == 1))
            def _():
                self.handed(index).wait()


def arrival(index):
    return jnp.where(index < 2, index, lax.bitwise_xor(index, 1))


class SeqSum:
    def __init__(self, at, src, near, inn, sem):
        self.at, self.src, self.near, self.inn, self.sem = at, src, near, inn, sem

    @staticmethod
    def scratch(S, rows, cols):
        return [
            pltpu.VMEM((S, rows, cols), BF),
            pltpu.VMEM((S // 2, rows, cols), BF),
            pltpu.VMEM((S // 2, rows, cols), BF),
            DMA((4, S)),
        ]

    def sibling(self, j):
        at = self.at
        return remote(
            self.src.at[at.peer(j)],
            self.near.at[j // 2],
            self.sem.at[0, j],
            self.sem.at[1, j],
            {"seq": at.peer(1)},
        )

    def direct(self, j):
        at = self.at
        return remote(
            self.src.at[at.peer(j)],
            self.inn.at[j // 2],
            self.sem.at[2, j],
            self.sem.at[3, j],
            {"seq": at.peer(j)},
        )

    def send(self, index):
        @pl.when((index == 1) | ((index >= 2) & (lax.rem(index, 2) == 0)))
        def _():
            self.sibling(lax.bitwise_or(index, 1)).start()

        if self.at.S > 2:

            @pl.when((index >= 2) & (lax.rem(index, 2) == 1))
            def _():
                j = index - 1
                self.sibling(index).wait()
                t = self.at.peer(j)
                step = min(64, self.src.shape[1])

                def add(i):
                    rows = pl.ds(pl.multiple_of(i * step, step), step)
                    both = self.src[t, rows, :].astype(F32) + self.near[j // 2, rows, :].astype(F32)
                    self.src[t, rows, :] = both.astype(BF)

                each(0, self.src.shape[1] // step, add)
                self.direct(j).start()

    def wait(self):
        self.sibling(1).wait()
        for j in range(2, self.at.S, 2):
            self.direct(j).wait()

    def total(self, rows):
        value = self.src[self.at.s, rows, :].astype(F32) + self.near[0, rows, :].astype(F32)
        for k in range(1, self.at.S // 2):
            value = value + self.inn[k, rows, :].astype(F32)
        return value


class FarGather:
    relayed = True

    def __init__(self, at, dst, sem):
        self.at, self.dst, self.sem = at, dst, sem
        self.line = self.relayed and at.F == 4

    @staticmethod
    def scratch(F):
        return DMA((7, F))

    def send(self, z_from, z_to, kind):
        pieces = self.half(z_from)
        held = self.origin() if kind == 0 else pieces
        for source, piece in zip(held, pieces):
            remote(
                source, piece, self.sem.at[kind, z_to], self.sem.at[2, z_from], {"fsdp": z_to}
            ).start()

    def origin(self):
        return self.half(self.at.z)

    def await_half(self, row, z):
        await_bytes(self.like(), self.sem.at[row, z])

    def around(self, step, body):
        at = self.at

        @pl.when(at.z >= step)
        def _():
            body(at.z - step)

        @pl.when(at.z + step < at.F)
        def _():
            body(at.z + step)

    def direct(self, step, body):
        if self.line and step == 3:
            return
        self.around(step, body)

    def start_far(self):
        for step in self.at.steps:
            self.direct(step, lambda z_to: self.send(self.at.z, z_to, 0))

    def service(self, step):
        at = self.at

        def take(z_from):
            self.await_half(2, z_from)
            for piece in self.half(z_from):
                remote(
                    piece, piece, self.sem.at[3, z_from], self.sem.at[4, z_from], at.flip()
                ).start()

        self.around(step, take)
        if self.line and step == 2:

            @pl.when((at.z == 1) | (at.z == 2))
            def _():
                far = jnp.where(at.z == 1, 3, 0)
                end = 3 - far
                self.send(far, end, 1)

    def finish_far(self):
        at = self.at

        def swapped(z_from):
            self.await_half(3, z_from)
            self.await_half(4, z_from)

        for step in range(1, at.F):
            self.around(step, swapped)
            self.direct(step, lambda z_to: self.await_half(0, z_to))
        if self.line:

            @pl.when((at.z == 1) | (at.z == 2))
            def _():
                self.await_half(1, jnp.where(at.z == 1, 0, 3))


class ColumnGather(FarGather):
    def __init__(self, at, src, dst, sem):
        super().__init__(at, dst, sem)
        self.src = src

    def half(self, z):
        at = self.at
        return [self.dst.at[z * at.S + 2 * k + at.y] for k in range(at.S // 2)]

    def like(self):
        return self.dst.at[pl.ds(0, self.at.S // 2)]

    def start(self):
        at, src, dst, sem = self.at, self.src, self.dst, self.sem

        def near(j):
            t = at.ss(j)
            remote(src.at[t], dst.at[at.me], sem.at[5, 0], sem.at[6, 0], {"seq": t}).start()

        each(1, at.S, near)
        local(src.at[at.s], dst.at[at.me], sem.at[5, 1]).start()

    def near_done(self):
        at, dst, sem = self.at, self.dst, self.sem
        local(self.src.at[at.s], dst.at[at.me], sem.at[5, 1]).wait()
        near = dst.at[pl.ds(0, at.S - 1)]
        await_bytes(near, sem.at[5, 0])
        await_bytes(near, sem.at[6, 0])


class RowGather(FarGather):
    def __init__(self, at, src, dst, sem):
        super().__init__(at, dst, sem)
        self.src = src

    def half(self, z):
        return [self.dst.at[z, self.at.y]]

    def origin(self):
        return [self.src.at[self.at.y]]

    def like(self):
        return self.dst.at[0, 0]

    def start(self):
        at = self.at
        local(self.src, self.dst.at[at.z], self.sem.at[5, 0]).start()

    def near_done(self):
        at = self.at
        local(self.src, self.dst.at[at.z], self.sem.at[5, 0]).wait()


class OwnGather(FarGather):
    relayed = False

    def __init__(self, at, src, dst, sem):
        super().__init__(at, dst, sem)
        self.src = src

    def half(self, z):
        return [self.dst.at[self.at.s, z]]

    def origin(self):
        return [self.src]

    def like(self):
        return self.src

    def start(self):
        at = self.at
        local(self.src, self.dst.at[at.s, at.z], self.sem.at[5, 0]).start()

    def near_done(self):
        at = self.at
        local(self.src, self.dst.at[at.s, at.z], self.sem.at[5, 0]).wait()

    def start_far(self):
        pl.when(self.at.mine)(super().start_far)

    def service(self, step):
        take = super().service
        pl.when(self.at.mine)(lambda: take(step))

    def finish_far(self):
        at = self.at

        def sent(z_from):
            self.await_half(3, z_from)

        def swapped(z_from):
            self.await_half(4, z_from)

        @pl.when(at.mine)
        def _():
            for step in range(1, at.F):
                self.around(step, sent)
                self.direct(step, lambda z_to: self.await_half(0, z_to))
            if self.line:

                @pl.when((at.z == 1) | (at.z == 2))
                def _():
                    self.await_half(1, jnp.where(at.z == 1, 0, 3))

        @pl.when(jnp.logical_not(at.mine))
        def _():
            for step in range(1, at.F):
                self.around(step, swapped)


def forward_kernel(sizes, *refs):
    at = Place(sizes)
    R, F, S, G = at.R, at.F, at.S, at.G
    cond, biases = refs[:2]
    i_latents, i_cotangent, i_ada, i_qkv, i_one, w_two, w_out = refs[2:9]
    refs = refs[:1] + refs
    o_mixed, o_heads, o_merged, o_branch, o_mix, o_grad, o_full_qkv, o_full_out = refs[10:18]
    log_sums, mod, silu_all, bias_one, bias_two, g_one, g_two = refs[18:25]
    silu_src, part, parts_in, mod_src, mod_in, qkv_src, one_src, pack_all = refs[25:33]
    g_qkv, g_out, wide, bias_qkv, bias_out, val_flip, att, merged_in = refs[33:41]
    silu_sem, part_sem, mod_sem, pack_sem, qkv_sem, one_sem, two_sem, out_sem = refs[41:49]
    mixed_sem, grad_sem, att_sem, mix_sem, spread_sem, load_sem, save_sem = refs[49:56]
    bias_pack, bias_pieces, bias_slot = refs[69:72]
    latents, cotangent, w_ada, w_qkv, w_one = refs[56:61]
    mixed_all, heads, merged, branch_one, mix_all, grad_all, full_qkv, full_out = refs[61:69]
    loads = Moves(
        load_sem,
        (i_qkv, w_qkv),
        (i_ada, w_ada),
        (i_one, w_one),
        (i_latents, latents),
        (i_cotangent, cotangent),
    )
    loads.start()
    saves = Moves(
        save_sem,
        (mixed_all, o_mixed),
        (heads, o_heads),
        (merged, o_merged),
        (branch_one, o_branch),
        (mix_all, o_mix),
        (grad_all, o_grad),
        (full_qkv, o_full_qkv),
        (full_out, o_full_out),
    )
    L, D = latents.shape
    C = D // S
    T = S * L
    local_heads = H // S
    size = D // H
    rows_own = silu_all.shape[2]
    hidden = one_src.shape[2]
    block = hidden // F
    greet(G, lambda i: {"fsdp": lax.rem(at.me + i, G) // S, "seq": lax.rem(at.me + i, S)})
    greet(2 * F, lambda i: {"rep": lax.rem(at.y + i // F, 2), "fsdp": at.zs(i)})
    width = bias_pieces.shape[2]
    bias_pack[...] = biases[:, width:].astype(F32)
    bias_pieces[...] = jnp.zeros_like(bias_pieces)
    bias_pieces[at.me] = biases[:, :width].astype(F32)
    for g in range(G):
        bias_slot[:, g * width : (g + 1) * width] = bias_pieces[g]

    value = cond[...].astype(F32)
    silu = (value * jax.nn.sigmoid(value)).astype(BF).astype(F32)
    for g in range(G):
        silu_src[g] = silu[:, g * rows_own : (g + 1) * rows_own]
    loads.wait(0)
    for t in range(S):
        for j in range(3):
            qkv_src[t, :, j * C : (j + 1) * C] = w_qkv[:, j * D + t * C : j * D + (t + 1) * C]
    loads.wait(2)
    for t in range(S):
        for f in range(F):
            col = (f * S + t) * block
            one_src[t, :, f * block : (f + 1) * block] = w_one[:, col : col + block]
    greet_wait(G - 1 + 2 * F - 1)
    slot = at.y * F + at.z

    def cond_copy(i):
        z_to = at.zs(i)
        return remote(
            silu_src.at[z_to * S + at.s],
            silu_all.at[slot],
            silu_sem.at[0, i],
            silu_sem.at[1, i],
            {"rep": lax.rem(at.y + i // F, 2), "fsdp": z_to},
        )

    each(1, 2 * F, lambda i: cond_copy(i).start())
    silu_all[slot] = silu_src[at.me]

    def pack_copy(i):
        to = lax.rem(at.me + i, G)
        return remote(
            bias_pack,
            pack_all.at[at.me],
            pack_sem.at[0, 0],
            pack_sem.at[1, 0],
            {"fsdp": to // S, "seq": lax.rem(to, S)},
        )

    each(1, G, lambda i: pack_copy(i).start())
    pack_all[at.me] = bias_pack[...]

    qkv = ColumnGather(at, qkv_src, g_qkv, qkv_sem)
    one = ColumnGather(at, one_src, g_one, one_sem)
    two = RowGather(at, w_two, g_two, two_sem)
    out = OwnGather(at, w_out, g_out, out_sem)
    qkv.start()
    two.start()
    out.start()

    each(1, 2 * F, lambda i: cond_copy(i).wait())
    left = jnp.concatenate([silu_all[at.y * F + f] for f in range(F)], axis=0).astype(BF)
    loads.wait(1)
    sums = mm(left, w_ada[...]) + bias_slot[...]
    for f in range(F):
        for v in range(6):
            for t in range(S):
                col = v * D + t * C
                part[f * S + t, v : v + 1, :] = sums[f : f + 1, col : col + C]

    def part_copy(i):
        to = lax.rem(at.me + i, G)
        return remote(
            part.at[to],
            parts_in.at[at.me],
            part_sem.at[0, i],
            part_sem.at[1, i],
            {"fsdp": to // S, "seq": lax.rem(to, S)},
        )

    each(1, G, lambda i: part_copy(i).start())
    parts_in[at.me] = part[at.me]
    qkv.near_done()
    qkv.start_far()
    each(1, G, lambda i: part_copy(i).wait())
    total = parts_in[0]
    for g in range(1, G):
        total = total + parts_in[g]
    mod_src[...] = total

    def mod_copy(i):
        return remote(
            mod_src, mod_in.at[at.s], mod_sem.at[0, i], mod_sem.at[1, i], {"seq": at.ss(i)}
        )

    each(1, S, lambda i: mod_copy(i).start())
    one.start()
    mod_in[at.s] = total
    out.start_far()
    each(1, S, lambda i: mod_copy(i).wait())
    for t in range(S):
        mod[:, t * C : (t + 1) * C] = mod_in[t]

    loads.wait(3)
    step = min(64, L)

    def norm(i):
        at_rows = pl.ds(pl.multiple_of(i * step, step), step)
        normed, _ = norm_stats(latents[at_rows, :].astype(F32))
        mixed_all[at.s, at_rows, :] = (normed * (1.0 + mod[1:2, :]) + mod[0:1, :]).astype(BF)

    each(0, L // step, norm)
    gather = SeqGather(at, mixed_all, mixed_sem)
    gather.start()
    loads.wait(4)
    grad_all[at.s] = (mod[5:6, :] * cotangent[...].astype(F32)).astype(BF)
    grad_gather = SeqGather(at, grad_all, grad_sem)
    grad_gather.start()
    one.near_done()
    qkv.service(at.steps[0])
    one.start_far()
    out.near_done()
    two.near_done()

    others = pack_all.at[pl.ds(0, G - 1)]
    await_bytes(others, pack_sem.at[0, 0])
    await_bytes(others, pack_sem.at[1, 0])
    qv = 2 * D // G
    own = F // 2
    bias_qkv[...] = jnp.zeros_like(bias_qkv)
    for i in range(own):
        bias_qkv[:, i * qv : (i + 1) * qv] = pack_all[at.s * own + i][:, 0:qv]
        bias_qkv[:, 2 * C + i * qv : 2 * C + (i + 1) * qv] = pack_all[G // 2 + at.s * own + i][
            :, 0:qv
        ]
    for g in range(G):
        cols = slice(g * rows_own, (g + 1) * rows_own)
        bias_out[:, cols] = pack_all[g][:, qv : qv + rows_own]
        bias_two[:, cols] = pack_all[g][:, qv + rows_own : qv + 2 * rows_own]
    for f in range(F):
        bias_one[:, f * block : (f + 1) * block] = pack_all[f * S + at.s][:, qv + 2 * rows_own :]

    for i in at.steps[1:]:
        qkv.service(i)
    for i in at.steps:
        out.service(i)
    qkv.finish_far()

    def join(slabs, whole):
        cols = whole.shape[1]
        for g in range(G):
            wide[g * rows_own : (g + 1) * rows_own, 0:cols] = slabs(g).astype(F32)
        tall = 128 if D % 128 == 0 else D

        def cast(i):
            at_rows = pl.ds(pl.multiple_of(i * tall, tall), tall)
            whole[at_rows, :] = wide[at_rows, 0:cols].astype(BF)

        each(0, D // tall, cast)

    join(lambda g: g_qkv[g], full_qkv)
    saves.start(6)

    pad = jnp.zeros((L, LANES - size), BF)

    def project(index):
        gather.arrive(index)
        t = at.peer(arrival(index))
        at_rows = pl.ds(pl.multiple_of(t * L, L), L)
        done = (mm(mixed_all[t], full_qkv[...]) + bias_qkv[...]).astype(BF)
        for c in range(3 * local_heads):
            heads[c, at_rows, :] = jnp.concatenate(
                [done[:, c * size : (c + 1) * size], pad], axis=1
            )

    each(0, S, project)
    saves.start(0, 1)
    out.finish_far()
    spread = SeqGather(at, g_out, spread_sem)
    spread.start()
    each(1, S, grad_gather.arrive)
    saves.start(5)
    for h in range(local_heads):
        val_flip[h] = heads[2 * local_heads + h].T

    def att_copy(j):
        t = at.peer(j)
        return remote(
            att.at[t], merged_in.at[at.s], att_sem.at[0, j], att_sem.at[1, j], {"seq": t}
        )

    factor = size ** (-0.5) * log2e

    def attention(index):
        j = S - 1 - index
        t = at.peer(j)
        at_rows = pl.ds(pl.multiple_of(t * L, L), L)
        for h in range(local_heads):
            scores = mm_nt(heads[local_heads + h], heads[h, at_rows, :]) * factor
            highest = jnp.max(scores, axis=0, keepdims=True)
            raised = jnp.exp2(scores - highest)
            summed = jnp.sum(raised, axis=0, keepdims=True)
            result = mm(val_flip[h], raised.astype(BF)) / summed
            log_sums[h, t] = highest + jnp.log2(summed)
            att[t, :, h * size : (h + 1) * size] = result.T[:, :size].astype(BF)

        @pl.when(j > 0)
        def _():
            att_copy(j).start()

    one.service(at.steps[0])
    one.service(at.steps[1])
    two.start_far()
    each(0, S, attention)
    merged_in[at.s] = att[at.s]
    each(1, S, spread.arrive)
    join(lambda g: g_out[g % S, g // S], full_out)
    saves.start(7)
    each(1, S, lambda j: att_copy(j).wait())
    for t in range(S):
        merged[:, t * C : (t + 1) * C] = merged_in[t]
    saves.start(2)

    def project_out(i):
        at_rows = pl.ds(pl.multiple_of(i * step, step), step)
        branch = mm(merged[at_rows, :], full_out[...]) + bias_out[...]
        branch_one[at_rows, :] = branch
        residual = latents[at_rows, :].astype(F32) + mod[2:3, :] * branch
        normed, _ = norm_stats(residual)
        mix_all[at.s, at_rows, :] = (normed * (1.0 + mod[4:5, :]) + mod[3:4, :]).astype(BF)

    each(0, L // step, project_out)
    saves.start(3)
    mix_gather = SeqGather(at, mix_all, mix_sem)
    mix_gather.start()
    for i in at.steps[2:]:
        one.service(i)
    for i in at.steps:
        two.service(i)
    one.finish_far()
    each(1, S, mix_gather.arrive)
    saves.start(4)
    two.finish_far()
    saves.wait()


def forward(sizes, cond, biases, latents, cotangent, w_ada, w_qkv, w_one, w_two, w_out):
    R, F, S = sizes
    G = F * S
    rows, D = w_out.shape
    L = latents.shape[0]
    T = S * L
    C = D // S
    local_heads = H // S
    hidden = w_one.shape[1] // S
    shape = jax.ShapeDtypeStruct
    width = 6 * D // G
    pack = biases.shape[1] - width
    kept = (
        ((S, L, D), BF),
        ((3 * local_heads, T, LANES), BF),
        ((L, D), BF),
        ((L, D), F32),
        ((S, L, D), BF),
        ((S, L, D), BF),
        ((D, 3 * C), BF),
        ((D, D), BF),
    )
    return pl.pallas_call(
        lambda *refs: forward_kernel(sizes, *refs),
        name="forward",
        out_shape=tuple(shape(*item) for item in kept)
        + (
            shape((local_heads, S, 1, L), F32),
            shape((6, D), F32),
            shape((R * F, 1, rows), F32),
            shape((1, hidden), F32),
            shape((1, D), F32),
            shape((G, rows, hidden), BF),
            shape((F,) + w_two.shape, BF),
        ),
        in_specs=[VM] * 2 + [HB] * 7,
        out_specs=(HB,) * 8 + (VM,) * 5 + (HB,) * 2,
        scratch_shapes=[
            pltpu.VMEM((G, 1, rows), F32),
            pltpu.VMEM((G, 6, C), F32),
            pltpu.VMEM((G, 6, C), F32),
            pltpu.VMEM((6, C), F32),
            pltpu.VMEM((S, 6, C), F32),
            pltpu.VMEM((S, rows, 3 * C), BF),
            pltpu.VMEM((S, rows, hidden), BF),
            pltpu.VMEM((G, 1, pack), F32),
            pltpu.VMEM((G, rows, 3 * C), BF),
            pltpu.VMEM((S, F, rows, D), BF),
            pltpu.VMEM((D, max(D, 3 * C)), F32),
            pltpu.VMEM((1, 3 * C), F32),
            pltpu.VMEM((1, D), F32),
            pltpu.VMEM((local_heads, LANES, T), BF),
            pltpu.VMEM((S, L, C), BF),
            pltpu.VMEM((S, L, C), BF),
            DMA((2, 2 * F)),
            DMA((2, G)),
            DMA((2, S)),
            DMA((2, 1)),
            ColumnGather.scratch(F),
            ColumnGather.scratch(F),
            RowGather.scratch(F),
            OwnGather.scratch(F),
            SeqGather.scratch(S),
            SeqGather.scratch(S),
            DMA((2, S)),
            SeqGather.scratch(S),
            SeqGather.scratch(S),
            DMA((5,)),
            DMA((8,)),
        ]
        + [pltpu.VMEM(x.shape, x.dtype) for x in (latents, cotangent, w_ada, w_qkv, w_one)]
        + [pltpu.VMEM(*item) for item in kept]
        + [
            pltpu.VMEM((1, pack), F32),
            pltpu.VMEM((G, 1, width), F32),
            pltpu.VMEM((1, 6 * D), F32),
        ],
        compiler_params=params(1, 60),
    )(cond, biases, latents, cotangent, w_ada, w_qkv, w_one, w_two, w_out)


class RowScatter:
    def __init__(self, at, src, got, stage, sem):
        self.at, self.src, self.got, self.stage, self.sem = at, src, got, stage, sem

    def start(self):
        at = self.at

        def far(i):
            z_to = at.zs(i)
            remote(
                self.src.at[z_to, 3 - at.y],
                self.got.at[z_to],
                self.sem.at[0, i],
                self.sem.at[1, i],
                at.flip(),
            ).start()

        each(0, at.F, far)

    def reduce(self):
        at = self.at

        def far(i):
            z_to = at.zs(i)
            await_bytes(self.got.at[0], self.sem.at[0, i])
            await_bytes(self.got.at[0], self.sem.at[1, i])
            total = self.src[z_to, 2 + at.y].astype(F32) + self.got[z_to].astype(F32)
            self.stage[z_to] = total.astype(BF)

        each(0, at.F, far)


class Line:
    def line_up(self):
        at = self.at
        self.line = at.F == 4
        self.inner = self.line & ((at.z == 1) | (at.z == 2))
        self.end = self.line & ((at.z == 0) | (at.z == 3))
        self.opposite = jnp.where(at.z < 2, 3, 0)
        self.beside = jnp.where(at.z == 0, 1, 2)


class RowOwner(Line):
    def __init__(self, at, piece, inn, far, sem):
        self.at, self.piece, self.inn, self.far, self.sem = at, piece, inn, far, sem
        self.line_up()

    @staticmethod
    def scratch(F, shape):
        return [pltpu.VMEM((F,) + shape, BF), pltpu.VMEM(shape, BF), DMA((3, F))]

    def out_copy(self, z_to):
        at = self.at
        return remote(
            self.piece(z_to),
            self.inn.at[at.z],
            self.sem.at[0, z_to],
            self.sem.at[1, at.z],
            {"fsdp": z_to},
        )

    def far_copy(self):
        return remote(
            self.piece(self.opposite),
            self.far,
            self.sem.at[0, self.opposite],
            self.sem.at[2, 0],
            {"fsdp": self.beside},
        )

    def start(self):
        at = self.at

        @pl.when(self.end)
        def _():
            self.far_copy().start()
            self.inn[self.opposite] = jnp.zeros_like(self.far)

        def one(i):
            z_to = at.zs(i)

            @pl.when(jnp.logical_not(self.line & (z_to == self.opposite)))
            def _():
                self.out_copy(z_to).start()

        each(1, at.F, one)
        self.inn[at.z] = self.piece(at.z)[...]

    def relay(self):
        @pl.when(self.inner)
        def _():
            await_bytes(self.far, self.sem.at[2, 0])
            z_to = self.opposite
            piece = self.piece(z_to)
            piece[...] = (piece[...].astype(F32) + self.far[...].astype(F32)).astype(BF)
            self.out_copy(z_to).start()

    def total(self):
        at = self.at

        def arrived(i):
            z = at.zs(i)
            await_bytes(self.far, self.sem.at[0, z])

            @pl.when(jnp.logical_not(self.end & (z == self.opposite)))
            def _():
                await_bytes(self.far, self.sem.at[1, z])

        each(1, at.F, arrived)
        total = self.inn[0].astype(F32)
        for f in range(1, at.F):
            total = total + self.inn[f].astype(F32)
        return total.astype(BF)


class Swap:
    def __init__(self, at, done, sem):
        self.at, self.done, self.sem = at, done, sem

    def copy(self):
        mine = self.done.at[self.at.y]
        return remote(mine, mine, self.sem.at[0], self.sem.at[1], self.at.flip())

    def start(self):
        self.copy().start()

    def finish(self):
        self.copy().wait()


class FullScatter:
    def __init__(self, at, src, near, got, stage, inn, done, sem):
        self.at, self.src, self.near, self.got, self.stage = at, src, near, got, stage
        self.inn, self.done, self.sem = inn, done, sem

    @staticmethod
    def scratch(sizes, rows, cols):
        R, F, S = sizes
        return [
            pltpu.VMEM((S // 2, F, rows, cols), BF),
            pltpu.VMEM((S // 2, F, rows, cols), BF),
            pltpu.VMEM((F, rows, cols), BF),
            pltpu.VMEM((F, rows, cols), BF),
            DMA((10, max(F, S))),
        ]

    def sibling(self, j):
        at = self.at
        return remote(
            self.src.at[at.peer(j)],
            self.near.at[j // 2],
            self.sem.at[0, j],
            self.sem.at[1, j],
            {"seq": at.peer(1)},
        )

    def direct(self, j):
        at = self.at
        return remote(
            self.near.at[j // 2],
            self.got.at[j // 2],
            self.sem.at[2, j],
            self.sem.at[3, j],
            {"seq": at.peer(j)},
        )

    def start(self):
        for j in range(3, self.at.S, 2):
            self.sibling(j).start()
        self.sibling(1).start()

    def cross(self):
        at = self.at
        for j in range(2, at.S, 2):
            self.sibling(j + 1).wait()
            k = j // 2

            def add(f):
                both = self.near[k, f].astype(F32) + self.src[at.peer(j), f].astype(F32)
                self.near[k, f] = both.astype(BF)

            each(0, at.F, add)
            self.direct(j).start()
        self.sibling(1).wait()

    def out_copy(self, i):
        at = self.at
        return remote(
            self.stage.at[at.zs(i)],
            self.inn.at[at.z],
            self.sem.at[4, i],
            self.sem.at[5, i],
            {"fsdp": at.zs(i)},
        )

    def scatter(self):
        at = self.at
        for j in range(2, at.S, 2):
            self.direct(j).wait()

        def far(i):
            z_to = at.zs(i)
            total = self.src[at.s, z_to].astype(F32) + self.near[0, z_to].astype(F32)
            for k in range(1, at.S // 2):
                total = total + self.got[k, z_to].astype(F32)
            self.stage[z_to] = total.astype(BF)

            @pl.when(i > 0)
            def _():
                self.out_copy(i).start()

        each(0, at.F, far)
        self.inn[at.z] = self.stage[at.z]

    def total(self):
        at = self.at
        each(1, at.F, lambda i: self.out_copy(i).wait())
        total = self.inn[0].astype(F32)
        for f in range(1, at.F):
            total = total + self.inn[f].astype(F32)
        self.done[at.y] = total.astype(BF)
        mine = self.done.at[at.y]
        remote(mine, mine, self.sem.at[6, 0], self.sem.at[7, 0], at.flip()).start()

    def finish(self):
        await_bytes(self.done.at[0], self.sem.at[6, 0])
        await_bytes(self.done.at[0], self.sem.at[7, 0])


def mlp_kernel(sizes, *refs):
    at = Place(sizes)
    R, F, S, G = at.R, at.F, at.S, at.G
    mod, bias_one, bias_two = refs[:3]
    given = refs[3:12]
    block_out, o_resid, o_heads, o_w_one, o_two_sum, o_two_part, o_out_g = refs[12:19]
    refs = refs[:11] + refs[12:]
    grad_b_one, grad_b_two, grad_b_out, mod_sums = refs[18:22]
    act_all, pre_wide, pre_all, grad_branch, wide, two_g, two_got, two_sem = refs[22:30]
    branch_refs, mix_refs = refs[30:34], refs[34:38]
    two_inn, two_far, part_sem, load_sem, save_sem = refs[38:43]
    held = refs[43:52]
    w_one, mix_all, w_two, grad_all, latents, branch_one, cotangent, w_out, merged = held
    grad_resid, grad_heads, grad_w_one, two_sum, two_part, out_g = refs[52:58]
    loads = Moves(load_sem, *zip(given, held))
    loads.start()
    saves = Moves(
        save_sem,
        (grad_w_one, o_w_one),
        (grad_resid, o_resid),
        (grad_heads, o_heads),
        (out_g, o_out_g),
        (two_sum, o_two_sum),
        (two_part, o_two_part),
    )
    _, L, D = mix_all.shape
    C = D // S
    hidden = w_one.shape[1]
    tokens = S * L
    greet(S, lambda i: {"seq": at.ss(i)})
    greet(2, lambda i: at.flip())
    greet(F, lambda i: {"fsdp": at.zs(i)})
    greet_wait(S + F - 1)
    gate_one = mod[2:3, :]
    scale = mod[4:5, :]
    gate_two = mod[5:6, :]
    branch_sum = SeqSum(at, *branch_refs)
    mix_sum = SeqSum(at, *mix_refs)
    branch_src = branch_refs[0]
    mix_src = mix_refs[0]
    two = RowScatter(at, two_g, two_got, two_sum, two_sem)
    part_two = RowOwner(at, lambda z: two_g.at[z, pl.ds(0, 2)], two_inn, two_far, part_sem)
    step = min(256, L)

    def ahead(order):
        index = lax.rem(order + 2, S)
        t = at.peer(arrival(index))

        def part(i):
            rows = pl.ds(pl.multiple_of(i * step, step), step)
            pre = mm(mix_all[t, rows, :], w_one[...]) + bias_one[...]
            pre_wide[t, rows, :] = pre
            inner = gelu_coef * (pre + 0.044715 * pre * pre * pre)
            act = (0.5 * pre * (1.0 + jnp.tanh(inner))).astype(BF)
            act_all[t, rows, :] = act
            branch_src[t, rows, :] = mm(act, w_two[...]).astype(BF)

        each(0, L // step, part)
        branch_sum.send(index)

    loads.wait(0, 1, 2)
    each(0, S, ahead)
    loads.wait(3)
    column = 384 if hidden % 384 == 0 else hidden
    for i in range(hidden // column):
        cols = slice(i * column, (i + 1) * column)
        wide[cols, :] = mm_tn(
            act_all[:, :, cols].reshape(tokens, column), grad_all[...].reshape(tokens, D)
        )
    part_rows = two_g.shape[2]
    for f in range(F):
        for quarter in range(4):
            first = (4 * f + quarter) * part_rows
            two_g[f, quarter] = wide[first : first + part_rows, :].astype(BF)
    part_two.start()
    two.start()

    def behind(order):
        index = lax.rem(order + 2, S)
        t = at.peer(arrival(index))

        def part(i):
            rows = pl.ds(pl.multiple_of(i * step, step), step)
            pre = pre_wide[t, rows, :]
            square = pre * pre
            tanh_val = jnp.tanh(gelu_coef * (pre + 0.044715 * square * pre))
            slope = 0.5 * (1.0 + tanh_val) + 0.5 * pre * (
                1.0 - tanh_val * tanh_val
            ) * gelu_coef * (1.0 + 3.0 * 0.044715 * square)
            grad_pre = (mm_nt(grad_all[t, rows, :], w_two[...]) * slope).astype(BF)
            pre_all[t, rows, :] = grad_pre
            mix_src[t, rows, :] = mm_nt(grad_pre, w_one[...]).astype(BF)

        each(0, L // step, part)
        mix_sum.send(index)

        @pl.when(order == S - 1)
        def _():
            part_two.relay()

    each(0, S, behind)
    for i in range(hidden // column):
        cols = slice(i * column, (i + 1) * column)
        grads = pre_all[:, :, cols].reshape(tokens, column)
        grad_w_one[:, cols] = mm_tn(mix_all[...].reshape(tokens, D), grads).astype(BF)
        grad_b_one[:, cols] = jnp.sum(grads.astype(F32), axis=0, keepdims=True)
    grad_b_two[...] = jnp.sum(grad_all[at.s].astype(F32), axis=0, keepdims=True)
    saves.start(0)
    loads.wait(4, 5, 6, 7, 8)

    mix_sum.wait()
    step_back = min(32, L)
    mod_sums[...] = jnp.zeros_like(mod_sums)
    grad_b_out[...] = jnp.zeros_like(grad_b_out)

    def back(i):
        rows = pl.ds(pl.multiple_of(i * step_back, step_back), step_back)
        grad_mixed = mix_sum.total(rows)
        branch = branch_one[rows, :]
        residual = latents[rows, :].astype(F32) + gate_one * branch
        normed, inv_std = norm_stats(residual)
        grad_out = cotangent[rows, :].astype(F32)
        grad = grad_out + norm_back(grad_mixed * (1.0 + scale), normed, inv_std)
        grad_resid[rows, :] = grad
        low = (gate_one * grad).astype(BF)
        grad_branch[rows, :] = low
        mod_sums[2:3, :] += jnp.sum(grad * branch, axis=0, keepdims=True)
        mod_sums[3:4, :] += jnp.sum(grad_mixed, axis=0, keepdims=True)
        mod_sums[4:5, :] += jnp.sum(grad_mixed * normed, axis=0, keepdims=True)
        grad_b_out[...] += jnp.sum(low.astype(F32), axis=0, keepdims=True)

    each(0, L // step_back, back)
    grad_merged = mm_nt(grad_branch[...], w_out[...]).astype(BF)
    for t in range(S):
        grad_heads[t] = grad_merged[:, t * C : (t + 1) * C]
    saves.start(1, 2)
    for i in range(D // 384):
        cols = slice(i * 384, (i + 1) * 384)
        wide[:D, cols] = mm_tn(merged[...], grad_branch[:, cols])
    rows_own = out_g.shape[2]
    for f in range(F):
        for t in range(S):
            first = (f * S + t) * rows_own
            out_g[t, f] = wide[first : first + rows_own, :].astype(BF)
    saves.start(3)

    branch_sum.wait()

    def finish(i):
        rows = pl.ds(pl.multiple_of(i * step_back, step_back), step_back)
        branch_two = branch_sum.total(rows) + bias_two[...]
        residual = latents[rows, :].astype(F32) + gate_one * branch_one[rows, :]
        block_out[rows, :] = (residual + gate_two * branch_two).astype(BF)
        grad_out = cotangent[rows, :].astype(F32)
        mod_sums[5:6, :] += jnp.sum(grad_out * branch_two, axis=0, keepdims=True)

    each(0, L // step_back, finish)
    two.reduce()
    saves.start(4)
    two_part[...] = part_two.total()
    saves.start(5)
    saves.wait()


def mlp(sizes, *args):
    R, F, S = sizes
    G = F * S
    D, hidden = args[3].shape
    L = args[7].shape[0]
    C = D // S
    quarter = hidden // F // 4
    shape = jax.ShapeDtypeStruct
    kept = (
        ((L, D), F32),
        ((S, L, C), BF),
        ((D, hidden), BF),
        ((F, quarter, D), BF),
        ((2, quarter, D), BF),
        ((S, F, D // G, D), BF),
    )
    return pl.pallas_call(
        lambda *refs: mlp_kernel(sizes, *refs),
        name="mlp",
        out_shape=(shape((L, D), BF),)
        + tuple(shape(*item) for item in kept)
        + (
            shape((1, hidden), F32),
            shape((1, D), F32),
            shape((1, D), F32),
            shape((6, D), F32),
        ),
        in_specs=[VM] * 3 + [HB] * 9,
        out_specs=(VM,) + (HB,) * 6 + (VM,) * 4,
        scratch_shapes=[
            pltpu.VMEM((S, L, hidden), BF),
            pltpu.VMEM((S, L, hidden), F32),
            pltpu.VMEM((S, L, hidden), BF),
            pltpu.VMEM((L, D), BF),
            pltpu.VMEM((max(hidden, D), D), F32),
            pltpu.VMEM((F, 4, quarter, D), BF),
            pltpu.VMEM((F, quarter, D), BF),
            DMA((2, F)),
        ]
        + SeqSum.scratch(S, L, D)
        + SeqSum.scratch(S, L, D)
        + RowOwner.scratch(F, (2, quarter, D))
        + [DMA((9,)), DMA((6,))]
        + [pltpu.VMEM(x.shape, x.dtype) for x in args[3:]]
        + [pltpu.VMEM(*item) for item in kept],
        compiler_params=params(3, 60),
    )(*args)


class ColumnScatter:
    def __init__(self, at, src, got, stage, inn, far, along_sem, summed, done, sem):
        self.at, self.src, self.got, self.stage = at, src, got, stage
        self.summed, self.done, self.sem = summed, done, sem
        self.along = RowOwner(at, lambda z: stage.at[z], inn, far, along_sem)

    @staticmethod
    def scratch(sizes, rows, cols):
        R, F, S = sizes
        shape = (S // 2, rows, cols)
        return (
            [pltpu.VMEM((F,) + shape, BF), pltpu.VMEM((F,) + shape, BF)]
            + RowOwner.scratch(F, shape)
            + [pltpu.VMEM(shape, BF), DMA((5, F))]
        )

    def start(self):
        at = self.at

        def far(i):
            z_to = at.zs(i)

            def one(k):
                slot = z_to * at.S + 2 * k + at.y
                local(self.src.at[slot], self.stage.at[z_to, k], self.sem.at[2, i]).start()
                remote(
                    self.src.at[z_to * at.S + 2 * k + 1 - at.y],
                    self.got.at[z_to, k],
                    self.sem.at[0, i],
                    self.sem.at[1, i],
                    at.flip(),
                ).start()

            each(0, at.S // 2, one)

        each(0, at.F, far)

    def scatter(self):
        at = self.at

        def step(i):
            z_to = at.zs(i)
            await_bytes(self.got.at[0], self.sem.at[1, i])
            await_bytes(self.got.at[0], self.sem.at[2, i])

            def one(k):
                total = self.stage[z_to, k].astype(F32) + self.got[z_to, k].astype(F32)
                self.stage[z_to, k] = total.astype(BF)

            each(0, at.S // 2, one)

        each(0, at.F, step)
        self.along.start()

    def relay(self):
        self.along.relay()

    def near(self):
        at = self.at
        self.summed[...] = self.along.total()

        def one(k):
            s_to = 2 * k + at.y

            @pl.when(s_to == at.s)
            def _():
                self.done[at.s] = self.summed[k]

            @pl.when(s_to != at.s)
            def _():
                remote(
                    self.summed.at[k],
                    self.done.at[at.s],
                    self.sem.at[3, 0],
                    self.sem.at[3, 1],
                    {"seq": s_to},
                ).start()

        each(0, at.S // 2, one)

    def total(self):
        at = self.at

        @pl.when(at.mine)
        def _():
            await_bytes(self.done.at[pl.ds(0, at.S - 1)], self.sem.at[3, 1])
            remote(
                self.done, self.done, self.sem.at[4, 0], self.sem.at[4, 1], at.flip()
            ).start()

    def finish(self):
        at = self.at
        each(0, at.F, lambda i: await_bytes(self.got.at[0], self.sem.at[0, i]))

        @pl.when(at.mine)
        def _():
            if at.S > 2:
                await_bytes(self.done.at[pl.ds(0, at.S // 2 - 1)], self.sem.at[3, 0])
            await_bytes(self.done, self.sem.at[4, 0])

        @pl.when(jnp.logical_not(at.mine))
        def _():
            await_bytes(self.summed, self.sem.at[3, 0])
            await_bytes(self.done, self.sem.at[4, 1])


class Tail:
    def __init__(self, at, mod_all, sums, first_in, mod_src, small_src, small_in, cond_src, cond_in, pieces, sem):
        self.at, self.sums, self.first_in = at, sums, first_in
        self.mod_src, self.mod_all = mod_src, mod_all
        self.small_src, self.small_in = small_src, small_in
        self.cond_src, self.cond_in, self.pieces, self.sem = cond_src, cond_in, pieces, sem

    @staticmethod
    def scratch(sizes, D, hidden, rows):
        R, F, S = sizes
        G = F * S
        C = D // S
        pack = 2 * D // G + 2 * rows + hidden // F
        wide = max(D, hidden, 3 * C)
        return [
            pltpu.VMEM((10, wide), F32),
            pltpu.VMEM((S, 10, wide), F32),
            pltpu.VMEM((6, D), BF),
            pltpu.VMEM((F, 1, pack), F32),
            pltpu.VMEM((R * F, 1, pack), F32),
            pltpu.VMEM((R * F, 1, rows), F32),
            pltpu.VMEM((G, 1, rows), F32),
            pltpu.VMEM((G, 1, pack), F32),
            DMA((8, max(S, 2 * F, G))),
        ]

    def first_copy(self, j):
        at = self.at
        return remote(
            self.sums, self.first_in.at[at.s], self.sem.at[0, j], self.sem.at[1, j], {"seq": at.ss(j)}
        )

    def start(self, mod_sums, b_one, b_two, b_out, b_qkv):
        sums = self.sums
        D = mod_sums.shape[1]
        hidden = b_one.shape[1]
        sums[...] = jnp.zeros_like(sums)
        sums[0:6, 0:D] = mod_sums[...]
        sums[6:7, 0:hidden] = b_one[...]
        sums[7:8, 0:D] = b_two[...]
        sums[8:9, 0:D] = b_out[...]
        sums[9:10, 0 : b_qkv.shape[1]] = b_qkv[...]
        each(1, self.at.S, lambda j: self.first_copy(j).start())
        self.first_in[self.at.s] = sums[...]

    def wide_copies(self, i):
        at = self.at
        slot = at.y * at.F + at.z
        device = {"rep": lax.rem(at.y + i // at.F, 2), "fsdp": at.zs(i)}
        return (
            remote(self.mod_src, self.mod_all.at[slot], self.sem.at[2, i], self.sem.at[3, i], device),
            remote(
                self.small_src.at[at.zs(i)],
                self.small_in.at[slot],
                self.sem.at[4, i],
                self.sem.at[5, i],
                device,
            ),
        )

    def middle(self, D, hidden, rows):
        at = self.at
        F, S, G = at.F, at.S, at.G
        C = D // S
        qv = 2 * D // G
        each(1, S, lambda j: self.first_copy(j).wait())
        total = self.first_in[0]
        for t in range(1, S):
            total = total + self.first_in[t]
        self.mod_src[...] = total[0:6, 0:D].astype(BF)
        for g in range(G):
            g_half = g % (G // 2)
            t = g_half // (F // 2)
            col = (g_half % (F // 2)) * qv + (2 * C if g >= G // 2 else 0)
            self.pieces[g, :, 0:qv] = self.first_in[t, 9:10, col : col + qv]
            self.pieces[g, :, qv : qv + rows] = total[8:9, g * rows : (g + 1) * rows]
            self.pieces[g, :, qv + rows : qv + 2 * rows] = total[7:8, g * rows : (g + 1) * rows]
        block = hidden // F
        for f in range(F):
            self.small_src[f, :, 0 : qv + 2 * rows] = self.pieces[f * S + at.s][:, 0 : qv + 2 * rows]
            self.small_src[f, :, qv + 2 * rows :] = self.sums[6:7, f * block : (f + 1) * block]

        def send(i):
            first, second = self.wide_copies(i)
            first.start()
            second.start()

        each(1, 2 * F, send)
        slot = at.y * F + at.z
        self.mod_all[slot] = self.mod_src[...]
        self.small_in[slot] = self.small_src[at.z]

    def cond_copy(self, i):
        at = self.at
        to = lax.rem(at.me + i, at.G)
        return remote(
            self.cond_src.at[at.y * at.F + to // at.S],
            self.cond_in.at[at.me],
            self.sem.at[6, i],
            self.sem.at[7, i],
            {"fsdp": to // at.S, "seq": lax.rem(to, at.S)},
        )

    def owners(self, w_ada, small_out):
        at = self.at
        F, G = at.F, at.G
        D = self.mod_src.shape[1]

        def arrive(i):
            first, second = self.wide_copies(i)
            first.wait()
            second.wait()

        each(1, 2 * F, arrive)
        cond = None
        for v in range(6):
            rows = self.mod_all[:, v, :]
            part = mm_nt(rows, w_ada[:, v * D : (v + 1) * D])
            cond = part if cond is None else cond + part
        for i in range(2 * F):
            self.cond_src[i] = cond[i : i + 1, :]
        each(1, G, lambda i: self.cond_copy(i).start())
        self.cond_in[at.me] = self.cond_src[at.y * F + at.z]
        total = self.small_in[0]
        for i in range(1, 2 * F):
            total = total + self.small_in[i]
        small_out[...] = total

    def finish(self, cond, grad_cond):
        at = self.at
        rows = self.cond_in.shape[2]
        each(1, at.G, lambda i: self.cond_copy(i).wait())
        for g in range(at.G):
            cols = slice(g * rows, (g + 1) * rows)
            value = cond[:, cols].astype(F32)
            gate = jax.nn.sigmoid(value)
            grad_cond[:, cols] = self.cond_in[g] * gate * (1.0 + value * (1.0 - gate))


def backward_kernel(sizes, *refs):
    at = Place(sizes)
    R, F, S, G = at.R, at.F, at.S, at.G
    grad_heads, heads, two_g, two_part, out_g, w_qkv, mixed_all, latents, grad_resid, w_ada = refs[-10:]
    log_sums, mod, sums_in, b_one, b_two, b_out, cond, one_g = refs[:8]
    given = refs[8:18]
    refs = refs[:7] + refs[8:]
    o_latents, o_qkv, o_one, o_two, o_part, o_out, o_mod, o_small, o_cond = refs[17:26]
    refs = refs[:16] + refs[17:]
    grad_in, key_flip, key_grad, val_grad, grad_proj, qkv_wide, qkv_g, mod_sums, b_qkv, in_sem = refs[25:35]
    rest = list(refs[35:])
    mix_sum = SeqSum(at, *rest[0:4])
    mix_src = rest[0]
    qkv = ColumnScatter(at, qkv_g, *rest[4:10], o_qkv, rest[10])
    one = ColumnScatter(at, one_g, *rest[11:17], o_one, rest[17])
    two = RowOwner(at, lambda z: two_g.at[z], rest[18], rest[19], rest[20])
    out = FullScatter(at, out_g, *rest[21:25], o_out, rest[25])
    tail = Tail(at, o_mod, *rest[26:35])
    load_sem, swap_sem, save_sem, grad_latents = rest[35:39]
    held = rest[39:49]
    two_swap = Swap(at, o_two, swap_sem.at[0])
    part_swap = Swap(at, o_part, swap_sem.at[1])
    saves = Moves(save_sem, (grad_latents, o_latents))
    loads = Moves(load_sem, *zip(given, held))
    loads.start()
    _, L, C = grad_heads.shape
    rows_own, D = o_out.shape[1:]
    hidden = one_g.shape[2]
    local_heads = H // S
    size = D // H
    greet(G, lambda i: {"fsdp": lax.rem(at.me + i, G) // S, "seq": lax.rem(at.me + i, S)})
    greet(2 * F, lambda i: {"rep": lax.rem(at.y + i // F, 2), "fsdp": at.zs(i)})
    loads.wait(0, 2, 3, 4)
    o_part[at.y] = two_part[...]
    greet_wait(G - 1 + 2 * F - 1)

    def in_copy(j):
        return remote(
            grad_heads.at[at.peer(j)],
            grad_in.at[at.s],
            in_sem.at[0, j],
            in_sem.at[1, j],
            {"seq": at.peer(j)},
        )

    each(1, S, lambda j: in_copy(j).start())
    one.start()
    two.start()
    out.start()
    grad_in[at.s] = grad_heads[at.s]
    key_grad[...] = jnp.zeros_like(key_grad)
    val_grad[...] = jnp.zeros_like(val_grad)
    loads.wait(1)
    for h in range(local_heads):
        key_flip[h] = heads[local_heads + h].T
    factor = size ** (-0.5) * log2e
    score_scale = size ** (-0.5)
    pad = jnp.zeros((L, LANES - size), BF)

    def block(j):
        t = at.peer(j)

        @pl.when(j > 0)
        def _():
            in_copy(j).wait()

        rows = pl.ds(pl.multiple_of(t * L, L), L)
        for h in range(local_heads):
            query = heads[h, rows, :]
            grad = jnp.concatenate([grad_in[t, :, h * size : (h + 1) * size], pad], axis=1)
            scores = mm_nt(heads[local_heads + h], query) * factor
            probs = jnp.exp2(scores - log_sums[h, t])
            grad_probs = mm_nt(heads[2 * local_heads + h], grad)
            inner = jnp.sum(probs * grad_probs, axis=0, keepdims=True)
            grad_scores = (probs * (grad_probs - inner)).astype(BF)
            query_grad = mm(key_flip[h], grad_scores) * score_scale
            grad_proj[t, :, h * size : (h + 1) * size] = query_grad.T[:, :size].astype(BF)
            key_grad[h] += mm(grad_scores, query)
            val_grad[h] += mm(probs.astype(BF), grad)

    block(0)
    out.cross()
    each(1, S, block)
    two.relay()
    for h in range(local_heads):
        low = (key_grad[h] * score_scale)[:, :size].astype(BF)
        grad_proj[:, :, C + h * size : C + (h + 1) * size] = low.reshape(S, L, size)
        low = val_grad[h][:, :size].astype(BF)
        grad_proj[:, :, 2 * C + h * size : 2 * C + (h + 1) * size] = low.reshape(S, L, size)

    loads.wait(5, 6)

    def spread(index):
        t = at.peer(arrival(index))
        mix_src[t] = mm_nt(grad_proj[t], w_qkv[...]).astype(BF)
        mix_sum.send(index)

    grads = grad_proj[...].reshape(S * L, 3 * C)
    qkv_wide[...] = mm_tn(mixed_all[...].reshape(S * L, D), grads)
    for g in range(G):
        qkv_g[g] = qkv_wide[g * rows_own : (g + 1) * rows_own, :].astype(BF)
    qkv.start()
    out.scatter()
    each(0, S, lambda index: spread(lax.rem(index + 2, S)))
    one.scatter()
    b_qkv[...] = jnp.sum(grads.astype(F32), axis=0, keepdims=True)
    mix_sum.wait()
    loads.wait(7, 8, 9)
    step = min(32, L)
    mod_sums[...] = sums_in[...]
    scale = mod[1:2, :]

    def back(i):
        rows = pl.ds(pl.multiple_of(i * step, step), step)
        grad_mixed = mix_sum.total(rows)
        normed, inv_std = norm_stats(latents[rows, :].astype(F32))
        grad_latents[rows, :] = grad_resid[rows, :] + norm_back(
            grad_mixed * (1.0 + scale), normed, inv_std
        )
        mod_sums[0:1, :] += jnp.sum(grad_mixed, axis=0, keepdims=True)
        mod_sums[1:2, :] += jnp.sum(grad_mixed * normed, axis=0, keepdims=True)

    each(0, L // step, back)
    saves.start()
    tail.start(mod_sums, b_one, b_two, b_out, b_qkv)
    one.relay()
    tail.middle(D, hidden, rows_own)
    qkv.scatter()
    o_two[at.y] = two.total()
    two_swap.start()
    part_swap.start()
    out.total()
    one.near()
    qkv.relay()
    tail.owners(w_ada, o_small)
    one.total()
    qkv.near()
    tail.finish(cond, o_cond)
    qkv.total()
    out.finish()
    two_swap.finish()
    part_swap.finish()
    one.finish()
    qkv.finish()
    saves.wait()


def backward(sizes, *args):
    R, F, S = sizes
    G = F * S
    one_g, grad_heads, two_g = args[7], args[8], args[10]
    two_part, latents, w_ada = args[11], args[15], args[17]
    _, L, C = grad_heads.shape
    D = latents.shape[1]
    T = S * L
    local_heads = H // S
    rows = w_ada.shape[0]
    hidden = one_g.shape[2]
    pack = 2 * D // G + 2 * rows + hidden // F
    shape = jax.ShapeDtypeStruct
    return pl.pallas_call(
        lambda *refs: backward_kernel(sizes, *refs),
        name="backward",
        out_shape=(
            shape((L, D), F32),
            shape((S, rows, 3 * C), BF),
            shape((S, rows, hidden), BF),
            shape((2,) + two_g.shape[1:], BF),
            shape((2,) + two_part.shape, BF),
            shape((2, rows, D), BF),
            shape((R * F, 6, D), BF),
            shape((1, pack), F32),
            shape((1, D), F32),
        ),
        in_specs=[VM] * 7 + [HB] * 11,
        out_specs=(HB,) + (VM,) * 8,
        scratch_shapes=[
            pltpu.VMEM((S, L, C), BF),
            pltpu.VMEM((local_heads, LANES, T), BF),
            pltpu.VMEM((local_heads, T, LANES), F32),
            pltpu.VMEM((local_heads, T, LANES), F32),
            pltpu.VMEM((S, L, 3 * C), BF),
            pltpu.VMEM((D, 3 * C), F32),
            pltpu.VMEM((G, rows, 3 * C), BF),
            pltpu.VMEM((6, D), F32),
            pltpu.VMEM((1, 3 * C), F32),
            DMA((2, S)),
        ]
        + SeqSum.scratch(S, L, D)
        + ColumnScatter.scratch(sizes, rows, 3 * C)
        + ColumnScatter.scratch(sizes, rows, hidden)
        + RowOwner.scratch(F, two_g.shape[1:])
        + FullScatter.scratch(sizes, rows, D)
        + Tail.scratch(sizes, D, hidden, rows)
        + [DMA((10,)), DMA((2, 2)), DMA((1,)), pltpu.VMEM((L, D), F32)]
        + [pltpu.VMEM(x.shape, x.dtype) for x in args[8:]],
        compiler_params=params(4, 60),
    )(*args)


def assemble_kernel(sizes, *refs):
    R, F, S = sizes
    G = F * S
    n = 11
    given, results = refs[:n], refs[n : n + 13]
    qkv, one, two, part, out, mod_all, silu_all, small = refs[n + 13 : n + 21]
    o_qkv, o_one, o_two, o_out, o_ada, b_ada, b_qv, b_out, b_one, b_two = refs[n + 21 : n + 31]
    flat, pieces, load_sem, save_sem, *passing = refs[n + 31 :]
    held = (qkv, one, two, part, out, mod_all, silu_all, small, *passing)
    loads = Moves(load_sem, *zip(given, held))
    loads.start()
    passed = tuple(zip(passing, results[:3]))
    made = (o_ada, b_ada, o_qkv, b_qv, o_out, b_out, o_one, b_one, o_two, b_two)
    saves = Moves(save_sem, *passed, *zip(made, results[3:]))
    rows, D = o_out.shape
    C = D // S
    hidden = one.shape[2]
    block = hidden // F
    loads.wait(5, 6)
    silu = silu_all[:, 0, :].astype(BF)
    width = b_ada.shape[1]
    for v in range(6):
        grads = mod_all[:, v, :]
        o_ada[:, v * D : (v + 1) * D] = mm_tn(silu, grads)
        flat[:, v * D : (v + 1) * D] = jnp.sum(grads.astype(F32), axis=0, keepdims=True)
    saves.start(3)
    for g in range(G):
        pieces[g] = flat[:, g * width : (g + 1) * width]
    b_ada[...] = pieces[lax.axis_index("fsdp") * S + lax.axis_index("seq")]
    loads.wait(7)
    first = b_qv.shape[1]
    b_qv[...] = small[:, :first]
    b_out[...] = small[:, first : first + rows]
    b_two[...] = small[:, first + rows : first + 2 * rows]
    b_one[...] = small[:, first + 2 * rows :]
    saves.start(4, 6, 8, 10, 12)
    loads.wait(1)
    for t in range(S):
        for f in range(F):
            col = (f * S + t) * block
            o_one[:, col : col + block] = one[t, :, f * block : (f + 1) * block].astype(F32)
    saves.start(9)
    loads.wait(2, 3)
    o_two[0:2] = part[0].astype(F32) + part[1].astype(F32)
    o_two[2:4] = two[...].astype(F32)
    saves.start(11)
    loads.wait(0)
    for t in range(S):
        for j in range(3):
            o_qkv[:, j * D + t * C : j * D + (t + 1) * C] = qkv[t, :, j * C : (j + 1) * C].astype(F32)
    saves.start(5)
    loads.wait(4, 8, 9, 10)
    saves.start(0, 1, 2)
    o_out[...] = out[0].astype(F32) + out[1].astype(F32)
    saves.start(7)
    saves.wait()


def assemble(sizes, qkv, one, two, part, out, mod_all, silu_all, small, *passed):
    R, F, S = sizes
    G = F * S
    rows, D = out.shape[1:]
    hidden = one.shape[2]
    made = (
        ((rows, 6 * D), F32),
        ((1, 6 * D // G), F32),
        ((rows, 3 * D), F32),
        ((1, 2 * D // G), F32),
        ((rows, D), F32),
        ((1, rows), F32),
        ((rows, hidden * S), F32),
        ((1, hidden // F), F32),
        ((4,) + two.shape[1:], F32),
        ((1, rows), F32),
    )
    given = (qkv, one, two, part, out, mod_all, silu_all, small)
    scratch = [pltpu.VMEM(x.shape, x.dtype) for x in given]
    order = (2, 6, 8, 4, 0, 1, 3, 5, 7, 9)
    return pl.pallas_call(
        lambda *refs: assemble_kernel(sizes, *refs),
        name="assemble",
        out_shape=tuple(jax.ShapeDtypeStruct(x.shape, x.dtype) for x in passed)
        + tuple(jax.ShapeDtypeStruct(*item) for item in made),
        in_specs=[HB] * 11,
        out_specs=(HB,) * 13,
        scratch_shapes=scratch
        + [pltpu.VMEM(*made[i]) for i in order]
        + [
            pltpu.VMEM((1, 6 * D), F32),
            pltpu.VMEM((G, 1, 6 * D // G), F32),
            DMA((11,)),
            DMA((13,)),
        ]
        + [pltpu.VMEM(x.shape, x.dtype) for x in passed],
        compiler_params=pltpu.CompilerParams(vmem_limit_bytes=60 * 1024 * 1024),
    )(*given, *passed)


def on_device(
    latents, cond, w_ada, b_ada, w_qkv, b_qv, w_out, b_out, w_one, b_one, w_two, b_two, cotangent
):
    sizes = R, F, S = tuple(lax.axis_size(name) for name in ("rep", "fsdp", "seq"))
    G = F * S
    _, L, D = latents.shape
    hidden = w_one.shape[1] // S
    rows = w_ada.shape[0]
    tokens = latents[0]
    two_rows = w_two.shape[0]
    (
        mixed_all,
        heads,
        merged,
        branch_one,
        mix_all,
        grad_all,
        full_qkv,
        full_out,
        log_sums,
        mod,
        silu_all,
        bias_one,
        bias_two,
        g_one,
        g_two,
    ) = forward(
        sizes,
        cond,
        jnp.concatenate([b.astype(F32) for b in (b_ada, b_qv, b_out, b_two, b_one)])[None],
        tokens,
        cotangent[0],
        w_ada,
        w_qkv,
        w_one,
        w_two.reshape(2, two_rows // 2, D),
        w_out,
    )
    full_one = g_one.reshape(D, hidden)
    full_two = g_two.reshape(hidden, D)
    (
        block_out,
        grad_resid,
        grad_heads,
        one_g,
        two_g,
        two_part,
        out_g,
        grad_b_one,
        grad_b_two,
        grad_b_out,
        mod_sums,
    ) = mlp(
        sizes,
        mod,
        bias_one,
        bias_two,
        full_one,
        mix_all,
        full_two,
        grad_all,
        tokens,
        branch_one,
        cotangent[0],
        full_out,
        merged,
    )
    grad_latents, qkv_sum, one_sum, two_sum, part_sum, out_sum, mod_all, o_small, o_cond = backward(
        sizes,
        log_sums,
        mod,
        mod_sums,
        grad_b_one,
        grad_b_two,
        grad_b_out,
        cond,
        one_g.reshape(G, rows, hidden),
        grad_heads,
        heads,
        two_g,
        two_part,
        out_g,
        full_qkv,
        mixed_all,
        tokens,
        grad_resid,
        w_ada,
    )
    outs = assemble(
        sizes,
        qkv_sum,
        one_sum,
        two_sum,
        part_sum,
        out_sum,
        mod_all,
        silu_all,
        o_small,
        block_out,
        grad_latents,
        o_cond,
    )
    shapes = (latents.shape, latents.shape, cond.shape, w_ada.shape, b_ada.shape, w_qkv.shape, b_qv.shape)
    shapes += (w_out.shape, b_out.shape, w_one.shape, b_one.shape, w_two.shape, b_two.shape)
    return tuple(out.reshape(want) for out, want in zip(outs, shapes))


def solution(mesh):
    owned = P(("fsdp", "seq"), None)
    owned_bias = P(("fsdp", "seq"))
    token_spec = P(("rep", "fsdp"), "seq", None)
    cond_spec = P(("rep", "fsdp"), None)
    weights = (owned, owned_bias) * 5
    in_specs = (token_spec, cond_spec) + weights + (token_spec,)
    out_specs = (token_spec, token_spec, cond_spec) + weights
    return jax.shard_map(
        on_device, mesh=mesh, in_specs=in_specs, out_specs=out_specs, check_vma=False
    )
```

```python
import math

import jax
import jax.numpy as jnp
from jax import lax
from jax.experimental import pallas as pl
from jax.experimental.pallas import tpu as pltpu
from jax.sharding import PartitionSpec as P

H = 16
epsilon = 1e-06
gelu_coef = math.sqrt(2.0 / math.pi)
log2e = math.log2(math.e)
BF = jnp.bfloat16
F32 = jnp.float32
LANES = 128
VM = pl.BlockSpec(memory_space=pltpu.VMEM)
HB = pl.BlockSpec(memory_space=pl.ANY)
DMA = pltpu.SemaphoreType.DMA


def params(ident, mib):
    return pltpu.CompilerParams(
        collective_id=ident, has_side_effects=True, vmem_limit_bytes=mib * 1024 * 1024
    )


def remote(src, dst, send, recv, device):
    return pltpu.make_async_remote_copy(
        src_ref=src,
        dst_ref=dst,
        send_sem=send,
        recv_sem=recv,
        device_id=device,
        device_id_type=pl.DeviceIdType.MESH,
    )


def local(src, dst, sem):
    return pltpu.make_async_copy(src, dst, sem)


def await_bytes(like, sem):
    pltpu.make_async_copy(like, like, sem).wait()


class Moves:
    def __init__(self, sem, *pairs):
        self.copies = [local(pair[0], pair[1], sem.at[i]) for i, pair in enumerate(pairs)]

    def start(self, *which):
        for i in which or range(len(self.copies)):
            self.copies[i].start()

    def wait(self, *which):
        for i in which or range(len(self.copies)):
            self.copies[i].wait()


def each(start, stop, body):
    def step(index, carry):
        body(index)
        return carry

    lax.fori_loop(start, stop, step, 0)


def greet(count, device_of):
    gate = pltpu.get_barrier_semaphore()
    each(
        1,
        count,
        lambda i: pl.semaphore_signal(
            gate, 1, device_id=device_of(i), device_id_type=pl.DeviceIdType.MESH
        ),
    )
    return count - 1


def greet_wait(count):
    pl.semaphore_wait(pltpu.get_barrier_semaphore(), count)


def norm_stats(values):
    center = values - jnp.mean(values, axis=-1, keepdims=True)
    inv_std = lax.rsqrt(jnp.mean(center * center, axis=-1, keepdims=True) + epsilon)
    return (center * inv_std, inv_std)


def norm_back(grad, normed, inv_std):
    return inv_std * (
        grad
        - jnp.mean(grad, axis=-1, keepdims=True)
        - normed * jnp.mean(grad * normed, axis=-1, keepdims=True)
    )


def mm(left, right):
    return jnp.dot(left, right, preferred_element_type=F32)


def mm_nt(left, right):
    return lax.dot_general(left, right, (((1,), (1,)), ((), ())), preferred_element_type=F32)


def mm_tn(left, right):
    return lax.dot_general(left, right, (((0,), (0,)), ((), ())), preferred_element_type=F32)


class Place:
    def __init__(self, sizes):
        self.R, self.F, self.S = sizes
        self.G = self.F * self.S
        self.y = lax.axis_index("rep")
        self.z = lax.axis_index("fsdp")
        self.s = lax.axis_index("seq")
        self.me = self.z * self.S + self.s
        self.mine = lax.rem(self.s, 2) == self.y
        self.steps = (2, 1, 3) if self.F == 4 else tuple(range(1, self.F))

    def zs(self, i):
        return lax.rem(self.z + i, self.F)

    def zs_back(self, i):
        return lax.rem(self.z - i + self.F, self.F)

    def ss(self, i):
        return lax.rem(self.s + i, self.S)

    def ss_back(self, i):
        return lax.rem(self.s - i + self.S, self.S)

    def flip(self):
        return {"rep": 1 - self.y}

    def peer(self, j):
        return lax.bitwise_xor(self.s, j)


class SeqGather:
    def __init__(self, at, dst, sem):
        self.at, self.dst, self.sem = at, dst, sem

    @staticmethod
    def scratch(S):
        return DMA((4, S))

    def direct(self, j):
        at, block = self.at, self.dst.at[self.at.s]
        return remote(block, block, self.sem.at[0, j], self.sem.at[1, j], {"seq": at.peer(j)})

    def handed(self, j):
        at = self.at
        block = self.dst.at[at.peer(j)]
        return remote(block, block, self.sem.at[2, j], self.sem.at[3, j], {"seq": at.peer(1)})

    def start(self):
        for j in range(3, self.at.S, 2):
            self.direct(j).start()
        self.direct(1).start()

    def arrive(self, index):
        @pl.when(index == 1)
        def _():
            self.direct(1).wait()

        if self.at.S > 2:

            @pl.when((index >= 2) & (lax.rem(index, 2) == 0))
            def _():
                self.direct(index + 1).wait()
                self.handed(index + 1).start()

            @pl.when((index >= 2) & (lax.rem(index, 2) == 1))
            def _():
                self.handed(index).wait()


def arrival(index):
    return jnp.where(index < 2, index, lax.bitwise_xor(index, 1))


class SeqSum:
    def __init__(self, at, src, near, inn, sem):
        self.at, self.src, self.near, self.inn, self.sem = at, src, near, inn, sem

    @staticmethod
    def scratch(S, rows, cols):
        return [
            pltpu.VMEM((S, rows, cols), BF),
            pltpu.VMEM((S // 2, rows, cols), BF),
            pltpu.VMEM((S // 2, rows, cols), BF),
            DMA((4, S)),
        ]

    def sibling(self, j):
        at = self.at
        return remote(
            self.src.at[at.peer(j)],
            self.near.at[j // 2],
            self.sem.at[0, j],
            self.sem.at[1, j],
            {"seq": at.peer(1)},
        )

    def direct(self, j):
        at = self.at
        return remote(
            self.src.at[at.peer(j)],
            self.inn.at[j // 2],
            self.sem.at[2, j],
            self.sem.at[3, j],
            {"seq": at.peer(j)},
        )

    def send(self, index):
        @pl.when((index == 1) | ((index >= 2) & (lax.rem(index, 2) == 0)))
        def _():
            self.sibling(lax.bitwise_or(index, 1)).start()

        if self.at.S > 2:

            @pl.when((index >= 2) & (lax.rem(index, 2) == 1))
            def _():
                j = index - 1
                self.sibling(index).wait()
                t = self.at.peer(j)
                step = min(64, self.src.shape[1])

                def add(i):
                    rows = pl.ds(pl.multiple_of(i * step, step), step)
                    both = self.src[t, rows, :].astype(F32) + self.near[j // 2, rows, :].astype(F32)
                    self.src[t, rows, :] = both.astype(BF)

                each(0, self.src.shape[1] // step, add)
                self.direct(j).start()

    def wait(self):
        self.sibling(1).wait()
        for j in range(2, self.at.S, 2):
            self.direct(j).wait()

    def total(self, rows):
        value = self.src[self.at.s, rows, :].astype(F32) + self.near[0, rows, :].astype(F32)
        for k in range(1, self.at.S // 2):
            value = value + self.inn[k, rows, :].astype(F32)
        return value


class FarGather:
    relayed = True

    def __init__(self, at, dst, sem):
        self.at, self.dst, self.sem = at, dst, sem
        self.line = self.relayed and at.F == 4

    @staticmethod
    def scratch(F):
        return DMA((7, F))

    def send(self, z_from, z_to, kind):
        pieces = self.half(z_from)
        held = self.origin() if kind == 0 else pieces
        for source, piece in zip(held, pieces):
            remote(
                source, piece, self.sem.at[kind, z_to], self.sem.at[2, z_from], {"fsdp": z_to}
            ).start()

    def origin(self):
        return self.half(self.at.z)

    def await_half(self, row, z):
        await_bytes(self.like(), self.sem.at[row, z])

    def around(self, step, body):
        at = self.at

        @pl.when(at.z >= step)
        def _():
            body(at.z - step)

        @pl.when(at.z + step < at.F)
        def _():
            body(at.z + step)

    def direct(self, step, body):
        if self.line and step == 3:
            return
        self.around(step, body)

    def start_far(self):
        for step in self.at.steps:
            self.direct(step, lambda z_to: self.send(self.at.z, z_to, 0))

    def service(self, step):
        at = self.at

        def take(z_from):
            self.await_half(2, z_from)
            for piece in self.half(z_from):
                remote(
                    piece, piece, self.sem.at[3, z_from], self.sem.at[4, z_from], at.flip()
                ).start()

        self.around(step, take)
        if self.line and step == 2:

            @pl.when((at.z == 1) | (at.z == 2))
            def _():
                far = jnp.where(at.z == 1, 3, 0)
                end = 3 - far
                self.send(far, end, 1)

    def finish_far(self):
        at = self.at

        def swapped(z_from):
            self.await_half(3, z_from)
            self.await_half(4, z_from)

        for step in range(1, at.F):
            self.around(step, swapped)
            self.direct(step, lambda z_to: self.await_half(0, z_to))
        if self.line:

            @pl.when((at.z == 1) | (at.z == 2))
            def _():
                self.await_half(1, jnp.where(at.z == 1, 0, 3))


class ColumnGather(FarGather):
    def __init__(self, at, src, dst, sem):
        super().__init__(at, dst, sem)
        self.src = src

    def half(self, z):
        at = self.at
        return [self.dst.at[z * at.S + 2 * k + at.y] for k in range(at.S // 2)]

    def like(self):
        return self.dst.at[pl.ds(0, self.at.S // 2)]

    def start(self):
        at, src, dst, sem = self.at, self.src, self.dst, self.sem

        def near(j):
            t = at.ss(j)
            remote(src.at[t], dst.at[at.me], sem.at[5, 0], sem.at[6, 0], {"seq": t}).start()

        each(1, at.S, near)
        local(src.at[at.s], dst.at[at.me], sem.at[5, 1]).start()

    def near_done(self):
        at, dst, sem = self.at, self.dst, self.sem
        local(self.src.at[at.s], dst.at[at.me], sem.at[5, 1]).wait()
        near = dst.at[pl.ds(0, at.S - 1)]
        await_bytes(near, sem.at[5, 0])
        await_bytes(near, sem.at[6, 0])


class RowGather(FarGather):
    def __init__(self, at, src, dst, sem):
        super().__init__(at, dst, sem)
        self.src = src

    def half(self, z):
        return [self.dst.at[z, self.at.y]]

    def origin(self):
        return [self.src.at[self.at.y]]

    def like(self):
        return self.dst.at[0, 0]

    def start(self):
        at = self.at
        local(self.src, self.dst.at[at.z], self.sem.at[5, 0]).start()

    def near_done(self):
        at = self.at
        local(self.src, self.dst.at[at.z], self.sem.at[5, 0]).wait()


class OwnGather(FarGather):
    relayed = False

    def __init__(self, at, src, dst, sem):
        super().__init__(at, dst, sem)
        self.src = src

    def half(self, z):
        return [self.dst.at[self.at.s, z]]

    def origin(self):
        return [self.src]

    def like(self):
        return self.src

    def start(self):
        at = self.at
        local(self.src, self.dst.at[at.s, at.z], self.sem.at[5, 0]).start()

    def near_done(self):
        at = self.at
        local(self.src, self.dst.at[at.s, at.z], self.sem.at[5, 0]).wait()

    def start_far(self):
        pl.when(self.at.mine)(super().start_far)

    def service(self, step):
        take = super().service
        pl.when(self.at.mine)(lambda: take(step))

    def finish_far(self):
        at = self.at

        def sent(z_from):
            self.await_half(3, z_from)

        def swapped(z_from):
            self.await_half(4, z_from)

        @pl.when(at.mine)
        def _():
            for step in range(1, at.F):
                self.around(step, sent)
                self.direct(step, lambda z_to: self.await_half(0, z_to))
            if self.line:

                @pl.when((at.z == 1) | (at.z == 2))
                def _():
                    self.await_half(1, jnp.where(at.z == 1, 0, 3))

        @pl.when(jnp.logical_not(at.mine))
        def _():
            for step in range(1, at.F):
                self.around(step, swapped)


def forward_kernel(sizes, *refs):
    at = Place(sizes)
    R, F, S, G = at.R, at.F, at.S, at.G
    cond, biases = refs[:2]
    i_latents, i_cotangent, i_ada, i_qkv, i_one, w_two, w_out = refs[2:9]
    refs = refs[:1] + refs
    o_mixed, o_heads, o_merged, o_branch, o_mix, o_grad, o_full_qkv, o_full_out = refs[10:18]
    log_sums, mod, silu_all, bias_one, bias_two, g_one, g_two = refs[18:25]
    silu_src, part, parts_in, mod_src, mod_in, qkv_src, one_src, pack_all = refs[25:33]
    g_qkv, g_out, wide, bias_qkv, bias_out, val_flip, att, merged_in = refs[33:41]
    silu_sem, part_sem, mod_sem, pack_sem, qkv_sem, one_sem, two_sem, out_sem = refs[41:49]
    mixed_sem, grad_sem, att_sem, mix_sem, spread_sem, load_sem, save_sem = refs[49:56]
    bias_pack, bias_pieces, bias_slot = refs[69:72]
    latents, cotangent, w_ada, w_qkv, w_one = refs[56:61]
    mixed_all, heads, merged, branch_one, mix_all, grad_all, full_qkv, full_out = refs[61:69]
    loads = Moves(
        load_sem,
        (i_qkv, w_qkv),
        (i_ada, w_ada),
        (i_one, w_one),
        (i_latents, latents),
        (i_cotangent, cotangent),
    )
    loads.start()
    saves = Moves(
        save_sem,
        (mixed_all, o_mixed),
        (heads, o_heads),
        (merged, o_merged),
        (branch_one, o_branch),
        (mix_all, o_mix),
        (grad_all, o_grad),
        (full_qkv, o_full_qkv),
        (full_out, o_full_out),
    )
    L, D = latents.shape
    C = D // S
    T = S * L
    local_heads = H // S
    size = D // H
    rows_own = silu_all.shape[2]
    hidden = one_src.shape[2]
    block = hidden // F
    greet(G, lambda i: {"fsdp": lax.rem(at.me + i, G) // S, "seq": lax.rem(at.me + i, S)})
    greet(2 * F, lambda i: {"rep": lax.rem(at.y + i // F, 2), "fsdp": at.zs(i)})
    width = bias_pieces.shape[2]
    bias_pack[...] = biases[:, width:].astype(F32)
    bias_pieces[...] = jnp.zeros_like(bias_pieces)
    bias_pieces[at.me] = biases[:, :width].astype(F32)
    for g in range(G):
        bias_slot[:, g * width : (g + 1) * width] = bias_pieces[g]

    value = cond[...].astype(F32)
    silu = (value * jax.nn.sigmoid(value)).astype(BF).astype(F32)
    for g in range(G):
        silu_src[g] = silu[:, g * rows_own : (g + 1) * rows_own]
    loads.wait(0)
    for t in range(S):
        for j in range(3):
            qkv_src[t, :, j * C : (j + 1) * C] = w_qkv[:, j * D + t * C : j * D + (t + 1) * C]
    loads.wait(2)
    for t in range(S):
        for f in range(F):
            col = (f * S + t) * block
            one_src[t, :, f * block : (f + 1) * block] = w_one[:, col : col + block]
    greet_wait(G - 1 + 2 * F - 1)
    slot = at.y * F + at.z

    def cond_copy(i):
        z_to = at.zs(i)
        return remote(
            silu_src.at[z_to * S + at.s],
            silu_all.at[slot],
            silu_sem.at[0, i],
            silu_sem.at[1, i],
            {"rep": lax.rem(at.y + i // F, 2), "fsdp": z_to},
        )

    each(1, 2 * F, lambda i: cond_copy(i).start())
    silu_all[slot] = silu_src[at.me]

    def pack_copy(i):
        to = lax.rem(at.me + i, G)
        return remote(
            bias_pack,
            pack_all.at[at.me],
            pack_sem.at[0, 0],
            pack_sem.at[1, 0],
            {"fsdp": to // S, "seq": lax.rem(to, S)},
        )

    each(1, G, lambda i: pack_copy(i).start())
    pack_all[at.me] = bias_pack[...]

    qkv = ColumnGather(at, qkv_src, g_qkv, qkv_sem)
    one = ColumnGather(at, one_src, g_one, one_sem)
    two = RowGather(at, w_two, g_two, two_sem)
    out = OwnGather(at, w_out, g_out, out_sem)
    qkv.start()
    two.start()
    out.start()

    each(1, 2 * F, lambda i: cond_copy(i).wait())
    left = jnp.concatenate([silu_all[at.y * F + f] for f in range(F)], axis=0).astype(BF)
    loads.wait(1)
    sums = mm(left, w_ada[...]) + bias_slot[...]
    for f in range(F):
        for v in range(6):
            for t in range(S):
                col = v * D + t * C
                part[f * S + t, v : v + 1, :] = sums[f : f + 1, col : col + C]

    def part_copy(i):
        to = lax.rem(at.me + i, G)
        return remote(
            part.at[to],
            parts_in.at[at.me],
            part_sem.at[0, i],
            part_sem.at[1, i],
            {"fsdp": to // S, "seq": lax.rem(to, S)},
        )

    each(1, G, lambda i: part_copy(i).start())
    parts_in[at.me] = part[at.me]
    qkv.near_done()
    qkv.start_far()
    each(1, G, lambda i: part_copy(i).wait())
    total = parts_in[0]
    for g in range(1, G):
        total = total + parts_in[g]
    mod_src[...] = total

    def mod_copy(i):
        return remote(
            mod_src, mod_in.at[at.s], mod_sem.at[0, i], mod_sem.at[1, i], {"seq": at.ss(i)}
        )

    each(1, S, lambda i: mod_copy(i).start())
    one.start()
    mod_in[at.s] = total
    out.start_far()
    each(1, S, lambda i: mod_copy(i).wait())
    for t in range(S):
        mod[:, t * C : (t + 1) * C] = mod_in[t]

    loads.wait(3)
    step = min(64, L)

    def norm(i):
        at_rows = pl.ds(pl.multiple_of(i * step, step), step)
        normed, _ = norm_stats(latents[at_rows, :].astype(F32))
        mixed_all[at.s, at_rows, :] = (normed * (1.0 + mod[1:2, :]) + mod[0:1, :]).astype(BF)

    each(0, L // step, norm)
    gather = SeqGather(at, mixed_all, mixed_sem)
    gather.start()
    loads.wait(4)
    grad_all[at.s] = (mod[5:6, :] * cotangent[...].astype(F32)).astype(BF)
    grad_gather = SeqGather(at, grad_all, grad_sem)
    grad_gather.start()
    one.near_done()
    qkv.service(at.steps[0])
    one.start_far()
    out.near_done()
    two.near_done()

    others = pack_all.at[pl.ds(0, G - 1)]
    await_bytes(others, pack_sem.at[0, 0])
    await_bytes(others, pack_sem.at[1, 0])
    qv = 2 * D // G
    own = F // 2
    bias_qkv[...] = jnp.zeros_like(bias_qkv)
    for i in range(own):
        bias_qkv[:, i * qv : (i + 1) * qv] = pack_all[at.s * own + i][:, 0:qv]
        bias_qkv[:, 2 * C + i * qv : 2 * C + (i + 1) * qv] = pack_all[G // 2 + at.s * own + i][
            :, 0:qv
        ]
    for g in range(G):
        cols = slice(g * rows_own, (g + 1) * rows_own)
        bias_out[:, cols] = pack_all[g][:, qv : qv + rows_own]
        bias_two[:, cols] = pack_all[g][:, qv + rows_own : qv + 2 * rows_own]
    for f in range(F):
        bias_one[:, f * block : (f + 1) * block] = pack_all[f * S + at.s][:, qv + 2 * rows_own :]

    for i in at.steps[1:]:
        qkv.service(i)
    for i in at.steps:
        out.service(i)
    qkv.finish_far()

    def join(slabs, whole):
        cols = whole.shape[1]
        for g in range(G):
            wide[g * rows_own : (g + 1) * rows_own, 0:cols] = slabs(g).astype(F32)
        tall = 128 if D % 128 == 0 else D

        def cast(i):
            at_rows = pl.ds(pl.multiple_of(i * tall, tall), tall)
            whole[at_rows, :] = wide[at_rows, 0:cols].astype(BF)

        each(0, D // tall, cast)

    join(lambda g: g_qkv[g], full_qkv)
    saves.start(6)

    pad = jnp.zeros((L, LANES - size), BF)

    def project(index):
        gather.arrive(index)
        t = at.peer(arrival(index))
        at_rows = pl.ds(pl.multiple_of(t * L, L), L)
        done = (mm(mixed_all[t], full_qkv[...]) + bias_qkv[...]).astype(BF)
        for c in range(3 * local_heads):
            heads[c, at_rows, :] = jnp.concatenate(
                [done[:, c * size : (c + 1) * size], pad], axis=1
            )

    each(0, S, project)
    saves.start(0, 1)
    out.finish_far()
    spread = SeqGather(at, g_out, spread_sem)
    spread.start()
    each(1, S, grad_gather.arrive)
    saves.start(5)
    for h in range(local_heads):
        val_flip[h] = heads[2 * local_heads + h].T

    def att_copy(j):
        t = at.peer(j)
        return remote(
            att.at[t], merged_in.at[at.s], att_sem.at[0, j], att_sem.at[1, j], {"seq": t}
        )

    factor = size ** (-0.5) * log2e

    def attention(index):
        j = S - 1 - index
        t = at.peer(j)
        at_rows = pl.ds(pl.multiple_of(t * L, L), L)
        for h in range(local_heads):
            scores = mm_nt(heads[local_heads + h], heads[h, at_rows, :]) * factor
            highest = jnp.max(scores, axis=0, keepdims=True)
            raised = jnp.exp2(scores - highest)
            summed = jnp.sum(raised, axis=0, keepdims=True)
            result = mm(val_flip[h], raised.astype(BF)) / summed
            log_sums[h, t] = highest + jnp.log2(summed)
            att[t, :, h * size : (h + 1) * size] = result.T[:, :size].astype(BF)

        @pl.when(j > 0)
        def _():
            att_copy(j).start()

    one.service(at.steps[0])
    one.service(at.steps[1])
    two.start_far()
    each(0, S, attention)
    merged_in[at.s] = att[at.s]
    each(1, S, spread.arrive)
    join(lambda g: g_out[g % S, g // S], full_out)
    saves.start(7)
    each(1, S, lambda j: att_copy(j).wait())
    for t in range(S):
        merged[:, t * C : (t + 1) * C] = merged_in[t]
    saves.start(2)

    def project_out(i):
        at_rows = pl.ds(pl.multiple_of(i * step, step), step)
        branch = mm(merged[at_rows, :], full_out[...]) + bias_out[...]
        branch_one[at_rows, :] = branch
        residual = latents[at_rows, :].astype(F32) + mod[2:3, :] * branch
        normed, _ = norm_stats(residual)
        mix_all[at.s, at_rows, :] = (normed * (1.0 + mod[4:5, :]) + mod[3:4, :]).astype(BF)

    each(0, L // step, project_out)
    saves.start(3)
    mix_gather = SeqGather(at, mix_all, mix_sem)
    mix_gather.start()
    for i in at.steps[2:]:
        one.service(i)
    for i in at.steps:
        two.service(i)
    one.finish_far()
    each(1, S, mix_gather.arrive)
    saves.start(4)
    two.finish_far()
    saves.wait()


def forward(sizes, cond, biases, latents, cotangent, w_ada, w_qkv, w_one, w_two, w_out):
    R, F, S = sizes
    G = F * S
    rows, D = w_out.shape
    L = latents.shape[0]
    T = S * L
    C = D // S
    local_heads = H // S
    hidden = w_one.shape[1] // S
    shape = jax.ShapeDtypeStruct
    width = 6 * D // G
    pack = biases.shape[1] - width
    kept = (
        ((S, L, D), BF),
        ((3 * local_heads, T, LANES), BF),
        ((L, D), BF),
        ((L, D), F32),
        ((S, L, D), BF),
        ((S, L, D), BF),
        ((D, 3 * C), BF),
        ((D, D), BF),
    )
    return pl.pallas_call(
        lambda *refs: forward_kernel(sizes, *refs),
        name="forward",
        out_shape=tuple(shape(*item) for item in kept)
        + (
            shape((local_heads, S, 1, L), F32),
            shape((6, D), F32),
            shape((R * F, 1, rows), F32),
            shape((1, hidden), F32),
            shape((1, D), F32),
            shape((G, rows, hidden), BF),
            shape((F,) + w_two.shape, BF),
        ),
        in_specs=[VM] * 2 + [HB] * 7,
        out_specs=(HB,) * 8 + (VM,) * 5 + (HB,) * 2,
        scratch_shapes=[
            pltpu.VMEM((G, 1, rows), F32),
            pltpu.VMEM((G, 6, C), F32),
            pltpu.VMEM((G, 6, C), F32),
            pltpu.VMEM((6, C), F32),
            pltpu.VMEM((S, 6, C), F32),
            pltpu.VMEM((S, rows, 3 * C), BF),
            pltpu.VMEM((S, rows, hidden), BF),
            pltpu.VMEM((G, 1, pack), F32),
            pltpu.VMEM((G, rows, 3 * C), BF),
            pltpu.VMEM((S, F, rows, D), BF),
            pltpu.VMEM((D, max(D, 3 * C)), F32),
            pltpu.VMEM((1, 3 * C), F32),
            pltpu.VMEM((1, D), F32),
            pltpu.VMEM((local_heads, LANES, T), BF),
            pltpu.VMEM((S, L, C), BF),
            pltpu.VMEM((S, L, C), BF),
            DMA((2, 2 * F)),
            DMA((2, G)),
            DMA((2, S)),
            DMA((2, 1)),
            ColumnGather.scratch(F),
            ColumnGather.scratch(F),
            RowGather.scratch(F),
            OwnGather.scratch(F),
            SeqGather.scratch(S),
            SeqGather.scratch(S),
            DMA((2, S)),
            SeqGather.scratch(S),
            SeqGather.scratch(S),
            DMA((5,)),
            DMA((8,)),
        ]
        + [pltpu.VMEM(x.shape, x.dtype) for x in (latents, cotangent, w_ada, w_qkv, w_one)]
        + [pltpu.VMEM(*item) for item in kept]
        + [
            pltpu.VMEM((1, pack), F32),
            pltpu.VMEM((G, 1, width), F32),
            pltpu.VMEM((1, 6 * D), F32),
        ],
        compiler_params=params(1, 60),
    )(cond, biases, latents, cotangent, w_ada, w_qkv, w_one, w_two, w_out)


class RowScatter:
    def __init__(self, at, src, got, stage, sem):
        self.at, self.src, self.got, self.stage, self.sem = at, src, got, stage, sem

    def start(self):
        at = self.at

        def far(i):
            z_to = at.zs(i)
            remote(
                self.src.at[z_to, 3 - at.y],
                self.got.at[z_to],
                self.sem.at[0, i],
                self.sem.at[1, i],
                at.flip(),
            ).start()

        each(0, at.F, far)

    def reduce(self):
        at = self.at

        def far(i):
            z_to = at.zs(i)
            await_bytes(self.got.at[0], self.sem.at[0, i])
            await_bytes(self.got.at[0], self.sem.at[1, i])
            total = self.src[z_to, 2 + at.y].astype(F32) + self.got[z_to].astype(F32)
            self.stage[z_to] = total.astype(BF)

        each(0, at.F, far)


class Line:
    def line_up(self):
        at = self.at
        self.line = at.F == 4
        self.inner = self.line & ((at.z == 1) | (at.z == 2))
        self.end = self.line & ((at.z == 0) | (at.z == 3))
        self.opposite = jnp.where(at.z < 2, 3, 0)
        self.beside = jnp.where(at.z == 0, 1, 2)


class RowOwner(Line):
    def __init__(self, at, piece, inn, far, sem):
        self.at, self.piece, self.inn, self.far, self.sem = at, piece, inn, far, sem
        self.line_up()

    @staticmethod
    def scratch(F, shape):
        return [pltpu.VMEM((F,) + shape, BF), pltpu.VMEM(shape, BF), DMA((3, F))]

    def out_copy(self, z_to):
        at = self.at
        return remote(
            self.piece(z_to),
            self.inn.at[at.z],
            self.sem.at[0, z_to],
            self.sem.at[1, at.z],
            {"fsdp": z_to},
        )

    def far_copy(self):
        return remote(
            self.piece(self.opposite),
            self.far,
            self.sem.at[0, self.opposite],
            self.sem.at[2, 0],
            {"fsdp": self.beside},
        )

    def start(self):
        at = self.at

        @pl.when(self.end)
        def _():
            self.far_copy().start()
            self.inn[self.opposite] = jnp.zeros_like(self.far)

        def one(i):
            z_to = at.zs(i)

            @pl.when(jnp.logical_not(self.line & (z_to == self.opposite)))
            def _():
                self.out_copy(z_to).start()

        each(1, at.F, one)
        self.inn[at.z] = self.piece(at.z)[...]

    def relay(self):
        @pl.when(self.inner)
        def _():
            await_bytes(self.far, self.sem.at[2, 0])
            z_to = self.opposite
            piece = self.piece(z_to)
            piece[...] = (piece[...].astype(F32) + self.far[...].astype(F32)).astype(BF)
            self.out_copy(z_to).start()

    def total(self):
        at = self.at

        def arrived(i):
            z = at.zs(i)
            await_bytes(self.far, self.sem.at[0, z])

            @pl.when(jnp.logical_not(self.end & (z == self.opposite)))
            def _():
                await_bytes(self.far, self.sem.at[1, z])

        each(1, at.F, arrived)
        total = self.inn[0].astype(F32)
        for f in range(1, at.F):
            total = total + self.inn[f].astype(F32)
        return total.astype(BF)


class Swap:
    def __init__(self, at, done, sem):
        self.at, self.done, self.sem = at, done, sem

    def copy(self):
        mine = self.done.at[self.at.y]
        return remote(mine, mine, self.sem.at[0], self.sem.at[1], self.at.flip())

    def start(self):
        self.copy().start()

    def finish(self):
        self.copy().wait()


class FullScatter:
    def __init__(self, at, src, near, got, stage, inn, done, sem):
        self.at, self.src, self.near, self.got, self.stage = at, src, near, got, stage
        self.inn, self.done, self.sem = inn, done, sem

    @staticmethod
    def scratch(sizes, rows, cols):
        R, F, S = sizes
        return [
            pltpu.VMEM((S // 2, F, rows, cols), BF),
            pltpu.VMEM((S // 2, F, rows, cols), BF),
            pltpu.VMEM((F, rows, cols), BF),
            pltpu.VMEM((F, rows, cols), BF),
            DMA((10, max(F, S))),
        ]

    def sibling(self, j):
        at = self.at
        return remote(
            self.src.at[at.peer(j)],
            self.near.at[j // 2],
            self.sem.at[0, j],
            self.sem.at[1, j],
            {"seq": at.peer(1)},
        )

    def direct(self, j):
        at = self.at
        return remote(
            self.near.at[j // 2],
            self.got.at[j // 2],
            self.sem.at[2, j],
            self.sem.at[3, j],
            {"seq": at.peer(j)},
        )

    def start(self):
        for j in range(3, self.at.S, 2):
            self.sibling(j).start()
        self.sibling(1).start()

    def cross(self):
        at = self.at
        for j in range(2, at.S, 2):
            self.sibling(j + 1).wait()
            k = j // 2

            def add(f):
                both = self.near[k, f].astype(F32) + self.src[at.peer(j), f].astype(F32)
                self.near[k, f] = both.astype(BF)

            each(0, at.F, add)
            self.direct(j).start()
        self.sibling(1).wait()

    def out_copy(self, i):
        at = self.at
        return remote(
            self.stage.at[at.zs(i)],
            self.inn.at[at.z],
            self.sem.at[4, i],
            self.sem.at[5, i],
            {"fsdp": at.zs(i)},
        )

    def scatter(self):
        at = self.at
        for j in range(2, at.S, 2):
            self.direct(j).wait()

        def far(i):
            z_to = at.zs(i)
            total = self.src[at.s, z_to].astype(F32) + self.near[0, z_to].astype(F32)
            for k in range(1, at.S // 2):
                total = total + self.got[k, z_to].astype(F32)
            self.stage[z_to] = total.astype(BF)

            @pl.when(i > 0)
            def _():
                self.out_copy(i).start()

        each(0, at.F, far)
        self.inn[at.z] = self.stage[at.z]

    def total(self):
        at = self.at
        each(1, at.F, lambda i: self.out_copy(i).wait())
        total = self.inn[0].astype(F32)
        for f in range(1, at.F):
            total = total + self.inn[f].astype(F32)
        self.done[at.y] = total.astype(BF)
        mine = self.done.at[at.y]
        remote(mine, mine, self.sem.at[6, 0], self.sem.at[7, 0], at.flip()).start()

    def finish(self):
        await_bytes(self.done.at[0], self.sem.at[6, 0])
        await_bytes(self.done.at[0], self.sem.at[7, 0])


def mlp_kernel(sizes, *refs):
    at = Place(sizes)
    R, F, S, G = at.R, at.F, at.S, at.G
    mod, bias_one, bias_two = refs[:3]
    given = refs[3:12]
    block_out, o_resid, o_heads, o_w_one, o_two_sum, o_two_part, o_out_g = refs[12:19]
    refs = refs[:11] + refs[12:]
    grad_b_one, grad_b_two, grad_b_out, mod_sums = refs[18:22]
    act_all, pre_wide, pre_all, grad_branch, wide, two_g, two_got, two_sem = refs[22:30]
    branch_refs, mix_refs = refs[30:34], refs[34:38]
    two_inn, two_far, part_sem, load_sem, save_sem = refs[38:43]
    held = refs[43:52]
    w_one, mix_all, w_two, grad_all, latents, branch_one, cotangent, w_out, merged = held
    grad_resid, grad_heads, grad_w_one, two_sum, two_part, out_g = refs[52:58]
    loads = Moves(load_sem, *zip(given, held))
    loads.start()
    saves = Moves(
        save_sem,
        (grad_w_one, o_w_one),
        (grad_resid, o_resid),
        (grad_heads, o_heads),
        (out_g, o_out_g),
        (two_sum, o_two_sum),
        (two_part, o_two_part),
    )
    _, L, D = mix_all.shape
    C = D // S
    hidden = w_one.shape[1]
    tokens = S * L
    greet(S, lambda i: {"seq": at.ss(i)})
    greet(2, lambda i: at.flip())
    greet(F, lambda i: {"fsdp": at.zs(i)})
    greet_wait(S + F - 1)
    gate_one = mod[2:3, :]
    scale = mod[4:5, :]
    gate_two = mod[5:6, :]
    branch_sum = SeqSum(at, *branch_refs)
    mix_sum = SeqSum(at, *mix_refs)
    branch_src = branch_refs[0]
    mix_src = mix_refs[0]
    two = RowScatter(at, two_g, two_got, two_sum, two_sem)
    part_two = RowOwner(at, lambda z: two_g.at[z, pl.ds(0, 2)], two_inn, two_far, part_sem)
    step = min(256, L)

    def ahead(order):
        index = lax.rem(order + 2, S)
        t = at.peer(arrival(index))

        def part(i):
            rows = pl.ds(pl.multiple_of(i * step, step), step)
            pre = mm(mix_all[t, rows, :], w_one[...]) + bias_one[...]
            pre_wide[t, rows, :] = pre
            inner = gelu_coef * (pre + 0.044715 * pre * pre * pre)
            act = (0.5 * pre * (1.0 + jnp.tanh(inner))).astype(BF)
            act_all[t, rows, :] = act
            branch_src[t, rows, :] = mm(act, w_two[...]).astype(BF)

        each(0, L // step, part)
        branch_sum.send(index)

    loads.wait(0, 1, 2)
    each(0, S, ahead)
    loads.wait(3)
    column = 384 if hidden % 384 == 0 else hidden
    for i in range(hidden // column):
        cols = slice(i * column, (i + 1) * column)
        wide[cols, :] = mm_tn(
            act_all[:, :, cols].reshape(tokens, column), grad_all[...].reshape(tokens, D)
        )
    part_rows = two_g.shape[2]
    for f in range(F):
        for quarter in range(4):
            first = (4 * f + quarter) * part_rows
            two_g[f, quarter] = wide[first : first + part_rows, :].astype(BF)
    part_two.start()
    two.start()

    def behind(order):
        index = lax.rem(order + 2, S)
        t = at.peer(arrival(index))

        def part(i):
            rows = pl.ds(pl.multiple_of(i * step, step), step)
            pre = pre_wide[t, rows, :]
            square = pre * pre
            tanh_val = jnp.tanh(gelu_coef * (pre + 0.044715 * square * pre))
            slope = 0.5 * (1.0 + tanh_val) + 0.5 * pre * (
                1.0 - tanh_val * tanh_val
            ) * gelu_coef * (1.0 + 3.0 * 0.044715 * square)
            grad_pre = (mm_nt(grad_all[t, rows, :], w_two[...]) * slope).astype(BF)
            pre_all[t, rows, :] = grad_pre
            mix_src[t, rows, :] = mm_nt(grad_pre, w_one[...]).astype(BF)

        each(0, L // step, part)
        mix_sum.send(index)

        @pl.when(order == S - 1)
        def _():
            part_two.relay()

    each(0, S, behind)
    for i in range(hidden // column):
        cols = slice(i * column, (i + 1) * column)
        grads = pre_all[:, :, cols].reshape(tokens, column)
        grad_w_one[:, cols] = mm_tn(mix_all[...].reshape(tokens, D), grads).astype(BF)
        grad_b_one[:, cols] = jnp.sum(grads.astype(F32), axis=0, keepdims=True)
    grad_b_two[...] = jnp.sum(grad_all[at.s].astype(F32), axis=0, keepdims=True)
    saves.start(0)
    loads.wait(4, 5, 6, 7, 8)

    mix_sum.wait()
    step_back = min(32, L)
    mod_sums[...] = jnp.zeros_like(mod_sums)
    grad_b_out[...] = jnp.zeros_like(grad_b_out)

    def back(i):
        rows = pl.ds(pl.multiple_of(i * step_back, step_back), step_back)
        grad_mixed = mix_sum.total(rows)
        branch = branch_one[rows, :]
        residual = latents[rows, :].astype(F32) + gate_one * branch
        normed, inv_std = norm_stats(residual)
        grad_out = cotangent[rows, :].astype(F32)
        grad = grad_out + norm_back(grad_mixed * (1.0 + scale), normed, inv_std)
        grad_resid[rows, :] = grad
        low = (gate_one * grad).astype(BF)
        grad_branch[rows, :] = low
        mod_sums[2:3, :] += jnp.sum(grad * branch, axis=0, keepdims=True)
        mod_sums[3:4, :] += jnp.sum(grad_mixed, axis=0, keepdims=True)
        mod_sums[4:5, :] += jnp.sum(grad_mixed * normed, axis=0, keepdims=True)
        grad_b_out[...] += jnp.sum(low.astype(F32), axis=0, keepdims=True)

    each(0, L // step_back, back)
    grad_merged = mm_nt(grad_branch[...], w_out[...]).astype(BF)
    for t in range(S):
        grad_heads[t] = grad_merged[:, t * C : (t + 1) * C]
    saves.start(1, 2)
    for i in range(D // 384):
        cols = slice(i * 384, (i + 1) * 384)
        wide[:D, cols] = mm_tn(merged[...], grad_branch[:, cols])
    rows_own = out_g.shape[2]
    for f in range(F):
        for t in range(S):
            first = (f * S + t) * rows_own
            out_g[t, f] = wide[first : first + rows_own, :].astype(BF)
    saves.start(3)

    branch_sum.wait()

    def finish(i):
        rows = pl.ds(pl.multiple_of(i * step_back, step_back), step_back)
        branch_two = branch_sum.total(rows) + bias_two[...]
        residual = latents[rows, :].astype(F32) + gate_one * branch_one[rows, :]
        block_out[rows, :] = (residual + gate_two * branch_two).astype(BF)
        grad_out = cotangent[rows, :].astype(F32)
        mod_sums[5:6, :] += jnp.sum(grad_out * branch_two, axis=0, keepdims=True)

    each(0, L // step_back, finish)
    two.reduce()
    saves.start(4)
    two_part[...] = part_two.total()
    saves.start(5)
    saves.wait()


def mlp(sizes, *args):
    R, F, S = sizes
    G = F * S
    D, hidden = args[3].shape
    L = args[7].shape[0]
    C = D // S
    quarter = hidden // F // 4
    shape = jax.ShapeDtypeStruct
    kept = (
        ((L, D), F32),
        ((S, L, C), BF),
        ((D, hidden), BF),
        ((F, quarter, D), BF),
        ((2, quarter, D), BF),
        ((S, F, D // G, D), BF),
    )
    return pl.pallas_call(
        lambda *refs: mlp_kernel(sizes, *refs),
        name="mlp",
        out_shape=(shape((L, D), BF),)
        + tuple(shape(*item) for item in kept)
        + (
            shape((1, hidden), F32),
            shape((1, D), F32),
            shape((1, D), F32),
            shape((6, D), F32),
        ),
        in_specs=[VM] * 3 + [HB] * 9,
        out_specs=(VM,) + (HB,) * 6 + (VM,) * 4,
        scratch_shapes=[
            pltpu.VMEM((S, L, hidden), BF),
            pltpu.VMEM((S, L, hidden), F32),
            pltpu.VMEM((S, L, hidden), BF),
            pltpu.VMEM((L, D), BF),
            pltpu.VMEM((max(hidden, D), D), F32),
            pltpu.VMEM((F, 4, quarter, D), BF),
            pltpu.VMEM((F, quarter, D), BF),
            DMA((2, F)),
        ]
        + SeqSum.scratch(S, L, D)
        + SeqSum.scratch(S, L, D)
        + RowOwner.scratch(F, (2, quarter, D))
        + [DMA((9,)), DMA((6,))]
        + [pltpu.VMEM(x.shape, x.dtype) for x in args[3:]]
        + [pltpu.VMEM(*item) for item in kept],
        compiler_params=params(3, 60),
    )(*args)


class ColumnScatter:
    def __init__(self, at, src, got, stage, inn, far, along_sem, summed, done, sem):
        self.at, self.src, self.got, self.stage = at, src, got, stage
        self.summed, self.done, self.sem = summed, done, sem
        self.along = RowOwner(at, lambda z: stage.at[z], inn, far, along_sem)

    @staticmethod
    def scratch(sizes, rows, cols):
        R, F, S = sizes
        shape = (S // 2, rows, cols)
        return (
            [pltpu.VMEM((F,) + shape, BF), pltpu.VMEM((F,) + shape, BF)]
            + RowOwner.scratch(F, shape)
            + [pltpu.VMEM(shape, BF), DMA((5, F))]
        )

    def start(self):
        at = self.at

        def far(i):
            z_to = at.zs(i)

            def one(k):
                slot = z_to * at.S + 2 * k + at.y
                local(self.src.at[slot], self.stage.at[z_to, k], self.sem.at[2, i]).start()
                remote(
                    self.src.at[z_to * at.S + 2 * k + 1 - at.y],
                    self.got.at[z_to, k],
                    self.sem.at[0, i],
                    self.sem.at[1, i],
                    at.flip(),
                ).start()

            each(0, at.S // 2, one)

        each(0, at.F, far)

    def scatter(self):
        at = self.at

        def step(i):
            z_to = at.zs(i)
            await_bytes(self.got.at[0], self.sem.at[1, i])
            await_bytes(self.got.at[0], self.sem.at[2, i])

            def one(k):
                total = self.stage[z_to, k].astype(F32) + self.got[z_to, k].astype(F32)
                self.stage[z_to, k] = total.astype(BF)

            each(0, at.S // 2, one)

        each(0, at.F, step)
        self.along.start()

    def relay(self):
        self.along.relay()

    def near(self):
        at = self.at
        self.summed[...] = self.along.total()

        def one(k):
            s_to = 2 * k + at.y

            @pl.when(s_to == at.s)
            def _():
                self.done[at.s] = self.summed[k]

            @pl.when(s_to != at.s)
            def _():
                remote(
                    self.summed.at[k],
                    self.done.at[at.s],
                    self.sem.at[3, 0],
                    self.sem.at[3, 1],
                    {"seq": s_to},
                ).start()

        each(0, at.S // 2, one)

    def total(self):
        at = self.at

        @pl.when(at.mine)
        def _():
            await_bytes(self.done.at[pl.ds(0, at.S - 1)], self.sem.at[3, 1])
            remote(
                self.done, self.done, self.sem.at[4, 0], self.sem.at[4, 1], at.flip()
            ).start()

    def finish(self):
        at = self.at
        each(0, at.F, lambda i: await_bytes(self.got.at[0], self.sem.at[0, i]))

        @pl.when(at.mine)
        def _():
            if at.S > 2:
                await_bytes(self.done.at[pl.ds(0, at.S // 2 - 1)], self.sem.at[3, 0])
            await_bytes(self.done, self.sem.at[4, 0])

        @pl.when(jnp.logical_not(at.mine))
        def _():
            await_bytes(self.summed, self.sem.at[3, 0])
            await_bytes(self.done, self.sem.at[4, 1])


class Tail:
    def __init__(self, at, mod_all, sums, first_in, mod_src, small_src, small_in, cond_src, cond_in, pieces, sem):
        self.at, self.sums, self.first_in = at, sums, first_in
        self.mod_src, self.mod_all = mod_src, mod_all
        self.small_src, self.small_in = small_src, small_in
        self.cond_src, self.cond_in, self.pieces, self.sem = cond_src, cond_in, pieces, sem

    @staticmethod
    def scratch(sizes, D, hidden, rows):
        R, F, S = sizes
        G = F * S
        C = D // S
        pack = 2 * D // G + 2 * rows + hidden // F
        wide = max(D, hidden, 3 * C)
        return [
            pltpu.VMEM((10, wide), F32),
            pltpu.VMEM((S, 10, wide), F32),
            pltpu.VMEM((6, D), BF),
            pltpu.VMEM((F, 1, pack), F32),
            pltpu.VMEM((R * F, 1, pack), F32),
            pltpu.VMEM((R * F, 1, rows), F32),
            pltpu.VMEM((G, 1, rows), F32),
            pltpu.VMEM((G, 1, pack), F32),
            DMA((8, max(S, 2 * F, G))),
        ]

    def first_copy(self, j):
        at = self.at
        return remote(
            self.sums, self.first_in.at[at.s], self.sem.at[0, j], self.sem.at[1, j], {"seq": at.ss(j)}
        )

    def start(self, mod_sums, b_one, b_two, b_out, b_qkv):
        sums = self.sums
        D = mod_sums.shape[1]
        hidden = b_one.shape[1]
        sums[...] = jnp.zeros_like(sums)
        sums[0:6, 0:D] = mod_sums[...]
        sums[6:7, 0:hidden] = b_one[...]
        sums[7:8, 0:D] = b_two[...]
        sums[8:9, 0:D] = b_out[...]
        sums[9:10, 0 : b_qkv.shape[1]] = b_qkv[...]
        each(1, self.at.S, lambda j: self.first_copy(j).start())
        self.first_in[self.at.s] = sums[...]

    def wide_copies(self, i):
        at = self.at
        slot = at.y * at.F + at.z
        device = {"rep": lax.rem(at.y + i // at.F, 2), "fsdp": at.zs(i)}
        return (
            remote(self.mod_src, self.mod_all.at[slot], self.sem.at[2, i], self.sem.at[3, i], device),
            remote(
                self.small_src.at[at.zs(i)],
                self.small_in.at[slot],
                self.sem.at[4, i],
                self.sem.at[5, i],
                device,
            ),
        )

    def middle(self, D, hidden, rows):
        at = self.at
        F, S, G = at.F, at.S, at.G
        C = D // S
        qv = 2 * D // G
        each(1, S, lambda j: self.first_copy(j).wait())
        total = self.first_in[0]
        for t in range(1, S):
            total = total + self.first_in[t]
        self.mod_src[...] = total[0:6, 0:D].astype(BF)
        for g in range(G):
            g_half = g % (G // 2)
            t = g_half // (F // 2)
            col = (g_half % (F // 2)) * qv + (2 * C if g >= G // 2 else 0)
            self.pieces[g, :, 0:qv] = self.first_in[t, 9:10, col : col + qv]
            self.pieces[g, :, qv : qv + rows] = total[8:9, g * rows : (g + 1) * rows]
            self.pieces[g, :, qv + rows : qv + 2 * rows] = total[7:8, g * rows : (g + 1) * rows]
        block = hidden // F
        for f in range(F):
            self.small_src[f, :, 0 : qv + 2 * rows] = self.pieces[f * S + at.s][:, 0 : qv + 2 * rows]
            self.small_src[f, :, qv + 2 * rows :] = self.sums[6:7, f * block : (f + 1) * block]

        def send(i):
            first, second = self.wide_copies(i)
            first.start()
            second.start()

        each(1, 2 * F, send)
        slot = at.y * F + at.z
        self.mod_all[slot] = self.mod_src[...]
        self.small_in[slot] = self.small_src[at.z]

    def cond_copy(self, i):
        at = self.at
        to = lax.rem(at.me + i, at.G)
        return remote(
            self.cond_src.at[at.y * at.F + to // at.S],
            self.cond_in.at[at.me],
            self.sem.at[6, i],
            self.sem.at[7, i],
            {"fsdp": to // at.S, "seq": lax.rem(to, at.S)},
        )

    def owners(self, w_ada, small_out):
        at = self.at
        F, G = at.F, at.G
        D = self.mod_src.shape[1]

        def arrive(i):
            first, second = self.wide_copies(i)
            first.wait()
            second.wait()

        each(1, 2 * F, arrive)
        cond = None
        for v in range(6):
            rows = self.mod_all[:, v, :]
            part = mm_nt(rows, w_ada[:, v * D : (v + 1) * D])
            cond = part if cond is None else cond + part
        for i in range(2 * F):
            self.cond_src[i] = cond[i : i + 1, :]
        each(1, G, lambda i: self.cond_copy(i).start())
        self.cond_in[at.me] = self.cond_src[at.y * F + at.z]
        total = self.small_in[0]
        for i in range(1, 2 * F):
            total = total + self.small_in[i]
        small_out[...] = total

    def finish(self, cond, grad_cond):
        at = self.at
        rows = self.cond_in.shape[2]
        each(1, at.G, lambda i: self.cond_copy(i).wait())
        for g in range(at.G):
            cols = slice(g * rows, (g + 1) * rows)
            value = cond[:, cols].astype(F32)
            gate = jax.nn.sigmoid(value)
            grad_cond[:, cols] = self.cond_in[g] * gate * (1.0 + value * (1.0 - gate))


def backward_kernel(sizes, *refs):
    at = Place(sizes)
    R, F, S, G = at.R, at.F, at.S, at.G
    grad_heads, heads, two_g, two_part, out_g, w_qkv, mixed_all, latents, grad_resid, w_ada = refs[-10:]
    log_sums, mod, sums_in, b_one, b_two, b_out, cond, one_g = refs[:8]
    given = refs[8:18]
    refs = refs[:7] + refs[8:]
    o_latents, o_qkv, o_one, o_two, o_part, o_out, o_mod, o_small, o_cond = refs[17:26]
    refs = refs[:16] + refs[17:]
    grad_in, key_flip, key_grad, val_grad, grad_proj, qkv_wide, qkv_g, mod_sums, b_qkv, in_sem = refs[25:35]
    rest = list(refs[35:])
    mix_sum = SeqSum(at, *rest[0:4])
    mix_src = rest[0]
    qkv = ColumnScatter(at, qkv_g, *rest[4:10], o_qkv, rest[10])
    one = ColumnScatter(at, one_g, *rest[11:17], o_one, rest[17])
    two = RowOwner(at, lambda z: two_g.at[z], rest[18], rest[19], rest[20])
    out = FullScatter(at, out_g, *rest[21:25], o_out, rest[25])
    tail = Tail(at, o_mod, *rest[26:35])
    load_sem, swap_sem, save_sem, grad_latents = rest[35:39]
    held = rest[39:49]
    two_swap = Swap(at, o_two, swap_sem.at[0])
    part_swap = Swap(at, o_part, swap_sem.at[1])
    saves = Moves(save_sem, (grad_latents, o_latents))
    loads = Moves(load_sem, *zip(given, held))
    loads.start()
    _, L, C = grad_heads.shape
    rows_own, D = o_out.shape[1:]
    hidden = one_g.shape[2]
    local_heads = H // S
    size = D // H
    greet(G, lambda i: {"fsdp": lax.rem(at.me + i, G) // S, "seq": lax.rem(at.me + i, S)})
    greet(2 * F, lambda i: {"rep": lax.rem(at.y + i // F, 2), "fsdp": at.zs(i)})
    loads.wait(0, 2, 3, 4)
    o_part[at.y] = two_part[...]
    greet_wait(G - 1 + 2 * F - 1)

    def in_copy(j):
        return remote(
            grad_heads.at[at.peer(j)],
            grad_in.at[at.s],
            in_sem.at[0, j],
            in_sem.at[1, j],
            {"seq": at.peer(j)},
        )

    each(1, S, lambda j: in_copy(j).start())
    one.start()
    two.start()
    out.start()
    grad_in[at.s] = grad_heads[at.s]
    key_grad[...] = jnp.zeros_like(key_grad)
    val_grad[...] = jnp.zeros_like(val_grad)
    loads.wait(1)
    for h in range(local_heads):
        key_flip[h] = heads[local_heads + h].T
    factor = size ** (-0.5) * log2e
    score_scale = size ** (-0.5)
    pad = jnp.zeros((L, LANES - size), BF)

    def block(j):
        t = at.peer(j)

        @pl.when(j > 0)
        def _():
            in_copy(j).wait()

        rows = pl.ds(pl.multiple_of(t * L, L), L)
        for h in range(local_heads):
            query = heads[h, rows, :]
            grad = jnp.concatenate([grad_in[t, :, h * size : (h + 1) * size], pad], axis=1)
            scores = mm_nt(heads[local_heads + h], query) * factor
            probs = jnp.exp2(scores - log_sums[h, t])
            grad_probs = mm_nt(heads[2 * local_heads + h], grad)
            inner = jnp.sum(probs * grad_probs, axis=0, keepdims=True)
            grad_scores = (probs * (grad_probs - inner)).astype(BF)
            query_grad = mm(key_flip[h], grad_scores) * score_scale
            grad_proj[t, :, h * size : (h + 1) * size] = query_grad.T[:, :size].astype(BF)
            key_grad[h] += mm(grad_scores, query)
            val_grad[h] += mm(probs.astype(BF), grad)

        pl.when(j == 0)(out.cross)

    each(0, S, block)
    two.relay()
    for h in range(local_heads):
        low = (key_grad[h] * score_scale)[:, :size].astype(BF)
        grad_proj[:, :, C + h * size : C + (h + 1) * size] = low.reshape(S, L, size)
        low = val_grad[h][:, :size].astype(BF)
        grad_proj[:, :, 2 * C + h * size : 2 * C + (h + 1) * size] = low.reshape(S, L, size)

    loads.wait(5, 6)

    def spread(index):
        t = at.peer(arrival(index))
        mix_src[t] = mm_nt(grad_proj[t], w_qkv[...]).astype(BF)
        mix_sum.send(index)

    grads = grad_proj[...].reshape(S * L, 3 * C)
    qkv_wide[...] = mm_tn(mixed_all[...].reshape(S * L, D), grads)
    for g in range(G):
        qkv_g[g] = qkv_wide[g * rows_own : (g + 1) * rows_own, :].astype(BF)
    qkv.start()
    out.scatter()
    each(0, S, lambda index: spread(lax.rem(index + 2, S)))
    one.scatter()
    b_qkv[...] = jnp.sum(grads.astype(F32), axis=0, keepdims=True)
    mix_sum.wait()
    loads.wait(7, 8, 9)
    step = min(32, L)
    mod_sums[...] = sums_in[...]
    scale = mod[1:2, :]

    def back(i):
        rows = pl.ds(pl.multiple_of(i * step, step), step)
        grad_mixed = mix_sum.total(rows)
        normed, inv_std = norm_stats(latents[rows, :].astype(F32))
        grad_latents[rows, :] = grad_resid[rows, :] + norm_back(
            grad_mixed * (1.0 + scale), normed, inv_std
        )
        mod_sums[0:1, :] += jnp.sum(grad_mixed, axis=0, keepdims=True)
        mod_sums[1:2, :] += jnp.sum(grad_mixed * normed, axis=0, keepdims=True)

    each(0, L // step, back)
    saves.start()
    tail.start(mod_sums, b_one, b_two, b_out, b_qkv)
    one.relay()
    tail.middle(D, hidden, rows_own)
    qkv.scatter()
    o_two[at.y] = two.total()
    two_swap.start()
    part_swap.start()
    out.total()
    one.near()
    qkv.relay()
    tail.owners(w_ada, o_small)
    one.total()
    qkv.near()
    tail.finish(cond, o_cond)
    qkv.total()
    out.finish()
    two_swap.finish()
    part_swap.finish()
    one.finish()
    qkv.finish()
    saves.wait()


def backward(sizes, *args):
    R, F, S = sizes
    G = F * S
    one_g, grad_heads, two_g = args[7], args[8], args[10]
    two_part, latents, w_ada = args[11], args[15], args[17]
    _, L, C = grad_heads.shape
    D = latents.shape[1]
    T = S * L
    local_heads = H // S
    rows = w_ada.shape[0]
    hidden = one_g.shape[2]
    pack = 2 * D // G + 2 * rows + hidden // F
    shape = jax.ShapeDtypeStruct
    return pl.pallas_call(
        lambda *refs: backward_kernel(sizes, *refs),
        name="backward",
        out_shape=(
            shape((L, D), F32),
            shape((S, rows, 3 * C), BF),
            shape((S, rows, hidden), BF),
            shape((2,) + two_g.shape[1:], BF),
            shape((2,) + two_part.shape, BF),
            shape((2, rows, D), BF),
            shape((R * F, 6, D), BF),
            shape((1, pack), F32),
            shape((1, D), F32),
        ),
        in_specs=[VM] * 7 + [HB] * 11,
        out_specs=(HB,) + (VM,) * 8,
        scratch_shapes=[
            pltpu.VMEM((S, L, C), BF),
            pltpu.VMEM((local_heads, LANES, T), BF),
            pltpu.VMEM((local_heads, T, LANES), F32),
            pltpu.VMEM((local_heads, T, LANES), F32),
            pltpu.VMEM((S, L, 3 * C), BF),
            pltpu.VMEM((D, 3 * C), F32),
            pltpu.VMEM((G, rows, 3 * C), BF),
            pltpu.VMEM((6, D), F32),
            pltpu.VMEM((1, 3 * C), F32),
            DMA((2, S)),
        ]
        + SeqSum.scratch(S, L, D)
        + ColumnScatter.scratch(sizes, rows, 3 * C)
        + ColumnScatter.scratch(sizes, rows, hidden)
        + RowOwner.scratch(F, two_g.shape[1:])
        + FullScatter.scratch(sizes, rows, D)
        + Tail.scratch(sizes, D, hidden, rows)
        + [DMA((10,)), DMA((2, 2)), DMA((1,)), pltpu.VMEM((L, D), F32)]
        + [pltpu.VMEM(x.shape, x.dtype) for x in args[8:]],
        compiler_params=params(4, 60),
    )(*args)


def assemble_kernel(sizes, *refs):
    R, F, S = sizes
    G = F * S
    n = 11
    given, results = refs[:n], refs[n : n + 13]
    qkv, one, two, part, out, mod_all, silu_all, small = refs[n + 13 : n + 21]
    o_qkv, o_one, o_two, o_out, o_ada, b_ada, b_qv, b_out, b_one, b_two = refs[n + 21 : n + 31]
    flat, pieces, load_sem, save_sem, *passing = refs[n + 31 :]
    held = (qkv, one, two, part, out, mod_all, silu_all, small, *passing)
    loads = Moves(load_sem, *zip(given, held))
    loads.start()
    passed = tuple(zip(passing, results[:3]))
    made = (o_ada, b_ada, o_qkv, b_qv, o_out, b_out, o_one, b_one, o_two, b_two)
    saves = Moves(save_sem, *passed, *zip(made, results[3:]))
    rows, D = o_out.shape
    C = D // S
    hidden = one.shape[2]
    block = hidden // F
    loads.wait(5, 6)
    silu = silu_all[:, 0, :].astype(BF)
    width = b_ada.shape[1]
    for v in range(6):
        grads = mod_all[:, v, :]
        o_ada[:, v * D : (v + 1) * D] = mm_tn(silu, grads)
        flat[:, v * D : (v + 1) * D] = jnp.sum(grads.astype(F32), axis=0, keepdims=True)
    saves.start(3)
    for g in range(G):
        pieces[g] = flat[:, g * width : (g + 1) * width]
    b_ada[...] = pieces[lax.axis_index("fsdp") * S + lax.axis_index("seq")]
    loads.wait(7)
    first = b_qv.shape[1]
    b_qv[...] = small[:, :first]
    b_out[...] = small[:, first : first + rows]
    b_two[...] = small[:, first + rows : first + 2 * rows]
    b_one[...] = small[:, first + 2 * rows :]
    saves.start(4, 6, 8, 10, 12)
    loads.wait(1)
    for t in range(S):
        for f in range(F):
            col = (f * S + t) * block
            o_one[:, col : col + block] = one[t, :, f * block : (f + 1) * block].astype(F32)
    saves.start(9)
    loads.wait(2, 3)
    o_two[0:2] = part[0].astype(F32) + part[1].astype(F32)
    o_two[2:4] = two[...].astype(F32)
    saves.start(11)
    loads.wait(0)
    for t in range(S):
        for j in range(3):
            o_qkv[:, j * D + t * C : j * D + (t + 1) * C] = qkv[t, :, j * C : (j + 1) * C].astype(F32)
    saves.start(5)
    loads.wait(4, 8, 9, 10)
    saves.start(0, 1, 2)
    o_out[...] = out[0].astype(F32) + out[1].astype(F32)
    saves.start(7)
    saves.wait()


def assemble(sizes, qkv, one, two, part, out, mod_all, silu_all, small, *passed):
    R, F, S = sizes
    G = F * S
    rows, D = out.shape[1:]
    hidden = one.shape[2]
    made = (
        ((rows, 6 * D), F32),
        ((1, 6 * D // G), F32),
        ((rows, 3 * D), F32),
        ((1, 2 * D // G), F32),
        ((rows, D), F32),
        ((1, rows), F32),
        ((rows, hidden * S), F32),
        ((1, hidden // F), F32),
        ((4,) + two.shape[1:], F32),
        ((1, rows), F32),
    )
    given = (qkv, one, two, part, out, mod_all, silu_all, small)
    scratch = [pltpu.VMEM(x.shape, x.dtype) for x in given]
    order = (2, 6, 8, 4, 0, 1, 3, 5, 7, 9)
    return pl.pallas_call(
        lambda *refs: assemble_kernel(sizes, *refs),
        name="assemble",
        out_shape=tuple(jax.ShapeDtypeStruct(x.shape, x.dtype) for x in passed)
        + tuple(jax.ShapeDtypeStruct(*item) for item in made),
        in_specs=[HB] * 11,
        out_specs=(HB,) * 13,
        scratch_shapes=scratch
        + [pltpu.VMEM(*made[i]) for i in order]
        + [
            pltpu.VMEM((1, 6 * D), F32),
            pltpu.VMEM((G, 1, 6 * D // G), F32),
            DMA((11,)),
            DMA((13,)),
        ]
        + [pltpu.VMEM(x.shape, x.dtype) for x in passed],
        compiler_params=pltpu.CompilerParams(vmem_limit_bytes=60 * 1024 * 1024),
    )(*given, *passed)


def on_device(
    latents, cond, w_ada, b_ada, w_qkv, b_qv, w_out, b_out, w_one, b_one, w_two, b_two, cotangent
):
    sizes = R, F, S = tuple(lax.axis_size(name) for name in ("rep", "fsdp", "seq"))
    G = F * S
    _, L, D = latents.shape
    hidden = w_one.shape[1] // S
    rows = w_ada.shape[0]
    tokens = latents[0]
    two_rows = w_two.shape[0]
    (
        mixed_all,
        heads,
        merged,
        branch_one,
        mix_all,
        grad_all,
        full_qkv,
        full_out,
        log_sums,
        mod,
        silu_all,
        bias_one,
        bias_two,
        g_one,
        g_two,
    ) = forward(
        sizes,
        cond,
        jnp.concatenate([b.astype(F32) for b in (b_ada, b_qv, b_out, b_two, b_one)])[None],
        tokens,
        cotangent[0],
        w_ada,
        w_qkv,
        w_one,
        w_two.reshape(2, two_rows // 2, D),
        w_out,
    )
    full_one = g_one.reshape(D, hidden)
    full_two = g_two.reshape(hidden, D)
    (
        block_out,
        grad_resid,
        grad_heads,
        one_g,
        two_g,
        two_part,
        out_g,
        grad_b_one,
        grad_b_two,
        grad_b_out,
        mod_sums,
    ) = mlp(
        sizes,
        mod,
        bias_one,
        bias_two,
        full_one,
        mix_all,
        full_two,
        grad_all,
        tokens,
        branch_one,
        cotangent[0],
        full_out,
        merged,
    )
    grad_latents, qkv_sum, one_sum, two_sum, part_sum, out_sum, mod_all, o_small, o_cond = backward(
        sizes,
        log_sums,
        mod,
        mod_sums,
        grad_b_one,
        grad_b_two,
        grad_b_out,
        cond,
        one_g.reshape(G, rows, hidden),
        grad_heads,
        heads,
        two_g,
        two_part,
        out_g,
        full_qkv,
        mixed_all,
        tokens,
        grad_resid,
        w_ada,
    )
    outs = assemble(
        sizes,
        qkv_sum,
        one_sum,
        two_sum,
        part_sum,
        out_sum,
        mod_all,
        silu_all,
        o_small,
        block_out,
        grad_latents,
        o_cond,
    )
    shapes = (latents.shape, latents.shape, cond.shape, w_ada.shape, b_ada.shape, w_qkv.shape, b_qv.shape)
    shapes += (w_out.shape, b_out.shape, w_one.shape, b_one.shape, w_two.shape, b_two.shape)
    return tuple(out.reshape(want) for out, want in zip(outs, shapes))


def solution(mesh):
    owned = P(("fsdp", "seq"), None)
    owned_bias = P(("fsdp", "seq"))
    token_spec = P(("rep", "fsdp"), "seq", None)
    cond_spec = P(("rep", "fsdp"), None)
    weights = (owned, owned_bias) * 5
    in_specs = (token_spec, cond_spec) + weights + (token_spec,)
    out_specs = (token_spec, token_spec, cond_spec) + weights
    return jax.shard_map(
        on_device, mesh=mesh, in_specs=in_specs, out_specs=out_specs, check_vma=False
    )
```

```python
import math

import jax
import jax.numpy as jnp
from jax import lax
from jax.experimental import pallas as pl
from jax.experimental.pallas import tpu as pltpu
from jax.sharding import PartitionSpec as P

H = 16
epsilon = 1e-06
gelu_coef = math.sqrt(2.0 / math.pi)
log2e = math.log2(math.e)
BF = jnp.bfloat16
F32 = jnp.float32
LANES = 128
VM = pl.BlockSpec(memory_space=pltpu.VMEM)
HB = pl.BlockSpec(memory_space=pl.ANY)
DMA = pltpu.SemaphoreType.DMA


def params(ident, mib):
    return pltpu.CompilerParams(
        collective_id=ident, has_side_effects=True, vmem_limit_bytes=mib * 1024 * 1024
    )


def remote(src, dst, send, recv, device):
    return pltpu.make_async_remote_copy(
        src_ref=src,
        dst_ref=dst,
        send_sem=send,
        recv_sem=recv,
        device_id=device,
        device_id_type=pl.DeviceIdType.MESH,
    )


def local(src, dst, sem):
    return pltpu.make_async_copy(src, dst, sem)


def await_bytes(like, sem):
    pltpu.make_async_copy(like, like, sem).wait()


class Moves:
    def __init__(self, sem, *pairs):
        self.copies = [local(pair[0], pair[1], sem.at[i]) for i, pair in enumerate(pairs)]

    def start(self, *which):
        for i in which or range(len(self.copies)):
            self.copies[i].start()

    def wait(self, *which):
        for i in which or range(len(self.copies)):
            self.copies[i].wait()


def each(start, stop, body):
    def step(index, carry):
        body(index)
        return carry

    lax.fori_loop(start, stop, step, 0)


def greet(count, device_of):
    gate = pltpu.get_barrier_semaphore()
    each(
        1,
        count,
        lambda i: pl.semaphore_signal(
            gate, 1, device_id=device_of(i), device_id_type=pl.DeviceIdType.MESH
        ),
    )
    return count - 1


def greet_wait(count):
    pl.semaphore_wait(pltpu.get_barrier_semaphore(), count)


def norm_stats(values):
    center = values - jnp.mean(values, axis=-1, keepdims=True)
    inv_std = lax.rsqrt(jnp.mean(center * center, axis=-1, keepdims=True) + epsilon)
    return (center * inv_std, inv_std)


def norm_back(grad, normed, inv_std):
    return inv_std * (
        grad
        - jnp.mean(grad, axis=-1, keepdims=True)
        - normed * jnp.mean(grad * normed, axis=-1, keepdims=True)
    )


def mm(left, right):
    return jnp.dot(left, right, preferred_element_type=F32)


def mm_nt(left, right):
    return lax.dot_general(left, right, (((1,), (1,)), ((), ())), preferred_element_type=F32)


def mm_tn(left, right):
    return lax.dot_general(left, right, (((0,), (0,)), ((), ())), preferred_element_type=F32)


class Place:
    def __init__(self, sizes):
        self.R, self.F, self.S = sizes
        self.G = self.F * self.S
        self.y = lax.axis_index("rep")
        self.z = lax.axis_index("fsdp")
        self.s = lax.axis_index("seq")
        self.me = self.z * self.S + self.s
        self.mine = lax.rem(self.s, 2) == self.y
        self.steps = (2, 1, 3) if self.F == 4 else tuple(range(1, self.F))

    def zs(self, i):
        return lax.rem(self.z + i, self.F)

    def zs_back(self, i):
        return lax.rem(self.z - i + self.F, self.F)

    def ss(self, i):
        return lax.rem(self.s + i, self.S)

    def ss_back(self, i):
        return lax.rem(self.s - i + self.S, self.S)

    def flip(self):
        return {"rep": 1 - self.y}

    def peer(self, j):
        return lax.bitwise_xor(self.s, j)


class SeqGather:
    def __init__(self, at, dst, sem):
        self.at, self.dst, self.sem = at, dst, sem

    @staticmethod
    def scratch(S):
        return DMA((4, S))

    def direct(self, j):
        at, block = self.at, self.dst.at[self.at.s]
        return remote(block, block, self.sem.at[0, j], self.sem.at[1, j], {"seq": at.peer(j)})

    def handed(self, j):
        at = self.at
        block = self.dst.at[at.peer(j)]
        return remote(block, block, self.sem.at[2, j], self.sem.at[3, j], {"seq": at.peer(1)})

    def start(self):
        for j in range(3, self.at.S, 2):
            self.direct(j).start()
        self.direct(1).start()

    def arrive(self, index):
        @pl.when(index == 1)
        def _():
            self.direct(1).wait()

        if self.at.S > 2:

            @pl.when((index >= 2) & (lax.rem(index, 2) == 0))
            def _():
                self.direct(index + 1).wait()
                self.handed(index + 1).start()

            @pl.when((index >= 2) & (lax.rem(index, 2) == 1))
            def _():
                self.handed(index).wait()


def arrival(index):
    return jnp.where(index < 2, index, lax.bitwise_xor(index, 1))


class SeqSum:
    def __init__(self, at, src, near, inn, sem):
        self.at, self.src, self.near, self.inn, self.sem = at, src, near, inn, sem

    @staticmethod
    def scratch(S, rows, cols):
        return [
            pltpu.VMEM((S, rows, cols), BF),
            pltpu.VMEM((S // 2, rows, cols), BF),
            pltpu.VMEM((S // 2, rows, cols), BF),
            DMA((4, S)),
        ]

    def sibling(self, j):
        at = self.at
        return remote(
            self.src.at[at.peer(j)],
            self.near.at[j // 2],
            self.sem.at[0, j],
            self.sem.at[1, j],
            {"seq": at.peer(1)},
        )

    def direct(self, j):
        at = self.at
        return remote(
            self.src.at[at.peer(j)],
            self.inn.at[j // 2],
            self.sem.at[2, j],
            self.sem.at[3, j],
            {"seq": at.peer(j)},
        )

    def send(self, index):
        @pl.when((index == 1) | ((index >= 2) & (lax.rem(index, 2) == 0)))
        def _():
            self.sibling(lax.bitwise_or(index, 1)).start()

        if self.at.S > 2:

            @pl.when((index >= 2) & (lax.rem(index, 2) == 1))
            def _():
                j = index - 1
                self.sibling(index).wait()
                t = self.at.peer(j)
                step = min(64, self.src.shape[1])

                def add(i):
                    rows = pl.ds(pl.multiple_of(i * step, step), step)
                    both = self.src[t, rows, :].astype(F32) + self.near[j // 2, rows, :].astype(F32)
                    self.src[t, rows, :] = both.astype(BF)

                each(0, self.src.shape[1] // step, add)
                self.direct(j).start()

    def wait(self):
        self.sibling(1).wait()
        for j in range(2, self.at.S, 2):
            self.direct(j).wait()

    def total(self, rows):
        value = self.src[self.at.s, rows, :].astype(F32) + self.near[0, rows, :].astype(F32)
        for k in range(1, self.at.S // 2):
            value = value + self.inn[k, rows, :].astype(F32)
        return value


class FarGather:
    relayed = True

    def __init__(self, at, dst, sem):
        self.at, self.dst, self.sem = at, dst, sem
        self.line = self.relayed and at.F == 4

    @staticmethod
    def scratch(F):
        return DMA((7, F))

    def send(self, z_from, z_to, kind):
        pieces = self.half(z_from)
        held = self.origin() if kind == 0 else pieces
        for source, piece in zip(held, pieces):
            remote(
                source, piece, self.sem.at[kind, z_to], self.sem.at[2, z_from], {"fsdp": z_to}
            ).start()

    def origin(self):
        return self.half(self.at.z)

    def await_half(self, row, z):
        await_bytes(self.like(), self.sem.at[row, z])

    def around(self, step, body):
        at = self.at

        @pl.when(at.z >= step)
        def _():
            body(at.z - step)

        @pl.when(at.z + step < at.F)
        def _():
            body(at.z + step)

    def direct(self, step, body):
        if self.line and step == 3:
            return
        self.around(step, body)

    def start_far(self):
        for step in self.at.steps:
            self.direct(step, lambda z_to: self.send(self.at.z, z_to, 0))

    def service(self, step):
        at = self.at

        def take(z_from):
            self.await_half(2, z_from)
            for piece in self.half(z_from):
                remote(
                    piece, piece, self.sem.at[3, z_from], self.sem.at[4, z_from], at.flip()
                ).start()

        self.around(step, take)
        if self.line and step == 2:

            @pl.when((at.z == 1) | (at.z == 2))
            def _():
                far = jnp.where(at.z == 1, 3, 0)
                end = 3 - far
                self.send(far, end, 1)

    def finish_far(self):
        at = self.at

        def swapped(z_from):
            self.await_half(3, z_from)
            self.await_half(4, z_from)

        for step in range(1, at.F):
            self.around(step, swapped)
            self.direct(step, lambda z_to: self.await_half(0, z_to))
        if self.line:

            @pl.when((at.z == 1) | (at.z == 2))
            def _():
                self.await_half(1, jnp.where(at.z == 1, 0, 3))


class ColumnGather(FarGather):
    def __init__(self, at, src, dst, sem):
        super().__init__(at, dst, sem)
        self.src = src

    def half(self, z):
        at = self.at
        return [self.dst.at[z * at.S + 2 * k + at.y] for k in range(at.S // 2)]

    def like(self):
        return self.dst.at[pl.ds(0, self.at.S // 2)]

    def start(self):
        at, src, dst, sem = self.at, self.src, self.dst, self.sem

        def near(j):
            t = at.ss(j)
            remote(src.at[t], dst.at[at.me], sem.at[5, 0], sem.at[6, 0], {"seq": t}).start()

        each(1, at.S, near)
        local(src.at[at.s], dst.at[at.me], sem.at[5, 1]).start()

    def near_done(self):
        at, dst, sem = self.at, self.dst, self.sem
        local(self.src.at[at.s], dst.at[at.me], sem.at[5, 1]).wait()
        near = dst.at[pl.ds(0, at.S - 1)]
        await_bytes(near, sem.at[5, 0])
        await_bytes(near, sem.at[6, 0])


class RowGather(FarGather):
    def __init__(self, at, src, dst, sem):
        super().__init__(at, dst, sem)
        self.src = src

    def half(self, z):
        return [self.dst.at[z, self.at.y]]

    def origin(self):
        return [self.src.at[self.at.y]]

    def like(self):
        return self.dst.at[0, 0]

    def start(self):
        at = self.at
        local(self.src, self.dst.at[at.z], self.sem.at[5, 0]).start()

    def near_done(self):
        at = self.at
        local(self.src, self.dst.at[at.z], self.sem.at[5, 0]).wait()


class OwnGather(FarGather):
    relayed = False

    def __init__(self, at, src, dst, sem):
        super().__init__(at, dst, sem)
        self.src = src

    def half(self, z):
        return [self.dst.at[self.at.s, z]]

    def origin(self):
        return [self.src]

    def like(self):
        return self.src

    def start(self):
        at = self.at
        local(self.src, self.dst.at[at.s, at.z], self.sem.at[5, 0]).start()

    def near_done(self):
        at = self.at
        local(self.src, self.dst.at[at.s, at.z], self.sem.at[5, 0]).wait()

    def start_far(self):
        pl.when(self.at.mine)(super().start_far)

    def service(self, step):
        take = super().service
        pl.when(self.at.mine)(lambda: take(step))

    def finish_far(self):
        at = self.at

        def sent(z_from):
            self.await_half(3, z_from)

        def swapped(z_from):
            self.await_half(4, z_from)

        @pl.when(at.mine)
        def _():
            for step in range(1, at.F):
                self.around(step, sent)
                self.direct(step, lambda z_to: self.await_half(0, z_to))
            if self.line:

                @pl.when((at.z == 1) | (at.z == 2))
                def _():
                    self.await_half(1, jnp.where(at.z == 1, 0, 3))

        @pl.when(jnp.logical_not(at.mine))
        def _():
            for step in range(1, at.F):
                self.around(step, swapped)


def forward_kernel(sizes, *refs):
    at = Place(sizes)
    R, F, S, G = at.R, at.F, at.S, at.G
    cond = refs[0]
    i_biases = refs[1:6]
    i_latents, i_cotangent, i_ada, i_qkv, i_one, w_two, w_out = refs[6:13]
    refs = refs[3:]
    o_mixed, o_heads, o_merged, o_branch, o_mix, o_grad, o_full_qkv, o_full_out = refs[10:18]
    log_sums, mod, silu_all, bias_one, bias_two, g_one, g_two = refs[18:25]
    silu_src, part, parts_in, mod_src, mod_in, qkv_src, one_src, pack_all = refs[25:33]
    g_qkv, g_out, wide, bias_qkv, bias_out, val_flip, att, merged_in = refs[33:41]
    silu_sem, part_sem, mod_sem, pack_sem, qkv_sem, one_sem, two_sem, out_sem = refs[41:49]
    mixed_sem, grad_sem, att_sem, mix_sem, spread_sem, load_sem, save_sem = refs[49:56]
    bias_pack, bias_pieces, bias_slot, bias_sem = refs[69:73]
    biases = refs[73:78]
    bias_loads = Moves(bias_sem, *zip(i_biases, biases))
    bias_loads.start()
    latents, cotangent, w_ada, w_qkv, w_one = refs[56:61]
    mixed_all, heads, merged, branch_one, mix_all, grad_all, full_qkv, full_out = refs[61:69]
    loads = Moves(
        load_sem,
        (i_qkv, w_qkv),
        (i_ada, w_ada),
        (i_one, w_one),
        (i_latents, latents),
        (i_cotangent, cotangent),
    )
    loads.start()
    saves = Moves(
        save_sem,
        (mixed_all, o_mixed),
        (heads, o_heads),
        (merged, o_merged),
        (branch_one, o_branch),
        (mix_all, o_mix),
        (grad_all, o_grad),
        (full_qkv, o_full_qkv),
        (full_out, o_full_out),
    )
    L, D = latents.shape
    C = D // S
    T = S * L
    local_heads = H // S
    size = D // H
    rows_own = silu_all.shape[2]
    hidden = one_src.shape[2]
    block = hidden // F
    greet(G, lambda i: {"fsdp": lax.rem(at.me + i, G) // S, "seq": lax.rem(at.me + i, S)})
    greet(2 * F, lambda i: {"rep": lax.rem(at.y + i // F, 2), "fsdp": at.zs(i)})
    width = bias_pieces.shape[2]
    bias_loads.wait()
    first = 0
    for bias in biases[1:]:
        length = bias.shape[0]
        bias_pack[:, first : first + length] = bias[...].astype(F32).reshape(1, length)
        first = first + length
    bias_pieces[...] = jnp.zeros_like(bias_pieces)
    bias_pieces[at.me] = biases[0][...].astype(F32).reshape(1, width)
    for g in range(G):
        bias_slot[:, g * width : (g + 1) * width] = bias_pieces[g]

    value = cond[...].astype(F32)
    silu = (value * jax.nn.sigmoid(value)).astype(BF).astype(F32)
    for g in range(G):
        silu_src[g] = silu[:, g * rows_own : (g + 1) * rows_own]
    loads.wait(0)
    for t in range(S):
        for j in range(3):
            qkv_src[t, :, j * C : (j + 1) * C] = w_qkv[:, j * D + t * C : j * D + (t + 1) * C]
    loads.wait(2)
    for t in range(S):
        for f in range(F):
            col = (f * S + t) * block
            one_src[t, :, f * block : (f + 1) * block] = w_one[:, col : col + block]
    greet_wait(G - 1 + 2 * F - 1)
    slot = at.y * F + at.z

    def cond_copy(i):
        z_to = at.zs(i)
        return remote(
            silu_src.at[z_to * S + at.s],
            silu_all.at[slot],
            silu_sem.at[0, i],
            silu_sem.at[1, i],
            {"rep": lax.rem(at.y + i // F, 2), "fsdp": z_to},
        )

    each(1, 2 * F, lambda i: cond_copy(i).start())
    silu_all[slot] = silu_src[at.me]

    def pack_copy(i):
        to = lax.rem(at.me + i, G)
        return remote(
            bias_pack,
            pack_all.at[at.me],
            pack_sem.at[0, 0],
            pack_sem.at[1, 0],
            {"fsdp": to // S, "seq": lax.rem(to, S)},
        )

    each(1, G, lambda i: pack_copy(i).start())
    pack_all[at.me] = bias_pack[...]

    qkv = ColumnGather(at, qkv_src, g_qkv, qkv_sem)
    one = ColumnGather(at, one_src, g_one, one_sem)
    two = RowGather(at, w_two, g_two, two_sem)
    out = OwnGather(at, w_out, g_out, out_sem)
    qkv.start()
    two.start()
    out.start()

    each(1, 2 * F, lambda i: cond_copy(i).wait())
    left = jnp.concatenate([silu_all[at.y * F + f] for f in range(F)], axis=0).astype(BF)
    loads.wait(1)
    sums = mm(left, w_ada[...]) + bias_slot[...]
    for f in range(F):
        for v in range(6):
            for t in range(S):
                col = v * D + t * C
                part[f * S + t, v : v + 1, :] = sums[f : f + 1, col : col + C]

    def part_copy(i):
        to = lax.rem(at.me + i, G)
        return remote(
            part.at[to],
            parts_in.at[at.me],
            part_sem.at[0, i],
            part_sem.at[1, i],
            {"fsdp": to // S, "seq": lax.rem(to, S)},
        )

    each(1, G, lambda i: part_copy(i).start())
    parts_in[at.me] = part[at.me]
    qkv.near_done()
    qkv.start_far()
    each(1, G, lambda i: part_copy(i).wait())
    total = parts_in[0]
    for g in range(1, G):
        total = total + parts_in[g]
    mod_src[...] = total

    def mod_copy(i):
        return remote(
            mod_src, mod_in.at[at.s], mod_sem.at[0, i], mod_sem.at[1, i], {"seq": at.ss(i)}
        )

    each(1, S, lambda i: mod_copy(i).start())
    one.start()
    mod_in[at.s] = total
    out.start_far()
    each(1, S, lambda i: mod_copy(i).wait())
    for t in range(S):
        mod[:, t * C : (t + 1) * C] = mod_in[t]

    loads.wait(3)
    step = min(64, L)

    def norm(i):
        at_rows = pl.ds(pl.multiple_of(i * step, step), step)
        normed, _ = norm_stats(latents[at_rows, :].astype(F32))
        mixed_all[at.s, at_rows, :] = (normed * (1.0 + mod[1:2, :]) + mod[0:1, :]).astype(BF)

    each(0, L // step, norm)
    gather = SeqGather(at, mixed_all, mixed_sem)
    gather.start()
    loads.wait(4)
    grad_all[at.s] = (mod[5:6, :] * cotangent[...].astype(F32)).astype(BF)
    grad_gather = SeqGather(at, grad_all, grad_sem)
    grad_gather.start()
    one.near_done()
    qkv.service(at.steps[0])
    one.start_far()
    out.near_done()
    two.near_done()

    others = pack_all.at[pl.ds(0, G - 1)]
    await_bytes(others, pack_sem.at[0, 0])
    await_bytes(others, pack_sem.at[1, 0])
    qv = 2 * D // G
    own = F // 2
    bias_qkv[...] = jnp.zeros_like(bias_qkv)
    for i in range(own):
        bias_qkv[:, i * qv : (i + 1) * qv] = pack_all[at.s * own + i][:, 0:qv]
        bias_qkv[:, 2 * C + i * qv : 2 * C + (i + 1) * qv] = pack_all[G // 2 + at.s * own + i][
            :, 0:qv
        ]
    for g in range(G):
        cols = slice(g * rows_own, (g + 1) * rows_own)
        bias_out[:, cols] = pack_all[g][:, qv : qv + rows_own]
        bias_two[:, cols] = pack_all[g][:, qv + rows_own : qv + 2 * rows_own]
    for f in range(F):
        bias_one[:, f * block : (f + 1) * block] = pack_all[f * S + at.s][:, qv + 2 * rows_own :]

    for i in at.steps[1:]:
        qkv.service(i)
    for i in at.steps:
        out.service(i)
    qkv.finish_far()

    def join(slabs, whole):
        cols = whole.shape[1]
        for g in range(G):
            wide[g * rows_own : (g + 1) * rows_own, 0:cols] = slabs(g).astype(F32)
        tall = 128 if D % 128 == 0 else D

        def cast(i):
            at_rows = pl.ds(pl.multiple_of(i * tall, tall), tall)
            whole[at_rows, :] = wide[at_rows, 0:cols].astype(BF)

        each(0, D // tall, cast)

    join(lambda g: g_qkv[g], full_qkv)
    saves.start(6)

    pad = jnp.zeros((L, LANES - size), BF)

    def project(index):
        gather.arrive(index)
        t = at.peer(arrival(index))
        at_rows = pl.ds(pl.multiple_of(t * L, L), L)
        done = (mm(mixed_all[t], full_qkv[...]) + bias_qkv[...]).astype(BF)
        for c in range(3 * local_heads):
            heads[c, at_rows, :] = jnp.concatenate(
                [done[:, c * size : (c + 1) * size], pad], axis=1
            )

    each(0, S, project)
    saves.start(0, 1)
    out.finish_far()
    spread = SeqGather(at, g_out, spread_sem)
    spread.start()
    each(1, S, grad_gather.arrive)
    saves.start(5)
    for h in range(local_heads):
        val_flip[h] = heads[2 * local_heads + h].T

    def att_copy(j):
        t = at.peer(j)
        return remote(
            att.at[t], merged_in.at[at.s], att_sem.at[0, j], att_sem.at[1, j], {"seq": t}
        )

    factor = size ** (-0.5) * log2e

    def attention(index):
        j = S - 1 - index
        t = at.peer(j)
        at_rows = pl.ds(pl.multiple_of(t * L, L), L)
        for h in range(local_heads):
            scores = mm_nt(heads[local_heads + h], heads[h, at_rows, :]) * factor
            highest = jnp.max(scores, axis=0, keepdims=True)
            raised = jnp.exp2(scores - highest)
            summed = jnp.sum(raised, axis=0, keepdims=True)
            result = mm(val_flip[h], raised.astype(BF)) / summed
            log_sums[h, t] = highest + jnp.log2(summed)
            att[t, :, h * size : (h + 1) * size] = result.T[:, :size].astype(BF)

        @pl.when(j > 0)
        def _():
            att_copy(j).start()

    one.service(at.steps[0])
    one.service(at.steps[1])
    two.start_far()
    each(0, S, attention)
    merged_in[at.s] = att[at.s]
    each(1, S, spread.arrive)
    join(lambda g: g_out[g % S, g // S], full_out)
    saves.start(7)
    each(1, S, lambda j: att_copy(j).wait())
    for t in range(S):
        merged[:, t * C : (t + 1) * C] = merged_in[t]
    saves.start(2)

    def project_out(i):
        at_rows = pl.ds(pl.multiple_of(i * step, step), step)
        branch = mm(merged[at_rows, :], full_out[...]) + bias_out[...]
        branch_one[at_rows, :] = branch
        residual = latents[at_rows, :].astype(F32) + mod[2:3, :] * branch
        normed, _ = norm_stats(residual)
        mix_all[at.s, at_rows, :] = (normed * (1.0 + mod[4:5, :]) + mod[3:4, :]).astype(BF)

    each(0, L // step, project_out)
    saves.start(3)
    mix_gather = SeqGather(at, mix_all, mix_sem)
    mix_gather.start()
    for i in at.steps[2:]:
        one.service(i)
    for i in at.steps:
        two.service(i)
    one.finish_far()
    each(1, S, mix_gather.arrive)
    saves.start(4)
    two.finish_far()
    saves.wait()


def forward(sizes, cond, *args):
    biases = args[:5]
    latents, cotangent, w_ada, w_qkv, w_one, w_two, w_out = args[5:]
    R, F, S = sizes
    G = F * S
    rows, D = w_out.shape
    L = latents.shape[0]
    T = S * L
    C = D // S
    local_heads = H // S
    hidden = w_one.shape[1] // S
    shape = jax.ShapeDtypeStruct
    width = 6 * D // G
    pack = sum(bias.shape[0] for bias in biases[1:])
    kept = (
        ((S, L, D), BF),
        ((3 * local_heads, T, LANES), BF),
        ((L, D), BF),
        ((L, D), F32),
        ((S, L, D), BF),
        ((S, L, D), BF),
        ((D, 3 * C), BF),
        ((D, D), BF),
    )
    return pl.pallas_call(
        lambda *refs: forward_kernel(sizes, *refs),
        name="forward",
        out_shape=tuple(shape(*item) for item in kept)
        + (
            shape((local_heads, S, 1, L), F32),
            shape((6, D), F32),
            shape((R * F, 1, rows), F32),
            shape((1, hidden), F32),
            shape((1, D), F32),
            shape((G, rows, hidden), BF),
            shape((F,) + w_two.shape, BF),
        ),
        in_specs=[VM] + [HB] * 12,
        out_specs=(HB,) * 8 + (VM,) * 5 + (HB,) * 2,
        scratch_shapes=[
            pltpu.VMEM((G, 1, rows), F32),
            pltpu.VMEM((G, 6, C), F32),
            pltpu.VMEM((G, 6, C), F32),
            pltpu.VMEM((6, C), F32),
            pltpu.VMEM((S, 6, C), F32),
            pltpu.VMEM((S, rows, 3 * C), BF),
            pltpu.VMEM((S, rows, hidden), BF),
            pltpu.VMEM((G, 1, pack), F32),
            pltpu.VMEM((G, rows, 3 * C), BF),
            pltpu.VMEM((S, F, rows, D), BF),
            pltpu.VMEM((D, max(D, 3 * C)), F32),
            pltpu.VMEM((1, 3 * C), F32),
            pltpu.VMEM((1, D), F32),
            pltpu.VMEM((local_heads, LANES, T), BF),
            pltpu.VMEM((S, L, C), BF),
            pltpu.VMEM((S, L, C), BF),
            DMA((2, 2 * F)),
            DMA((2, G)),
            DMA((2, S)),
            DMA((2, 1)),
            ColumnGather.scratch(F),
            ColumnGather.scratch(F),
            RowGather.scratch(F),
            OwnGather.scratch(F),
            SeqGather.scratch(S),
            SeqGather.scratch(S),
            DMA((2, S)),
            SeqGather.scratch(S),
            SeqGather.scratch(S),
            DMA((5,)),
            DMA((8,)),
        ]
        + [pltpu.VMEM(x.shape, x.dtype) for x in (latents, cotangent, w_ada, w_qkv, w_one)]
        + [pltpu.VMEM(*item) for item in kept]
        + [
            pltpu.VMEM((1, pack), F32),
            pltpu.VMEM((G, 1, width), F32),
            pltpu.VMEM((1, 6 * D), F32),
            DMA((5,)),
        ]
        + [pltpu.VMEM(bias.shape, BF) for bias in biases],
        compiler_params=params(1, 60),
    )(cond, *args)


class RowScatter:
    def __init__(self, at, src, got, stage, sem):
        self.at, self.src, self.got, self.stage, self.sem = at, src, got, stage, sem

    def start(self):
        at = self.at

        def far(i):
            z_to = at.zs(i)
            remote(
                self.src.at[z_to, 3 - at.y],
                self.got.at[z_to],
                self.sem.at[0, i],
                self.sem.at[1, i],
                at.flip(),
            ).start()

        each(0, at.F, far)

    def reduce(self):
        at = self.at

        def far(i):
            z_to = at.zs(i)
            await_bytes(self.got.at[0], self.sem.at[0, i])
            await_bytes(self.got.at[0], self.sem.at[1, i])
            total = self.src[z_to, 2 + at.y].astype(F32) + self.got[z_to].astype(F32)
            self.stage[z_to] = total.astype(BF)

        each(0, at.F, far)


class Line:
    def line_up(self):
        at = self.at
        self.line = at.F == 4
        self.inner = self.line & ((at.z == 1) | (at.z == 2))
        self.end = self.line & ((at.z == 0) | (at.z == 3))
        self.opposite = jnp.where(at.z < 2, 3, 0)
        self.beside = jnp.where(at.z == 0, 1, 2)


class RowOwner(Line):
    def __init__(self, at, piece, inn, far, sem):
        self.at, self.piece, self.inn, self.far, self.sem = at, piece, inn, far, sem
        self.line_up()

    @staticmethod
    def scratch(F, shape):
        return [pltpu.VMEM((F,) + shape, BF), pltpu.VMEM(shape, BF), DMA((3, F))]

    def out_copy(self, z_to):
        at = self.at
        return remote(
            self.piece(z_to),
            self.inn.at[at.z],
            self.sem.at[0, z_to],
            self.sem.at[1, at.z],
            {"fsdp": z_to},
        )

    def far_copy(self):
        return remote(
            self.piece(self.opposite),
            self.far,
            self.sem.at[0, self.opposite],
            self.sem.at[2, 0],
            {"fsdp": self.beside},
        )

    def start(self):
        at = self.at

        @pl.when(self.end)
        def _():
            self.far_copy().start()
            self.inn[self.opposite] = jnp.zeros_like(self.far)

        def one(i):
            z_to = at.zs(i)

            @pl.when(jnp.logical_not(self.line & (z_to == self.opposite)))
            def _():
                self.out_copy(z_to).start()

        each(1, at.F, one)
        self.inn[at.z] = self.piece(at.z)[...]

    def relay(self):
        @pl.when(self.inner)
        def _():
            await_bytes(self.far, self.sem.at[2, 0])
            z_to = self.opposite
            piece = self.piece(z_to)
            piece[...] = (piece[...].astype(F32) + self.far[...].astype(F32)).astype(BF)
            self.out_copy(z_to).start()

    def total(self):
        at = self.at

        def arrived(i):
            z = at.zs(i)
            await_bytes(self.far, self.sem.at[0, z])

            @pl.when(jnp.logical_not(self.end & (z == self.opposite)))
            def _():
                await_bytes(self.far, self.sem.at[1, z])

        each(1, at.F, arrived)
        total = self.inn[0].astype(F32)
        for f in range(1, at.F):
            total = total + self.inn[f].astype(F32)
        return total.astype(BF)


class Swap:
    def __init__(self, at, done, sem):
        self.at, self.done, self.sem = at, done, sem

    def copy(self):
        mine = self.done.at[self.at.y]
        return remote(mine, mine, self.sem.at[0], self.sem.at[1], self.at.flip())

    def start(self):
        self.copy().start()

    def finish(self):
        self.copy().wait()


class FullScatter:
    def __init__(self, at, src, near, got, stage, inn, done, sem):
        self.at, self.src, self.near, self.got, self.stage = at, src, near, got, stage
        self.inn, self.done, self.sem = inn, done, sem

    @staticmethod
    def scratch(sizes, rows, cols):
        R, F, S = sizes
        return [
            pltpu.VMEM((S // 2, F, rows, cols), BF),
            pltpu.VMEM((S // 2, F, rows, cols), BF),
            pltpu.VMEM((F, rows, cols), BF),
            pltpu.VMEM((F, rows, cols), BF),
            DMA((10, max(F, S))),
        ]

    def sibling(self, j):
        at = self.at
        return remote(
            self.src.at[at.peer(j)],
            self.near.at[j // 2],
            self.sem.at[0, j],
            self.sem.at[1, j],
            {"seq": at.peer(1)},
        )

    def direct(self, j):
        at = self.at
        return remote(
            self.near.at[j // 2],
            self.got.at[j // 2],
            self.sem.at[2, j],
            self.sem.at[3, j],
            {"seq": at.peer(j)},
        )

    def start(self):
        for j in range(3, self.at.S, 2):
            self.sibling(j).start()
        self.sibling(1).start()

    def cross(self):
        at = self.at
        for j in range(2, at.S, 2):
            self.sibling(j + 1).wait()
            k = j // 2

            def add(f):
                both = self.near[k, f].astype(F32) + self.src[at.peer(j), f].astype(F32)
                self.near[k, f] = both.astype(BF)

            each(0, at.F, add)
            self.direct(j).start()
        self.sibling(1).wait()

    def out_copy(self, i):
        at = self.at
        return remote(
            self.stage.at[at.zs(i)],
            self.inn.at[at.z],
            self.sem.at[4, i],
            self.sem.at[5, i],
            {"fsdp": at.zs(i)},
        )

    def scatter(self):
        at = self.at
        for j in range(2, at.S, 2):
            self.direct(j).wait()

        def far(i):
            z_to = at.zs(i)
            total = self.src[at.s, z_to].astype(F32) + self.near[0, z_to].astype(F32)
            for k in range(1, at.S // 2):
                total = total + self.got[k, z_to].astype(F32)
            self.stage[z_to] = total.astype(BF)

            @pl.when(i > 0)
            def _():
                self.out_copy(i).start()

        each(0, at.F, far)
        self.inn[at.z] = self.stage[at.z]

    def total(self):
        at = self.at
        each(1, at.F, lambda i: self.out_copy(i).wait())
        total = self.inn[0].astype(F32)
        for f in range(1, at.F):
            total = total + self.inn[f].astype(F32)
        self.done[at.y] = total.astype(BF)
        mine = self.done.at[at.y]
        remote(mine, mine, self.sem.at[6, 0], self.sem.at[7, 0], at.flip()).start()

    def finish(self):
        await_bytes(self.done.at[0], self.sem.at[6, 0])
        await_bytes(self.done.at[0], self.sem.at[7, 0])


def mlp_kernel(sizes, *refs):
    at = Place(sizes)
    R, F, S, G = at.R, at.F, at.S, at.G
    mod, bias_one, bias_two = refs[:3]
    given = refs[3:12]
    block_out, o_resid, o_heads, o_w_one, o_two_sum, o_two_part, o_out_g = refs[12:19]
    refs = refs[:11] + refs[12:]
    grad_b_one, grad_b_two, grad_b_out, mod_sums = refs[18:22]
    act_all, pre_wide, pre_all, grad_branch, wide, two_g, two_got, two_sem = refs[22:30]
    branch_refs, mix_refs = refs[30:34], refs[34:38]
    two_inn, two_far, part_sem, load_sem, save_sem = refs[38:43]
    held = refs[43:52]
    w_one, mix_all, w_two, grad_all, latents, branch_one, cotangent, w_out, merged = held
    grad_resid, grad_heads, grad_w_one, two_sum, two_part, out_g = refs[52:58]
    loads = Moves(load_sem, *zip(given, held))
    loads.start()
    saves = Moves(
        save_sem,
        (grad_w_one, o_w_one),
        (grad_resid, o_resid),
        (grad_heads, o_heads),
        (out_g, o_out_g),
        (two_sum, o_two_sum),
        (two_part, o_two_part),
    )
    _, L, D = mix_all.shape
    C = D // S
    hidden = w_one.shape[1]
    tokens = S * L
    greet(S, lambda i: {"seq": at.ss(i)})
    greet(2, lambda i: at.flip())
    greet(F, lambda i: {"fsdp": at.zs(i)})
    greet_wait(S + F - 1)
    gate_one = mod[2:3, :]
    scale = mod[4:5, :]
    gate_two = mod[5:6, :]
    branch_sum = SeqSum(at, *branch_refs)
    mix_sum = SeqSum(at, *mix_refs)
    branch_src = branch_refs[0]
    mix_src = mix_refs[0]
    two = RowScatter(at, two_g, two_got, two_sum, two_sem)
    part_two = RowOwner(at, lambda z: two_g.at[z, pl.ds(0, 2)], two_inn, two_far, part_sem)
    step = min(256, L)

    def ahead(order):
        index = lax.rem(order + 2, S)
        t = at.peer(arrival(index))

        def part(i):
            rows = pl.ds(pl.multiple_of(i * step, step), step)
            pre = mm(mix_all[t, rows, :], w_one[...]) + bias_one[...]
            pre_wide[t, rows, :] = pre
            inner = gelu_coef * (pre + 0.044715 * pre * pre * pre)
            act = (0.5 * pre * (1.0 + jnp.tanh(inner))).astype(BF)
            act_all[t, rows, :] = act
            branch_src[t, rows, :] = mm(act, w_two[...]).astype(BF)

        each(0, L // step, part)
        branch_sum.send(index)

    loads.wait(0, 1, 2)
    each(0, S, ahead)
    loads.wait(3)
    column = 384 if hidden % 384 == 0 else hidden
    for i in range(hidden // column):
        cols = slice(i * column, (i + 1) * column)
        wide[cols, :] = mm_tn(
            act_all[:, :, cols].reshape(tokens, column), grad_all[...].reshape(tokens, D)
        )
    part_rows = two_g.shape[2]
    for f in range(F):
        for quarter in range(4):
            first = (4 * f + quarter) * part_rows
            two_g[f, quarter] = wide[first : first + part_rows, :].astype(BF)
    part_two.start()
    two.start()

    def behind(order):
        index = lax.rem(order + 2, S)
        t = at.peer(arrival(index))

        def part(i):
            rows = pl.ds(pl.multiple_of(i * step, step), step)
            pre = pre_wide[t, rows, :]
            square = pre * pre
            tanh_val = jnp.tanh(gelu_coef * (pre + 0.044715 * square * pre))
            slope = 0.5 * (1.0 + tanh_val) + 0.5 * pre * (
                1.0 - tanh_val * tanh_val
            ) * gelu_coef * (1.0 + 3.0 * 0.044715 * square)
            grad_pre = (mm_nt(grad_all[t, rows, :], w_two[...]) * slope).astype(BF)
            pre_all[t, rows, :] = grad_pre
            mix_src[t, rows, :] = mm_nt(grad_pre, w_one[...]).astype(BF)

        each(0, L // step, part)
        mix_sum.send(index)

        @pl.when(order == S - 1)
        def _():
            part_two.relay()

    each(0, S, behind)
    for i in range(hidden // column):
        cols = slice(i * column, (i + 1) * column)
        grads = pre_all[:, :, cols].reshape(tokens, column)
        grad_w_one[:, cols] = mm_tn(mix_all[...].reshape(tokens, D), grads).astype(BF)
        grad_b_one[:, cols] = jnp.sum(grads.astype(F32), axis=0, keepdims=True)
    grad_b_two[...] = jnp.sum(grad_all[at.s].astype(F32), axis=0, keepdims=True)
    saves.start(0)
    loads.wait(4, 5, 6, 7, 8)

    mix_sum.wait()
    step_back = min(32, L)
    mod_sums[...] = jnp.zeros_like(mod_sums)
    grad_b_out[...] = jnp.zeros_like(grad_b_out)

    def back(i):
        rows = pl.ds(pl.multiple_of(i * step_back, step_back), step_back)
        grad_mixed = mix_sum.total(rows)
        branch = branch_one[rows, :]
        residual = latents[rows, :].astype(F32) + gate_one * branch
        normed, inv_std = norm_stats(residual)
        grad_out = cotangent[rows, :].astype(F32)
        grad = grad_out + norm_back(grad_mixed * (1.0 + scale), normed, inv_std)
        grad_resid[rows, :] = grad
        low = (gate_one * grad).astype(BF)
        grad_branch[rows, :] = low
        mod_sums[2:3, :] += jnp.sum(grad * branch, axis=0, keepdims=True)
        mod_sums[3:4, :] += jnp.sum(grad_mixed, axis=0, keepdims=True)
        mod_sums[4:5, :] += jnp.sum(grad_mixed * normed, axis=0, keepdims=True)
        grad_b_out[...] += jnp.sum(low.astype(F32), axis=0, keepdims=True)

    each(0, L // step_back, back)
    grad_merged = mm_nt(grad_branch[...], w_out[...]).astype(BF)
    for t in range(S):
        grad_heads[t] = grad_merged[:, t * C : (t + 1) * C]
    saves.start(1, 2)
    for i in range(D // 384):
        cols = slice(i * 384, (i + 1) * 384)
        wide[:D, cols] = mm_tn(merged[...], grad_branch[:, cols])
    rows_own = out_g.shape[2]
    for f in range(F):
        for t in range(S):
            first = (f * S + t) * rows_own
            out_g[t, f] = wide[first : first + rows_own, :].astype(BF)
    saves.start(3)

    branch_sum.wait()

    def finish(i):
        rows = pl.ds(pl.multiple_of(i * step_back, step_back), step_back)
        branch_two = branch_sum.total(rows) + bias_two[...]
        residual = latents[rows, :].astype(F32) + gate_one * branch_one[rows, :]
        block_out[rows, :] = (residual + gate_two * branch_two).astype(BF)
        grad_out = cotangent[rows, :].astype(F32)
        mod_sums[5:6, :] += jnp.sum(grad_out * branch_two, axis=0, keepdims=True)

    each(0, L // step_back, finish)
    two.reduce()
    saves.start(4)
    two_part[...] = part_two.total()
    saves.start(5)
    saves.wait()


def mlp(sizes, *args):
    R, F, S = sizes
    G = F * S
    D, hidden = args[3].shape
    L = args[7].shape[0]
    C = D // S
    quarter = hidden // F // 4
    shape = jax.ShapeDtypeStruct
    kept = (
        ((L, D), F32),
        ((S, L, C), BF),
        ((D, hidden), BF),
        ((F, quarter, D), BF),
        ((2, quarter, D), BF),
        ((S, F, D // G, D), BF),
    )
    return pl.pallas_call(
        lambda *refs: mlp_kernel(sizes, *refs),
        name="mlp",
        out_shape=(shape((L, D), BF),)
        + tuple(shape(*item) for item in kept)
        + (
            shape((1, hidden), F32),
            shape((1, D), F32),
            shape((1, D), F32),
            shape((6, D), F32),
        ),
        in_specs=[VM] * 3 + [HB] * 9,
        out_specs=(VM,) + (HB,) * 6 + (VM,) * 4,
        scratch_shapes=[
            pltpu.VMEM((S, L, hidden), BF),
            pltpu.VMEM((S, L, hidden), F32),
            pltpu.VMEM((S, L, hidden), BF),
            pltpu.VMEM((L, D), BF),
            pltpu.VMEM((max(hidden, D), D), F32),
            pltpu.VMEM((F, 4, quarter, D), BF),
            pltpu.VMEM((F, quarter, D), BF),
            DMA((2, F)),
        ]
        + SeqSum.scratch(S, L, D)
        + SeqSum.scratch(S, L, D)
        + RowOwner.scratch(F, (2, quarter, D))
        + [DMA((9,)), DMA((6,))]
        + [pltpu.VMEM(x.shape, x.dtype) for x in args[3:]]
        + [pltpu.VMEM(*item) for item in kept],
        compiler_params=params(3, 60),
    )(*args)


class ColumnScatter:
    def __init__(self, at, src, got, stage, inn, far, along_sem, summed, done, sem):
        self.at, self.src, self.got, self.stage = at, src, got, stage
        self.summed, self.done, self.sem = summed, done, sem
        self.along = RowOwner(at, lambda z: stage.at[z], inn, far, along_sem)

    @staticmethod
    def scratch(sizes, rows, cols):
        R, F, S = sizes
        shape = (S // 2, rows, cols)
        return (
            [pltpu.VMEM((F,) + shape, BF), pltpu.VMEM((F,) + shape, BF)]
            + RowOwner.scratch(F, shape)
            + [pltpu.VMEM(shape, BF), DMA((5, F))]
        )

    def start(self):
        at = self.at

        def far(i):
            z_to = at.zs(i)

            def one(k):
                slot = z_to * at.S + 2 * k + at.y
                local(self.src.at[slot], self.stage.at[z_to, k], self.sem.at[2, i]).start()
                remote(
                    self.src.at[z_to * at.S + 2 * k + 1 - at.y],
                    self.got.at[z_to, k],
                    self.sem.at[0, i],
                    self.sem.at[1, i],
                    at.flip(),
                ).start()

            each(0, at.S // 2, one)

        each(0, at.F, far)

    def scatter(self):
        at = self.at

        def step(i):
            z_to = at.zs(i)
            await_bytes(self.got.at[0], self.sem.at[1, i])
            await_bytes(self.got.at[0], self.sem.at[2, i])

            def one(k):
                total = self.stage[z_to, k].astype(F32) + self.got[z_to, k].astype(F32)
                self.stage[z_to, k] = total.astype(BF)

            each(0, at.S // 2, one)

        each(0, at.F, step)
        self.along.start()

    def relay(self):
        self.along.relay()

    def near(self):
        at = self.at
        self.summed[...] = self.along.total()

        def one(k):
            s_to = 2 * k + at.y

            @pl.when(s_to == at.s)
            def _():
                self.done[at.s] = self.summed[k]

            @pl.when(s_to != at.s)
            def _():
                remote(
                    self.summed.at[k],
                    self.done.at[at.s],
                    self.sem.at[3, 0],
                    self.sem.at[3, 1],
                    {"seq": s_to},
                ).start()

        each(0, at.S // 2, one)

    def total(self):
        at = self.at

        @pl.when(at.mine)
        def _():
            await_bytes(self.done.at[pl.ds(0, at.S - 1)], self.sem.at[3, 1])
            remote(
                self.done, self.done, self.sem.at[4, 0], self.sem.at[4, 1], at.flip()
            ).start()

    def finish(self):
        at = self.at
        each(0, at.F, lambda i: await_bytes(self.got.at[0], self.sem.at[0, i]))

        @pl.when(at.mine)
        def _():
            if at.S > 2:
                await_bytes(self.done.at[pl.ds(0, at.S // 2 - 1)], self.sem.at[3, 0])
            await_bytes(self.done, self.sem.at[4, 0])

        @pl.when(jnp.logical_not(at.mine))
        def _():
            await_bytes(self.summed, self.sem.at[3, 0])
            await_bytes(self.done, self.sem.at[4, 1])


class Tail:
    def __init__(self, at, mod_all, sums, first_in, mod_src, small_src, small_in, cond_src, cond_in, pieces, sem):
        self.at, self.sums, self.first_in = at, sums, first_in
        self.mod_src, self.mod_all = mod_src, mod_all
        self.small_src, self.small_in = small_src, small_in
        self.cond_src, self.cond_in, self.pieces, self.sem = cond_src, cond_in, pieces, sem

    @staticmethod
    def scratch(sizes, D, hidden, rows):
        R, F, S = sizes
        G = F * S
        C = D // S
        pack = 2 * D // G + 2 * rows + hidden // F
        wide = max(D, hidden, 3 * C)
        return [
            pltpu.VMEM((10, wide), F32),
            pltpu.VMEM((S, 10, wide), F32),
            pltpu.VMEM((6, D), BF),
            pltpu.VMEM((F, 1, pack), F32),
            pltpu.VMEM((R * F, 1, pack), F32),
            pltpu.VMEM((R * F, 1, rows), F32),
            pltpu.VMEM((G, 1, rows), F32),
            pltpu.VMEM((G, 1, pack), F32),
            DMA((8, max(S, 2 * F, G))),
        ]

    def first_copy(self, j):
        at = self.at
        return remote(
            self.sums, self.first_in.at[at.s], self.sem.at[0, j], self.sem.at[1, j], {"seq": at.ss(j)}
        )

    def start(self, mod_sums, b_one, b_two, b_out, b_qkv):
        sums = self.sums
        D = mod_sums.shape[1]
        hidden = b_one.shape[1]
        sums[...] = jnp.zeros_like(sums)
        sums[0:6, 0:D] = mod_sums[...]
        sums[6:7, 0:hidden] = b_one[...]
        sums[7:8, 0:D] = b_two[...]
        sums[8:9, 0:D] = b_out[...]
        sums[9:10, 0 : b_qkv.shape[1]] = b_qkv[...]
        each(1, self.at.S, lambda j: self.first_copy(j).start())
        self.first_in[self.at.s] = sums[...]

    def wide_copies(self, i):
        at = self.at
        slot = at.y * at.F + at.z
        device = {"rep": lax.rem(at.y + i // at.F, 2), "fsdp": at.zs(i)}
        return (
            remote(self.mod_src, self.mod_all.at[slot], self.sem.at[2, i], self.sem.at[3, i], device),
            remote(
                self.small_src.at[at.zs(i)],
                self.small_in.at[slot],
                self.sem.at[4, i],
                self.sem.at[5, i],
                device,
            ),
        )

    def middle(self, D, hidden, rows):
        at = self.at
        F, S, G = at.F, at.S, at.G
        C = D // S
        qv = 2 * D // G
        each(1, S, lambda j: self.first_copy(j).wait())
        total = self.first_in[0]
        for t in range(1, S):
            total = total + self.first_in[t]
        self.mod_src[...] = total[0:6, 0:D].astype(BF)
        for g in range(G):
            g_half = g % (G // 2)
            t = g_half // (F // 2)
            col = (g_half % (F // 2)) * qv + (2 * C if g >= G // 2 else 0)
            self.pieces[g, :, 0:qv] = self.first_in[t, 9:10, col : col + qv]
            self.pieces[g, :, qv : qv + rows] = total[8:9, g * rows : (g + 1) * rows]
            self.pieces[g, :, qv + rows : qv + 2 * rows] = total[7:8, g * rows : (g + 1) * rows]
        block = hidden // F
        for f in range(F):
            self.small_src[f, :, 0 : qv + 2 * rows] = self.pieces[f * S + at.s][:, 0 : qv + 2 * rows]
            self.small_src[f, :, qv + 2 * rows :] = self.sums[6:7, f * block : (f + 1) * block]

        def send(i):
            first, second = self.wide_copies(i)
            first.start()
            second.start()

        each(1, 2 * F, send)
        slot = at.y * F + at.z
        self.mod_all[slot] = self.mod_src[...]
        self.small_in[slot] = self.small_src[at.z]

    def cond_copy(self, i):
        at = self.at
        to = lax.rem(at.me + i, at.G)
        return remote(
            self.cond_src.at[at.y * at.F + to // at.S],
            self.cond_in.at[at.me],
            self.sem.at[6, i],
            self.sem.at[7, i],
            {"fsdp": to // at.S, "seq": lax.rem(to, at.S)},
        )

    def owners(self, w_ada, small_out):
        at = self.at
        F, G = at.F, at.G
        D = self.mod_src.shape[1]

        def arrive(i):
            first, second = self.wide_copies(i)
            first.wait()
            second.wait()

        each(1, 2 * F, arrive)
        cond = None
        for v in range(6):
            rows = self.mod_all[:, v, :]
            part = mm_nt(rows, w_ada[:, v * D : (v + 1) * D])
            cond = part if cond is None else cond + part
        for i in range(2 * F):
            self.cond_src[i] = cond[i : i + 1, :]
        each(1, G, lambda i: self.cond_copy(i).start())
        self.cond_in[at.me] = self.cond_src[at.y * F + at.z]
        total = self.small_in[0]
        for i in range(1, 2 * F):
            total = total + self.small_in[i]
        small_out[...] = total

    def finish(self, cond, grad_cond):
        at = self.at
        rows = self.cond_in.shape[2]
        each(1, at.G, lambda i: self.cond_copy(i).wait())
        for g in range(at.G):
            cols = slice(g * rows, (g + 1) * rows)
            value = cond[:, cols].astype(F32)
            gate = jax.nn.sigmoid(value)
            grad_cond[:, cols] = self.cond_in[g] * gate * (1.0 + value * (1.0 - gate))


def backward_kernel(sizes, *refs):
    at = Place(sizes)
    R, F, S, G = at.R, at.F, at.S, at.G
    grad_heads, heads, two_g, two_part, out_g, w_qkv, mixed_all, latents, grad_resid, w_ada = refs[-10:]
    log_sums, mod, sums_in, b_one, b_two, b_out, cond, one_g = refs[:8]
    given = refs[8:18]
    refs = refs[:7] + refs[8:]
    targets = refs[17:24]
    o_small, o_cond = refs[24:26]
    refs = refs[:16] + refs[17:]
    grad_in, key_flip, key_grad, val_grad, grad_proj, qkv_wide, qkv_g, mod_sums, b_qkv, in_sem = refs[25:35]
    rest = list(refs[35:])
    mix_sum = SeqSum(at, *rest[0:4])
    mix_src = rest[0]
    load_sem, swap_sem, save_sem = rest[35:38]
    kept = rest[38:45]
    grad_latents, o_qkv, o_one, o_two, o_part, o_out, o_mod = kept
    held = rest[45:55]
    qkv = ColumnScatter(at, qkv_g, *rest[4:10], o_qkv, rest[10])
    one = ColumnScatter(at, one_g, *rest[11:17], o_one, rest[17])
    two = RowOwner(at, lambda z: two_g.at[z], rest[18], rest[19], rest[20])
    out = FullScatter(at, out_g, *rest[21:25], o_out, rest[25])
    tail = Tail(at, o_mod, *rest[26:35])
    two_swap = Swap(at, o_two, swap_sem.at[0])
    part_swap = Swap(at, o_part, swap_sem.at[1])
    saves = Moves(save_sem, *zip(kept, targets))
    loads = Moves(load_sem, *zip(given, held))
    loads.start()
    _, L, C = grad_heads.shape
    rows_own, D = o_out.shape[1:]
    hidden = one_g.shape[2]
    local_heads = H // S
    size = D // H
    greet(G, lambda i: {"fsdp": lax.rem(at.me + i, G) // S, "seq": lax.rem(at.me + i, S)})
    greet(2 * F, lambda i: {"rep": lax.rem(at.y + i // F, 2), "fsdp": at.zs(i)})
    loads.wait(0, 2, 3, 4)
    o_part[at.y] = two_part[...]
    greet_wait(G - 1 + 2 * F - 1)

    def in_copy(j):
        return remote(
            grad_heads.at[at.peer(j)],
            grad_in.at[at.s],
            in_sem.at[0, j],
            in_sem.at[1, j],
            {"seq": at.peer(j)},
        )

    each(1, S, lambda j: in_copy(j).start())
    one.start()
    two.start()
    out.start()
    grad_in[at.s] = grad_heads[at.s]
    key_grad[...] = jnp.zeros_like(key_grad)
    val_grad[...] = jnp.zeros_like(val_grad)
    loads.wait(1)
    for h in range(local_heads):
        key_flip[h] = heads[local_heads + h].T
    factor = size ** (-0.5) * log2e
    score_scale = size ** (-0.5)
    pad = jnp.zeros((L, LANES - size), BF)

    def block(j):
        t = at.peer(j)

        @pl.when(j > 0)
        def _():
            in_copy(j).wait()

        rows = pl.ds(pl.multiple_of(t * L, L), L)
        for h in range(local_heads):
            query = heads[h, rows, :]
            grad = jnp.concatenate([grad_in[t, :, h * size : (h + 1) * size], pad], axis=1)
            scores = mm_nt(heads[local_heads + h], query) * factor
            probs = jnp.exp2(scores - log_sums[h, t])
            grad_probs = mm_nt(heads[2 * local_heads + h], grad)
            inner = jnp.sum(probs * grad_probs, axis=0, keepdims=True)
            grad_scores = (probs * (grad_probs - inner)).astype(BF)
            query_grad = mm(key_flip[h], grad_scores) * score_scale
            grad_proj[t, :, h * size : (h + 1) * size] = query_grad.T[:, :size].astype(BF)
            key_grad[h] += mm(grad_scores, query)
            val_grad[h] += mm(probs.astype(BF), grad)

        pl.when(j == 0)(out.cross)

    each(0, S, block)
    two.relay()
    for h in range(local_heads):
        low = (key_grad[h] * score_scale)[:, :size].astype(BF)
        grad_proj[:, :, C + h * size : C + (h + 1) * size] = low.reshape(S, L, size)
        low = val_grad[h][:, :size].astype(BF)
        grad_proj[:, :, 2 * C + h * size : 2 * C + (h + 1) * size] = low.reshape(S, L, size)

    loads.wait(5, 6)

    def spread(index):
        t = at.peer(arrival(index))
        mix_src[t] = mm_nt(grad_proj[t], w_qkv[...]).astype(BF)
        mix_sum.send(index)

    grads = grad_proj[...].reshape(S * L, 3 * C)
    qkv_wide[...] = mm_tn(mixed_all[...].reshape(S * L, D), grads)
    for g in range(G):
        qkv_g[g] = qkv_wide[g * rows_own : (g + 1) * rows_own, :].astype(BF)
    qkv.start()
    out.scatter()
    each(0, S, lambda index: spread(lax.rem(index + 2, S)))
    one.scatter()
    b_qkv[...] = jnp.sum(grads.astype(F32), axis=0, keepdims=True)
    mix_sum.wait()
    loads.wait(7, 8, 9)
    step = min(32, L)
    mod_sums[...] = sums_in[...]
    scale = mod[1:2, :]

    def back(i):
        rows = pl.ds(pl.multiple_of(i * step, step), step)
        grad_mixed = mix_sum.total(rows)
        normed, inv_std = norm_stats(latents[rows, :].astype(F32))
        grad_latents[rows, :] = grad_resid[rows, :] + norm_back(
            grad_mixed * (1.0 + scale), normed, inv_std
        )
        mod_sums[0:1, :] += jnp.sum(grad_mixed, axis=0, keepdims=True)
        mod_sums[1:2, :] += jnp.sum(grad_mixed * normed, axis=0, keepdims=True)

    each(0, L // step, back)
    saves.start(0)
    tail.start(mod_sums, b_one, b_two, b_out, b_qkv)
    one.relay()
    tail.middle(D, hidden, rows_own)
    qkv.scatter()
    o_two[at.y] = two.total()
    two_swap.start()
    part_swap.start()
    out.total()
    one.near()
    qkv.relay()
    tail.owners(w_ada, o_small)
    saves.start(6)
    one.total()
    qkv.near()
    tail.finish(cond, o_cond)
    qkv.total()
    two_swap.finish()
    part_swap.finish()
    saves.start(3, 4)
    out.finish()
    saves.start(5)
    one.finish()
    saves.start(2)
    qkv.finish()
    saves.start(1)
    saves.wait()


def backward(sizes, *args):
    R, F, S = sizes
    G = F * S
    one_g, grad_heads, two_g = args[7], args[8], args[10]
    two_part, latents, w_ada = args[11], args[15], args[17]
    _, L, C = grad_heads.shape
    D = latents.shape[1]
    T = S * L
    local_heads = H // S
    rows = w_ada.shape[0]
    hidden = one_g.shape[2]
    pack = 2 * D // G + 2 * rows + hidden // F
    shape = jax.ShapeDtypeStruct
    kept = (
        ((L, D), F32),
        ((S, rows, 3 * C), BF),
        ((S, rows, hidden), BF),
        ((2,) + two_g.shape[1:], BF),
        ((2,) + two_part.shape, BF),
        ((2, rows, D), BF),
        ((R * F, 6, D), BF),
    )
    return pl.pallas_call(
        lambda *refs: backward_kernel(sizes, *refs),
        name="backward",
        out_shape=tuple(shape(*item) for item in kept)
        + (
            shape((1, pack), F32),
            shape((1, D), F32),
        ),
        in_specs=[VM] * 7 + [HB] * 11,
        out_specs=(HB,) * 7 + (VM,) * 2,
        scratch_shapes=[
            pltpu.VMEM((S, L, C), BF),
            pltpu.VMEM((local_heads, LANES, T), BF),
            pltpu.VMEM((local_heads, T, LANES), F32),
            pltpu.VMEM((local_heads, T, LANES), F32),
            pltpu.VMEM((S, L, 3 * C), BF),
            pltpu.VMEM((D, 3 * C), F32),
            pltpu.VMEM((G, rows, 3 * C), BF),
            pltpu.VMEM((6, D), F32),
            pltpu.VMEM((1, 3 * C), F32),
            DMA((2, S)),
        ]
        + SeqSum.scratch(S, L, D)
        + ColumnScatter.scratch(sizes, rows, 3 * C)
        + ColumnScatter.scratch(sizes, rows, hidden)
        + RowOwner.scratch(F, two_g.shape[1:])
        + FullScatter.scratch(sizes, rows, D)
        + Tail.scratch(sizes, D, hidden, rows)
        + [DMA((10,)), DMA((2, 2)), DMA((7,))]
        + [pltpu.VMEM(*item) for item in kept]
        + [pltpu.VMEM(x.shape, x.dtype) for x in args[8:]],
        compiler_params=params(4, 60),
    )(*args)


def assemble_kernel(sizes, *refs):
    R, F, S = sizes
    G = F * S
    n = 11
    given, results = refs[:n], refs[n : n + 13]
    qkv, one, two, part, out, mod_all, silu_all, small = refs[n + 13 : n + 21]
    o_qkv, o_one, o_two, o_out, o_ada, b_ada, b_qv, b_out, b_one, b_two = refs[n + 21 : n + 31]
    flat, pieces, load_sem, save_sem, *passing = refs[n + 31 :]
    held = (qkv, one, two, part, out, mod_all, silu_all, small, *passing)
    loads = Moves(load_sem, *zip(given, held))
    loads.start()
    passed = tuple(zip(passing, results[:3]))
    made = (o_ada, b_ada, o_qkv, b_qv, o_out, b_out, o_one, b_one, o_two, b_two)
    saves = Moves(save_sem, *passed, *zip(made, results[3:]))
    rows, D = o_out.shape
    C = D // S
    hidden = one.shape[2]
    block = hidden // F
    loads.wait(5, 6)
    silu = silu_all[:, 0, :].astype(BF)
    width = b_ada.shape[0]
    for v in range(6):
        grads = mod_all[:, v, :]
        o_ada[:, v * D : (v + 1) * D] = mm_tn(silu, grads)
        flat[:, v * D : (v + 1) * D] = jnp.sum(grads.astype(F32), axis=0, keepdims=True)
    saves.start(3)
    for g in range(G):
        pieces[g] = flat[:, g * width : (g + 1) * width]
    b_ada[...] = pieces[lax.axis_index("fsdp") * S + lax.axis_index("seq")].reshape(width)
    loads.wait(7)
    first = 0
    for bias in (b_qv, b_out, b_two, b_one):
        length = bias.shape[0]
        bias[...] = small[:, first : first + length].reshape(length)
        first = first + length
    saves.start(4, 6, 8, 10, 12)
    loads.wait(1)
    for t in range(S):
        for f in range(F):
            col = (f * S + t) * block
            o_one[:, col : col + block] = one[t, :, f * block : (f + 1) * block].astype(F32)
    saves.start(9)
    loads.wait(2, 3)
    o_two[0:2] = part[0].astype(F32) + part[1].astype(F32)
    o_two[2:4] = two[...].astype(F32)
    saves.start(11)
    loads.wait(0)
    for t in range(S):
        for j in range(3):
            o_qkv[:, j * D + t * C : j * D + (t + 1) * C] = qkv[t, :, j * C : (j + 1) * C].astype(F32)
    saves.start(5)
    loads.wait(4, 8, 9, 10)
    saves.start(0, 1, 2)
    o_out[...] = out[0].astype(F32) + out[1].astype(F32)
    saves.start(7)
    saves.wait()


def assemble(sizes, qkv, one, two, part, out, mod_all, silu_all, small, *passed):
    R, F, S = sizes
    G = F * S
    rows, D = out.shape[1:]
    hidden = one.shape[2]
    made = (
        ((rows, 6 * D), F32),
        ((6 * D // G,), F32),
        ((rows, 3 * D), F32),
        ((2 * D // G,), F32),
        ((rows, D), F32),
        ((rows,), F32),
        ((rows, hidden * S), F32),
        ((hidden // F,), F32),
        ((4,) + two.shape[1:], F32),
        ((rows,), F32),
    )
    given = (qkv, one, two, part, out, mod_all, silu_all, small)
    scratch = [pltpu.VMEM(x.shape, x.dtype) for x in given]
    order = (2, 6, 8, 4, 0, 1, 3, 5, 7, 9)
    return pl.pallas_call(
        lambda *refs: assemble_kernel(sizes, *refs),
        name="assemble",
        out_shape=tuple(jax.ShapeDtypeStruct(x.shape, x.dtype) for x in passed)
        + tuple(jax.ShapeDtypeStruct(*item) for item in made),
        in_specs=[HB] * 11,
        out_specs=(HB,) * 13,
        scratch_shapes=scratch
        + [pltpu.VMEM(*made[i]) for i in order]
        + [
            pltpu.VMEM((1, 6 * D), F32),
            pltpu.VMEM((G, 1, 6 * D // G), F32),
            DMA((11,)),
            DMA((13,)),
        ]
        + [pltpu.VMEM(x.shape, x.dtype) for x in passed],
        compiler_params=pltpu.CompilerParams(vmem_limit_bytes=60 * 1024 * 1024),
    )(*given, *passed)


def on_device(
    latents, cond, w_ada, b_ada, w_qkv, b_qv, w_out, b_out, w_one, b_one, w_two, b_two, cotangent
):
    sizes = R, F, S = tuple(lax.axis_size(name) for name in ("rep", "fsdp", "seq"))
    G = F * S
    _, L, D = latents.shape
    hidden = w_one.shape[1] // S
    rows = w_ada.shape[0]
    tokens = latents[0]
    two_rows = w_two.shape[0]
    (
        mixed_all,
        heads,
        merged,
        branch_one,
        mix_all,
        grad_all,
        full_qkv,
        full_out,
        log_sums,
        mod,
        silu_all,
        bias_one,
        bias_two,
        g_one,
        g_two,
    ) = forward(
        sizes,
        cond,
        b_ada,
        b_qv,
        b_out,
        b_two,
        b_one,
        tokens,
        cotangent[0],
        w_ada,
        w_qkv,
        w_one,
        w_two.reshape(2, two_rows // 2, D),
        w_out,
    )
    full_one = g_one.reshape(D, hidden)
    full_two = g_two.reshape(hidden, D)
    (
        block_out,
        grad_resid,
        grad_heads,
        one_g,
        two_g,
        two_part,
        out_g,
        grad_b_one,
        grad_b_two,
        grad_b_out,
        mod_sums,
    ) = mlp(
        sizes,
        mod,
        bias_one,
        bias_two,
        full_one,
        mix_all,
        full_two,
        grad_all,
        tokens,
        branch_one,
        cotangent[0],
        full_out,
        merged,
    )
    grad_latents, qkv_sum, one_sum, two_sum, part_sum, out_sum, mod_all, o_small, o_cond = backward(
        sizes,
        log_sums,
        mod,
        mod_sums,
        grad_b_one,
        grad_b_two,
        grad_b_out,
        cond,
        one_g.reshape(G, rows, hidden),
        grad_heads,
        heads,
        two_g,
        two_part,
        out_g,
        full_qkv,
        mixed_all,
        tokens,
        grad_resid,
        w_ada,
    )
    outs = assemble(
        sizes,
        qkv_sum,
        one_sum,
        two_sum,
        part_sum,
        out_sum,
        mod_all,
        silu_all,
        o_small,
        block_out,
        grad_latents,
        o_cond,
    )
    shapes = (latents.shape, latents.shape, cond.shape, w_ada.shape, b_ada.shape, w_qkv.shape, b_qv.shape)
    shapes += (w_out.shape, b_out.shape, w_one.shape, b_one.shape, w_two.shape, b_two.shape)
    return tuple(out.reshape(want) for out, want in zip(outs, shapes))


def solution(mesh):
    owned = P(("fsdp", "seq"), None)
    owned_bias = P(("fsdp", "seq"))
    token_spec = P(("rep", "fsdp"), "seq", None)
    cond_spec = P(("rep", "fsdp"), None)
    weights = (owned, owned_bias) * 5
    in_specs = (token_spec, cond_spec) + weights + (token_spec,)
    out_specs = (token_spec, token_spec, cond_spec) + weights
    return jax.shard_map(
        on_device, mesh=mesh, in_specs=in_specs, out_specs=out_specs, check_vma=False
    )
```

```python
import math

import jax
import jax.numpy as jnp
from jax import lax
from jax.experimental import pallas as pl
from jax.experimental.pallas import tpu as pltpu
from jax.sharding import PartitionSpec as P

H = 16
epsilon = 1e-06
gelu_coef = math.sqrt(2.0 / math.pi)
log2e = math.log2(math.e)
BF = jnp.bfloat16
F32 = jnp.float32
LANES = 128
VM = pl.BlockSpec(memory_space=pltpu.VMEM)
HB = pl.BlockSpec(memory_space=pl.ANY)
DMA = pltpu.SemaphoreType.DMA


def params(ident, mib):
    return pltpu.CompilerParams(
        collective_id=ident, has_side_effects=True, vmem_limit_bytes=mib * 1024 * 1024
    )


def remote(src, dst, send, recv, device):
    return pltpu.make_async_remote_copy(
        src_ref=src,
        dst_ref=dst,
        send_sem=send,
        recv_sem=recv,
        device_id=device,
        device_id_type=pl.DeviceIdType.MESH,
    )


def local(src, dst, sem):
    return pltpu.make_async_copy(src, dst, sem)


def await_bytes(like, sem):
    pltpu.make_async_copy(like, like, sem).wait()


class Moves:
    def __init__(self, sem, *pairs):
        self.copies = [local(pair[0], pair[1], sem.at[i]) for i, pair in enumerate(pairs)]

    def start(self, *which):
        for i in which or range(len(self.copies)):
            self.copies[i].start()

    def wait(self, *which):
        for i in which or range(len(self.copies)):
            self.copies[i].wait()


def each(start, stop, body):
    def step(index, carry):
        body(index)
        return carry

    lax.fori_loop(start, stop, step, 0)


def greet(count, device_of):
    gate = pltpu.get_barrier_semaphore()
    each(
        1,
        count,
        lambda i: pl.semaphore_signal(
            gate, 1, device_id=device_of(i), device_id_type=pl.DeviceIdType.MESH
        ),
    )
    return count - 1


def greet_wait(count):
    pl.semaphore_wait(pltpu.get_barrier_semaphore(), count)


def norm_stats(values):
    center = values - jnp.mean(values, axis=-1, keepdims=True)
    inv_std = lax.rsqrt(jnp.mean(center * center, axis=-1, keepdims=True) + epsilon)
    return (center * inv_std, inv_std)


def norm_back(grad, normed, inv_std):
    return inv_std * (
        grad
        - jnp.mean(grad, axis=-1, keepdims=True)
        - normed * jnp.mean(grad * normed, axis=-1, keepdims=True)
    )


def mm(left, right):
    return jnp.dot(left, right, preferred_element_type=F32)


def mm_nt(left, right):
    return lax.dot_general(left, right, (((1,), (1,)), ((), ())), preferred_element_type=F32)


def mm_tn(left, right):
    return lax.dot_general(left, right, (((0,), (0,)), ((), ())), preferred_element_type=F32)


class Place:
    def __init__(self, sizes):
        self.R, self.F, self.S = sizes
        self.G = self.F * self.S
        self.y = lax.axis_index("rep")
        self.z = lax.axis_index("fsdp")
        self.s = lax.axis_index("seq")
        self.me = self.z * self.S + self.s
        self.mine = lax.rem(self.s, 2) == self.y
        self.steps = (2, 1, 3) if self.F == 4 else tuple(range(1, self.F))

    def zs(self, i):
        return lax.rem(self.z + i, self.F)

    def zs_back(self, i):
        return lax.rem(self.z - i + self.F, self.F)

    def ss(self, i):
        return lax.rem(self.s + i, self.S)

    def ss_back(self, i):
        return lax.rem(self.s - i + self.S, self.S)

    def flip(self):
        return {"rep": 1 - self.y}

    def peer(self, j):
        return lax.bitwise_xor(self.s, j)


class SeqGather:
    def __init__(self, at, dst, sem):
        self.at, self.dst, self.sem = at, dst, sem

    @staticmethod
    def scratch(S):
        return DMA((4, S))

    def direct(self, j):
        at, block = self.at, self.dst.at[self.at.s]
        return remote(block, block, self.sem.at[0, j], self.sem.at[1, j], {"seq": at.peer(j)})

    def handed(self, j):
        at = self.at
        block = self.dst.at[at.peer(j)]
        return remote(block, block, self.sem.at[2, j], self.sem.at[3, j], {"seq": at.peer(1)})

    def start(self):
        for j in range(3, self.at.S, 2):
            self.direct(j).start()
        self.direct(1).start()

    def arrive(self, index):
        @pl.when(index == 1)
        def _():
            self.direct(1).wait()

        if self.at.S > 2:

            @pl.when((index >= 2) & (lax.rem(index, 2) == 0))
            def _():
                self.direct(index + 1).wait()
                self.handed(index + 1).start()

            @pl.when((index >= 2) & (lax.rem(index, 2) == 1))
            def _():
                self.handed(index).wait()


def arrival(index):
    return jnp.where(index < 2, index, lax.bitwise_xor(index, 1))


class SeqSum:
    def __init__(self, at, src, near, inn, sem):
        self.at, self.src, self.near, self.inn, self.sem = at, src, near, inn, sem

    @staticmethod
    def scratch(S, rows, cols):
        return [
            pltpu.VMEM((S, rows, cols), BF),
            pltpu.VMEM((S // 2, rows, cols), BF),
            pltpu.VMEM((S // 2, rows, cols), BF),
            DMA((4, S)),
        ]

    def sibling(self, j):
        at = self.at
        return remote(
            self.src.at[at.peer(j)],
            self.near.at[j // 2],
            self.sem.at[0, j],
            self.sem.at[1, j],
            {"seq": at.peer(1)},
        )

    def direct(self, j):
        at = self.at
        return remote(
            self.src.at[at.peer(j)],
            self.inn.at[j // 2],
            self.sem.at[2, j],
            self.sem.at[3, j],
            {"seq": at.peer(j)},
        )

    def send(self, index):
        @pl.when((index == 1) | ((index >= 2) & (lax.rem(index, 2) == 0)))
        def _():
            self.sibling(lax.bitwise_or(index, 1)).start()

        if self.at.S > 2:

            @pl.when((index >= 2) & (lax.rem(index, 2) == 1))
            def _():
                j = index - 1
                self.sibling(index).wait()
                t = self.at.peer(j)
                step = min(64, self.src.shape[1])

                def add(i):
                    rows = pl.ds(pl.multiple_of(i * step, step), step)
                    both = self.src[t, rows, :].astype(F32) + self.near[j // 2, rows, :].astype(F32)
                    self.src[t, rows, :] = both.astype(BF)

                each(0, self.src.shape[1] // step, add)
                self.direct(j).start()

    def wait(self):
        self.sibling(1).wait()
        for j in range(2, self.at.S, 2):
            self.direct(j).wait()

    def total(self, rows):
        value = self.src[self.at.s, rows, :].astype(F32) + self.near[0, rows, :].astype(F32)
        for k in range(1, self.at.S // 2):
            value = value + self.inn[k, rows, :].astype(F32)
        return value


class FarGather:
    relayed = True

    def __init__(self, at, dst, sem):
        self.at, self.dst, self.sem = at, dst, sem
        self.line = self.relayed and at.F == 4

    @staticmethod
    def scratch(F):
        return DMA((7, F))

    def send(self, z_from, z_to, kind):
        pieces = self.half(z_from)
        held = self.origin() if kind == 0 else pieces
        for source, piece in zip(held, pieces):
            remote(
                source, piece, self.sem.at[kind, z_to], self.sem.at[2, z_from], {"fsdp": z_to}
            ).start()

    def origin(self):
        return self.half(self.at.z)

    def await_half(self, row, z):
        await_bytes(self.like(), self.sem.at[row, z])

    def around(self, step, body):
        at = self.at

        @pl.when(at.z >= step)
        def _():
            body(at.z - step)

        @pl.when(at.z + step < at.F)
        def _():
            body(at.z + step)

    def direct(self, step, body):
        if self.line and step == 3:
            return
        self.around(step, body)

    def start_far(self):
        for step in self.at.steps:
            self.direct(step, lambda z_to: self.send(self.at.z, z_to, 0))

    def service(self, step):
        at = self.at

        def take(z_from):
            self.await_half(2, z_from)
            for piece in self.half(z_from):
                remote(
                    piece, piece, self.sem.at[3, z_from], self.sem.at[4, z_from], at.flip()
                ).start()

        self.around(step, take)
        if self.line and step == 2:

            @pl.when((at.z == 1) | (at.z == 2))
            def _():
                far = jnp.where(at.z == 1, 3, 0)
                end = 3 - far
                self.send(far, end, 1)

    def finish_far(self):
        at = self.at

        def swapped(z_from):
            self.await_half(3, z_from)
            self.await_half(4, z_from)

        for step in range(1, at.F):
            self.around(step, swapped)
            self.direct(step, lambda z_to: self.await_half(0, z_to))
        if self.line:

            @pl.when((at.z == 1) | (at.z == 2))
            def _():
                self.await_half(1, jnp.where(at.z == 1, 0, 3))


class ColumnGather(FarGather):
    def __init__(self, at, src, dst, sem):
        super().__init__(at, dst, sem)
        self.src = src

    def half(self, z):
        at = self.at
        return [self.dst.at[z * at.S + 2 * k + at.y] for k in range(at.S // 2)]

    def like(self):
        return self.dst.at[pl.ds(0, self.at.S // 2)]

    def start(self):
        at, src, dst, sem = self.at, self.src, self.dst, self.sem

        def near(j):
            t = at.ss(j)
            remote(src.at[t], dst.at[at.me], sem.at[5, 0], sem.at[6, 0], {"seq": t}).start()

        each(1, at.S, near)
        local(src.at[at.s], dst.at[at.me], sem.at[5, 1]).start()

    def near_done(self):
        at, dst, sem = self.at, self.dst, self.sem
        local(self.src.at[at.s], dst.at[at.me], sem.at[5, 1]).wait()
        near = dst.at[pl.ds(0, at.S - 1)]
        await_bytes(near, sem.at[5, 0])
        await_bytes(near, sem.at[6, 0])


class RowGather(FarGather):
    def __init__(self, at, src, dst, sem):
        super().__init__(at, dst, sem)
        self.src = src

    def half(self, z):
        return [self.dst.at[z, self.at.y]]

    def origin(self):
        return [self.src.at[self.at.y]]

    def like(self):
        return self.dst.at[0, 0]

    def start(self):
        at = self.at
        local(self.src, self.dst.at[at.z], self.sem.at[5, 0]).start()

    def near_done(self):
        at = self.at
        local(self.src, self.dst.at[at.z], self.sem.at[5, 0]).wait()


class OwnGather(FarGather):
    relayed = False

    def __init__(self, at, src, dst, sem):
        super().__init__(at, dst, sem)
        self.src = src

    def half(self, z):
        return [self.dst.at[self.at.s, z]]

    def origin(self):
        return [self.src]

    def like(self):
        return self.src

    def start(self):
        at = self.at
        local(self.src, self.dst.at[at.s, at.z], self.sem.at[5, 0]).start()

    def near_done(self):
        at = self.at
        local(self.src, self.dst.at[at.s, at.z], self.sem.at[5, 0]).wait()

    def start_far(self):
        pl.when(self.at.mine)(super().start_far)

    def service(self, step):
        take = super().service
        pl.when(self.at.mine)(lambda: take(step))

    def finish_far(self):
        at = self.at

        def sent(z_from):
            self.await_half(3, z_from)

        def swapped(z_from):
            self.await_half(4, z_from)

        @pl.when(at.mine)
        def _():
            for step in range(1, at.F):
                self.around(step, sent)
                self.direct(step, lambda z_to: self.await_half(0, z_to))
            if self.line:

                @pl.when((at.z == 1) | (at.z == 2))
                def _():
                    self.await_half(1, jnp.where(at.z == 1, 0, 3))

        @pl.when(jnp.logical_not(at.mine))
        def _():
            for step in range(1, at.F):
                self.around(step, swapped)


def forward_kernel(sizes, *refs):
    at = Place(sizes)
    R, F, S, G = at.R, at.F, at.S, at.G
    cond = refs[0]
    i_biases = refs[1:6]
    i_latents, i_cotangent, i_ada, i_qkv, i_one, w_two, w_out = refs[6:13]
    refs = refs[3:]
    o_mixed, o_heads, o_merged, o_branch, o_mix, o_grad, o_full_qkv, o_full_out = refs[10:18]
    log_sums, mod, silu_all, bias_one, bias_two, g_one, g_two = refs[18:25]
    silu_src, part, parts_in, mod_src, mod_in, qkv_src, one_src, pack_all = refs[25:33]
    g_qkv, g_out, wide, bias_qkv, bias_out, val_flip, att, merged_in = refs[33:41]
    silu_sem, part_sem, mod_sem, pack_sem, qkv_sem, one_sem, two_sem, out_sem = refs[41:49]
    mixed_sem, grad_sem, att_sem, mix_sem, spread_sem, load_sem, save_sem = refs[49:56]
    bias_pack, bias_pieces, bias_slot, bias_sem = refs[69:73]
    biases = refs[73:78]
    bias_loads = Moves(bias_sem, *zip(i_biases, biases))
    bias_loads.start()
    latents, cotangent, w_ada, w_qkv, w_one = refs[56:61]
    mixed_all, heads, merged, branch_one, mix_all, grad_all, full_qkv, full_out = refs[61:69]
    loads = Moves(
        load_sem,
        (i_qkv, w_qkv),
        (i_ada, w_ada),
        (i_one, w_one),
        (i_latents, latents),
        (i_cotangent, cotangent),
    )
    loads.start()
    saves = Moves(
        save_sem,
        (mixed_all, o_mixed),
        (heads, o_heads),
        (merged, o_merged),
        (branch_one, o_branch),
        (mix_all, o_mix),
        (grad_all, o_grad),
        (full_qkv, o_full_qkv),
        (full_out, o_full_out),
    )
    L, D = latents.shape
    C = D // S
    T = S * L
    local_heads = H // S
    size = D // H
    rows_own = silu_all.shape[2]
    hidden = one_src.shape[2]
    block = hidden // F
    greet(G, lambda i: {"fsdp": lax.rem(at.me + i, G) // S, "seq": lax.rem(at.me + i, S)})
    greet(2 * F, lambda i: {"rep": lax.rem(at.y + i // F, 2), "fsdp": at.zs(i)})
    width = bias_pieces.shape[2]
    bias_loads.wait()
    first = 0
    for bias in biases[1:]:
        length = bias.shape[0]
        bias_pack[:, first : first + length] = bias[...].astype(F32).reshape(1, length)
        first = first + length
    bias_pieces[...] = jnp.zeros_like(bias_pieces)
    bias_pieces[at.me] = biases[0][...].astype(F32).reshape(1, width)
    for g in range(G):
        bias_slot[:, g * width : (g + 1) * width] = bias_pieces[g]

    value = cond[...].astype(F32)
    silu = (value * jax.nn.sigmoid(value)).astype(BF).astype(F32)
    for g in range(G):
        silu_src[g] = silu[:, g * rows_own : (g + 1) * rows_own]
    loads.wait(0)
    for t in range(S):
        for j in range(3):
            qkv_src[t, :, j * C : (j + 1) * C] = w_qkv[:, j * D + t * C : j * D + (t + 1) * C]
    loads.wait(2)
    for t in range(S):
        for f in range(F):
            col = (f * S + t) * block
            one_src[t, :, f * block : (f + 1) * block] = w_one[:, col : col + block]
    greet_wait(G - 1 + 2 * F - 1)
    slot = at.y * F + at.z

    def cond_copy(i):
        z_to = at.zs(i)
        return remote(
            silu_src.at[z_to * S + at.s],
            silu_all.at[slot],
            silu_sem.at[0, i],
            silu_sem.at[1, i],
            {"rep": lax.rem(at.y + i // F, 2), "fsdp": z_to},
        )

    each(1, 2 * F, lambda i: cond_copy(i).start())
    silu_all[slot] = silu_src[at.me]

    def pack_copy(i):
        to = lax.rem(at.me + i, G)
        return remote(
            bias_pack,
            pack_all.at[at.me],
            pack_sem.at[0, 0],
            pack_sem.at[1, 0],
            {"fsdp": to // S, "seq": lax.rem(to, S)},
        )

    each(1, G, lambda i: pack_copy(i).start())
    pack_all[at.me] = bias_pack[...]

    qkv = ColumnGather(at, qkv_src, g_qkv, qkv_sem)
    one = ColumnGather(at, one_src, g_one, one_sem)
    two = RowGather(at, w_two, g_two, two_sem)
    out = OwnGather(at, w_out, g_out, out_sem)
    qkv.start()
    two.start()
    out.start()

    each(1, 2 * F, lambda i: cond_copy(i).wait())
    left = jnp.concatenate([silu_all[at.y * F + f] for f in range(F)], axis=0).astype(BF)
    loads.wait(1)
    sums = mm(left, w_ada[...]) + bias_slot[...]
    for f in range(F):
        for v in range(6):
            for t in range(S):
                col = v * D + t * C
                part[f * S + t, v : v + 1, :] = sums[f : f + 1, col : col + C]

    def part_copy(i):
        to = lax.rem(at.me + i, G)
        return remote(
            part.at[to],
            parts_in.at[at.me],
            part_sem.at[0, i],
            part_sem.at[1, i],
            {"fsdp": to // S, "seq": lax.rem(to, S)},
        )

    each(1, G, lambda i: part_copy(i).start())
    parts_in[at.me] = part[at.me]
    qkv.near_done()
    qkv.start_far()
    each(1, G, lambda i: part_copy(i).wait())
    total = parts_in[0]
    for g in range(1, G):
        total = total + parts_in[g]
    mod_src[...] = total

    def mod_copy(i):
        return remote(
            mod_src, mod_in.at[at.s], mod_sem.at[0, i], mod_sem.at[1, i], {"seq": at.ss(i)}
        )

    each(1, S, lambda i: mod_copy(i).start())
    one.start()
    mod_in[at.s] = total
    out.start_far()
    each(1, S, lambda i: mod_copy(i).wait())
    for t in range(S):
        mod[:, t * C : (t + 1) * C] = mod_in[t]

    loads.wait(3)
    step = min(64, L)

    def norm(i):
        at_rows = pl.ds(pl.multiple_of(i * step, step), step)
        normed, _ = norm_stats(latents[at_rows, :].astype(F32))
        mixed_all[at.s, at_rows, :] = (normed * (1.0 + mod[1:2, :]) + mod[0:1, :]).astype(BF)

    each(0, L // step, norm)
    gather = SeqGather(at, mixed_all, mixed_sem)
    gather.start()
    loads.wait(4)
    grad_all[at.s] = (mod[5:6, :] * cotangent[...].astype(F32)).astype(BF)
    grad_gather = SeqGather(at, grad_all, grad_sem)
    grad_gather.start()
    one.near_done()
    qkv.service(at.steps[0])
    one.start_far()
    out.near_done()
    two.near_done()

    others = pack_all.at[pl.ds(0, G - 1)]
    await_bytes(others, pack_sem.at[0, 0])
    await_bytes(others, pack_sem.at[1, 0])
    qv = 2 * D // G
    own = F // 2
    bias_qkv[...] = jnp.zeros_like(bias_qkv)
    for i in range(own):
        bias_qkv[:, i * qv : (i + 1) * qv] = pack_all[at.s * own + i][:, 0:qv]
        bias_qkv[:, 2 * C + i * qv : 2 * C + (i + 1) * qv] = pack_all[G // 2 + at.s * own + i][
            :, 0:qv
        ]
    for g in range(G):
        cols = slice(g * rows_own, (g + 1) * rows_own)
        bias_out[:, cols] = pack_all[g][:, qv : qv + rows_own]
        bias_two[:, cols] = pack_all[g][:, qv + rows_own : qv + 2 * rows_own]
    for f in range(F):
        bias_one[:, f * block : (f + 1) * block] = pack_all[f * S + at.s][:, qv + 2 * rows_own :]

    for i in at.steps[1:]:
        qkv.service(i)
    for i in at.steps:
        out.service(i)
    qkv.finish_far()

    def join(slabs, whole):
        cols = whole.shape[1]
        for g in range(G):
            wide[g * rows_own : (g + 1) * rows_own, 0:cols] = slabs(g).astype(F32)
        tall = 128 if D % 128 == 0 else D

        def cast(i):
            at_rows = pl.ds(pl.multiple_of(i * tall, tall), tall)
            whole[at_rows, :] = wide[at_rows, 0:cols].astype(BF)

        each(0, D // tall, cast)

    join(lambda g: g_qkv[g], full_qkv)
    saves.start(6)

    pad = jnp.zeros((L, LANES - size), BF)

    def project(index):
        gather.arrive(index)
        t = at.peer(arrival(index))
        at_rows = pl.ds(pl.multiple_of(t * L, L), L)
        done = (mm(mixed_all[t], full_qkv[...]) + bias_qkv[...]).astype(BF)
        for c in range(3 * local_heads):
            heads[c, at_rows, :] = jnp.concatenate(
                [done[:, c * size : (c + 1) * size], pad], axis=1
            )

    each(0, S, project)
    saves.start(0, 1)
    out.finish_far()
    spread = SeqGather(at, g_out, spread_sem)
    spread.start()
    each(1, S, grad_gather.arrive)
    saves.start(5)
    for h in range(local_heads):
        val_flip[h] = heads[2 * local_heads + h].T

    def att_copy(j):
        t = at.peer(j)
        return remote(
            att.at[t], merged_in.at[at.s], att_sem.at[0, j], att_sem.at[1, j], {"seq": t}
        )

    factor = size ** (-0.5) * log2e

    def attention(index):
        j = S - 1 - index
        t = at.peer(j)
        at_rows = pl.ds(pl.multiple_of(t * L, L), L)
        for h in range(local_heads):
            scores = mm_nt(heads[local_heads + h], heads[h, at_rows, :]) * factor
            highest = jnp.max(scores, axis=0, keepdims=True)
            raised = jnp.exp2(scores - highest)
            summed = jnp.sum(raised, axis=0, keepdims=True)
            result = mm(val_flip[h], raised.astype(BF)) / summed
            log_sums[h, t] = highest + jnp.log2(summed)
            att[t, :, h * size : (h + 1) * size] = result.T[:, :size].astype(BF)

        @pl.when(j > 0)
        def _():
            att_copy(j).start()

    one.service(at.steps[0])
    one.service(at.steps[1])
    two.start_far()
    each(0, S, attention)
    merged_in[at.s] = att[at.s]
    each(1, S, spread.arrive)
    join(lambda g: g_out[g % S, g // S], full_out)
    saves.start(7)
    each(1, S, lambda j: att_copy(j).wait())
    for t in range(S):
        merged[:, t * C : (t + 1) * C] = merged_in[t]
    saves.start(2)

    def project_out(i):
        at_rows = pl.ds(pl.multiple_of(i * step, step), step)
        branch = mm(merged[at_rows, :], full_out[...]) + bias_out[...]
        branch_one[at_rows, :] = branch
        residual = latents[at_rows, :].astype(F32) + mod[2:3, :] * branch
        normed, _ = norm_stats(residual)
        mix_all[at.s, at_rows, :] = (normed * (1.0 + mod[4:5, :]) + mod[3:4, :]).astype(BF)

    each(0, L // step, project_out)
    saves.start(3)
    mix_gather = SeqGather(at, mix_all, mix_sem)
    mix_gather.start()
    for i in at.steps[2:]:
        one.service(i)
    for i in at.steps:
        two.service(i)
    one.finish_far()
    each(1, S, mix_gather.arrive)
    saves.start(4)
    two.finish_far()
    saves.wait()


def forward(sizes, cond, *args):
    biases = args[:5]
    latents, cotangent, w_ada, w_qkv, w_one, w_two, w_out = args[5:]
    R, F, S = sizes
    G = F * S
    rows, D = w_out.shape
    L = latents.shape[0]
    T = S * L
    C = D // S
    local_heads = H // S
    hidden = w_one.shape[1] // S
    shape = jax.ShapeDtypeStruct
    width = 6 * D // G
    pack = sum(bias.shape[0] for bias in biases[1:])
    kept = (
        ((S, L, D), BF),
        ((3 * local_heads, T, LANES), BF),
        ((L, D), BF),
        ((L, D), F32),
        ((S, L, D), BF),
        ((S, L, D), BF),
        ((D, 3 * C), BF),
        ((D, D), BF),
    )
    return pl.pallas_call(
        lambda *refs: forward_kernel(sizes, *refs),
        name="forward",
        out_shape=tuple(shape(*item) for item in kept)
        + (
            shape((local_heads, S, 1, L), F32),
            shape((6, D), F32),
            shape((R * F, 1, rows), F32),
            shape((1, hidden), F32),
            shape((1, D), F32),
            shape((G, rows, hidden), BF),
            shape((F,) + w_two.shape, BF),
        ),
        in_specs=[VM] + [HB] * 12,
        out_specs=(HB,) * 8 + (VM,) * 5 + (HB,) * 2,
        scratch_shapes=[
            pltpu.VMEM((G, 1, rows), F32),
            pltpu.VMEM((G, 6, C), F32),
            pltpu.VMEM((G, 6, C), F32),
            pltpu.VMEM((6, C), F32),
            pltpu.VMEM((S, 6, C), F32),
            pltpu.VMEM((S, rows, 3 * C), BF),
            pltpu.VMEM((S, rows, hidden), BF),
            pltpu.VMEM((G, 1, pack), F32),
            pltpu.VMEM((G, rows, 3 * C), BF),
            pltpu.VMEM((S, F, rows, D), BF),
            pltpu.VMEM((D, max(D, 3 * C)), F32),
            pltpu.VMEM((1, 3 * C), F32),
            pltpu.VMEM((1, D), F32),
            pltpu.VMEM((local_heads, LANES, T), BF),
            pltpu.VMEM((S, L, C), BF),
            pltpu.VMEM((S, L, C), BF),
            DMA((2, 2 * F)),
            DMA((2, G)),
            DMA((2, S)),
            DMA((2, 1)),
            ColumnGather.scratch(F),
            ColumnGather.scratch(F),
            RowGather.scratch(F),
            OwnGather.scratch(F),
            SeqGather.scratch(S),
            SeqGather.scratch(S),
            DMA((2, S)),
            SeqGather.scratch(S),
            SeqGather.scratch(S),
            DMA((5,)),
            DMA((8,)),
        ]
        + [pltpu.VMEM(x.shape, x.dtype) for x in (latents, cotangent, w_ada, w_qkv, w_one)]
        + [pltpu.VMEM(*item) for item in kept]
        + [
            pltpu.VMEM((1, pack), F32),
            pltpu.VMEM((G, 1, width), F32),
            pltpu.VMEM((1, 6 * D), F32),
            DMA((5,)),
        ]
        + [pltpu.VMEM(bias.shape, BF) for bias in biases],
        compiler_params=params(1, 60),
    )(cond, *args)


class RowScatter:
    def __init__(self, at, src, got, stage, sem):
        self.at, self.src, self.got, self.stage, self.sem = at, src, got, stage, sem

    def start(self):
        at = self.at

        def far(i):
            z_to = at.zs(i)
            remote(
                self.src.at[z_to, 3 - at.y],
                self.got.at[z_to],
                self.sem.at[0, i],
                self.sem.at[1, i],
                at.flip(),
            ).start()

        each(0, at.F, far)

    def reduce(self):
        at = self.at

        def far(i):
            z_to = at.zs(i)
            await_bytes(self.got.at[0], self.sem.at[0, i])
            await_bytes(self.got.at[0], self.sem.at[1, i])
            total = self.src[z_to, 2 + at.y].astype(F32) + self.got[z_to].astype(F32)
            self.stage[z_to] = total.astype(BF)

        each(0, at.F, far)


class Line:
    def line_up(self):
        at = self.at
        self.line = at.F == 4
        self.inner = self.line & ((at.z == 1) | (at.z == 2))
        self.end = self.line & ((at.z == 0) | (at.z == 3))
        self.opposite = jnp.where(at.z < 2, 3, 0)
        self.beside = jnp.where(at.z == 0, 1, 2)


class RowOwner(Line):
    def __init__(self, at, piece, inn, far, sem):
        self.at, self.piece, self.inn, self.far, self.sem = at, piece, inn, far, sem
        self.line_up()

    @staticmethod
    def scratch(F, shape):
        return [pltpu.VMEM((F,) + shape, BF), pltpu.VMEM(shape, BF), DMA((3, F))]

    def out_copy(self, z_to):
        at = self.at
        return remote(
            self.piece(z_to),
            self.inn.at[at.z],
            self.sem.at[0, z_to],
            self.sem.at[1, at.z],
            {"fsdp": z_to},
        )

    def far_copy(self):
        return remote(
            self.piece(self.opposite),
            self.far,
            self.sem.at[0, self.opposite],
            self.sem.at[2, 0],
            {"fsdp": self.beside},
        )

    def start(self):
        at = self.at

        @pl.when(self.end)
        def _():
            self.far_copy().start()
            self.inn[self.opposite] = jnp.zeros_like(self.far)

        def one(i):
            z_to = at.zs(i)

            @pl.when(jnp.logical_not(self.line & (z_to == self.opposite)))
            def _():
                self.out_copy(z_to).start()

        each(1, at.F, one)
        self.inn[at.z] = self.piece(at.z)[...]

    def relay(self):
        @pl.when(self.inner)
        def _():
            await_bytes(self.far, self.sem.at[2, 0])
            z_to = self.opposite
            piece = self.piece(z_to)
            piece[...] = (piece[...].astype(F32) + self.far[...].astype(F32)).astype(BF)
            self.out_copy(z_to).start()

    def total(self):
        at = self.at

        def arrived(i):
            z = at.zs(i)
            await_bytes(self.far, self.sem.at[0, z])

            @pl.when(jnp.logical_not(self.end & (z == self.opposite)))
            def _():
                await_bytes(self.far, self.sem.at[1, z])

        each(1, at.F, arrived)
        total = self.inn[0].astype(F32)
        for f in range(1, at.F):
            total = total + self.inn[f].astype(F32)
        return total.astype(BF)


class Swap:
    def __init__(self, at, done, sem):
        self.at, self.done, self.sem = at, done, sem

    def copy(self):
        mine = self.done.at[self.at.y]
        return remote(mine, mine, self.sem.at[0], self.sem.at[1], self.at.flip())

    def start(self):
        self.copy().start()

    def finish(self):
        self.copy().wait()


class FullScatter:
    def __init__(self, at, src, near, got, stage, inn, far, along_sem, done, sem):
        self.at, self.src, self.near, self.got, self.stage = at, src, near, got, stage
        self.done, self.sem = done, sem
        self.along = RowOwner(at, lambda z: stage.at[z], inn, far, along_sem)

    @staticmethod
    def scratch(sizes, rows, cols):
        R, F, S = sizes
        return (
            [
                pltpu.VMEM((S // 2, F, rows, cols), BF),
                pltpu.VMEM((S // 2, F, rows, cols), BF),
                pltpu.VMEM((F, rows, cols), BF),
            ]
            + RowOwner.scratch(F, (rows, cols))
            + [DMA((6, max(F, S)))]
        )

    def sibling(self, j):
        at = self.at
        return remote(
            self.src.at[at.peer(j)],
            self.near.at[j // 2],
            self.sem.at[0, j],
            self.sem.at[1, j],
            {"seq": at.peer(1)},
        )

    def direct(self, j):
        at = self.at
        return remote(
            self.near.at[j // 2],
            self.got.at[j // 2],
            self.sem.at[2, j],
            self.sem.at[3, j],
            {"seq": at.peer(j)},
        )

    def start(self):
        for j in range(3, self.at.S, 2):
            self.sibling(j).start()
        self.sibling(1).start()

    def cross(self):
        at = self.at
        for j in range(2, at.S, 2):
            self.sibling(j + 1).wait()
            k = j // 2

            def add(f):
                both = self.near[k, f].astype(F32) + self.src[at.peer(j), f].astype(F32)
                self.near[k, f] = both.astype(BF)

            each(0, at.F, add)
            self.direct(j).start()
        self.sibling(1).wait()

    def scatter(self):
        at = self.at
        for j in range(2, at.S, 2):
            self.direct(j).wait()

        def far(i):
            z_to = at.zs(i)
            total = self.src[at.s, z_to].astype(F32) + self.near[0, z_to].astype(F32)
            for k in range(1, at.S // 2):
                total = total + self.got[k, z_to].astype(F32)
            self.stage[z_to] = total.astype(BF)

        each(0, at.F, far)
        self.along.start()

    def total(self):
        at = self.at
        self.done[at.y] = self.along.total()
        mine = self.done.at[at.y]
        remote(mine, mine, self.sem.at[4, 0], self.sem.at[5, 0], at.flip()).start()

    def finish(self):
        await_bytes(self.done.at[0], self.sem.at[4, 0])
        await_bytes(self.done.at[0], self.sem.at[5, 0])


def mlp_kernel(sizes, *refs):
    at = Place(sizes)
    R, F, S, G = at.R, at.F, at.S, at.G
    mod, bias_one, bias_two = refs[:3]
    given = refs[3:12]
    block_out, o_resid, o_heads, o_w_one, o_two_sum, o_two_part, o_out_g = refs[12:19]
    refs = refs[:11] + refs[12:]
    grad_b_one, grad_b_two, grad_b_out, mod_sums = refs[18:22]
    act_all, pre_wide, pre_all, grad_branch, wide, two_g, two_got, two_sem = refs[22:30]
    branch_refs, mix_refs = refs[30:34], refs[34:38]
    two_inn, two_far, part_sem, load_sem, save_sem = refs[38:43]
    held = refs[43:52]
    w_one, mix_all, w_two, grad_all, latents, branch_one, cotangent, w_out, merged = held
    grad_resid, grad_heads, grad_w_one, two_sum, two_part, out_g = refs[52:58]
    loads = Moves(load_sem, *zip(given, held))
    loads.start()
    saves = Moves(
        save_sem,
        (grad_w_one, o_w_one),
        (grad_resid, o_resid),
        (grad_heads, o_heads),
        (out_g, o_out_g),
        (two_sum, o_two_sum),
        (two_part, o_two_part),
    )
    _, L, D = mix_all.shape
    C = D // S
    hidden = w_one.shape[1]
    tokens = S * L
    greet(S, lambda i: {"seq": at.ss(i)})
    greet(2, lambda i: at.flip())
    greet(F, lambda i: {"fsdp": at.zs(i)})
    greet_wait(S + F - 1)
    gate_one = mod[2:3, :]
    scale = mod[4:5, :]
    gate_two = mod[5:6, :]
    branch_sum = SeqSum(at, *branch_refs)
    mix_sum = SeqSum(at, *mix_refs)
    branch_src = branch_refs[0]
    mix_src = mix_refs[0]
    two = RowScatter(at, two_g, two_got, two_sum, two_sem)
    part_two = RowOwner(at, lambda z: two_g.at[z, pl.ds(0, 2)], two_inn, two_far, part_sem)
    step = min(256, L)

    def ahead(order):
        index = lax.rem(order + 2, S)
        t = at.peer(arrival(index))

        def part(i):
            rows = pl.ds(pl.multiple_of(i * step, step), step)
            pre = mm(mix_all[t, rows, :], w_one[...]) + bias_one[...]
            pre_wide[t, rows, :] = pre
            inner = gelu_coef * (pre + 0.044715 * pre * pre * pre)
            act = (0.5 * pre * (1.0 + jnp.tanh(inner))).astype(BF)
            act_all[t, rows, :] = act
            branch_src[t, rows, :] = mm(act, w_two[...]).astype(BF)

        each(0, L // step, part)
        branch_sum.send(index)

    loads.wait(0, 1, 2)
    each(0, S, ahead)
    loads.wait(3)
    column = 384 if hidden % 384 == 0 else hidden
    for i in range(hidden // column):
        cols = slice(i * column, (i + 1) * column)
        wide[cols, :] = mm_tn(
            act_all[:, :, cols].reshape(tokens, column), grad_all[...].reshape(tokens, D)
        )
    part_rows = two_g.shape[2]
    for f in range(F):
        for quarter in range(4):
            first = (4 * f + quarter) * part_rows
            two_g[f, quarter] = wide[first : first + part_rows, :].astype(BF)
    part_two.start()
    two.start()

    def behind(order):
        index = lax.rem(order + 2, S)
        t = at.peer(arrival(index))

        def part(i):
            rows = pl.ds(pl.multiple_of(i * step, step), step)
            pre = pre_wide[t, rows, :]
            square = pre * pre
            tanh_val = jnp.tanh(gelu_coef * (pre + 0.044715 * square * pre))
            slope = 0.5 * (1.0 + tanh_val) + 0.5 * pre * (
                1.0 - tanh_val * tanh_val
            ) * gelu_coef * (1.0 + 3.0 * 0.044715 * square)
            grad_pre = (mm_nt(grad_all[t, rows, :], w_two[...]) * slope).astype(BF)
            pre_all[t, rows, :] = grad_pre
            mix_src[t, rows, :] = mm_nt(grad_pre, w_one[...]).astype(BF)

        each(0, L // step, part)
        mix_sum.send(index)

        @pl.when(order == S - 1)
        def _():
            part_two.relay()

    each(0, S, behind)
    for i in range(hidden // column):
        cols = slice(i * column, (i + 1) * column)
        grads = pre_all[:, :, cols].reshape(tokens, column)
        grad_w_one[:, cols] = mm_tn(mix_all[...].reshape(tokens, D), grads).astype(BF)
        grad_b_one[:, cols] = jnp.sum(grads.astype(F32), axis=0, keepdims=True)
    grad_b_two[...] = jnp.sum(grad_all[at.s].astype(F32), axis=0, keepdims=True)
    saves.start(0)
    loads.wait(4, 5, 6, 7, 8)

    mix_sum.wait()
    step_back = min(32, L)
    mod_sums[...] = jnp.zeros_like(mod_sums)
    grad_b_out[...] = jnp.zeros_like(grad_b_out)

    def back(i):
        rows = pl.ds(pl.multiple_of(i * step_back, step_back), step_back)
        grad_mixed = mix_sum.total(rows)
        branch = branch_one[rows, :]
        residual = latents[rows, :].astype(F32) + gate_one * branch
        normed, inv_std = norm_stats(residual)
        grad_out = cotangent[rows, :].astype(F32)
        grad = grad_out + norm_back(grad_mixed * (1.0 + scale), normed, inv_std)
        grad_resid[rows, :] = grad
        low = (gate_one * grad).astype(BF)
        grad_branch[rows, :] = low
        mod_sums[2:3, :] += jnp.sum(grad * branch, axis=0, keepdims=True)
        mod_sums[3:4, :] += jnp.sum(grad_mixed, axis=0, keepdims=True)
        mod_sums[4:5, :] += jnp.sum(grad_mixed * normed, axis=0, keepdims=True)
        grad_b_out[...] += jnp.sum(low.astype(F32), axis=0, keepdims=True)

    each(0, L // step_back, back)
    grad_merged = mm_nt(grad_branch[...], w_out[...]).astype(BF)
    for t in range(S):
        grad_heads[t] = grad_merged[:, t * C : (t + 1) * C]
    saves.start(1, 2)
    for i in range(D // 384):
        cols = slice(i * 384, (i + 1) * 384)
        wide[:D, cols] = mm_tn(merged[...], grad_branch[:, cols])
    rows_own = out_g.shape[2]
    for f in range(F):
        for t in range(S):
            first = (f * S + t) * rows_own
            out_g[t, f] = wide[first : first + rows_own, :].astype(BF)
    saves.start(3)

    branch_sum.wait()

    def finish(i):
        rows = pl.ds(pl.multiple_of(i * step_back, step_back), step_back)
        branch_two = branch_sum.total(rows) + bias_two[...]
        residual = latents[rows, :].astype(F32) + gate_one * branch_one[rows, :]
        block_out[rows, :] = (residual + gate_two * branch_two).astype(BF)
        grad_out = cotangent[rows, :].astype(F32)
        mod_sums[5:6, :] += jnp.sum(grad_out * branch_two, axis=0, keepdims=True)

    each(0, L // step_back, finish)
    two.reduce()
    saves.start(4)
    two_part[...] = part_two.total()
    saves.start(5)
    saves.wait()


def mlp(sizes, *args):
    R, F, S = sizes
    G = F * S
    D, hidden = args[3].shape
    L = args[7].shape[0]
    C = D // S
    quarter = hidden // F // 4
    shape = jax.ShapeDtypeStruct
    kept = (
        ((L, D), F32),
        ((S, L, C), BF),
        ((D, hidden), BF),
        ((F, quarter, D), BF),
        ((2, quarter, D), BF),
        ((S, F, D // G, D), BF),
    )
    return pl.pallas_call(
        lambda *refs: mlp_kernel(sizes, *refs),
        name="mlp",
        out_shape=(shape((L, D), BF),)
        + tuple(shape(*item) for item in kept)
        + (
            shape((1, hidden), F32),
            shape((1, D), F32),
            shape((1, D), F32),
            shape((6, D), F32),
        ),
        in_specs=[VM] * 3 + [HB] * 9,
        out_specs=(VM,) + (HB,) * 6 + (VM,) * 4,
        scratch_shapes=[
            pltpu.VMEM((S, L, hidden), BF),
            pltpu.VMEM((S, L, hidden), F32),
            pltpu.VMEM((S, L, hidden), BF),
            pltpu.VMEM((L, D), BF),
            pltpu.VMEM((max(hidden, D), D), F32),
            pltpu.VMEM((F, 4, quarter, D), BF),
            pltpu.VMEM((F, quarter, D), BF),
            DMA((2, F)),
        ]
        + SeqSum.scratch(S, L, D)
        + SeqSum.scratch(S, L, D)
        + RowOwner.scratch(F, (2, quarter, D))
        + [DMA((9,)), DMA((6,))]
        + [pltpu.VMEM(x.shape, x.dtype) for x in args[3:]]
        + [pltpu.VMEM(*item) for item in kept],
        compiler_params=params(3, 60),
    )(*args)


class ColumnScatter:
    def __init__(self, at, src, got, stage, inn, far, along_sem, summed, done, sem):
        self.at, self.src, self.got, self.stage = at, src, got, stage
        self.summed, self.done, self.sem = summed, done, sem
        self.along = RowOwner(at, lambda z: stage.at[z], inn, far, along_sem)

    @staticmethod
    def scratch(sizes, rows, cols):
        R, F, S = sizes
        shape = (S // 2, rows, cols)
        return (
            [pltpu.VMEM((F,) + shape, BF), pltpu.VMEM((F,) + shape, BF)]
            + RowOwner.scratch(F, shape)
            + [pltpu.VMEM(shape, BF), DMA((5, F))]
        )

    def start(self):
        at = self.at

        def far(i):
            z_to = at.zs(i)

            def one(k):
                slot = z_to * at.S + 2 * k + at.y
                local(self.src.at[slot], self.stage.at[z_to, k], self.sem.at[2, i]).start()
                remote(
                    self.src.at[z_to * at.S + 2 * k + 1 - at.y],
                    self.got.at[z_to, k],
                    self.sem.at[0, i],
                    self.sem.at[1, i],
                    at.flip(),
                ).start()

            each(0, at.S // 2, one)

        each(0, at.F, far)

    def scatter(self):
        at = self.at

        def step(i):
            z_to = at.zs(i)
            await_bytes(self.got.at[0], self.sem.at[1, i])
            await_bytes(self.got.at[0], self.sem.at[2, i])

            def one(k):
                total = self.stage[z_to, k].astype(F32) + self.got[z_to, k].astype(F32)
                self.stage[z_to, k] = total.astype(BF)

            each(0, at.S // 2, one)

        each(0, at.F, step)
        self.along.start()

    def relay(self):
        self.along.relay()

    def near(self):
        at = self.at
        self.summed[...] = self.along.total()

        def one(k):
            s_to = 2 * k + at.y

            @pl.when(s_to == at.s)
            def _():
                self.done[at.s] = self.summed[k]

            @pl.when(s_to != at.s)
            def _():
                remote(
                    self.summed.at[k],
                    self.done.at[at.s],
                    self.sem.at[3, 0],
                    self.sem.at[3, 1],
                    {"seq": s_to},
                ).start()

        each(0, at.S // 2, one)

    def total(self):
        at = self.at

        @pl.when(at.mine)
        def _():
            await_bytes(self.done.at[pl.ds(0, at.S - 1)], self.sem.at[3, 1])
            remote(
                self.done, self.done, self.sem.at[4, 0], self.sem.at[4, 1], at.flip()
            ).start()

    def finish(self):
        at = self.at
        each(0, at.F, lambda i: await_bytes(self.got.at[0], self.sem.at[0, i]))

        @pl.when(at.mine)
        def _():
            if at.S > 2:
                await_bytes(self.done.at[pl.ds(0, at.S // 2 - 1)], self.sem.at[3, 0])
            await_bytes(self.done, self.sem.at[4, 0])

        @pl.when(jnp.logical_not(at.mine))
        def _():
            await_bytes(self.summed, self.sem.at[3, 0])
            await_bytes(self.done, self.sem.at[4, 1])


class Tail:
    def __init__(self, at, mod_all, sums, first_in, mod_src, small_src, small_in, cond_src, cond_in, pieces, sem):
        self.at, self.sums, self.first_in = at, sums, first_in
        self.mod_src, self.mod_all = mod_src, mod_all
        self.small_src, self.small_in = small_src, small_in
        self.cond_src, self.cond_in, self.pieces, self.sem = cond_src, cond_in, pieces, sem

    @staticmethod
    def scratch(sizes, D, hidden, rows):
        R, F, S = sizes
        G = F * S
        C = D // S
        pack = 2 * D // G + 2 * rows + hidden // F
        wide = max(D, hidden, 3 * C)
        return [
            pltpu.VMEM((10, wide), F32),
            pltpu.VMEM((S, 10, wide), F32),
            pltpu.VMEM((6, D), BF),
            pltpu.VMEM((F, 1, pack), F32),
            pltpu.VMEM((R * F, 1, pack), F32),
            pltpu.VMEM((R * F, 1, rows), F32),
            pltpu.VMEM((G, 1, rows), F32),
            pltpu.VMEM((G, 1, pack), F32),
            DMA((8, max(S, 2 * F, G))),
        ]

    def first_copy(self, j):
        at = self.at
        return remote(
            self.sums, self.first_in.at[at.s], self.sem.at[0, j], self.sem.at[1, j], {"seq": at.ss(j)}
        )

    def start(self, mod_sums, b_one, b_two, b_out, b_qkv):
        sums = self.sums
        D = mod_sums.shape[1]
        hidden = b_one.shape[1]
        sums[...] = jnp.zeros_like(sums)
        sums[0:6, 0:D] = mod_sums[...]
        sums[6:7, 0:hidden] = b_one[...]
        sums[7:8, 0:D] = b_two[...]
        sums[8:9, 0:D] = b_out[...]
        sums[9:10, 0 : b_qkv.shape[1]] = b_qkv[...]
        each(1, self.at.S, lambda j: self.first_copy(j).start())
        self.first_in[self.at.s] = sums[...]

    def wide_copies(self, i):
        at = self.at
        slot = at.y * at.F + at.z
        device = {"rep": lax.rem(at.y + i // at.F, 2), "fsdp": at.zs(i)}
        return (
            remote(self.mod_src, self.mod_all.at[slot], self.sem.at[2, i], self.sem.at[3, i], device),
            remote(
                self.small_src.at[at.zs(i)],
                self.small_in.at[slot],
                self.sem.at[4, i],
                self.sem.at[5, i],
                device,
            ),
        )

    def middle(self, D, hidden, rows):
        at = self.at
        F, S, G = at.F, at.S, at.G
        C = D // S
        qv = 2 * D // G
        each(1, S, lambda j: self.first_copy(j).wait())
        total = self.first_in[0]
        for t in range(1, S):
            total = total + self.first_in[t]
        self.mod_src[...] = total[0:6, 0:D].astype(BF)
        for g in range(G):
            g_half = g % (G // 2)
            t = g_half // (F // 2)
            col = (g_half % (F // 2)) * qv + (2 * C if g >= G // 2 else 0)
            self.pieces[g, :, 0:qv] = self.first_in[t, 9:10, col : col + qv]
            self.pieces[g, :, qv : qv + rows] = total[8:9, g * rows : (g + 1) * rows]
            self.pieces[g, :, qv + rows : qv + 2 * rows] = total[7:8, g * rows : (g + 1) * rows]
        block = hidden // F
        for f in range(F):
            self.small_src[f, :, 0 : qv + 2 * rows] = self.pieces[f * S + at.s][:, 0 : qv + 2 * rows]
            self.small_src[f, :, qv + 2 * rows :] = self.sums[6:7, f * block : (f + 1) * block]

        def send(i):
            first, second = self.wide_copies(i)
            first.start()
            second.start()

        each(1, 2 * F, send)
        slot = at.y * F + at.z
        self.mod_all[slot] = self.mod_src[...]
        self.small_in[slot] = self.small_src[at.z]

    def cond_copy(self, i):
        at = self.at
        to = lax.rem(at.me + i, at.G)
        return remote(
            self.cond_src.at[at.y * at.F + to // at.S],
            self.cond_in.at[at.me],
            self.sem.at[6, i],
            self.sem.at[7, i],
            {"fsdp": to // at.S, "seq": lax.rem(to, at.S)},
        )

    def owners(self, w_ada, small_out):
        at = self.at
        F, G = at.F, at.G
        D = self.mod_src.shape[1]

        def arrive(i):
            first, second = self.wide_copies(i)
            first.wait()
            second.wait()

        each(1, 2 * F, arrive)
        cond = None
        for v in range(6):
            rows = self.mod_all[:, v, :]
            part = mm_nt(rows, w_ada[:, v * D : (v + 1) * D])
            cond = part if cond is None else cond + part
        for i in range(2 * F):
            self.cond_src[i] = cond[i : i + 1, :]
        each(1, G, lambda i: self.cond_copy(i).start())
        self.cond_in[at.me] = self.cond_src[at.y * F + at.z]
        total = self.small_in[0]
        for i in range(1, 2 * F):
            total = total + self.small_in[i]
        small_out[...] = total

    def finish(self, cond, grad_cond):
        at = self.at
        rows = self.cond_in.shape[2]
        each(1, at.G, lambda i: self.cond_copy(i).wait())
        for g in range(at.G):
            cols = slice(g * rows, (g + 1) * rows)
            value = cond[:, cols].astype(F32)
            gate = jax.nn.sigmoid(value)
            grad_cond[:, cols] = self.cond_in[g] * gate * (1.0 + value * (1.0 - gate))


def backward_kernel(sizes, *refs):
    at = Place(sizes)
    R, F, S, G = at.R, at.F, at.S, at.G
    grad_heads, heads, two_g, two_part, out_g, w_qkv, mixed_all, latents, grad_resid, w_ada = refs[-10:]
    log_sums, mod, sums_in, b_one, b_two, b_out, cond, one_g = refs[:8]
    given = refs[8:18]
    refs = refs[:7] + refs[8:]
    targets = refs[17:24]
    o_small, o_cond = refs[24:26]
    refs = refs[:16] + refs[17:]
    grad_in, key_flip, key_grad, val_grad, grad_proj, qkv_wide, qkv_g, mod_sums, b_qkv, in_sem = refs[25:35]
    rest = list(refs[35:])
    mix_sum = SeqSum(at, *rest[0:4])
    mix_src = rest[0]
    load_sem, swap_sem, save_sem = rest[37:40]
    kept = rest[40:47]
    grad_latents, o_qkv, o_one, o_two, o_part, o_out, o_mod = kept
    held = rest[47:57]
    qkv = ColumnScatter(at, qkv_g, *rest[4:10], o_qkv, rest[10])
    one = ColumnScatter(at, one_g, *rest[11:17], o_one, rest[17])
    two = RowOwner(at, lambda z: two_g.at[z], rest[18], rest[19], rest[20])
    out = FullScatter(at, out_g, *rest[21:27], o_out, rest[27])
    tail = Tail(at, o_mod, *rest[28:37])
    two_swap = Swap(at, o_two, swap_sem.at[0])
    part_swap = Swap(at, o_part, swap_sem.at[1])
    saves = Moves(save_sem, *zip(kept, targets))
    loads = Moves(load_sem, *zip(given, held))
    loads.start()
    _, L, C = grad_heads.shape
    rows_own, D = o_out.shape[1:]
    hidden = one_g.shape[2]
    local_heads = H // S
    size = D // H
    greet(G, lambda i: {"fsdp": lax.rem(at.me + i, G) // S, "seq": lax.rem(at.me + i, S)})
    greet(2 * F, lambda i: {"rep": lax.rem(at.y + i // F, 2), "fsdp": at.zs(i)})
    loads.wait(0, 2, 3, 4)
    o_part[at.y] = two_part[...]
    greet_wait(G - 1 + 2 * F - 1)

    def in_copy(j):
        return remote(
            grad_heads.at[at.peer(j)],
            grad_in.at[at.s],
            in_sem.at[0, j],
            in_sem.at[1, j],
            {"seq": at.peer(j)},
        )

    each(1, S, lambda j: in_copy(j).start())
    one.start()
    two.start()
    out.start()
    grad_in[at.s] = grad_heads[at.s]
    key_grad[...] = jnp.zeros_like(key_grad)
    val_grad[...] = jnp.zeros_like(val_grad)
    loads.wait(1)
    for h in range(local_heads):
        key_flip[h] = heads[local_heads + h].T
    factor = size ** (-0.5) * log2e
    score_scale = size ** (-0.5)
    pad = jnp.zeros((L, LANES - size), BF)

    def block(j):
        t = at.peer(j)

        @pl.when(j > 0)
        def _():
            in_copy(j).wait()

        rows = pl.ds(pl.multiple_of(t * L, L), L)
        for h in range(local_heads):
            query = heads[h, rows, :]
            grad = jnp.concatenate([grad_in[t, :, h * size : (h + 1) * size], pad], axis=1)
            scores = mm_nt(heads[local_heads + h], query) * factor
            probs = jnp.exp2(scores - log_sums[h, t])
            grad_probs = mm_nt(heads[2 * local_heads + h], grad)
            inner = jnp.sum(probs * grad_probs, axis=0, keepdims=True)
            grad_scores = (probs * (grad_probs - inner)).astype(BF)
            query_grad = mm(key_flip[h], grad_scores) * score_scale
            grad_proj[t, :, h * size : (h + 1) * size] = query_grad.T[:, :size].astype(BF)
            key_grad[h] += mm(grad_scores, query)
            val_grad[h] += mm(probs.astype(BF), grad)

        pl.when(j == 0)(out.cross)

    each(0, S, block)
    two.relay()
    for h in range(local_heads):
        low = (key_grad[h] * score_scale)[:, :size].astype(BF)
        grad_proj[:, :, C + h * size : C + (h + 1) * size] = low.reshape(S, L, size)
        low = val_grad[h][:, :size].astype(BF)
        grad_proj[:, :, 2 * C + h * size : 2 * C + (h + 1) * size] = low.reshape(S, L, size)

    loads.wait(5, 6)

    def spread(index):
        t = at.peer(arrival(index))
        mix_src[t] = mm_nt(grad_proj[t], w_qkv[...]).astype(BF)
        mix_sum.send(index)

    grads = grad_proj[...].reshape(S * L, 3 * C)
    qkv_wide[...] = mm_tn(mixed_all[...].reshape(S * L, D), grads)
    for g in range(G):
        qkv_g[g] = qkv_wide[g * rows_own : (g + 1) * rows_own, :].astype(BF)
    qkv.start()
    out.scatter()
    each(0, S, lambda index: spread(lax.rem(index + 2, S)))
    one.scatter()
    b_qkv[...] = jnp.sum(grads.astype(F32), axis=0, keepdims=True)
    out.along.relay()
    one.relay()
    mix_sum.wait()
    loads.wait(7, 8, 9)
    step = min(32, L)
    mod_sums[...] = sums_in[...]
    scale = mod[1:2, :]

    def back(i):
        rows = pl.ds(pl.multiple_of(i * step, step), step)
        grad_mixed = mix_sum.total(rows)
        normed, inv_std = norm_stats(latents[rows, :].astype(F32))
        grad_latents[rows, :] = grad_resid[rows, :] + norm_back(
            grad_mixed * (1.0 + scale), normed, inv_std
        )
        mod_sums[0:1, :] += jnp.sum(grad_mixed, axis=0, keepdims=True)
        mod_sums[1:2, :] += jnp.sum(grad_mixed * normed, axis=0, keepdims=True)

    each(0, L // step, back)
    saves.start(0)
    tail.start(mod_sums, b_one, b_two, b_out, b_qkv)
    tail.middle(D, hidden, rows_own)
    qkv.scatter()
    o_two[at.y] = two.total()
    two_swap.start()
    part_swap.start()
    out.total()
    one.near()
    qkv.relay()
    tail.owners(w_ada, o_small)
    saves.start(6)
    one.total()
    qkv.near()
    tail.finish(cond, o_cond)
    qkv.total()
    two_swap.finish()
    part_swap.finish()
    saves.start(3, 4)
    out.finish()
    saves.start(5)
    one.finish()
    saves.start(2)
    qkv.finish()
    saves.start(1)
    saves.wait()


def backward(sizes, *args):
    R, F, S = sizes
    G = F * S
    one_g, grad_heads, two_g = args[7], args[8], args[10]
    two_part, latents, w_ada = args[11], args[15], args[17]
    _, L, C = grad_heads.shape
    D = latents.shape[1]
    T = S * L
    local_heads = H // S
    rows = w_ada.shape[0]
    hidden = one_g.shape[2]
    pack = 2 * D // G + 2 * rows + hidden // F
    shape = jax.ShapeDtypeStruct
    kept = (
        ((L, D), F32),
        ((S, rows, 3 * C), BF),
        ((S, rows, hidden), BF),
        ((2,) + two_g.shape[1:], BF),
        ((2,) + two_part.shape, BF),
        ((2, rows, D), BF),
        ((R * F, 6, D), BF),
    )
    return pl.pallas_call(
        lambda *refs: backward_kernel(sizes, *refs),
        name="backward",
        out_shape=tuple(shape(*item) for item in kept)
        + (
            shape((1, pack), F32),
            shape((1, D), F32),
        ),
        in_specs=[VM] * 7 + [HB] * 11,
        out_specs=(HB,) * 7 + (VM,) * 2,
        scratch_shapes=[
            pltpu.VMEM((S, L, C), BF),
            pltpu.VMEM((local_heads, LANES, T), BF),
            pltpu.VMEM((local_heads, T, LANES), F32),
            pltpu.VMEM((local_heads, T, LANES), F32),
            pltpu.VMEM((S, L, 3 * C), BF),
            pltpu.VMEM((D, 3 * C), F32),
            pltpu.VMEM((G, rows, 3 * C), BF),
            pltpu.VMEM((6, D), F32),
            pltpu.VMEM((1, 3 * C), F32),
            DMA((2, S)),
        ]
        + SeqSum.scratch(S, L, D)
        + ColumnScatter.scratch(sizes, rows, 3 * C)
        + ColumnScatter.scratch(sizes, rows, hidden)
        + RowOwner.scratch(F, two_g.shape[1:])
        + FullScatter.scratch(sizes, rows, D)
        + Tail.scratch(sizes, D, hidden, rows)
        + [DMA((10,)), DMA((2, 2)), DMA((7,))]
        + [pltpu.VMEM(*item) for item in kept]
        + [pltpu.VMEM(x.shape, x.dtype) for x in args[8:]],
        compiler_params=params(4, 60),
    )(*args)


def assemble_kernel(sizes, *refs):
    R, F, S = sizes
    G = F * S
    n = 11
    given, results = refs[:n], refs[n : n + 13]
    qkv, one, two, part, out, mod_all, silu_all, small = refs[n + 13 : n + 21]
    o_qkv, o_one, o_two, o_out, o_ada, b_ada, b_qv, b_out, b_one, b_two = refs[n + 21 : n + 31]
    flat, pieces, load_sem, save_sem, *passing = refs[n + 31 :]
    held = (qkv, one, two, part, out, mod_all, silu_all, small, *passing)
    loads = Moves(load_sem, *zip(given, held))
    loads.start()
    passed = tuple(zip(passing, results[:3]))
    made = (o_ada, b_ada, o_qkv, b_qv, o_out, b_out, o_one, b_one, o_two, b_two)
    saves = Moves(save_sem, *passed, *zip(made, results[3:]))
    rows, D = o_out.shape
    C = D // S
    hidden = one.shape[2]
    block = hidden // F
    loads.wait(5, 6)
    silu = silu_all[:, 0, :].astype(BF)
    width = b_ada.shape[0]
    for v in range(6):
        grads = mod_all[:, v, :]
        o_ada[:, v * D : (v + 1) * D] = mm_tn(silu, grads)
        flat[:, v * D : (v + 1) * D] = jnp.sum(grads.astype(F32), axis=0, keepdims=True)
    saves.start(3)
    for g in range(G):
        pieces[g] = flat[:, g * width : (g + 1) * width]
    b_ada[...] = pieces[lax.axis_index("fsdp") * S + lax.axis_index("seq")].reshape(width)
    loads.wait(7)
    first = 0
    for bias in (b_qv, b_out, b_two, b_one):
        length = bias.shape[0]
        bias[...] = small[:, first : first + length].reshape(length)
        first = first + length
    saves.start(4, 6, 8, 10, 12)
    loads.wait(1)
    for t in range(S):
        for f in range(F):
            col = (f * S + t) * block
            o_one[:, col : col + block] = one[t, :, f * block : (f + 1) * block].astype(F32)
    saves.start(9)
    loads.wait(2, 3)
    o_two[0:2] = part[0].astype(F32) + part[1].astype(F32)
    o_two[2:4] = two[...].astype(F32)
    saves.start(11)
    loads.wait(0)
    for t in range(S):
        for j in range(3):
            o_qkv[:, j * D + t * C : j * D + (t + 1) * C] = qkv[t, :, j * C : (j + 1) * C].astype(F32)
    saves.start(5)
    loads.wait(4, 8, 9, 10)
    saves.start(0, 1, 2)
    o_out[...] = out[0].astype(F32) + out[1].astype(F32)
    saves.start(7)
    saves.wait()


def assemble(sizes, qkv, one, two, part, out, mod_all, silu_all, small, *passed):
    R, F, S = sizes
    G = F * S
    rows, D = out.shape[1:]
    hidden = one.shape[2]
    made = (
        ((rows, 6 * D), F32),
        ((6 * D // G,), F32),
        ((rows, 3 * D), F32),
        ((2 * D // G,), F32),
        ((rows, D), F32),
        ((rows,), F32),
        ((rows, hidden * S), F32),
        ((hidden // F,), F32),
        ((4,) + two.shape[1:], F32),
        ((rows,), F32),
    )
    given = (qkv, one, two, part, out, mod_all, silu_all, small)
    scratch = [pltpu.VMEM(x.shape, x.dtype) for x in given]
    order = (2, 6, 8, 4, 0, 1, 3, 5, 7, 9)
    return pl.pallas_call(
        lambda *refs: assemble_kernel(sizes, *refs),
        name="assemble",
        out_shape=tuple(jax.ShapeDtypeStruct(x.shape, x.dtype) for x in passed)
        + tuple(jax.ShapeDtypeStruct(*item) for item in made),
        in_specs=[HB] * 11,
        out_specs=(HB,) * 13,
        scratch_shapes=scratch
        + [pltpu.VMEM(*made[i]) for i in order]
        + [
            pltpu.VMEM((1, 6 * D), F32),
            pltpu.VMEM((G, 1, 6 * D // G), F32),
            DMA((11,)),
            DMA((13,)),
        ]
        + [pltpu.VMEM(x.shape, x.dtype) for x in passed],
        compiler_params=pltpu.CompilerParams(vmem_limit_bytes=60 * 1024 * 1024),
    )(*given, *passed)


def on_device(
    latents, cond, w_ada, b_ada, w_qkv, b_qv, w_out, b_out, w_one, b_one, w_two, b_two, cotangent
):
    sizes = R, F, S = tuple(lax.axis_size(name) for name in ("rep", "fsdp", "seq"))
    G = F * S
    _, L, D = latents.shape
    hidden = w_one.shape[1] // S
    rows = w_ada.shape[0]
    tokens = latents[0]
    two_rows = w_two.shape[0]
    (
        mixed_all,
        heads,
        merged,
        branch_one,
        mix_all,
        grad_all,
        full_qkv,
        full_out,
        log_sums,
        mod,
        silu_all,
        bias_one,
        bias_two,
        g_one,
        g_two,
    ) = forward(
        sizes,
        cond,
        b_ada,
        b_qv,
        b_out,
        b_two,
        b_one,
        tokens,
        cotangent[0],
        w_ada,
        w_qkv,
        w_one,
        w_two.reshape(2, two_rows // 2, D),
        w_out,
    )
    full_one = g_one.reshape(D, hidden)
    full_two = g_two.reshape(hidden, D)
    (
        block_out,
        grad_resid,
        grad_heads,
        one_g,
        two_g,
        two_part,
        out_g,
        grad_b_one,
        grad_b_two,
        grad_b_out,
        mod_sums,
    ) = mlp(
        sizes,
        mod,
        bias_one,
        bias_two,
        full_one,
        mix_all,
        full_two,
        grad_all,
        tokens,
        branch_one,
        cotangent[0],
        full_out,
        merged,
    )
    grad_latents, qkv_sum, one_sum, two_sum, part_sum, out_sum, mod_all, o_small, o_cond = backward(
        sizes,
        log_sums,
        mod,
        mod_sums,
        grad_b_one,
        grad_b_two,
        grad_b_out,
        cond,
        one_g.reshape(G, rows, hidden),
        grad_heads,
        heads,
        two_g,
        two_part,
        out_g,
        full_qkv,
        mixed_all,
        tokens,
        grad_resid,
        w_ada,
    )
    outs = assemble(
        sizes,
        qkv_sum,
        one_sum,
        two_sum,
        part_sum,
        out_sum,
        mod_all,
        silu_all,
        o_small,
        block_out,
        grad_latents,
        o_cond,
    )
    shapes = (latents.shape, latents.shape, cond.shape, w_ada.shape, b_ada.shape, w_qkv.shape, b_qv.shape)
    shapes += (w_out.shape, b_out.shape, w_one.shape, b_one.shape, w_two.shape, b_two.shape)
    return tuple(out.reshape(want) for out, want in zip(outs, shapes))


def solution(mesh):
    owned = P(("fsdp", "seq"), None)
    owned_bias = P(("fsdp", "seq"))
    token_spec = P(("rep", "fsdp"), "seq", None)
    cond_spec = P(("rep", "fsdp"), None)
    weights = (owned, owned_bias) * 5
    in_specs = (token_spec, cond_spec) + weights + (token_spec,)
    out_specs = (token_spec, token_spec, cond_spec) + weights
    return jax.shard_map(
        on_device, mesh=mesh, in_specs=in_specs, out_specs=out_specs, check_vma=False
    )
```

```python
import math

import jax
import jax.numpy as jnp
from jax import lax
from jax.experimental import pallas as pl
from jax.experimental.pallas import tpu as pltpu
from jax.sharding import PartitionSpec as P

H = 16
epsilon = 1e-06
gelu_coef = math.sqrt(2.0 / math.pi)
log2e = math.log2(math.e)
BF = jnp.bfloat16
F32 = jnp.float32
LANES = 128
VM = pl.BlockSpec(memory_space=pltpu.VMEM)
HB = pl.BlockSpec(memory_space=pl.ANY)
DMA = pltpu.SemaphoreType.DMA


def params(ident, mib):
    return pltpu.CompilerParams(
        collective_id=ident, has_side_effects=True, vmem_limit_bytes=mib * 1024 * 1024
    )


def remote(src, dst, send, recv, device):
    return pltpu.make_async_remote_copy(
        src_ref=src,
        dst_ref=dst,
        send_sem=send,
        recv_sem=recv,
        device_id=device,
        device_id_type=pl.DeviceIdType.MESH,
    )


def local(src, dst, sem):
    return pltpu.make_async_copy(src, dst, sem)


def await_bytes(like, sem):
    pltpu.make_async_copy(like, like, sem).wait()


class Moves:
    def __init__(self, sem, *pairs):
        self.copies = [local(pair[0], pair[1], sem.at[i]) for i, pair in enumerate(pairs)]

    def start(self, *which):
        for i in which or range(len(self.copies)):
            self.copies[i].start()

    def wait(self, *which):
        for i in which or range(len(self.copies)):
            self.copies[i].wait()


def each(start, stop, body):
    def step(index, carry):
        body(index)
        return carry

    lax.fori_loop(start, stop, step, 0)


def greet(count, device_of):
    gate = pltpu.get_barrier_semaphore()
    each(
        1,
        count,
        lambda i: pl.semaphore_signal(
            gate, 1, device_id=device_of(i), device_id_type=pl.DeviceIdType.MESH
        ),
    )
    return count - 1


def greet_wait(count):
    pl.semaphore_wait(pltpu.get_barrier_semaphore(), count)


def norm_stats(values):
    center = values - jnp.mean(values, axis=-1, keepdims=True)
    inv_std = lax.rsqrt(jnp.mean(center * center, axis=-1, keepdims=True) + epsilon)
    return (center * inv_std, inv_std)


def norm_back(grad, normed, inv_std):
    return inv_std * (
        grad
        - jnp.mean(grad, axis=-1, keepdims=True)
        - normed * jnp.mean(grad * normed, axis=-1, keepdims=True)
    )


def mm(left, right):
    return jnp.dot(left, right, preferred_element_type=F32)


def mm_nt(left, right):
    return lax.dot_general(left, right, (((1,), (1,)), ((), ())), preferred_element_type=F32)


def mm_tn(left, right):
    return lax.dot_general(left, right, (((0,), (0,)), ((), ())), preferred_element_type=F32)


class Place:
    def __init__(self, sizes):
        self.R, self.F, self.S = sizes
        self.G = self.F * self.S
        self.y = lax.axis_index("rep")
        self.z = lax.axis_index("fsdp")
        self.s = lax.axis_index("seq")
        self.me = self.z * self.S + self.s
        self.mine = lax.rem(self.s, 2) == self.y
        self.steps = (2, 1, 3) if self.F == 4 else tuple(range(1, self.F))

    def zs(self, i):
        return lax.rem(self.z + i, self.F)

    def zs_back(self, i):
        return lax.rem(self.z - i + self.F, self.F)

    def ss(self, i):
        return lax.rem(self.s + i, self.S)

    def ss_back(self, i):
        return lax.rem(self.s - i + self.S, self.S)

    def flip(self):
        return {"rep": 1 - self.y}

    def peer(self, j):
        return lax.bitwise_xor(self.s, j)


class SeqGather:
    def __init__(self, at, dst, sem):
        self.at, self.dst, self.sem = at, dst, sem

    @staticmethod
    def scratch(S):
        return DMA((4, S))

    def direct(self, j):
        at, block = self.at, self.dst.at[self.at.s]
        return remote(block, block, self.sem.at[0, j], self.sem.at[1, j], {"seq": at.peer(j)})

    def handed(self, j):
        at = self.at
        block = self.dst.at[at.peer(j)]
        return remote(block, block, self.sem.at[2, j], self.sem.at[3, j], {"seq": at.peer(1)})

    def start(self):
        for j in range(3, self.at.S, 2):
            self.direct(j).start()
        self.direct(1).start()

    def arrive(self, index):
        @pl.when(index == 1)
        def _():
            self.direct(1).wait()

        if self.at.S > 2:

            @pl.when((index >= 2) & (lax.rem(index, 2) == 0))
            def _():
                self.direct(index + 1).wait()
                self.handed(index + 1).start()

            @pl.when((index >= 2) & (lax.rem(index, 2) == 1))
            def _():
                self.handed(index).wait()


def arrival(index):
    return jnp.where(index < 2, index, lax.bitwise_xor(index, 1))


class SeqSum:
    def __init__(self, at, src, near, inn, sem):
        self.at, self.src, self.near, self.inn, self.sem = at, src, near, inn, sem

    @staticmethod
    def scratch(S, rows, cols):
        return [
            pltpu.VMEM((S, rows, cols), BF),
            pltpu.VMEM((S // 2, rows, cols), BF),
            pltpu.VMEM((S // 2, rows, cols), BF),
            DMA((4, S)),
        ]

    def sibling(self, j):
        at = self.at
        return remote(
            self.src.at[at.peer(j)],
            self.near.at[j // 2],
            self.sem.at[0, j],
            self.sem.at[1, j],
            {"seq": at.peer(1)},
        )

    def direct(self, j):
        at = self.at
        return remote(
            self.src.at[at.peer(j)],
            self.inn.at[j // 2],
            self.sem.at[2, j],
            self.sem.at[3, j],
            {"seq": at.peer(j)},
        )

    def send(self, index):
        @pl.when((index == 1) | ((index >= 2) & (lax.rem(index, 2) == 0)))
        def _():
            self.sibling(lax.bitwise_or(index, 1)).start()

        if self.at.S > 2:

            @pl.when((index >= 2) & (lax.rem(index, 2) == 1))
            def _():
                j = index - 1
                self.sibling(index).wait()
                t = self.at.peer(j)
                step = min(64, self.src.shape[1])

                def add(i):
                    rows = pl.ds(pl.multiple_of(i * step, step), step)
                    both = self.src[t, rows, :].astype(F32) + self.near[j // 2, rows, :].astype(F32)
                    self.src[t, rows, :] = both.astype(BF)

                each(0, self.src.shape[1] // step, add)
                self.direct(j).start()

    def wait(self):
        self.sibling(1).wait()
        for j in range(2, self.at.S, 2):
            self.direct(j).wait()

    def total(self, rows):
        value = self.src[self.at.s, rows, :].astype(F32) + self.near[0, rows, :].astype(F32)
        for k in range(1, self.at.S // 2):
            value = value + self.inn[k, rows, :].astype(F32)
        return value


class FarGather:
    relayed = True

    def __init__(self, at, dst, sem):
        self.at, self.dst, self.sem = at, dst, sem
        self.line = self.relayed and at.F == 4

    @staticmethod
    def scratch(F):
        return DMA((7, F))

    def send(self, z_from, z_to, kind):
        pieces = self.half(z_from)
        held = self.origin() if kind == 0 else pieces
        for source, piece in zip(held, pieces):
            remote(
                source, piece, self.sem.at[kind, z_to], self.sem.at[2, z_from], {"fsdp": z_to}
            ).start()

    def origin(self):
        return self.half(self.at.z)

    def await_half(self, row, z):
        await_bytes(self.like(), self.sem.at[row, z])

    def around(self, step, body):
        at = self.at

        @pl.when(at.z >= step)
        def _():
            body(at.z - step)

        @pl.when(at.z + step < at.F)
        def _():
            body(at.z + step)

    def direct(self, step, body):
        if self.line and step == 3:
            return
        self.around(step, body)

    def start_far(self):
        for step in self.at.steps:
            self.direct(step, lambda z_to: self.send(self.at.z, z_to, 0))

    def service(self, step):
        at = self.at

        def take(z_from):
            self.await_half(2, z_from)
            for piece in self.half(z_from):
                remote(
                    piece, piece, self.sem.at[3, z_from], self.sem.at[4, z_from], at.flip()
                ).start()

        self.around(step, take)
        if self.line and step == 2:

            @pl.when((at.z == 1) | (at.z == 2))
            def _():
                far = jnp.where(at.z == 1, 3, 0)
                end = 3 - far
                self.send(far, end, 1)

    def finish_far(self):
        at = self.at

        def swapped(z_from):
            self.await_half(3, z_from)
            self.await_half(4, z_from)

        for step in range(1, at.F):
            self.around(step, swapped)
            self.direct(step, lambda z_to: self.await_half(0, z_to))
        if self.line:

            @pl.when((at.z == 1) | (at.z == 2))
            def _():
                self.await_half(1, jnp.where(at.z == 1, 0, 3))


class ColumnGather(FarGather):
    def __init__(self, at, src, dst, sem):
        super().__init__(at, dst, sem)
        self.src = src

    def half(self, z):
        at = self.at
        return [self.dst.at[z * at.S + 2 * k + at.y] for k in range(at.S // 2)]

    def like(self):
        return self.dst.at[pl.ds(0, self.at.S // 2)]

    def start(self):
        at, src, dst, sem = self.at, self.src, self.dst, self.sem

        def near(j):
            t = at.ss(j)
            remote(src.at[t], dst.at[at.me], sem.at[5, 0], sem.at[6, 0], {"seq": t}).start()

        each(1, at.S, near)
        local(src.at[at.s], dst.at[at.me], sem.at[5, 1]).start()

    def near_done(self):
        at, dst, sem = self.at, self.dst, self.sem
        local(self.src.at[at.s], dst.at[at.me], sem.at[5, 1]).wait()
        near = dst.at[pl.ds(0, at.S - 1)]
        await_bytes(near, sem.at[5, 0])
        await_bytes(near, sem.at[6, 0])


class RowGather(FarGather):
    def __init__(self, at, src, dst, sem):
        super().__init__(at, dst, sem)
        self.src = src

    def half(self, z):
        return [self.dst.at[z, self.at.y]]

    def origin(self):
        return [self.src.at[self.at.y]]

    def like(self):
        return self.dst.at[0, 0]

    def start(self):
        at = self.at
        local(self.src, self.dst.at[at.z], self.sem.at[5, 0]).start()

    def near_done(self):
        at = self.at
        local(self.src, self.dst.at[at.z], self.sem.at[5, 0]).wait()


class OwnGather(FarGather):
    relayed = False

    def __init__(self, at, src, dst, sem):
        super().__init__(at, dst, sem)
        self.src = src

    def half(self, z):
        return [self.dst.at[self.at.s, z]]

    def origin(self):
        return [self.src]

    def like(self):
        return self.src

    def start(self):
        at = self.at
        local(self.src, self.dst.at[at.s, at.z], self.sem.at[5, 0]).start()

    def near_done(self):
        at = self.at
        local(self.src, self.dst.at[at.s, at.z], self.sem.at[5, 0]).wait()

    def start_far(self):
        pl.when(self.at.mine)(super().start_far)

    def service(self, step):
        take = super().service
        pl.when(self.at.mine)(lambda: take(step))

    def finish_far(self):
        at = self.at

        def sent(z_from):
            self.await_half(3, z_from)

        def swapped(z_from):
            self.await_half(4, z_from)

        @pl.when(at.mine)
        def _():
            for step in range(1, at.F):
                self.around(step, sent)
                self.direct(step, lambda z_to: self.await_half(0, z_to))
            if self.line:

                @pl.when((at.z == 1) | (at.z == 2))
                def _():
                    self.await_half(1, jnp.where(at.z == 1, 0, 3))

        @pl.when(jnp.logical_not(at.mine))
        def _():
            for step in range(1, at.F):
                self.around(step, swapped)


def forward_kernel(sizes, *refs):
    at = Place(sizes)
    R, F, S, G = at.R, at.F, at.S, at.G
    cond = refs[0]
    i_biases = refs[1:6]
    i_latents, i_cotangent, i_ada, i_qkv, i_one, w_two, w_out = refs[6:13]
    refs = refs[3:]
    o_mixed, o_heads, o_merged, o_branch, o_mix, o_grad, o_full_qkv, o_full_out = refs[10:18]
    log_sums, mod, silu_all, bias_one, bias_two, g_one, g_two = refs[18:25]
    silu_src, part, parts_in, mod_src, mod_in, qkv_src, one_src, pack_all = refs[25:33]
    g_qkv, g_out, wide, bias_qkv, bias_out, val_flip, att, merged_in = refs[33:41]
    silu_sem, part_sem, mod_sem, pack_sem, qkv_sem, one_sem, two_sem, out_sem = refs[41:49]
    mixed_sem, grad_sem, att_sem, mix_sem, spread_sem, load_sem, save_sem = refs[49:56]
    bias_pack, bias_pieces, bias_slot, bias_sem = refs[69:73]
    biases = refs[73:78]
    bias_loads = Moves(bias_sem, *zip(i_biases, biases))
    bias_loads.start()
    latents, cotangent, w_ada, w_qkv, w_one = refs[56:61]
    mixed_all, heads, merged, branch_one, mix_all, grad_all, full_qkv, full_out = refs[61:69]
    loads = Moves(
        load_sem,
        (i_qkv, w_qkv),
        (i_ada, w_ada),
        (i_one, w_one),
        (i_latents, latents),
        (i_cotangent, cotangent),
    )
    loads.start()
    saves = Moves(
        save_sem,
        (mixed_all, o_mixed),
        (heads, o_heads),
        (merged, o_merged),
        (branch_one, o_branch),
        (mix_all, o_mix),
        (grad_all, o_grad),
        (full_qkv, o_full_qkv),
        (full_out, o_full_out),
    )
    L, D = latents.shape
    C = D // S
    T = S * L
    local_heads = H // S
    size = D // H
    rows_own = silu_all.shape[2]
    hidden = one_src.shape[2]
    block = hidden // F
    greet(G, lambda i: {"fsdp": lax.rem(at.me + i, G) // S, "seq": lax.rem(at.me + i, S)})
    greet(2 * F, lambda i: {"rep": lax.rem(at.y + i // F, 2), "fsdp": at.zs(i)})
    width = bias_pieces.shape[2]
    bias_loads.wait()
    first = 0
    for bias in biases[1:]:
        length = bias.shape[0]
        bias_pack[:, first : first + length] = bias[...].astype(F32).reshape(1, length)
        first = first + length
    bias_pieces[...] = jnp.zeros_like(bias_pieces)
    bias_pieces[at.me] = biases[0][...].astype(F32).reshape(1, width)
    for g in range(G):
        bias_slot[:, g * width : (g + 1) * width] = bias_pieces[g]

    value = cond[...].astype(F32)
    silu = (value * jax.nn.sigmoid(value)).astype(BF).astype(F32)
    for g in range(G):
        silu_src[g] = silu[:, g * rows_own : (g + 1) * rows_own]
    loads.wait(0)
    for t in range(S):
        for j in range(3):
            qkv_src[t, :, j * C : (j + 1) * C] = w_qkv[:, j * D + t * C : j * D + (t + 1) * C]
    loads.wait(2)
    for t in range(S):
        for f in range(F):
            col = (f * S + t) * block
            one_src[t, :, f * block : (f + 1) * block] = w_one[:, col : col + block]
    greet_wait(G - 1 + 2 * F - 1)
    slot = at.y * F + at.z

    def cond_copy(i):
        z_to = at.zs(i)
        return remote(
            silu_src.at[z_to * S + at.s],
            silu_all.at[slot],
            silu_sem.at[0, i],
            silu_sem.at[1, i],
            {"rep": lax.rem(at.y + i // F, 2), "fsdp": z_to},
        )

    each(1, 2 * F, lambda i: cond_copy(i).start())
    silu_all[slot] = silu_src[at.me]

    def pack_copy(i):
        to = lax.rem(at.me + i, G)
        return remote(
            bias_pack,
            pack_all.at[at.me],
            pack_sem.at[0, 0],
            pack_sem.at[1, 0],
            {"fsdp": to // S, "seq": lax.rem(to, S)},
        )

    each(1, G, lambda i: pack_copy(i).start())
    pack_all[at.me] = bias_pack[...]

    qkv = ColumnGather(at, qkv_src, g_qkv, qkv_sem)
    one = ColumnGather(at, one_src, g_one, one_sem)
    two = RowGather(at, w_two, g_two, two_sem)
    out = OwnGather(at, w_out, g_out, out_sem)
    qkv.start()
    two.start()
    out.start()

    each(1, 2 * F, lambda i: cond_copy(i).wait())
    left = jnp.concatenate([silu_all[at.y * F + f] for f in range(F)], axis=0).astype(BF)
    loads.wait(1)
    sums = mm(left, w_ada[...]) + bias_slot[...]
    for f in range(F):
        for v in range(6):
            for t in range(S):
                col = v * D + t * C
                part[f * S + t, v : v + 1, :] = sums[f : f + 1, col : col + C]

    def part_copy(i):
        to = lax.rem(at.me + i, G)
        return remote(
            part.at[to],
            parts_in.at[at.me],
            part_sem.at[0, i],
            part_sem.at[1, i],
            {"fsdp": to // S, "seq": lax.rem(to, S)},
        )

    each(1, G, lambda i: part_copy(i).start())
    parts_in[at.me] = part[at.me]
    qkv.near_done()
    qkv.start_far()
    each(1, G, lambda i: part_copy(i).wait())
    total = parts_in[0]
    for g in range(1, G):
        total = total + parts_in[g]
    mod_src[...] = total

    def mod_copy(i):
        return remote(
            mod_src, mod_in.at[at.s], mod_sem.at[0, i], mod_sem.at[1, i], {"seq": at.ss(i)}
        )

    each(1, S, lambda i: mod_copy(i).start())
    one.start()
    mod_in[at.s] = total
    out.start_far()
    each(1, S, lambda i: mod_copy(i).wait())
    for t in range(S):
        mod[:, t * C : (t + 1) * C] = mod_in[t]

    loads.wait(3)
    step = min(64, L)

    def norm(i):
        at_rows = pl.ds(pl.multiple_of(i * step, step), step)
        normed, _ = norm_stats(latents[at_rows, :].astype(F32))
        mixed_all[at.s, at_rows, :] = (normed * (1.0 + mod[1:2, :]) + mod[0:1, :]).astype(BF)

    each(0, L // step, norm)
    gather = SeqGather(at, mixed_all, mixed_sem)
    gather.start()
    loads.wait(4)
    grad_all[at.s] = (mod[5:6, :] * cotangent[...].astype(F32)).astype(BF)
    grad_gather = SeqGather(at, grad_all, grad_sem)
    grad_gather.start()
    one.near_done()
    qkv.service(at.steps[0])
    one.start_far()
    out.near_done()
    two.near_done()

    others = pack_all.at[pl.ds(0, G - 1)]
    await_bytes(others, pack_sem.at[0, 0])
    await_bytes(others, pack_sem.at[1, 0])
    qv = 2 * D // G
    own = F // 2
    bias_qkv[...] = jnp.zeros_like(bias_qkv)
    for i in range(own):
        bias_qkv[:, i * qv : (i + 1) * qv] = pack_all[at.s * own + i][:, 0:qv]
        bias_qkv[:, 2 * C + i * qv : 2 * C + (i + 1) * qv] = pack_all[G // 2 + at.s * own + i][
            :, 0:qv
        ]
    for g in range(G):
        cols = slice(g * rows_own, (g + 1) * rows_own)
        bias_out[:, cols] = pack_all[g][:, qv : qv + rows_own]
        bias_two[:, cols] = pack_all[g][:, qv + rows_own : qv + 2 * rows_own]
    for f in range(F):
        bias_one[:, f * block : (f + 1) * block] = pack_all[f * S + at.s][:, qv + 2 * rows_own :]

    for i in at.steps[1:]:
        qkv.service(i)
    for i in at.steps:
        out.service(i)
    qkv.finish_far()

    def join(slabs, whole):
        cols = whole.shape[1]
        for g in range(G):
            wide[g * rows_own : (g + 1) * rows_own, 0:cols] = slabs(g).astype(F32)
        tall = 128 if D % 128 == 0 else D

        def cast(i):
            at_rows = pl.ds(pl.multiple_of(i * tall, tall), tall)
            whole[at_rows, :] = wide[at_rows, 0:cols].astype(BF)

        each(0, D // tall, cast)

    join(lambda g: g_qkv[g], full_qkv)
    saves.start(6)

    pad = jnp.zeros((L, LANES - size), BF)

    def project(index):
        gather.arrive(index)
        t = at.peer(arrival(index))
        at_rows = pl.ds(pl.multiple_of(t * L, L), L)
        done = (mm(mixed_all[t], full_qkv[...]) + bias_qkv[...]).astype(BF)
        for c in range(3 * local_heads):
            heads[c, at_rows, :] = jnp.concatenate(
                [done[:, c * size : (c + 1) * size], pad], axis=1
            )

    each(0, S, project)
    saves.start(0, 1)
    out.finish_far()
    spread = SeqGather(at, g_out, spread_sem)
    spread.start()
    each(1, S, grad_gather.arrive)
    saves.start(5)
    for h in range(local_heads):
        val_flip[h] = heads[2 * local_heads + h].T

    def att_copy(j):
        t = at.peer(j)
        return remote(
            att.at[t], merged_in.at[at.s], att_sem.at[0, j], att_sem.at[1, j], {"seq": t}
        )

    factor = size ** (-0.5) * log2e

    def attention(index):
        j = S - 1 - index
        t = at.peer(j)
        at_rows = pl.ds(pl.multiple_of(t * L, L), L)
        for h in range(local_heads):
            scores = mm_nt(heads[local_heads + h], heads[h, at_rows, :]) * factor
            highest = jnp.max(scores, axis=0, keepdims=True)
            raised = jnp.exp2(scores - highest)
            summed = jnp.sum(raised, axis=0, keepdims=True)
            result = mm(val_flip[h], raised.astype(BF)) / summed
            log_sums[h, t] = highest + jnp.log2(summed)
            att[t, :, h * size : (h + 1) * size] = result.T[:, :size].astype(BF)

        @pl.when(j > 0)
        def _():
            att_copy(j).start()

    one.service(at.steps[0])
    one.service(at.steps[1])
    two.start_far()
    each(0, S, attention)
    merged_in[at.s] = att[at.s]
    each(1, S, spread.arrive)
    join(lambda g: g_out[g % S, g // S], full_out)
    saves.start(7)
    each(1, S, lambda j: att_copy(j).wait())
    for t in range(S):
        merged[:, t * C : (t + 1) * C] = merged_in[t]
    saves.start(2)

    def project_out(i):
        at_rows = pl.ds(pl.multiple_of(i * step, step), step)
        branch = mm(merged[at_rows, :], full_out[...]) + bias_out[...]
        branch_one[at_rows, :] = branch
        residual = latents[at_rows, :].astype(F32) + mod[2:3, :] * branch
        normed, _ = norm_stats(residual)
        mix_all[at.s, at_rows, :] = (normed * (1.0 + mod[4:5, :]) + mod[3:4, :]).astype(BF)

    each(0, L // step, project_out)
    saves.start(3)
    mix_gather = SeqGather(at, mix_all, mix_sem)
    mix_gather.start()
    for i in at.steps[2:]:
        one.service(i)
    for i in at.steps:
        two.service(i)
    one.finish_far()
    each(1, S, mix_gather.arrive)
    saves.start(4)
    two.finish_far()
    saves.wait()


def forward(sizes, cond, *args):
    biases = args[:5]
    latents, cotangent, w_ada, w_qkv, w_one, w_two, w_out = args[5:]
    R, F, S = sizes
    G = F * S
    rows, D = w_out.shape
    L = latents.shape[0]
    T = S * L
    C = D // S
    local_heads = H // S
    hidden = w_one.shape[1] // S
    shape = jax.ShapeDtypeStruct
    width = 6 * D // G
    pack = sum(bias.shape[0] for bias in biases[1:])
    kept = (
        ((S, L, D), BF),
        ((3 * local_heads, T, LANES), BF),
        ((L, D), BF),
        ((L, D), F32),
        ((S, L, D), BF),
        ((S, L, D), BF),
        ((D, 3 * C), BF),
        ((D, D), BF),
    )
    return pl.pallas_call(
        lambda *refs: forward_kernel(sizes, *refs),
        name="forward",
        out_shape=tuple(shape(*item) for item in kept)
        + (
            shape((local_heads, S, 1, L), F32),
            shape((6, D), F32),
            shape((R * F, 1, rows), F32),
            shape((1, hidden), F32),
            shape((1, D), F32),
            shape((G, rows, hidden), BF),
            shape((F,) + w_two.shape, BF),
        ),
        in_specs=[VM] + [HB] * 12,
        out_specs=(HB,) * 8 + (VM,) * 5 + (HB,) * 2,
        scratch_shapes=[
            pltpu.VMEM((G, 1, rows), F32),
            pltpu.VMEM((G, 6, C), F32),
            pltpu.VMEM((G, 6, C), F32),
            pltpu.VMEM((6, C), F32),
            pltpu.VMEM((S, 6, C), F32),
            pltpu.VMEM((S, rows, 3 * C), BF),
            pltpu.VMEM((S, rows, hidden), BF),
            pltpu.VMEM((G, 1, pack), F32),
            pltpu.VMEM((G, rows, 3 * C), BF),
            pltpu.VMEM((S, F, rows, D), BF),
            pltpu.VMEM((D, max(D, 3 * C)), F32),
            pltpu.VMEM((1, 3 * C), F32),
            pltpu.VMEM((1, D), F32),
            pltpu.VMEM((local_heads, LANES, T), BF),
            pltpu.VMEM((S, L, C), BF),
            pltpu.VMEM((S, L, C), BF),
            DMA((2, 2 * F)),
            DMA((2, G)),
            DMA((2, S)),
            DMA((2, 1)),
            ColumnGather.scratch(F),
            ColumnGather.scratch(F),
            RowGather.scratch(F),
            OwnGather.scratch(F),
            SeqGather.scratch(S),
            SeqGather.scratch(S),
            DMA((2, S)),
            SeqGather.scratch(S),
            SeqGather.scratch(S),
            DMA((5,)),
            DMA((8,)),
        ]
        + [pltpu.VMEM(x.shape, x.dtype) for x in (latents, cotangent, w_ada, w_qkv, w_one)]
        + [pltpu.VMEM(*item) for item in kept]
        + [
            pltpu.VMEM((1, pack), F32),
            pltpu.VMEM((G, 1, width), F32),
            pltpu.VMEM((1, 6 * D), F32),
            DMA((5,)),
        ]
        + [pltpu.VMEM(bias.shape, BF) for bias in biases],
        compiler_params=params(1, 60),
    )(cond, *args)


class RowScatter:
    def __init__(self, at, src, got, stage, sem):
        self.at, self.src, self.got, self.stage, self.sem = at, src, got, stage, sem

    def start(self):
        at = self.at

        def far(i):
            z_to = at.zs(i)
            remote(
                self.src.at[z_to, 3 - at.y],
                self.got.at[z_to],
                self.sem.at[0, i],
                self.sem.at[1, i],
                at.flip(),
            ).start()

        each(0, at.F, far)

    def reduce(self):
        at = self.at

        def far(i):
            z_to = at.zs(i)
            await_bytes(self.got.at[0], self.sem.at[0, i])
            await_bytes(self.got.at[0], self.sem.at[1, i])
            total = self.src[z_to, 2 + at.y].astype(F32) + self.got[z_to].astype(F32)
            self.stage[z_to] = total.astype(BF)

        each(0, at.F, far)


class Line:
    def line_up(self):
        at = self.at
        self.line = at.F == 4
        self.inner = self.line & ((at.z == 1) | (at.z == 2))
        self.end = self.line & ((at.z == 0) | (at.z == 3))
        self.opposite = jnp.where(at.z < 2, 3, 0)
        self.beside = jnp.where(at.z == 0, 1, 2)


class RowOwner(Line):
    def __init__(self, at, piece, inn, far, sem):
        self.at, self.piece, self.inn, self.far, self.sem = at, piece, inn, far, sem
        self.line_up()

    @staticmethod
    def scratch(F, shape):
        return [pltpu.VMEM((F,) + shape, BF), pltpu.VMEM(shape, BF), DMA((3, F))]

    def out_copy(self, z_to):
        at = self.at
        return remote(
            self.piece(z_to),
            self.inn.at[at.z],
            self.sem.at[0, z_to],
            self.sem.at[1, at.z],
            {"fsdp": z_to},
        )

    def far_copy(self):
        return remote(
            self.piece(self.opposite),
            self.far,
            self.sem.at[0, self.opposite],
            self.sem.at[2, 0],
            {"fsdp": self.beside},
        )

    def start(self):
        at = self.at

        @pl.when(self.end)
        def _():
            self.far_copy().start()
            self.inn[self.opposite] = jnp.zeros_like(self.far)

        def one(i):
            z_to = at.zs(i)

            @pl.when(jnp.logical_not(self.line & (z_to == self.opposite)))
            def _():
                self.out_copy(z_to).start()

        each(1, at.F, one)
        self.inn[at.z] = self.piece(at.z)[...]

    def relay(self):
        @pl.when(self.inner)
        def _():
            await_bytes(self.far, self.sem.at[2, 0])
            z_to = self.opposite
            piece = self.piece(z_to)
            piece[...] = (piece[...].astype(F32) + self.far[...].astype(F32)).astype(BF)
            self.out_copy(z_to).start()

    def total(self):
        at = self.at

        def arrived(i):
            z = at.zs(i)
            await_bytes(self.far, self.sem.at[0, z])

            @pl.when(jnp.logical_not(self.end & (z == self.opposite)))
            def _():
                await_bytes(self.far, self.sem.at[1, z])

        each(1, at.F, arrived)
        total = self.inn[0].astype(F32)
        for f in range(1, at.F):
            total = total + self.inn[f].astype(F32)
        return total.astype(BF)


class Swap:
    def __init__(self, at, done, sem):
        self.at, self.done, self.sem = at, done, sem

    def copy(self):
        mine = self.done.at[self.at.y]
        return remote(mine, mine, self.sem.at[0], self.sem.at[1], self.at.flip())

    def start(self):
        self.copy().start()

    def finish(self):
        self.copy().wait()


class FullScatter:
    def __init__(self, at, src, near, got, stage, inn, far, along_sem, done, sem):
        self.at, self.src, self.near, self.got, self.stage = at, src, near, got, stage
        self.done, self.sem = done, sem
        self.along = RowOwner(at, lambda z: stage.at[z], inn, far, along_sem)

    @staticmethod
    def scratch(sizes, rows, cols):
        R, F, S = sizes
        return (
            [
                pltpu.VMEM((S // 2, F, rows, cols), BF),
                pltpu.VMEM((S // 2, F, rows, cols), BF),
                pltpu.VMEM((F, rows, cols), BF),
            ]
            + RowOwner.scratch(F, (rows, cols))
            + [DMA((6, max(F, S)))]
        )

    def sibling(self, j):
        at = self.at
        return remote(
            self.src.at[at.peer(j)],
            self.near.at[j // 2],
            self.sem.at[0, j],
            self.sem.at[1, j],
            {"seq": at.peer(1)},
        )

    def direct(self, j):
        at = self.at
        return remote(
            self.near.at[j // 2],
            self.got.at[j // 2],
            self.sem.at[2, j],
            self.sem.at[3, j],
            {"seq": at.peer(j)},
        )

    def start(self):
        for j in range(3, self.at.S, 2):
            self.sibling(j).start()
        self.sibling(1).start()

    def cross(self):
        at = self.at
        for j in range(2, at.S, 2):
            self.sibling(j + 1).wait()
            k = j // 2

            def add(f):
                both = self.near[k, f].astype(F32) + self.src[at.peer(j), f].astype(F32)
                self.near[k, f] = both.astype(BF)

            each(0, at.F, add)
            self.direct(j).start()
        self.sibling(1).wait()

    def scatter(self):
        at = self.at
        for j in range(2, at.S, 2):
            self.direct(j).wait()

        def far(i):
            z_to = at.zs(i)
            total = self.src[at.s, z_to].astype(F32) + self.near[0, z_to].astype(F32)
            for k in range(1, at.S // 2):
                total = total + self.got[k, z_to].astype(F32)
            self.stage[z_to] = total.astype(BF)

        each(0, at.F, far)
        self.along.start()

    def total(self):
        at = self.at
        self.done[at.y] = self.along.total()
        mine = self.done.at[at.y]
        remote(mine, mine, self.sem.at[4, 0], self.sem.at[5, 0], at.flip()).start()

    def finish(self):
        await_bytes(self.done.at[0], self.sem.at[4, 0])
        await_bytes(self.done.at[0], self.sem.at[5, 0])


def mlp_kernel(sizes, *refs):
    at = Place(sizes)
    R, F, S, G = at.R, at.F, at.S, at.G
    mod, bias_one, bias_two = refs[:3]
    given = refs[3:12]
    block_out, o_resid, o_heads, o_w_one, o_two_sum, o_two_part, o_out_g = refs[12:19]
    refs = refs[:11] + refs[12:]
    grad_b_one, grad_b_two, grad_b_out, mod_sums = refs[18:22]
    act_all, pre_wide, pre_all, grad_branch, wide, two_g, two_got, two_sem = refs[22:30]
    branch_refs, mix_refs = refs[30:34], refs[34:38]
    two_inn, two_far, part_sem, load_sem, save_sem = refs[38:43]
    held = refs[43:52]
    w_one, mix_all, w_two, grad_all, latents, branch_one, cotangent, w_out, merged = held
    grad_resid, grad_heads, grad_w_one, two_sum, two_part, out_g = refs[52:58]
    loads = Moves(load_sem, *zip(given, held))
    loads.start()
    saves = Moves(
        save_sem,
        (grad_w_one, o_w_one),
        (grad_resid, o_resid),
        (grad_heads, o_heads),
        (out_g, o_out_g),
        (two_sum, o_two_sum),
        (two_part, o_two_part),
    )
    _, L, D = mix_all.shape
    C = D // S
    hidden = w_one.shape[1]
    tokens = S * L
    greet(S, lambda i: {"seq": at.ss(i)})
    greet(2, lambda i: at.flip())
    greet(F, lambda i: {"fsdp": at.zs(i)})
    greet_wait(S + F - 1)
    gate_one = mod[2:3, :]
    scale = mod[4:5, :]
    gate_two = mod[5:6, :]
    branch_sum = SeqSum(at, *branch_refs)
    mix_sum = SeqSum(at, *mix_refs)
    branch_src = branch_refs[0]
    mix_src = mix_refs[0]
    two = RowScatter(at, two_g, two_got, two_sum, two_sem)
    part_two = RowOwner(at, lambda z: two_g.at[z, pl.ds(0, 2)], two_inn, two_far, part_sem)
    step = min(256, L)

    def ahead(order):
        index = lax.rem(order + 2, S)
        t = at.peer(arrival(index))

        def part(i):
            rows = pl.ds(pl.multiple_of(i * step, step), step)
            pre = mm(mix_all[t, rows, :], w_one[...]) + bias_one[...]
            pre_wide[t, rows, :] = pre
            inner = gelu_coef * (pre + 0.044715 * pre * pre * pre)
            act = (0.5 * pre * (1.0 + jnp.tanh(inner))).astype(BF)
            act_all[t, rows, :] = act
            branch_src[t, rows, :] = mm(act, w_two[...]).astype(BF)

        each(0, L // step, part)
        branch_sum.send(index)

    loads.wait(0, 1, 2)
    each(0, S, ahead)
    loads.wait(3)
    column = 384 if hidden % 384 == 0 else hidden
    for i in range(hidden // column):
        cols = slice(i * column, (i + 1) * column)
        wide[cols, :] = mm_tn(
            act_all[:, :, cols].reshape(tokens, column), grad_all[...].reshape(tokens, D)
        )
    part_rows = two_g.shape[2]
    for f in range(F):
        for quarter in range(4):
            first = (4 * f + quarter) * part_rows
            two_g[f, quarter] = wide[first : first + part_rows, :].astype(BF)
    part_two.start()
    two.start()

    def behind(order):
        index = lax.rem(order + 2, S)
        t = at.peer(arrival(index))

        def part(i):
            rows = pl.ds(pl.multiple_of(i * step, step), step)
            pre = pre_wide[t, rows, :]
            square = pre * pre
            tanh_val = jnp.tanh(gelu_coef * (pre + 0.044715 * square * pre))
            slope = 0.5 * (1.0 + tanh_val) + 0.5 * pre * (
                1.0 - tanh_val * tanh_val
            ) * gelu_coef * (1.0 + 3.0 * 0.044715 * square)
            grad_pre = (mm_nt(grad_all[t, rows, :], w_two[...]) * slope).astype(BF)
            pre_all[t, rows, :] = grad_pre
            mix_src[t, rows, :] = mm_nt(grad_pre, w_one[...]).astype(BF)

        each(0, L // step, part)
        mix_sum.send(index)

        @pl.when(order == S - 1)
        def _():
            part_two.relay()

    each(0, S, behind)
    for i in range(hidden // column):
        cols = slice(i * column, (i + 1) * column)
        grads = pre_all[:, :, cols].reshape(tokens, column)
        grad_w_one[:, cols] = mm_tn(mix_all[...].reshape(tokens, D), grads).astype(BF)
        grad_b_one[:, cols] = jnp.sum(grads.astype(F32), axis=0, keepdims=True)
    grad_b_two[...] = jnp.sum(grad_all[at.s].astype(F32), axis=0, keepdims=True)
    saves.start(0)
    loads.wait(4, 5, 6, 7, 8)

    mix_sum.wait()
    step_back = min(128, L)
    mod_sums[...] = jnp.zeros_like(mod_sums)
    grad_b_out[...] = jnp.zeros_like(grad_b_out)

    def back(i):
        rows = pl.ds(pl.multiple_of(i * step_back, step_back), step_back)
        grad_mixed = mix_sum.total(rows)
        branch = branch_one[rows, :]
        residual = latents[rows, :].astype(F32) + gate_one * branch
        normed, inv_std = norm_stats(residual)
        grad_out = cotangent[rows, :].astype(F32)
        grad = grad_out + norm_back(grad_mixed * (1.0 + scale), normed, inv_std)
        grad_resid[rows, :] = grad
        low = (gate_one * grad).astype(BF)
        grad_branch[rows, :] = low
        mod_sums[2:3, :] += jnp.sum(grad * branch, axis=0, keepdims=True)
        mod_sums[3:4, :] += jnp.sum(grad_mixed, axis=0, keepdims=True)
        mod_sums[4:5, :] += jnp.sum(grad_mixed * normed, axis=0, keepdims=True)
        grad_b_out[...] += jnp.sum(low.astype(F32), axis=0, keepdims=True)

    each(0, L // step_back, back)
    grad_merged = mm_nt(grad_branch[...], w_out[...]).astype(BF)
    for t in range(S):
        grad_heads[t] = grad_merged[:, t * C : (t + 1) * C]
    saves.start(1, 2)
    for i in range(D // 384):
        cols = slice(i * 384, (i + 1) * 384)
        wide[:D, cols] = mm_tn(merged[...], grad_branch[:, cols])
    rows_own = out_g.shape[2]
    for f in range(F):
        for t in range(S):
            first = (f * S + t) * rows_own
            out_g[t, f] = wide[first : first + rows_own, :].astype(BF)
    saves.start(3)

    branch_sum.wait()

    def finish(i):
        rows = pl.ds(pl.multiple_of(i * step_back, step_back), step_back)
        branch_two = branch_sum.total(rows) + bias_two[...]
        residual = latents[rows, :].astype(F32) + gate_one * branch_one[rows, :]
        block_out[rows, :] = (residual + gate_two * branch_two).astype(BF)
        grad_out = cotangent[rows, :].astype(F32)
        mod_sums[5:6, :] += jnp.sum(grad_out * branch_two, axis=0, keepdims=True)

    each(0, L // step_back, finish)
    two.reduce()
    saves.start(4)
    two_part[...] = part_two.total()
    saves.start(5)
    saves.wait()


def mlp(sizes, *args):
    R, F, S = sizes
    G = F * S
    D, hidden = args[3].shape
    L = args[7].shape[0]
    C = D // S
    quarter = hidden // F // 4
    shape = jax.ShapeDtypeStruct
    kept = (
        ((L, D), F32),
        ((S, L, C), BF),
        ((D, hidden), BF),
        ((F, quarter, D), BF),
        ((2, quarter, D), BF),
        ((S, F, D // G, D), BF),
    )
    return pl.pallas_call(
        lambda *refs: mlp_kernel(sizes, *refs),
        name="mlp",
        out_shape=(shape((L, D), BF),)
        + tuple(shape(*item) for item in kept)
        + (
            shape((1, hidden), F32),
            shape((1, D), F32),
            shape((1, D), F32),
            shape((6, D), F32),
        ),
        in_specs=[VM] * 3 + [HB] * 9,
        out_specs=(VM,) + (HB,) * 6 + (VM,) * 4,
        scratch_shapes=[
            pltpu.VMEM((S, L, hidden), BF),
            pltpu.VMEM((S, L, hidden), F32),
            pltpu.VMEM((S, L, hidden), BF),
            pltpu.VMEM((L, D), BF),
            pltpu.VMEM((max(hidden, D), D), F32),
            pltpu.VMEM((F, 4, quarter, D), BF),
            pltpu.VMEM((F, quarter, D), BF),
            DMA((2, F)),
        ]
        + SeqSum.scratch(S, L, D)
        + SeqSum.scratch(S, L, D)
        + RowOwner.scratch(F, (2, quarter, D))
        + [DMA((9,)), DMA((6,))]
        + [pltpu.VMEM(x.shape, x.dtype) for x in args[3:]]
        + [pltpu.VMEM(*item) for item in kept],
        compiler_params=params(3, 60),
    )(*args)


class ColumnScatter:
    def __init__(self, at, src, got, stage, inn, far, along_sem, summed, done, sem):
        self.at, self.src, self.got, self.stage = at, src, got, stage
        self.summed, self.done, self.sem = summed, done, sem
        self.along = RowOwner(at, lambda z: stage.at[z], inn, far, along_sem)

    @staticmethod
    def scratch(sizes, rows, cols):
        R, F, S = sizes
        shape = (S // 2, rows, cols)
        return (
            [pltpu.VMEM((F,) + shape, BF), pltpu.VMEM((F,) + shape, BF)]
            + RowOwner.scratch(F, shape)
            + [pltpu.VMEM(shape, BF), DMA((5, F))]
        )

    def start(self):
        at = self.at

        def far(i):
            z_to = at.zs(i)

            def one(k):
                slot = z_to * at.S + 2 * k + at.y
                local(self.src.at[slot], self.stage.at[z_to, k], self.sem.at[2, i]).start()
                remote(
                    self.src.at[z_to * at.S + 2 * k + 1 - at.y],
                    self.got.at[z_to, k],
                    self.sem.at[0, i],
                    self.sem.at[1, i],
                    at.flip(),
                ).start()

            each(0, at.S // 2, one)

        each(0, at.F, far)

    def scatter(self):
        at = self.at

        def step(i):
            z_to = at.zs(i)
            await_bytes(self.got.at[0], self.sem.at[1, i])
            await_bytes(self.got.at[0], self.sem.at[2, i])

            def one(k):
                total = self.stage[z_to, k].astype(F32) + self.got[z_to, k].astype(F32)
                self.stage[z_to, k] = total.astype(BF)

            each(0, at.S // 2, one)

        each(0, at.F, step)
        self.along.start()

    def relay(self):
        self.along.relay()

    def near(self):
        at = self.at
        self.summed[...] = self.along.total()

        def one(k):
            s_to = 2 * k + at.y

            @pl.when(s_to == at.s)
            def _():
                self.done[at.s] = self.summed[k]

            @pl.when(s_to != at.s)
            def _():
                remote(
                    self.summed.at[k],
                    self.done.at[at.s],
                    self.sem.at[3, 0],
                    self.sem.at[3, 1],
                    {"seq": s_to},
                ).start()

        each(0, at.S // 2, one)

    def total(self):
        at = self.at

        @pl.when(at.mine)
        def _():
            await_bytes(self.done.at[pl.ds(0, at.S - 1)], self.sem.at[3, 1])
            remote(
                self.done, self.done, self.sem.at[4, 0], self.sem.at[4, 1], at.flip()
            ).start()

    def finish(self):
        at = self.at
        each(0, at.F, lambda i: await_bytes(self.got.at[0], self.sem.at[0, i]))

        @pl.when(at.mine)
        def _():
            if at.S > 2:
                await_bytes(self.done.at[pl.ds(0, at.S // 2 - 1)], self.sem.at[3, 0])
            await_bytes(self.done, self.sem.at[4, 0])

        @pl.when(jnp.logical_not(at.mine))
        def _():
            await_bytes(self.summed, self.sem.at[3, 0])
            await_bytes(self.done, self.sem.at[4, 1])


class Tail:
    def __init__(self, at, mod_all, sums, first_in, mod_src, small_src, small_in, cond_src, cond_in, pieces, sem):
        self.at, self.sums, self.first_in = at, sums, first_in
        self.mod_src, self.mod_all = mod_src, mod_all
        self.small_src, self.small_in = small_src, small_in
        self.cond_src, self.cond_in, self.pieces, self.sem = cond_src, cond_in, pieces, sem

    @staticmethod
    def scratch(sizes, D, hidden, rows):
        R, F, S = sizes
        G = F * S
        C = D // S
        pack = 2 * D // G + 2 * rows + hidden // F
        wide = max(D, hidden, 3 * C)
        return [
            pltpu.VMEM((10, wide), F32),
            pltpu.VMEM((S, 10, wide), F32),
            pltpu.VMEM((6, D), BF),
            pltpu.VMEM((F, 1, pack), F32),
            pltpu.VMEM((R * F, 1, pack), F32),
            pltpu.VMEM((R * F, 1, rows), F32),
            pltpu.VMEM((G, 1, rows), F32),
            pltpu.VMEM((G, 1, pack), F32),
            DMA((8, max(S, 2 * F, G))),
        ]

    def first_copy(self, j):
        at = self.at
        return remote(
            self.sums, self.first_in.at[at.s], self.sem.at[0, j], self.sem.at[1, j], {"seq": at.ss(j)}
        )

    def start(self, mod_sums, b_one, b_two, b_out, b_qkv):
        sums = self.sums
        D = mod_sums.shape[1]
        hidden = b_one.shape[1]
        sums[...] = jnp.zeros_like(sums)
        sums[0:6, 0:D] = mod_sums[...]
        sums[6:7, 0:hidden] = b_one[...]
        sums[7:8, 0:D] = b_two[...]
        sums[8:9, 0:D] = b_out[...]
        sums[9:10, 0 : b_qkv.shape[1]] = b_qkv[...]
        each(1, self.at.S, lambda j: self.first_copy(j).start())
        self.first_in[self.at.s] = sums[...]

    def wide_copies(self, i):
        at = self.at
        slot = at.y * at.F + at.z
        device = {"rep": lax.rem(at.y + i // at.F, 2), "fsdp": at.zs(i)}
        return (
            remote(self.mod_src, self.mod_all.at[slot], self.sem.at[2, i], self.sem.at[3, i], device),
            remote(
                self.small_src.at[at.zs(i)],
                self.small_in.at[slot],
                self.sem.at[4, i],
                self.sem.at[5, i],
                device,
            ),
        )

    def middle(self, D, hidden, rows):
        at = self.at
        F, S, G = at.F, at.S, at.G
        C = D // S
        qv = 2 * D // G
        each(1, S, lambda j: self.first_copy(j).wait())
        total = self.first_in[0]
        for t in range(1, S):
            total = total + self.first_in[t]
        self.mod_src[...] = total[0:6, 0:D].astype(BF)
        for g in range(G):
            g_half = g % (G // 2)
            t = g_half // (F // 2)
            col = (g_half % (F // 2)) * qv + (2 * C if g >= G // 2 else 0)
            self.pieces[g, :, 0:qv] = self.first_in[t, 9:10, col : col + qv]
            self.pieces[g, :, qv : qv + rows] = total[8:9, g * rows : (g + 1) * rows]
            self.pieces[g, :, qv + rows : qv + 2 * rows] = total[7:8, g * rows : (g + 1) * rows]
        block = hidden // F
        for f in range(F):
            self.small_src[f, :, 0 : qv + 2 * rows] = self.pieces[f * S + at.s][:, 0 : qv + 2 * rows]
            self.small_src[f, :, qv + 2 * rows :] = self.sums[6:7, f * block : (f + 1) * block]

        def send(i):
            first, second = self.wide_copies(i)
            first.start()
            second.start()

        each(1, 2 * F, send)
        slot = at.y * F + at.z
        self.mod_all[slot] = self.mod_src[...]
        self.small_in[slot] = self.small_src[at.z]

    def cond_copy(self, i):
        at = self.at
        to = lax.rem(at.me + i, at.G)
        return remote(
            self.cond_src.at[at.y * at.F + to // at.S],
            self.cond_in.at[at.me],
            self.sem.at[6, i],
            self.sem.at[7, i],
            {"fsdp": to // at.S, "seq": lax.rem(to, at.S)},
        )

    def owners(self, w_ada, small_out):
        at = self.at
        F, G = at.F, at.G
        D = self.mod_src.shape[1]

        def arrive(i):
            first, second = self.wide_copies(i)
            first.wait()
            second.wait()

        each(1, 2 * F, arrive)
        cond = None
        for v in range(6):
            rows = self.mod_all[:, v, :]
            part = mm_nt(rows, w_ada[:, v * D : (v + 1) * D])
            cond = part if cond is None else cond + part
        for i in range(2 * F):
            self.cond_src[i] = cond[i : i + 1, :]
        each(1, G, lambda i: self.cond_copy(i).start())
        self.cond_in[at.me] = self.cond_src[at.y * F + at.z]
        total = self.small_in[0]
        for i in range(1, 2 * F):
            total = total + self.small_in[i]
        small_out[...] = total

    def finish(self, cond, grad_cond):
        at = self.at
        rows = self.cond_in.shape[2]
        each(1, at.G, lambda i: self.cond_copy(i).wait())
        for g in range(at.G):
            cols = slice(g * rows, (g + 1) * rows)
            value = cond[:, cols].astype(F32)
            gate = jax.nn.sigmoid(value)
            grad_cond[:, cols] = self.cond_in[g] * gate * (1.0 + value * (1.0 - gate))


def backward_kernel(sizes, *refs):
    at = Place(sizes)
    R, F, S, G = at.R, at.F, at.S, at.G
    grad_heads, heads, two_g, two_part, out_g, w_qkv, mixed_all, latents, grad_resid, w_ada = refs[-10:]
    log_sums, mod, sums_in, b_one, b_two, b_out, cond, one_g = refs[:8]
    given = refs[8:18]
    refs = refs[:7] + refs[8:]
    targets = refs[17:24]
    o_small, o_cond = refs[24:26]
    refs = refs[:16] + refs[17:]
    grad_in, key_flip, key_grad, val_grad, grad_proj, qkv_wide, qkv_g, mod_sums, b_qkv, in_sem = refs[25:35]
    rest = list(refs[35:])
    mix_sum = SeqSum(at, *rest[0:4])
    mix_src = rest[0]
    load_sem, swap_sem, save_sem = rest[37:40]
    kept = rest[40:47]
    grad_latents, o_qkv, o_one, o_two, o_part, o_out, o_mod = kept
    held = rest[47:57]
    qkv = ColumnScatter(at, qkv_g, *rest[4:10], o_qkv, rest[10])
    one = ColumnScatter(at, one_g, *rest[11:17], o_one, rest[17])
    two = RowOwner(at, lambda z: two_g.at[z], rest[18], rest[19], rest[20])
    out = FullScatter(at, out_g, *rest[21:27], o_out, rest[27])
    tail = Tail(at, o_mod, *rest[28:37])
    two_swap = Swap(at, o_two, swap_sem.at[0])
    part_swap = Swap(at, o_part, swap_sem.at[1])
    saves = Moves(save_sem, *zip(kept, targets))
    loads = Moves(load_sem, *zip(given, held))
    loads.start()
    _, L, C = grad_heads.shape
    rows_own, D = o_out.shape[1:]
    hidden = one_g.shape[2]
    local_heads = H // S
    size = D // H
    greet(G, lambda i: {"fsdp": lax.rem(at.me + i, G) // S, "seq": lax.rem(at.me + i, S)})
    greet(2 * F, lambda i: {"rep": lax.rem(at.y + i // F, 2), "fsdp": at.zs(i)})
    loads.wait(0, 2, 3, 4)
    o_part[at.y] = two_part[...]
    greet_wait(G - 1 + 2 * F - 1)

    def in_copy(j):
        return remote(
            grad_heads.at[at.peer(j)],
            grad_in.at[at.s],
            in_sem.at[0, j],
            in_sem.at[1, j],
            {"seq": at.peer(j)},
        )

    each(1, S, lambda j: in_copy(j).start())
    one.start()
    two.start()
    out.start()
    grad_in[at.s] = grad_heads[at.s]
    key_grad[...] = jnp.zeros_like(key_grad)
    val_grad[...] = jnp.zeros_like(val_grad)
    loads.wait(1)
    for h in range(local_heads):
        key_flip[h] = heads[local_heads + h].T
    factor = size ** (-0.5) * log2e
    score_scale = size ** (-0.5)
    pad = jnp.zeros((L, LANES - size), BF)

    def block(j):
        t = at.peer(j)

        @pl.when(j > 0)
        def _():
            in_copy(j).wait()

        rows = pl.ds(pl.multiple_of(t * L, L), L)
        for h in range(local_heads):
            query = heads[h, rows, :]
            grad = jnp.concatenate([grad_in[t, :, h * size : (h + 1) * size], pad], axis=1)
            scores = mm_nt(heads[local_heads + h], query) * factor
            probs = jnp.exp2(scores - log_sums[h, t])
            grad_probs = mm_nt(heads[2 * local_heads + h], grad)
            inner = jnp.sum(probs * grad_probs, axis=0, keepdims=True)
            grad_scores = (probs * (grad_probs - inner)).astype(BF)
            query_grad = mm(key_flip[h], grad_scores) * score_scale
            grad_proj[t, :, h * size : (h + 1) * size] = query_grad.T[:, :size].astype(BF)
            key_grad[h] += mm(grad_scores, query)
            val_grad[h] += mm(probs.astype(BF), grad)

        pl.when(j == 0)(out.cross)

    each(0, S, block)
    two.relay()
    for h in range(local_heads):
        low = (key_grad[h] * score_scale)[:, :size].astype(BF)
        grad_proj[:, :, C + h * size : C + (h + 1) * size] = low.reshape(S, L, size)
        low = val_grad[h][:, :size].astype(BF)
        grad_proj[:, :, 2 * C + h * size : 2 * C + (h + 1) * size] = low.reshape(S, L, size)

    loads.wait(5, 6)

    def spread(index):
        t = at.peer(arrival(index))
        mix_src[t] = mm_nt(grad_proj[t], w_qkv[...]).astype(BF)
        mix_sum.send(index)

    grads = grad_proj[...].reshape(S * L, 3 * C)
    qkv_wide[...] = mm_tn(mixed_all[...].reshape(S * L, D), grads)
    for g in range(G):
        qkv_g[g] = qkv_wide[g * rows_own : (g + 1) * rows_own, :].astype(BF)
    qkv.start()
    out.scatter()
    each(0, S, lambda index: spread(lax.rem(index + 2, S)))
    one.scatter()
    b_qkv[...] = jnp.sum(grads.astype(F32), axis=0, keepdims=True)
    out.along.relay()
    one.relay()
    mix_sum.wait()
    loads.wait(7, 8, 9)
    step = min(128, L)
    mod_sums[...] = sums_in[...]
    scale = mod[1:2, :]

    def back(i):
        rows = pl.ds(pl.multiple_of(i * step, step), step)
        grad_mixed = mix_sum.total(rows)
        normed, inv_std = norm_stats(latents[rows, :].astype(F32))
        grad_latents[rows, :] = grad_resid[rows, :] + norm_back(
            grad_mixed * (1.0 + scale), normed, inv_std
        )
        mod_sums[0:1, :] += jnp.sum(grad_mixed, axis=0, keepdims=True)
        mod_sums[1:2, :] += jnp.sum(grad_mixed * normed, axis=0, keepdims=True)

    each(0, L // step, back)
    saves.start(0)
    tail.start(mod_sums, b_one, b_two, b_out, b_qkv)
    tail.middle(D, hidden, rows_own)
    qkv.scatter()
    o_two[at.y] = two.total()
    two_swap.start()
    part_swap.start()
    out.total()
    one.near()
    qkv.relay()
    tail.owners(w_ada, o_small)
    saves.start(6)
    one.total()
    qkv.near()
    tail.finish(cond, o_cond)
    qkv.total()
    two_swap.finish()
    part_swap.finish()
    saves.start(3, 4)
    out.finish()
    saves.start(5)
    one.finish()
    saves.start(2)
    qkv.finish()
    saves.start(1)
    saves.wait()


def backward(sizes, *args):
    R, F, S = sizes
    G = F * S
    one_g, grad_heads, two_g = args[7], args[8], args[10]
    two_part, latents, w_ada = args[11], args[15], args[17]
    _, L, C = grad_heads.shape
    D = latents.shape[1]
    T = S * L
    local_heads = H // S
    rows = w_ada.shape[0]
    hidden = one_g.shape[2]
    pack = 2 * D // G + 2 * rows + hidden // F
    shape = jax.ShapeDtypeStruct
    kept = (
        ((L, D), F32),
        ((S, rows, 3 * C), BF),
        ((S, rows, hidden), BF),
        ((2,) + two_g.shape[1:], BF),
        ((2,) + two_part.shape, BF),
        ((2, rows, D), BF),
        ((R * F, 6, D), BF),
    )
    return pl.pallas_call(
        lambda *refs: backward_kernel(sizes, *refs),
        name="backward",
        out_shape=tuple(shape(*item) for item in kept)
        + (
            shape((1, pack), F32),
            shape((1, D), F32),
        ),
        in_specs=[VM] * 7 + [HB] * 11,
        out_specs=(HB,) * 7 + (VM,) * 2,
        scratch_shapes=[
            pltpu.VMEM((S, L, C), BF),
            pltpu.VMEM((local_heads, LANES, T), BF),
            pltpu.VMEM((local_heads, T, LANES), F32),
            pltpu.VMEM((local_heads, T, LANES), F32),
            pltpu.VMEM((S, L, 3 * C), BF),
            pltpu.VMEM((D, 3 * C), F32),
            pltpu.VMEM((G, rows, 3 * C), BF),
            pltpu.VMEM((6, D), F32),
            pltpu.VMEM((1, 3 * C), F32),
            DMA((2, S)),
        ]
        + SeqSum.scratch(S, L, D)
        + ColumnScatter.scratch(sizes, rows, 3 * C)
        + ColumnScatter.scratch(sizes, rows, hidden)
        + RowOwner.scratch(F, two_g.shape[1:])
        + FullScatter.scratch(sizes, rows, D)
        + Tail.scratch(sizes, D, hidden, rows)
        + [DMA((10,)), DMA((2, 2)), DMA((7,))]
        + [pltpu.VMEM(*item) for item in kept]
        + [pltpu.VMEM(x.shape, x.dtype) for x in args[8:]],
        compiler_params=params(4, 60),
    )(*args)


def assemble_kernel(sizes, *refs):
    R, F, S = sizes
    G = F * S
    n = 11
    given, results = refs[:n], refs[n : n + 13]
    qkv, one, two, part, out, mod_all, silu_all, small = refs[n + 13 : n + 21]
    o_qkv, o_one, o_two, o_out, o_ada, b_ada, b_qv, b_out, b_one, b_two = refs[n + 21 : n + 31]
    flat, pieces, load_sem, save_sem, *passing = refs[n + 31 :]
    held = (qkv, one, two, part, out, mod_all, silu_all, small, *passing)
    loads = Moves(load_sem, *zip(given, held))
    loads.start()
    passed = tuple(zip(passing, results[:3]))
    made = (o_ada, b_ada, o_qkv, b_qv, o_out, b_out, o_one, b_one, o_two, b_two)
    saves = Moves(save_sem, *passed, *zip(made, results[3:]))
    rows, D = o_out.shape
    C = D // S
    hidden = one.shape[2]
    block = hidden // F
    loads.wait(5, 6)
    silu = silu_all[:, 0, :].astype(BF)
    width = b_ada.shape[0]
    for v in range(6):
        grads = mod_all[:, v, :]
        o_ada[:, v * D : (v + 1) * D] = mm_tn(silu, grads)
        flat[:, v * D : (v + 1) * D] = jnp.sum(grads.astype(F32), axis=0, keepdims=True)
    saves.start(3)
    for g in range(G):
        pieces[g] = flat[:, g * width : (g + 1) * width]
    b_ada[...] = pieces[lax.axis_index("fsdp") * S + lax.axis_index("seq")].reshape(width)
    loads.wait(7)
    first = 0
    for bias in (b_qv, b_out, b_two, b_one):
        length = bias.shape[0]
        bias[...] = small[:, first : first + length].reshape(length)
        first = first + length
    saves.start(4, 6, 8, 10, 12)
    loads.wait(1)
    for t in range(S):
        for f in range(F):
            col = (f * S + t) * block
            o_one[:, col : col + block] = one[t, :, f * block : (f + 1) * block].astype(F32)
    saves.start(9)
    loads.wait(2, 3)
    o_two[0:2] = part[0].astype(F32) + part[1].astype(F32)
    o_two[2:4] = two[...].astype(F32)
    saves.start(11)
    loads.wait(0)
    for t in range(S):
        for j in range(3):
            o_qkv[:, j * D + t * C : j * D + (t + 1) * C] = qkv[t, :, j * C : (j + 1) * C].astype(F32)
    saves.start(5)
    loads.wait(4, 8, 9, 10)
    saves.start(0, 1, 2)
    o_out[...] = out[0].astype(F32) + out[1].astype(F32)
    saves.start(7)
    saves.wait()


def assemble(sizes, qkv, one, two, part, out, mod_all, silu_all, small, *passed):
    R, F, S = sizes
    G = F * S
    rows, D = out.shape[1:]
    hidden = one.shape[2]
    made = (
        ((rows, 6 * D), F32),
        ((6 * D // G,), F32),
        ((rows, 3 * D), F32),
        ((2 * D // G,), F32),
        ((rows, D), F32),
        ((rows,), F32),
        ((rows, hidden * S), F32),
        ((hidden // F,), F32),
        ((4,) + two.shape[1:], F32),
        ((rows,), F32),
    )
    given = (qkv, one, two, part, out, mod_all, silu_all, small)
    scratch = [pltpu.VMEM(x.shape, x.dtype) for x in given]
    order = (2, 6, 8, 4, 0, 1, 3, 5, 7, 9)
    return pl.pallas_call(
        lambda *refs: assemble_kernel(sizes, *refs),
        name="assemble",
        out_shape=tuple(jax.ShapeDtypeStruct(x.shape, x.dtype) for x in passed)
        + tuple(jax.ShapeDtypeStruct(*item) for item in made),
        in_specs=[HB] * 11,
        out_specs=(HB,) * 13,
        scratch_shapes=scratch
        + [pltpu.VMEM(*made[i]) for i in order]
        + [
            pltpu.VMEM((1, 6 * D), F32),
            pltpu.VMEM((G, 1, 6 * D // G), F32),
            DMA((11,)),
            DMA((13,)),
        ]
        + [pltpu.VMEM(x.shape, x.dtype) for x in passed],
        compiler_params=pltpu.CompilerParams(vmem_limit_bytes=60 * 1024 * 1024),
    )(*given, *passed)


def on_device(
    latents, cond, w_ada, b_ada, w_qkv, b_qv, w_out, b_out, w_one, b_one, w_two, b_two, cotangent
):
    sizes = R, F, S = tuple(lax.axis_size(name) for name in ("rep", "fsdp", "seq"))
    G = F * S
    _, L, D = latents.shape
    hidden = w_one.shape[1] // S
    rows = w_ada.shape[0]
    tokens = latents[0]
    two_rows = w_two.shape[0]
    (
        mixed_all,
        heads,
        merged,
        branch_one,
        mix_all,
        grad_all,
        full_qkv,
        full_out,
        log_sums,
        mod,
        silu_all,
        bias_one,
        bias_two,
        g_one,
        g_two,
    ) = forward(
        sizes,
        cond,
        b_ada,
        b_qv,
        b_out,
        b_two,
        b_one,
        tokens,
        cotangent[0],
        w_ada,
        w_qkv,
        w_one,
        w_two.reshape(2, two_rows // 2, D),
        w_out,
    )
    full_one = g_one.reshape(D, hidden)
    full_two = g_two.reshape(hidden, D)
    (
        block_out,
        grad_resid,
        grad_heads,
        one_g,
        two_g,
        two_part,
        out_g,
        grad_b_one,
        grad_b_two,
        grad_b_out,
        mod_sums,
    ) = mlp(
        sizes,
        mod,
        bias_one,
        bias_two,
        full_one,
        mix_all,
        full_two,
        grad_all,
        tokens,
        branch_one,
        cotangent[0],
        full_out,
        merged,
    )
    grad_latents, qkv_sum, one_sum, two_sum, part_sum, out_sum, mod_all, o_small, o_cond = backward(
        sizes,
        log_sums,
        mod,
        mod_sums,
        grad_b_one,
        grad_b_two,
        grad_b_out,
        cond,
        one_g.reshape(G, rows, hidden),
        grad_heads,
        heads,
        two_g,
        two_part,
        out_g,
        full_qkv,
        mixed_all,
        tokens,
        grad_resid,
        w_ada,
    )
    outs = assemble(
        sizes,
        qkv_sum,
        one_sum,
        two_sum,
        part_sum,
        out_sum,
        mod_all,
        silu_all,
        o_small,
        block_out,
        grad_latents,
        o_cond,
    )
    shapes = (latents.shape, latents.shape, cond.shape, w_ada.shape, b_ada.shape, w_qkv.shape, b_qv.shape)
    shapes += (w_out.shape, b_out.shape, w_one.shape, b_one.shape, w_two.shape, b_two.shape)
    return tuple(out.reshape(want) for out, want in zip(outs, shapes))


def solution(mesh):
    owned = P(("fsdp", "seq"), None)
    owned_bias = P(("fsdp", "seq"))
    token_spec = P(("rep", "fsdp"), "seq", None)
    cond_spec = P(("rep", "fsdp"), None)
    weights = (owned, owned_bias) * 5
    in_specs = (token_spec, cond_spec) + weights + (token_spec,)
    out_specs = (token_spec, token_spec, cond_spec) + weights
    return jax.shard_map(
        on_device, mesh=mesh, in_specs=in_specs, out_specs=out_specs, check_vma=False
    )
```
